32 devices in a mesh: rep: 2 (over x), dp: 16 (over z, y, core).
Axes of the slice: x: 2, y: 2, z: 4, core: 2. Of those that a mesh axis runs over, the one named last changes fastest.
Arguments:
- hidden: bfloat16 [2, 2, 1, 1024, 768], P('rep', None, None, 'dp')
- bounds: int32 [2, 2, 1, 65], P('rep'), may hold values from 0 to 1024, as said below
- cotangent: bfloat16 [2, 2, 1, 1024, 768], P('rep', None, None, 'dp'), may hold values from -6 to 6
- weights: float32 [2, 9216, 768], P(None, 'dp')
- small_params: float32 [2, 9612], replicated
- first_big: float32 [2, 2, 9216, 768], P('rep', None, 'dp')
- second_big: float32 [2, 2, 9216, 768], P('rep', None, 'dp')
- first_small: float32 [2, 2, 9612], P('rep')
- second_small: float32 [2, 2, 9612], P('rep')
- outer_big: float32 [2, 9216, 768], P(None, 'dp'), may hold values from -0.012 to 0.012
- outer_small: float32 [2, 9612], replicated, may hold values from -0.06 to 0.06
Outputs:
- outputs: float32 [2, 2, 1, 1024, 768], P('rep', None, None, 'dp')
- input_grads: float32 [2, 2, 1, 1024, 768], P('rep', None, None, 'dp')
- first_big_new: float32 [2, 2, 9216, 768], P('rep', None, 'dp')
- second_big_new: float32 [2, 2, 9216, 768], P('rep', None, 'dp')
- first_small_new: float32 [2, 2, 9612], P('rep')
- second_small_new: float32 [2, 2, 9612], P('rep')
- outer_big_new: float32 [2, 9216, 768], P(None, 'dp')
- outer_small_new: float32 [2, 9612], replicated
- weights_new: float32 [2, 9216, 768], P(None, 'dp')
- small_new: float32 [2, 9612], replicated
- weights_low: bfloat16 [2, 9216, 768], P(None, 'dp')
The draws below stay inside these ranges and needn't reach their ends.
Inputs may be any that keep to these rules, and one draw needn't show every extreme that they name: For each sequence bounds[..., 0] = 0, the entries rise strictly, every segment holds 2 or more positions, and bounds[..., 64] is the sequence's length, 256 or more; bounds[0, 0, 0, 64] = 1024.
All inputs are finite; a program needn't handle non-finite values.
Results may differ from the reference program's by a relative error of at most 0.025.
Values may be sent and summed in bfloat16 or wider, within the bound.
A program may use at most 512 MiB of HBM per device.

```python
import math
import jax
import jax.numpy as jnp
from jax import lax

D = 768
HEADS = 12
HEAD_DIM = 64
FF = 3072
LANDMARKS = 64
TAPS = 33
NS_ITERS = 6
LAYERS = 2
MICRO = 2
STEP_COUNT = 5
SEQS = 1
REPS = 2
CAP = 1024
WROWS = 9216
SMALL = 9612


def draw_hidden(key, part):
    full_shape = (REPS, MICRO, SEQS, CAP, D)
    rough_key, amp_key, phase_key = jax.random.split(key, 3)
    rough_part = jax.random.normal(rough_key, full_shape, jnp.float32)
    amplitude = 0.35 * jax.random.normal(amp_key, (REPS, MICRO, SEQS, 8, D), jnp.float32)
    phases = jax.random.uniform(phase_key, (REPS, MICRO, SEQS, 8, D), jnp.float32, 0.0, 2.0 * math.pi)
    where_at = jnp.arange(CAP, dtype=jnp.float32) / CAP
    result = 0.8 * rough_part
    for harmonic in range(8):
        angles = math.pi * (harmonic + 1) * where_at[:, None] + phases[:, :, :, harmonic, None, :]
        result = result + amplitude[:, :, :, harmonic, None, :] * jnp.cos(angles)
    return result.astype(jnp.bfloat16)


def draw_bounds(key, part):
    length_key, jitter_key = jax.random.split(key)
    drawn_lengths = jax.random.randint(length_key, (REPS, MICRO, SEQS), CAP // 4, CAP + 1)
    rep_index = jnp.arange(REPS, dtype=jnp.int32)[:, None, None]
    micro_index = jnp.arange(MICRO, dtype=jnp.int32)[None, :, None]
    seq_index = jnp.arange(SEQS, dtype=jnp.int32)[None, None, :]
    first_one = (rep_index == 0) & (micro_index == 0) & (seq_index == 0)
    lengths = jnp.where(first_one, CAP, drawn_lengths).astype(jnp.int32)
    quantum = lengths // LANDMARKS
    raw_bits = jax.random.randint(jitter_key, (REPS, MICRO, SEQS, LANDMARKS - 1), 0, 1 << 20)
    jitter = raw_bits % jnp.maximum(quantum // 2, 1)[..., None]
    interior = jnp.arange(1, LANDMARKS, dtype=jnp.int32)[None, None, None, :] * quantum[..., None] + jitter
    leading = jnp.zeros((REPS, MICRO, SEQS, 1), jnp.int32)
    return jnp.concatenate([leading, interior.astype(jnp.int32), lengths[..., None]], axis=-1)


def draw_weights(key, part):
    full_shape = (LAYERS, WROWS, D)
    base_draw = jax.random.normal(key, full_shape, jnp.float32)
    row_index = jnp.arange(WROWS)
    factor = jnp.where(row_index < 3 * D, D ** (-0.5), jnp.where(row_index < 4 * D, (D / 8.0) ** (-0.5), jnp.where(row_index < 4 * D + FF, D ** (-0.5), FF ** (-0.5))))
    return base_draw * factor[None, :, None]


def draw_small_params(key, part):
    normal_draw = jax.random.normal(key, (LAYERS, SMALL), jnp.float32)
    index_all = jnp.arange(SMALL)
    is_gain = (index_all >= 4 * D) & (index_all < 5 * D) | (index_all >= 6 * D) & (index_all < 7 * D)
    is_taps = index_all >= 8 * D + FF
    return jnp.where(is_gain[None, :], 1.0 + 0.15 * normal_draw, jnp.where(is_taps[None, :], 0.06 * normal_draw, 0.2 * normal_draw))


def big_grad_scale():
    row_index = jnp.arange(WROWS)
    factor = jnp.where(row_index < 2 * D, 0.05, jnp.where(row_index < 3 * D, 0.3, jnp.where(row_index < 4 * D, 0.25, jnp.where(row_index < 4 * D + FF, 0.3, 0.4))))
    return factor * (0.7 * MICRO * SEQS * CAP) ** 0.5


def small_grad_scale():
    index_all = jnp.arange(SMALL)
    factor = jnp.where(index_all < D, 0.05, jnp.where(index_all < 2 * D, 0.3, jnp.where(index_all < 8 * D, 0.7, jnp.where(index_all < 8 * D + FF, 0.3, 5.6))))
    return factor * (0.7 * MICRO * SEQS * CAP) ** 0.5


def draw_first_big(key, part):
    normal_draw = jax.random.normal(key, (REPS, LAYERS, WROWS, D), jnp.float32)
    return 0.11 * normal_draw * big_grad_scale()[None, None, :, None]


def draw_second_big(key, part):
    spread = jnp.exp(jax.random.uniform(key, (REPS, LAYERS, WROWS, D), jnp.float32, math.log(0.5), math.log(8.0)))
    scale_row = big_grad_scale()
    return 0.053 * spread * (scale_row * scale_row)[None, None, :, None]


def draw_first_small(key, part):
    normal_draw = jax.random.normal(key, (REPS, LAYERS, SMALL), jnp.float32)
    return 0.11 * normal_draw * small_grad_scale()[None, None, :]


def draw_second_small(key, part):
    spread = jnp.exp(jax.random.uniform(key, (REPS, LAYERS, SMALL), jnp.float32, math.log(0.5), math.log(8.0)))
    scale_row = small_grad_scale()
    return 0.053 * spread * (scale_row * scale_row)[None, None, :]


def block_scale(rng, dims, pieces, low, top_value):
    gain, own = 1.0, jax.random.fold_in(rng, 6)
    for axis_at, shards_of in pieces:
        heights = jnp.exp(jax.random.uniform(jax.random.fold_in(own, axis_at), (shards_of,), jnp.float32, low / len(pieces), top_value / len(pieces)))
        gain = gain * jnp.repeat(heights, dims[axis_at] // shards_of).reshape([-1 if axis == axis_at else 1 for axis in range(len(dims))])
    return gain


def noise(rng, dims, scale, limit, shards=(), kind=jnp.bfloat16):
    values = jax.random.normal(rng, dims, jnp.float32) * scale
    if len(shards) > 0:
        values = block_scale(rng, dims, shards, -0.22, 0.18) * values
    return jnp.clip(values, min=-limit, max=limit).astype(kind)


def setup_inputs(seed: int = 0) -> dict:
    splits = jax.random.split(jax.random.key(seed), 12)
    return {
        "hidden": draw_hidden(jax.random.fold_in(splits[11], 71), 0),
        "bounds": draw_bounds(jax.random.fold_in(splits[11], 71), 0),
        "cotangent": noise(splits[2], (REPS, MICRO, SEQS, CAP, D), 1.0, 6.0, ((0, 2), (3, 16))),
        "weights": draw_weights(jax.random.fold_in(splits[11], 71), 0),
        "small_params": draw_small_params(jax.random.fold_in(splits[11], 71), 0),
        "first_big": draw_first_big(jax.random.fold_in(splits[11], 71), 0),
        "second_big": draw_second_big(jax.random.fold_in(splits[11], 71), 0),
        "first_small": draw_first_small(jax.random.fold_in(splits[11], 71), 0),
        "second_small": draw_second_small(jax.random.fold_in(splits[11], 71), 0),
        "outer_big": noise(splits[9], (LAYERS, WROWS, D), 0.002, 0.012, ((1, 16),), jnp.float32),
        "outer_small": noise(splits[10], (LAYERS, SMALL), 0.01, 0.06, (), jnp.float32),
    }


PRECISE = lax.Precision.HIGHEST
ADAM_ONE = 0.9
ADAM_TWO = 0.95
ADAM_EPSILON = 1e-08
WEIGHT_DECAY = 0.1
LR_INNER = 0.04
LR_SMALL = 0.2
LR_OUTER = 0.7
MOMENTUM = 0.9

@jax.custom_vjp
def low(v):
    return lax.optimization_barrier(v.astype(jnp.bfloat16)).astype(jnp.float32)

@jax.custom_vjp
def low_back(v):
    return v

def low_keep(v):
    return (low(v), None)

def low_pass(kept, grad):
    return (grad,)

def back_keep(v):
    return (v, None)

def back_low(kept, grad):
    return (low(grad),)
low.defvjp(low_keep, low_pass)
low_back.defvjp(back_keep, back_low)

def exact_einsum(pattern, operand_one, operand_two):
    return jnp.einsum(pattern, operand_one, operand_two, precision=PRECISE)

def layer_norm(values, gain_vec, shift_vec):
    row_mean = lax.optimization_barrier(jnp.mean(values, axis=-1, keepdims=True))
    centred = values - row_mean
    variance = lax.optimization_barrier(jnp.mean(centred * centred, axis=-1, keepdims=True))
    return centred * lax.rsqrt(variance + 1e-05) * gain_vec + shift_vec

def pseudo_inverse(matrix):
    scale_sum = lax.optimization_barrier(jnp.sum(matrix * matrix, axis=(-2, -1), keepdims=True))
    approx = jnp.swapaxes(matrix, -1, -2) / scale_sum
    identity = jnp.eye(matrix.shape[-1], dtype=jnp.float32)
    for sweep_index in range(NS_ITERS):
        product = exact_einsum('...ij,...jk->...ik', matrix, approx)
        nested = 7.0 * identity - product
        nested = 15.0 * identity - exact_einsum('...ij,...jk->...ik', product, nested)
        nested = 13.0 * identity - exact_einsum('...ij,...jk->...ik', product, nested)
        approx = 0.25 * exact_einsum('...ij,...jk->...ik', approx, nested)
    return approx

def unpack(params):
    blocks = [params[index * D:(index + 1) * D] for index in range(8)]
    bias_up = params[8 * D:8 * D + FF]
    conv_taps = params[8 * D + FF:].reshape(HEADS, TAPS)
    return (blocks, bias_up, conv_taps)

def segments(bounds_row):
    positions = jnp.arange(CAP, dtype=jnp.int32)
    member = ((bounds_row[:, None, :-1] <= positions[None, :, None]) & (positions[None, :, None] < bounds_row[:, None, 1:])).astype(jnp.float32)
    counts = (bounds_row[:, 1:] - bounds_row[:, :-1]).astype(jnp.float32)
    valid_mask = (positions[None, :] < bounds_row[:, -1:]).astype(jnp.float32)
    return (member, counts, valid_mask)

def attention(queries, keys_all, values, query_marks, key_marks, valid_mask, conv_taps):
    seq_count, length, model_width = queries.shape
    scale = HEAD_DIM ** (-0.5)
    query_heads = queries.reshape(seq_count, length, HEADS, HEAD_DIM)
    key_heads = keys_all.reshape(seq_count, length, HEADS, HEAD_DIM)
    value_heads = values.reshape(seq_count, length, HEADS, HEAD_DIM)
    mark_queries = query_marks.reshape(seq_count, LANDMARKS, HEADS, HEAD_DIM)
    mark_keys = key_marks.reshape(seq_count, LANDMARKS, HEADS, HEAD_DIM)
    token_weights = jax.nn.softmax(scale * exact_einsum('sthe,smhe->shtm', query_heads, mark_keys), axis=-1)
    inverse = pseudo_inverse(jax.nn.softmax(scale * exact_einsum('sjhe,smhe->shjm', mark_queries, mark_keys), axis=-1))
    key_scores = scale * exact_einsum('sjhe,sthe->shjt', mark_queries, key_heads)
    key_scores = jnp.where(valid_mask[:, None, None, :] > 0, key_scores, -1e+30)
    key_weights = jax.nn.softmax(key_scores, axis=-1)
    summary = exact_einsum('shjt,sthe->shje', key_weights, value_heads)
    mixed_marks = exact_einsum('shij,shje->shie', inverse, summary)
    attended = exact_einsum('shtm,shme->sthe', token_weights, mixed_marks)
    masked = value_heads * valid_mask[:, :, None, None]
    half_width = TAPS // 2
    padded = jnp.pad(masked, ((0, 0), (half_width, half_width), (0, 0), (0, 0)))
    conv_out = conv_taps[:, 0][None, None, :, None] * padded[:, 0:length]
    for offset in range(1, TAPS):
        conv_out = conv_out + conv_taps[:, offset][None, None, :, None] * padded[:, offset:offset + length]
    return (attended + conv_out).reshape(seq_count, length, model_width)

def layer(inputs, weight_rows, params, member, counts, valid_mask):
    blocks, bias_up, conv_taps = unpack(params)
    low_rows = low(weight_rows)
    query_weight = low_rows[0:D]
    key_weight = low_rows[D:2 * D]
    value_weight = low_rows[2 * D:3 * D]
    out_weight = low_rows[3 * D:4 * D]
    up_weight = low_rows[4 * D:4 * D + FF]
    down_weight = low_rows[4 * D + FF:]
    low_in = low(inputs)
    queries = low_back(exact_einsum('std,de->ste', low_in, query_weight) + blocks[0])
    keys_all = low_back(exact_einsum('std,de->ste', low_in, key_weight))
    values = low_back(exact_einsum('std,de->ste', low_in, value_weight) + blocks[1])
    query_marks = exact_einsum('stm,ste->sme', member, queries) / counts[:, :, None]
    key_marks = exact_einsum('stm,ste->sme', member, keys_all) / counts[:, :, None]
    combined = attention(queries, keys_all, values, query_marks, key_marks, valid_mask, conv_taps)
    branch = low_back(exact_einsum('std,de->ste', low(combined), out_weight) + blocks[2])
    hidden_one = layer_norm(inputs + branch, blocks[4], blocks[5])
    upward = low_back(exact_einsum('std,fd->stf', low(hidden_one), up_weight) + bias_up)
    down_out = low_back(exact_einsum('stf,fd->std', low(jax.nn.gelu(upward)), down_weight) + blocks[3])
    return layer_norm(hidden_one + down_out, blocks[6], blocks[7])

def forward_all(activation, weight_all, small_all, member, counts, valid_mask):
    for level_index in range(LAYERS):
        activation = layer(activation, weight_all[level_index], small_all[level_index], member, counts, valid_mask)
    return activation

def reference(hidden, bounds, cotangent, weights, small_params, first_big, second_big, first_small, second_small, outer_big, outer_small):
    correct_one = 1.0 - ADAM_ONE ** STEP_COUNT
    correct_two = 1.0 - ADAM_TWO ** STEP_COUNT
    all_outputs, all_grads = ([], [])
    first_big_list, second_big_list, first_small_list, second_small_list = ([], [], [], [])
    delta_big_total = jnp.zeros(weights.shape, jnp.float32)
    delta_small_total = jnp.zeros(small_params.shape, jnp.float32)
    for replica in range(REPS):
        grad_big = jnp.zeros(weights.shape, jnp.float32)
        grad_small = jnp.zeros(small_params.shape, jnp.float32)
        replica_out, replica_grad = ([], [])
        for micro_index in range(MICRO):
            member, counts, valid_mask = segments(bounds[replica, micro_index])
            result, pullback = jax.vjp(lambda acts_in, weight_all, small_all: forward_all(acts_in, weight_all, small_all, member, counts, valid_mask), hidden[replica, micro_index].astype(jnp.float32), weights, small_params)
            seed_grad = cotangent[replica, micro_index].astype(jnp.float32) * valid_mask[:, :, None]
            grad_in, grad_weights, grad_params = pullback(seed_grad)
            grad_big = grad_big + grad_weights
            grad_small = grad_small + grad_params
            replica_out.append(result)
            replica_grad.append(grad_in)
        all_outputs.append(jnp.stack(replica_out))
        all_grads.append(jnp.stack(replica_grad))
        new_first = ADAM_ONE * first_big[replica] + (1.0 - ADAM_ONE) * grad_big
        new_second = ADAM_TWO * second_big[replica] + (1.0 - ADAM_TWO) * grad_big * grad_big
        inner_big = weights - LR_INNER * (new_first / correct_one / (jnp.sqrt(new_second / correct_two) + ADAM_EPSILON) + WEIGHT_DECAY * weights)
        delta_big_total = delta_big_total + (weights - inner_big)
        new_first_small = ADAM_ONE * first_small[replica] + (1.0 - ADAM_ONE) * grad_small
        new_second_small = ADAM_TWO * second_small[replica] + (1.0 - ADAM_TWO) * grad_small * grad_small
        inner_small = small_params - LR_SMALL * (new_first_small / correct_one / (jnp.sqrt(new_second_small / correct_two) + ADAM_EPSILON))
        delta_small_total = delta_small_total + (small_params - inner_small)
        first_big_list.append(new_first)
        second_big_list.append(new_second)
        first_small_list.append(new_first_small)
        second_small_list.append(new_second_small)
    mean_big = delta_big_total / REPS
    mean_small = delta_small_total / REPS
    outer_big_new = MOMENTUM * outer_big + mean_big
    outer_small_new = MOMENTUM * outer_small + mean_small
    weights_new = weights - LR_OUTER * (mean_big + MOMENTUM * outer_big_new)
    small_new = small_params - LR_OUTER * (mean_small + MOMENTUM * outer_small_new)
    return (jnp.stack(all_outputs), jnp.stack(all_grads), jnp.stack(first_big_list), jnp.stack(second_big_list), jnp.stack(first_small_list), jnp.stack(second_small_list), outer_big_new, outer_small_new, weights_new, small_new, weights_new.astype(jnp.bfloat16))
```

```python
import functools

import jax
import jax.numpy as jnp
from jax import lax
from jax.experimental import pallas as pl
from jax.experimental.pallas import tpu as pltpu
from jax.sharding import PartitionSpec as P

D = 768
HEADS = 12
FF = 3072
TAPS = 33
NS_ITERS = 6
LAYERS = 2
MICRO = 2
STEP_COUNT = 5


PRECISE = lax.Precision.HIGHEST
ADAM_ONE = 0.9
ADAM_TWO = 0.95
ADAM_EPSILON = 1e-08
WEIGHT_DECAY = 0.1
LR_INNER = 0.04
LR_SMALL = 0.2
LR_OUTER = 0.7
MOMENTUM = 0.9

HEAD_DIM = 64
MARKS = 64
HALF = TAPS // 2
PAIRS = HEADS // 2
LANES = 128
SCALE = HEAD_DIM**-0.5
NEG = -1e30
MESH = pl.DeviceIdType.MESH
F32 = jnp.float32
BF16 = jnp.bfloat16
NN = (((1,), (0,)), ((), ()))
NT = (((1,), (1,)), ((), ()))
TN = (((0,), (0,)), ((), ()))


def mm(a, b, dims=NN):
    return lax.dot_general(a, b, dims, preferred_element_type=F32)


def halves(a):
    high = a.astype(BF16)
    return high, (a - high.astype(F32)).astype(BF16)


def mm_left(a, b, dims=NN):
    high, rest = halves(a)
    return mm(high, b, dims) + mm(rest, b, dims)


def mm_both(a, b, dims=NN):
    ah, al = halves(a)
    bh, bl = halves(b)
    return mm(ah, bh, dims) + (mm(ah, bl, dims) + mm(al, bh, dims))


def exact(a, b, dims=NN):
    return lax.dot_general(a, b, dims, precision=PRECISE, preferred_element_type=F32)


def iota(shape, dim):
    return lax.broadcasted_iota(jnp.int32, shape, dim)


def diagonal_blocks():
    return (iota((LANES, LANES), 0) < MARKS) == (iota((LANES, LANES), 1) < HEAD_DIM)


def unit():
    return (iota((LANES, LANES), 0) == iota((LANES, LANES), 1)).astype(F32)


def per_head(marks):
    first = iota(marks.shape, 1) < HEAD_DIM
    return jnp.concatenate([jnp.where(first, marks, 0.0), jnp.where(first, 0.0, marks)], axis=0)


def head_sums(a):
    rows, cols = a.shape
    split = a.reshape(2, rows // 2, cols)
    return jnp.broadcast_to(jnp.sum(split, axis=1, keepdims=True), split.shape).reshape(rows, cols)


def head_tops(a):
    rows, cols = a.shape
    split = a.reshape(2, rows // 2, cols)
    return jnp.broadcast_to(jnp.max(split, axis=1, keepdims=True), split.shape).reshape(rows, cols)


def band(taps_row):
    wide = jnp.broadcast_to(taps_row, (LANES, 2 * LANES))
    return pltpu.roll(wide, 0, 1, stride=1, stride_axis=0)


def convolve(padded, bands, length, store):
    first = iota((LANES, LANES), 1) < HEAD_DIM
    pairs = [halves(one) for one in bands]

    def block(at, carry):
        start = pl.multiple_of(at * LANES, LANES)
        window = padded[pl.ds(start, 2 * LANES), :]
        out = [mm(high, window) + mm(rest, window) for high, rest in pairs]
        store(start, jnp.where(first, out[0], out[1]))
        return carry

    lax.fori_loop(0, length // LANES, block, 0)


def attend(queries, keys, values, low_marks, high_marks, taps, keep, padded, blended, result):
    length = queries.shape[0]
    at = iota((MARKS, length), 1)
    member = ((low_marks <= at) & (at < high_marks)).astype(F32).astype(BF16)
    counts = (high_marks - low_marks).astype(F32)
    blocks, eye = diagonal_blocks(), unit()
    q_marks = per_head(mm(member, queries) / counts)
    k_marks = per_head(mm(member, keys) / counts)
    scores = jnp.where(blocks, SCALE * exact(q_marks, k_marks, NT), NEG)
    weights = jnp.exp(scores - jnp.max(scores, axis=1, keepdims=True))
    kernel = weights / jnp.sum(weights, axis=1, keepdims=True)
    total = head_sums(jnp.broadcast_to(jnp.sum(kernel * kernel, axis=1, keepdims=True), kernel.shape))
    inverse = kernel.T / total
    keep["q_marks"][...] = q_marks
    keep["k_marks"][...] = k_marks
    keep["kernel"][...] = kernel
    keep["total"][...] = total
    for sweep in range(NS_ITERS):
        product = exact(kernel, inverse)
        one = 7.0 * eye - product
        two = 15.0 * eye - exact(product, one)
        three = 13.0 * eye - exact(product, two)
        keep["inverse"][sweep] = inverse
        keep["product"][sweep] = product
        keep["two"][sweep] = two
        keep["three"][sweep] = three
        inverse = 0.25 * exact(inverse, three)
    keep["inverse"][NS_ITERS] = inverse
    valid = at[:1] < high_marks[MARKS - 1 :]
    key_scores = jnp.where(valid, SCALE * mm_left(q_marks, keys, NT), NEG)
    key_exp = jnp.where(valid, jnp.exp(key_scores - jnp.max(key_scores, axis=1, keepdims=True)), 0.0)
    key_weights = key_exp / jnp.sum(key_exp, axis=1, keepdims=True)
    keep["key_weights"][...] = key_weights
    summary = jnp.where(blocks, mm_left(key_weights, values), 0.0)
    mixed = exact(inverse, summary)
    keep["summary"][...] = summary
    keep["mixed"][...] = mixed
    token_scores = SCALE * mm_left(k_marks, queries, NT)
    token_exp = jnp.exp(token_scores - head_tops(token_scores))
    token_weights = token_exp / head_sums(token_exp)
    keep["token_weights"][...] = token_weights
    blended[...] = mm_both(token_weights, mixed, TN)
    valid_column = iota((length, 1), 0) < high_marks[MARKS - 1 :]
    padded[0:HALF, :] = jnp.zeros((HALF, LANES), BF16)
    padded[HALF : HALF + length, :] = jnp.where(valid_column, values, jnp.zeros_like(values))
    padded[HALF + length :, :] = jnp.zeros((LANES - HALF, LANES), BF16)

    def store(start, block):
        result[pl.ds(start, LANES), :] = (blended[pl.ds(start, LANES), :] + block).astype(BF16)

    convolve(padded, [band(taps[0:1]), band(taps[1:2])], length, store)


def attend_back(grads, queries, keys, values, low_marks, high_marks, low_row, high_row, taps, keep, padded, padded_grads, blended, result, grad_taps):
    length = grads.shape[0]
    at = iota((length, MARKS), 0)
    member = ((low_row <= at) & (at < high_row)).astype(F32).astype(BF16)
    counts = (high_marks - low_marks).astype(F32)
    blocks, eye = diagonal_blocks(), unit()
    q_marks, k_marks = keep["q_marks"][...], keep["k_marks"][...]
    token_weights, key_weights = keep["token_weights"][...], keep["key_weights"][...]
    summary, mixed = keep["summary"][...], keep["mixed"][...]
    kernel = keep["kernel"][...]
    inverse = keep["inverse"][NS_ITERS]
    grad_mixed = jnp.where(blocks, mm_left(token_weights, grads), 0.0)
    grad_token = token_weights * mm_left(mixed, grads, NT)
    grad_token = SCALE * (grad_token - token_weights * head_sums(grad_token))
    grad_summary = exact(inverse, grad_mixed, TN)
    grad_inverse = exact(grad_mixed, summary, NT)
    grad_kernel = jnp.zeros_like(kernel)
    for sweep in reversed(range(NS_ITERS)):
        before, product = keep["inverse"][sweep], keep["product"][sweep]
        one = 7.0 * eye - product
        two, three = keep["two"][sweep], keep["three"][sweep]
        grad_three = 0.25 * exact(before, grad_inverse, TN)
        grad_two = -exact(product, grad_three, TN)
        grad_one = -exact(product, grad_two, TN)
        grad_product = -(exact(grad_three, two, NT) + exact(grad_two, one, NT) + grad_one)
        grad_kernel = grad_kernel + exact(grad_product, before, NT)
        grad_inverse = 0.25 * exact(grad_inverse, three, NT) + exact(kernel, grad_product, TN)
    total = keep["total"][...]
    turned = grad_inverse.T / total
    weighted = jnp.sum(jnp.where(blocks, turned * kernel, 0.0), axis=1, keepdims=True)
    weighted = head_sums(jnp.broadcast_to(weighted, kernel.shape))
    grad_kernel = grad_kernel + turned - 2.0 * kernel * weighted / total
    grad_scores = SCALE * kernel * (grad_kernel - jnp.sum(kernel * grad_kernel, axis=1, keepdims=True))
    grad_q_marks = exact(grad_scores, k_marks)
    grad_k_marks = exact(grad_scores, q_marks, TN)
    grad_k_marks = grad_k_marks + jnp.where(blocks, mm_left(grad_token, queries), 0.0)
    grad_key = mm_left(grad_summary, values, NT) - jnp.sum(grad_summary * summary, axis=1, keepdims=True)
    grad_key = SCALE * key_weights * grad_key
    grad_q_marks = grad_q_marks + jnp.where(blocks, mm_left(grad_key, keys), 0.0)
    grad_q_marks = (grad_q_marks[:MARKS] + grad_q_marks[MARKS:]) / counts
    grad_k_marks = (grad_k_marks[:MARKS] + grad_k_marks[MARKS:]) / counts
    high, rest = halves(grad_q_marks)
    result[0] = (mm_both(grad_token, k_marks, TN) + mm(member, high) + mm(member, rest)).astype(BF16)
    high, rest = halves(grad_k_marks)
    result[1] = (mm_both(grad_key, q_marks, TN) + mm(member, high) + mm(member, rest)).astype(BF16)
    blended[...] = mm_both(key_weights, grad_summary, TN)
    last = high_marks[MARKS - 1 :]
    valid_column = iota((length, 1), 0) < last
    padded[0:HALF, :] = jnp.zeros((HALF, LANES), BF16)
    padded[HALF : HALF + length, :] = jnp.where(valid_column, values, jnp.zeros_like(values))
    padded[HALF + length :, :] = jnp.zeros((LANES - HALF, LANES), BF16)
    padded_grads[0:HALF, :] = jnp.zeros((HALF, LANES), BF16)
    padded_grads[HALF : HALF + length, :] = grads
    padded_grads[HALF + length :, :] = jnp.zeros((LANES - HALF, LANES), BF16)

    def store(start, block):
        rows = start + iota((LANES, 1), 0)
        total_rows = blended[pl.ds(start, LANES), :] + jnp.where(rows < last, block, 0.0)
        result[2, pl.ds(start, LANES), :] = total_rows.astype(BF16)

    convolve(padded_grads, [band(taps[2:3]), band(taps[3:4])], length, store)
    first = iota((LANES, LANES), 1) < HEAD_DIM

    def block(step, carry):
        start = pl.multiple_of(step * LANES, LANES)
        own = padded_grads[pl.ds(start + HALF, LANES), :]
        window = padded[pl.ds(start, 2 * LANES), :]
        none = jnp.zeros_like(own)
        return (
            carry[0] + mm(jnp.where(first, own, none), window, NT),
            carry[1] + mm(jnp.where(first, none, own), window, NT),
        )

    start_sum = jnp.zeros((LANES, 2 * LANES), F32)
    sums = lax.fori_loop(0, length // LANES, block, (start_sum, start_sum))
    wide = 2 * LANES
    for head in range(2):
        folded = sums[head][0:8]
        for group in range(1, LANES // 8):
            rows = sums[head][8 * group : 8 * group + 8]
            folded = folded + pltpu.roll(rows, wide - 8 * group, 1)
        line = folded[0:1]
        for row in range(1, 8):
            line = line + pltpu.roll(folded[row : row + 1], wide - row, 1)
        grad_taps[head : head + 1, :] = line


TASKS = MICRO * PAIRS
KEPT = ("q_marks", "k_marks", "kernel", "total", "inverse", "product", "two", "three", "key_weights", "summary", "mixed", "token_weights")


def kept_shapes(length):
    square = (LANES, LANES)
    shapes = {name: square for name in KEPT}
    shapes["inverse"] = (NS_ITERS + 1,) + square
    for name in ("product", "two", "three"):
        shapes[name] = (NS_ITERS,) + square
    shapes["key_weights"] = shapes["token_weights"] = (LANES, length)
    return shapes


def owner_of(task, count):
    return task * count // TASKS


def task_of(me, count):
    task = (me * TASKS + count - 1) // count
    return task, owner_of(task, count) == me


def greet(count):
    me = lax.axis_index("dp")
    barrier = pltpu.get_barrier_semaphore()

    def signal(step, carry):
        pl.semaphore_signal(barrier, inc=1, device_id={"dp": lax.rem(me + step, count)}, device_id_type=MESH)
        return carry

    lax.fori_loop(1, count, signal, 0)
    pl.semaphore_wait(barrier, count - 1)


def scatter_tasks(count, piece, source, slab, send, receive):
    me = lax.axis_index("dp")

    def one(step, finish):
        task = lax.rem(task_of(me, count)[0] + step, TASKS)
        owner = owner_of(task, count)
        micro = task // PAIRS
        lanes = pl.ds(pl.multiple_of(lax.rem(task, PAIRS) * LANES, LANES), LANES)
        rows = pl.ds(pl.multiple_of(me * piece, piece), piece)
        outgoing = source.at[:, micro, :, lanes]
        landing = slab.at[:, rows, :]

        @pl.when(owner != me)
        def _():
            copy = pltpu.make_async_remote_copy(outgoing, landing, send.at[task], receive.at[me], device_id={"dp": owner}, device_id_type=MESH)
            if finish:
                copy.wait_send()
            else:
                copy.start()

        @pl.when((owner == me) & (not finish))
        def _():
            pltpu.make_async_copy(outgoing, landing, receive.at[me]).start()

    def run(finish):
        def body(step, carry):
            one(step, finish)
            return carry

        lax.fori_loop(0, TASKS, body, 0)

    return run


def await_slab(count, piece, slab, receive):
    def body(origin, carry):
        landing = slab.at[:, pl.ds(pl.multiple_of(origin * piece, piece), piece), :]
        pltpu.make_async_copy(landing, landing, receive.at[origin]).wait()
        return carry

    lax.fori_loop(0, count, body, 0)


def return_rows(count, piece, result, target, send, receive):
    me = lax.axis_index("dp")
    task = task_of(me, count)[0]
    micro = task // PAIRS
    lanes = pl.ds(pl.multiple_of(lax.rem(task, PAIRS) * LANES, LANES), LANES)

    def run(finish):
        def body(step, carry):
            peer = lax.rem(me + step, count)
            rows = pl.ds(pl.multiple_of(peer * piece, piece), piece)
            outgoing = result.at[:, rows, :]
            landing = target.at[:, micro, :, lanes]

            @pl.when(peer != me)
            def _():
                copy = pltpu.make_async_remote_copy(outgoing, landing, send.at[peer], receive.at[task], device_id={"dp": peer}, device_id_type=MESH)
                if finish:
                    copy.wait_send()
                else:
                    copy.start()

            @pl.when((peer == me) & (not finish))
            def _():
                pltpu.make_async_copy(outgoing, landing, receive.at[task]).start()

            return carry

        lax.fori_loop(0, count, body, 0)

    return run


def await_rows(target, receive):
    def body(task, carry):
        lanes = pl.ds(pl.multiple_of(lax.rem(task, PAIRS) * LANES, LANES), LANES)
        landing = target.at[:, task // PAIRS, :, lanes]
        pltpu.make_async_copy(landing, landing, receive.at[task]).wait()
        return carry

    lax.fori_loop(0, TASKS, body, 0)


def forward_kernel(count, piece, qkv, low_col, high_col, taps, mixed_rows, slab, *refs):
    keep = dict(zip(KEPT, refs))
    padded, blended, result, send_one, receive_one, send_two, receive_two = refs[len(KEPT) :]
    me = lax.axis_index("dp")
    task, owns = task_of(me, count)
    greet(count)
    out = scatter_tasks(count, piece, qkv, slab, send_one, receive_one)
    out(False)
    back = return_rows(count, piece, result, mixed_rows, send_two, receive_two)

    @pl.when(owns)
    def _():
        micro, pair = task // PAIRS, lax.rem(task, PAIRS)
        await_slab(count, piece, slab, receive_one)
        attend(slab[0], slab[1], slab[2], low_col[micro], high_col[micro], taps[pair], keep, padded, blended, result.at[0])
        back(False)

    out(True)
    await_rows(mixed_rows, receive_two)

    @pl.when(owns)
    def _():
        back(True)


def backward_kernel(count, piece, grads, low_col, high_col, low_row, high_row, taps, slab, *refs):
    keep = dict(zip(KEPT, refs))
    out_grads, grad_taps, grad_slab, padded, padded_grads, blended, result, send_one, receive_one, send_two, receive_two = refs[len(KEPT) :]
    me = lax.axis_index("dp")
    task, owns = task_of(me, count)
    greet(count)
    out = scatter_tasks(count, piece, grads, grad_slab, send_one, receive_one)
    out(False)
    back = return_rows(count, piece, result, out_grads, send_two, receive_two)
    grad_taps[...] = jnp.zeros(grad_taps.shape, F32)

    @pl.when(owns)
    def _():
        micro, pair = task // PAIRS, lax.rem(task, PAIRS)
        await_slab(count, piece, grad_slab, receive_one)
        attend_back(
            grad_slab[0], slab[0], slab[1], slab[2], low_col[micro], high_col[micro], low_row[micro], high_row[micro],
            taps[pair], keep, padded, padded_grads, blended, result, grad_taps.at[pair],
        )
        back(False)

    out(True)
    await_rows(out_grads, receive_two)

    @pl.when(owns)
    def _():
        back(True)


VMEM = pl.BlockSpec(memory_space=pltpu.VMEM)
DMA = pltpu.SemaphoreType.DMA


def attention_forward(count, qkv, marks, taps, ident):
    piece = qkv.shape[2]
    length = piece * count
    shapes = kept_shapes(length)
    results = pl.pallas_call(
        functools.partial(forward_kernel, count, piece),
        out_shape=[
            jax.ShapeDtypeStruct((1, MICRO, piece, D), BF16),
            jax.ShapeDtypeStruct((3, length, LANES), BF16),
        ]
        + [jax.ShapeDtypeStruct(shapes[name], F32) for name in KEPT],
        in_specs=[VMEM] * 4,
        out_specs=[VMEM] * (2 + len(KEPT)),
        scratch_shapes=[
            pltpu.VMEM((length + LANES, LANES), BF16),
            pltpu.VMEM((length, LANES), F32),
            pltpu.VMEM((1, length, LANES), BF16),
            DMA((TASKS,)),
            DMA((count,)),
            DMA((count,)),
            DMA((TASKS,)),
        ],
        compiler_params=pltpu.CompilerParams(collective_id=ident, has_side_effects=True, vmem_limit_bytes=60 << 20),
        name="attend_forward",
    )(qkv, marks[0], marks[1], taps)
    return results[0][0], results[1:]


def attention_backward(count, grads, marks, taps, kept, ident):
    piece = grads.shape[2]
    length = piece * count
    return pl.pallas_call(
        functools.partial(backward_kernel, count, piece),
        out_shape=[
            jax.ShapeDtypeStruct((3, MICRO, piece, D), BF16),
            jax.ShapeDtypeStruct((PAIRS, 2, 2 * LANES), F32),
        ],
        in_specs=[VMEM] * (7 + len(KEPT)),
        out_specs=[VMEM] * 2,
        scratch_shapes=[
            pltpu.VMEM((1, length, LANES), BF16),
            pltpu.VMEM((length + LANES, LANES), BF16),
            pltpu.VMEM((length + LANES, LANES), BF16),
            pltpu.VMEM((length, LANES), F32),
            pltpu.VMEM((3, length, LANES), BF16),
            DMA((TASKS,)),
            DMA((count,)),
            DMA((count,)),
            DMA((TASKS,)),
        ],
        compiler_params=pltpu.CompilerParams(collective_id=ident, has_side_effects=True, vmem_limit_bytes=60 << 20),
        name="attend_backward",
    )(grads, *marks, taps, *kept)


def dense(a, b, dims=NN):
    return mm(a, b, dims)


def layer_norm(values, gain_vec, shift_vec):
    row_mean = jnp.mean(values, axis=-1, keepdims=True)
    centred = values - row_mean
    variance = jnp.mean(centred * centred, axis=-1, keepdims=True)
    return centred * lax.rsqrt(variance + 1e-05) * gain_vec + shift_vec


def unpack(params):
    blocks = [params[index * D : (index + 1) * D] for index in range(8)]
    bias_up = params[8 * D : 8 * D + FF]
    conv_taps = params[8 * D + FF :].reshape(HEADS, TAPS)
    return (blocks, bias_up, conv_taps)


def pair_taps(conv_taps):
    both = jnp.stack([conv_taps.reshape(PAIRS, 2, TAPS), conv_taps[:, ::-1].reshape(PAIRS, 2, TAPS)], axis=1)
    both = both.reshape(PAIRS, 4, TAPS)
    return jnp.pad(both, ((0, 0), (0, 0), (0, 2 * LANES - TAPS)))


def split_rows(rows):
    return rows[: 3 * D].reshape(3, D, D), rows[3 * D : 4 * D], rows[4 * D : 4 * D + FF], rows[4 * D + FF :]


def forward_layer(count, inputs, rows, params, marks, ident):
    piece = inputs.shape[0] // MICRO
    blocks, bias_up, conv_taps = unpack(params)
    proj, out_weight, up_weight, down_weight = split_rows(rows)
    low_in = inputs.astype(BF16)
    bias = jnp.stack([blocks[0], jnp.zeros_like(blocks[0]), blocks[1]])
    qkv = jnp.stack([(dense(low_in, proj[part]) + bias[part]).astype(BF16) for part in range(3)])
    low_comb, kept = attention_forward(count, qkv.reshape(3, MICRO, piece, D), marks, pair_taps(conv_taps), ident)
    low_comb = low_comb.reshape(MICRO * piece, D)
    resid_one = inputs + (dense(low_comb, out_weight) + blocks[2])
    hidden_one = layer_norm(resid_one, blocks[4], blocks[5])
    low_hidden = hidden_one.astype(BF16)
    upward = dense(low_hidden, up_weight, NT) + bias_up
    low_act = jax.nn.gelu(upward).astype(BF16)
    resid_two = hidden_one + (dense(low_act, down_weight) + blocks[3])
    output = layer_norm(resid_two, blocks[6], blocks[7])
    return output, (low_in, kept, low_comb, resid_one, low_hidden, upward, low_act, resid_two)


def backward_layer(count, grad_output, rows, params, marks, state, ident):
    low_in, kept, low_comb, resid_one, low_hidden, upward, low_act, resid_two = state
    total = low_in.shape[0]
    piece = total // MICRO
    blocks, bias_up, conv_taps = unpack(params)
    proj, out_weight, up_weight, down_weight = split_rows(rows)
    _, pull_two = jax.vjp(layer_norm, resid_two, blocks[6], blocks[7])
    grad_two, grad_gain_two, grad_shift_two = pull_two(grad_output)
    low_down = grad_two.astype(BF16)
    grad_bias_down = jnp.sum(low_down.astype(F32), axis=0)
    grad_act = dense(low_down, down_weight, NT)
    _, pull_gelu = jax.vjp(jax.nn.gelu, upward)
    low_up = pull_gelu(grad_act)[0].astype(BF16)
    grad_bias_up = jnp.sum(low_up.astype(F32), axis=0)
    grad_hidden = grad_two + dense(low_up, up_weight)
    _, pull_one = jax.vjp(layer_norm, resid_one, blocks[4], blocks[5])
    grad_one, grad_gain_one, grad_shift_one = pull_one(grad_hidden)
    low_branch = grad_one.astype(BF16)
    grad_bias_out = jnp.sum(low_branch.astype(F32), axis=0)
    grad_comb = dense(low_branch, out_weight, NT).astype(BF16)
    low_grads, grad_taps = attention_backward(count, grad_comb.reshape(1, MICRO, piece, D), marks, pair_taps(conv_taps), kept, ident)
    low_grads = low_grads.reshape(3, total, D)
    grad_bias_q = jnp.sum(low_grads[0].astype(F32), axis=0)
    grad_bias_v = jnp.sum(low_grads[2].astype(F32), axis=0)
    grad_in = grad_one + sum(dense(low_grads[part], proj[part], NT) for part in range(3))
    parts = [dense(low_in, low_grads[part], TN).astype(BF16) for part in range(3)]
    parts = parts + [
        dense(low_comb, low_branch, TN).astype(BF16),
        dense(low_up, low_hidden, TN).astype(BF16),
        dense(low_act, low_down, TN).astype(BF16),
    ]
    grad_small = jnp.concatenate(
        [
            grad_bias_q,
            grad_bias_v,
            grad_bias_out,
            grad_bias_down,
            grad_gain_one,
            grad_shift_one,
            grad_gain_two,
            grad_shift_two,
            grad_bias_up,
            grad_taps[:, :, :TAPS].reshape(-1),
        ]
    )
    return grad_in, jnp.concatenate(parts, axis=0), grad_small


def adam(weights, first, second, grad, rate, decay):
    correct_one = 1.0 - ADAM_ONE**STEP_COUNT
    correct_two = 1.0 - ADAM_TWO**STEP_COUNT
    new_first = ADAM_ONE * first + (1.0 - ADAM_ONE) * grad
    new_second = ADAM_TWO * second + (1.0 - ADAM_TWO) * grad * grad
    step = new_first / correct_one / (jnp.sqrt(new_second / correct_two) + ADAM_EPSILON)
    return new_first, new_second, rate * (step + decay * weights)


def shards(
    hidden,
    bounds,
    cotangent,
    weights,
    small_params,
    first_big,
    second_big,
    first_small,
    second_small,
    outer_big,
    outer_small,
):
    count = lax.axis_size("dp")
    piece = hidden.shape[3]
    total = MICRO * piece
    held = [lax.all_gather(weights[level].astype(BF16), "dp", axis=0, tiled=True) for level in range(LAYERS)]
    edges = bounds[0, :, 0, :]
    low_edges, high_edges = edges[:, :-1], edges[:, 1:]
    marks = (low_edges[:, :, None], high_edges[:, :, None], low_edges[:, None, :], high_edges[:, None, :])
    positions = lax.axis_index("dp") * piece + jnp.arange(piece, dtype=jnp.int32)
    valid = (positions[None, :] < edges[:, -1:]).astype(F32).reshape(total, 1)
    activation = hidden[0, :, 0].reshape(total, D).astype(F32)
    states = []
    for level in range(LAYERS):
        activation, state = forward_layer(count, activation, held[level], small_params[level], marks, 1)
        states.append(state)
    gradient = cotangent[0, :, 0].reshape(total, D).astype(F32) * valid
    grad_parts, small_parts = [None] * LAYERS, [None] * LAYERS
    for level in reversed(range(LAYERS)):
        gradient, grad_rows, small_parts[level] = backward_layer(count, gradient, held[level], small_params[level], marks, states[level], 2)
        grad_parts[level] = lax.psum_scatter(grad_rows, "dp", scatter_dimension=0, tiled=True).astype(F32)
    grad_big = jnp.stack(grad_parts)
    grad_small = lax.psum(jnp.stack(small_parts), "dp")
    new_first, new_second, delta_big = adam(weights, first_big[0], second_big[0], grad_big, LR_INNER, WEIGHT_DECAY)
    new_first_small, new_second_small, delta_small = adam(small_params, first_small[0], second_small[0], grad_small, LR_SMALL, 0.0)
    reps = lax.axis_size("rep")
    mean_big = lax.psum(delta_big.astype(BF16), "rep").astype(F32) / reps
    mean_small = lax.psum(delta_small.astype(BF16), "rep").astype(F32) / reps
    outer_big_new = MOMENTUM * outer_big + mean_big
    outer_small_new = MOMENTUM * outer_small + mean_small
    weights_new = weights - LR_OUTER * (mean_big + MOMENTUM * outer_big_new)
    small_new = small_params - LR_OUTER * (mean_small + MOMENTUM * outer_small_new)
    shape = (1, MICRO, 1, piece, D)
    return (
        activation.reshape(shape),
        gradient.reshape(shape),
        new_first[None],
        new_second[None],
        new_first_small[None],
        new_second_small[None],
        outer_big_new,
        outer_small_new,
        weights_new,
        small_new,
        weights_new.astype(BF16),
    )


def solution(mesh):
    placed = (
        P("rep", None, None, "dp", None),
        P("rep", None, None, None),
        P("rep", None, None, "dp", None),
        P(None, "dp", None),
        P(),
        P("rep", None, "dp", None),
        P("rep", None, "dp", None),
        P("rep", None, None),
        P("rep", None, None),
        P(None, "dp", None),
        P(),
    )
    return jax.shard_map(
        shards,
        mesh=mesh,
        in_specs=placed,
        out_specs=(
            P("rep", None, None, "dp", None),
            P("rep", None, None, "dp", None),
            P("rep", None, "dp", None),
            P("rep", None, "dp", None),
            P("rep", None, None),
            P("rep", None, None),
            P(None, "dp", None),
            P(),
            P(None, "dp", None),
            P(),
            P(None, "dp", None),
        ),
        check_vma=False,
    )
```

```python
import functools

import jax
import jax.numpy as jnp
from jax import lax
from jax.experimental import pallas as pl
from jax.experimental.pallas import tpu as pltpu
from jax.sharding import PartitionSpec as P

D = 768
HEADS = 12
FF = 3072
TAPS = 33
NS_ITERS = 6
LAYERS = 2
MICRO = 2
STEP_COUNT = 5


PRECISE = lax.Precision.HIGHEST
ADAM_ONE = 0.9
ADAM_TWO = 0.95
ADAM_EPSILON = 1e-08
WEIGHT_DECAY = 0.1
LR_INNER = 0.04
LR_SMALL = 0.2
LR_OUTER = 0.7
MOMENTUM = 0.9

HEAD_DIM = 64
MARKS = 64
HALF = TAPS // 2
PAIRS = HEADS // 2
LANES = 128
SCALE = HEAD_DIM**-0.5
NEG = -1e30
MESH = pl.DeviceIdType.MESH
F32 = jnp.float32
BF16 = jnp.bfloat16
NN = (((1,), (0,)), ((), ()))
NT = (((1,), (1,)), ((), ()))
TN = (((0,), (0,)), ((), ()))


def mm(a, b, dims=NN):
    return lax.dot_general(a, b, dims, preferred_element_type=F32)


def halves(a):
    high = a.astype(BF16)
    return high, (a - high.astype(F32)).astype(BF16)


def mm_left(a, b, dims=NN):
    high, rest = halves(a)
    return mm(high, b, dims) + mm(rest, b, dims)


def mm_both(a, b, dims=NN):
    ah, al = halves(a)
    bh, bl = halves(b)
    return mm(ah, bh, dims) + (mm(ah, bl, dims) + mm(al, bh, dims))


def exact(a, b, dims=NN):
    return lax.dot_general(a, b, dims, precision=PRECISE, preferred_element_type=F32)


def iota(shape, dim):
    return lax.broadcasted_iota(jnp.int32, shape, dim)


def diagonal_blocks():
    return (iota((LANES, LANES), 0) < MARKS) == (iota((LANES, LANES), 1) < HEAD_DIM)


def unit():
    return (iota((LANES, LANES), 0) == iota((LANES, LANES), 1)).astype(F32)


def per_head(marks):
    first = iota(marks.shape, 1) < HEAD_DIM
    return jnp.concatenate([jnp.where(first, marks, 0.0), jnp.where(first, 0.0, marks)], axis=0)


def head_sums(a):
    rows, cols = a.shape
    split = a.reshape(2, rows // 2, cols)
    return jnp.broadcast_to(jnp.sum(split, axis=1, keepdims=True), split.shape).reshape(rows, cols)


def head_tops(a):
    rows, cols = a.shape
    split = a.reshape(2, rows // 2, cols)
    return jnp.broadcast_to(jnp.max(split, axis=1, keepdims=True), split.shape).reshape(rows, cols)


def band(taps_row):
    wide = jnp.broadcast_to(taps_row, (LANES, 2 * LANES))
    return pltpu.roll(wide, 0, 1, stride=1, stride_axis=0)


def convolve(padded, bands, length, store):
    first = iota((LANES, LANES), 1) < HEAD_DIM
    pairs = [halves(one) for one in bands]

    def block(at, carry):
        start = pl.multiple_of(at * LANES, LANES)
        window = padded[pl.ds(start, 2 * LANES), :]
        out = [mm(high, window) + mm(rest, window) for high, rest in pairs]
        store(start, jnp.where(first, out[0], out[1]))
        return carry

    lax.fori_loop(0, length // LANES, block, 0)


def attend(queries, keys, values, low_marks, high_marks, taps, keep, padded, blended, result):
    length = queries.shape[0]
    at = iota((MARKS, length), 1)
    member = ((low_marks <= at) & (at < high_marks)).astype(F32).astype(BF16)
    counts = (high_marks - low_marks).astype(F32)
    blocks, eye = diagonal_blocks(), unit()
    q_marks = per_head(mm(member, queries) / counts)
    k_marks = per_head(mm(member, keys) / counts)
    scores = jnp.where(blocks, SCALE * exact(q_marks, k_marks, NT), NEG)
    weights = jnp.exp(scores - jnp.max(scores, axis=1, keepdims=True))
    kernel = weights / jnp.sum(weights, axis=1, keepdims=True)
    total = head_sums(jnp.broadcast_to(jnp.sum(kernel * kernel, axis=1, keepdims=True), kernel.shape))
    inverse = kernel.T / total
    keep["q_marks"][...] = q_marks
    keep["k_marks"][...] = k_marks
    keep["kernel"][...] = kernel
    keep["total"][...] = total
    for sweep in range(NS_ITERS):
        product = exact(kernel, inverse)
        one = 7.0 * eye - product
        two = 15.0 * eye - exact(product, one)
        three = 13.0 * eye - exact(product, two)
        keep["inverse"][sweep] = inverse
        keep["product"][sweep] = product
        keep["two"][sweep] = two
        keep["three"][sweep] = three
        inverse = 0.25 * exact(inverse, three)
    keep["inverse"][NS_ITERS] = inverse
    valid = at[:1] < high_marks[MARKS - 1 :]
    key_scores = jnp.where(valid, SCALE * mm_left(q_marks, keys, NT), NEG)
    key_exp = jnp.where(valid, jnp.exp(key_scores - jnp.max(key_scores, axis=1, keepdims=True)), 0.0)
    key_weights = key_exp / jnp.sum(key_exp, axis=1, keepdims=True)
    keep["key_weights"][...] = key_weights
    summary = jnp.where(blocks, mm_left(key_weights, values), 0.0)
    mixed = exact(inverse, summary)
    keep["summary"][...] = summary
    keep["mixed"][...] = mixed
    token_scores = SCALE * mm_left(k_marks, queries, NT)
    token_exp = jnp.exp(token_scores - head_tops(token_scores))
    token_weights = token_exp / head_sums(token_exp)
    keep["token_weights"][...] = token_weights
    blended[...] = mm_both(token_weights, mixed, TN)
    valid_column = iota((length, 1), 0) < high_marks[MARKS - 1 :]
    padded[0:HALF, :] = jnp.zeros((HALF, LANES), BF16)
    padded[HALF : HALF + length, :] = jnp.where(valid_column, values, jnp.zeros_like(values))
    padded[HALF + length :, :] = jnp.zeros((LANES - HALF, LANES), BF16)

    def store(start, block):
        result[pl.ds(start, LANES), :] = (blended[pl.ds(start, LANES), :] + block).astype(BF16)

    convolve(padded, [band(taps[0:1]), band(taps[1:2])], length, store)


def attend_back(grads, queries, keys, values, low_marks, high_marks, low_row, high_row, taps, keep, padded, padded_grads, blended, result, grad_taps):
    length = grads.shape[0]
    at = iota((length, MARKS), 0)
    member = ((low_row <= at) & (at < high_row)).astype(F32).astype(BF16)
    counts = (high_marks - low_marks).astype(F32)
    blocks, eye = diagonal_blocks(), unit()
    q_marks, k_marks = keep["q_marks"][...], keep["k_marks"][...]
    token_weights, key_weights = keep["token_weights"][...], keep["key_weights"][...]
    summary, mixed = keep["summary"][...], keep["mixed"][...]
    kernel = keep["kernel"][...]
    inverse = keep["inverse"][NS_ITERS]
    grad_mixed = jnp.where(blocks, mm_left(token_weights, grads), 0.0)
    grad_token = token_weights * mm_left(mixed, grads, NT)
    grad_token = SCALE * (grad_token - token_weights * head_sums(grad_token))
    grad_summary = exact(inverse, grad_mixed, TN)
    grad_inverse = exact(grad_mixed, summary, NT)
    grad_kernel = jnp.zeros_like(kernel)
    for sweep in reversed(range(NS_ITERS)):
        before, product = keep["inverse"][sweep], keep["product"][sweep]
        one = 7.0 * eye - product
        two, three = keep["two"][sweep], keep["three"][sweep]
        grad_three = 0.25 * exact(before, grad_inverse, TN)
        grad_two = -exact(product, grad_three, TN)
        grad_one = -exact(product, grad_two, TN)
        grad_product = -(exact(grad_three, two, NT) + exact(grad_two, one, NT) + grad_one)
        grad_kernel = grad_kernel + exact(grad_product, before, NT)
        grad_inverse = 0.25 * exact(grad_inverse, three, NT) + exact(kernel, grad_product, TN)
    total = keep["total"][...]
    turned = grad_inverse.T / total
    weighted = jnp.sum(jnp.where(blocks, turned * kernel, 0.0), axis=1, keepdims=True)
    weighted = head_sums(jnp.broadcast_to(weighted, kernel.shape))
    grad_kernel = grad_kernel + turned - 2.0 * kernel * weighted / total
    grad_scores = SCALE * kernel * (grad_kernel - jnp.sum(kernel * grad_kernel, axis=1, keepdims=True))
    grad_q_marks = exact(grad_scores, k_marks)
    grad_k_marks = exact(grad_scores, q_marks, TN)
    grad_k_marks = grad_k_marks + jnp.where(blocks, mm_left(grad_token, queries), 0.0)
    grad_key = mm_left(grad_summary, values, NT) - jnp.sum(grad_summary * summary, axis=1, keepdims=True)
    grad_key = SCALE * key_weights * grad_key
    grad_q_marks = grad_q_marks + jnp.where(blocks, mm_left(grad_key, keys), 0.0)
    grad_q_marks = (grad_q_marks[:MARKS] + grad_q_marks[MARKS:]) / counts
    grad_k_marks = (grad_k_marks[:MARKS] + grad_k_marks[MARKS:]) / counts
    high, rest = halves(grad_q_marks)
    result[0] = (mm_both(grad_token, k_marks, TN) + mm(member, high) + mm(member, rest)).astype(BF16)
    high, rest = halves(grad_k_marks)
    result[1] = (mm_both(grad_key, q_marks, TN) + mm(member, high) + mm(member, rest)).astype(BF16)
    blended[...] = mm_both(key_weights, grad_summary, TN)
    last = high_marks[MARKS - 1 :]
    valid_column = iota((length, 1), 0) < last
    padded[0:HALF, :] = jnp.zeros((HALF, LANES), BF16)
    padded[HALF : HALF + length, :] = jnp.where(valid_column, values, jnp.zeros_like(values))
    padded[HALF + length :, :] = jnp.zeros((LANES - HALF, LANES), BF16)
    padded_grads[0:HALF, :] = jnp.zeros((HALF, LANES), BF16)
    padded_grads[HALF : HALF + length, :] = grads
    padded_grads[HALF + length :, :] = jnp.zeros((LANES - HALF, LANES), BF16)

    def store(start, block):
        rows = start + iota((LANES, 1), 0)
        total_rows = blended[pl.ds(start, LANES), :] + jnp.where(rows < last, block, 0.0)
        result[2, pl.ds(start, LANES), :] = total_rows.astype(BF16)

    convolve(padded_grads, [band(taps[2:3]), band(taps[3:4])], length, store)
    first = iota((LANES, LANES), 1) < HEAD_DIM

    def block(step, carry):
        start = pl.multiple_of(step * LANES, LANES)
        own = padded_grads[pl.ds(start + HALF, LANES), :]
        window = padded[pl.ds(start, 2 * LANES), :]
        none = jnp.zeros_like(own)
        return (
            carry[0] + mm(jnp.where(first, own, none), window, NT),
            carry[1] + mm(jnp.where(first, none, own), window, NT),
        )

    start_sum = jnp.zeros((LANES, 2 * LANES), F32)
    sums = lax.fori_loop(0, length // LANES, block, (start_sum, start_sum))
    wide = 2 * LANES
    for head in range(2):
        folded = sums[head][0:8]
        for group in range(1, LANES // 8):
            rows = sums[head][8 * group : 8 * group + 8]
            folded = folded + pltpu.roll(rows, wide - 8 * group, 1)
        line = folded[0:1]
        for row in range(1, 8):
            line = line + pltpu.roll(folded[row : row + 1], wide - row, 1)
        grad_taps[head : head + 1, :] = line


TASKS = MICRO * PAIRS
KEPT = ("q_marks", "k_marks", "kernel", "total", "inverse", "product", "two", "three", "key_weights", "summary", "mixed", "token_weights")


def kept_shapes(length):
    square = (LANES, LANES)
    shapes = {name: square for name in KEPT}
    shapes["inverse"] = (NS_ITERS + 1,) + square
    for name in ("product", "two", "three"):
        shapes[name] = (NS_ITERS,) + square
    shapes["key_weights"] = shapes["token_weights"] = (LANES, length)
    return shapes


def owner_of(task, count):
    return task * count // TASKS


def task_of(me, count):
    task = (me * TASKS + count - 1) // count
    return task, owner_of(task, count) == me


def greet(count):
    me = lax.axis_index("dp")
    barrier = pltpu.get_barrier_semaphore()

    def signal(step, carry):
        pl.semaphore_signal(barrier, inc=1, device_id={"dp": lax.rem(me + step, count)}, device_id_type=MESH)
        return carry

    lax.fori_loop(1, count, signal, 0)
    pl.semaphore_wait(barrier, count - 1)


def scatter_tasks(count, piece, source, slab, send, receive):
    me = lax.axis_index("dp")

    def one(step, finish):
        task = lax.rem(task_of(me, count)[0] + step, TASKS)
        owner = owner_of(task, count)
        micro = task // PAIRS
        lanes = pl.ds(pl.multiple_of(lax.rem(task, PAIRS) * LANES, LANES), LANES)
        rows = pl.ds(pl.multiple_of(me * piece, piece), piece)
        outgoing = source.at[:, micro, :, lanes]
        landing = slab.at[:, rows, :]

        @pl.when(owner != me)
        def _():
            copy = pltpu.make_async_remote_copy(outgoing, landing, send.at[task], receive.at[me], device_id={"dp": owner}, device_id_type=MESH)
            if finish:
                copy.wait_send()
            else:
                copy.start()

        @pl.when((owner == me) & (not finish))
        def _():
            pltpu.make_async_copy(outgoing, landing, receive.at[me]).start()

    def run(finish):
        def body(step, carry):
            one(step, finish)
            return carry

        lax.fori_loop(0, TASKS, body, 0)

    return run


def await_slab(count, piece, slab, receive):
    def body(origin, carry):
        landing = slab.at[:, pl.ds(pl.multiple_of(origin * piece, piece), piece), :]
        pltpu.make_async_copy(landing, landing, receive.at[origin]).wait()
        return carry

    lax.fori_loop(0, count, body, 0)


def return_rows(count, piece, result, target, send, receive):
    me = lax.axis_index("dp")
    task = task_of(me, count)[0]
    micro = task // PAIRS
    lanes = pl.ds(pl.multiple_of(lax.rem(task, PAIRS) * LANES, LANES), LANES)

    def run(finish):
        def body(step, carry):
            peer = lax.rem(me + step, count)
            rows = pl.ds(pl.multiple_of(peer * piece, piece), piece)
            outgoing = result.at[:, rows, :]
            landing = target.at[:, micro, :, lanes]

            @pl.when(peer != me)
            def _():
                copy = pltpu.make_async_remote_copy(outgoing, landing, send.at[peer], receive.at[task], device_id={"dp": peer}, device_id_type=MESH)
                if finish:
                    copy.wait_send()
                else:
                    copy.start()

            @pl.when((peer == me) & (not finish))
            def _():
                pltpu.make_async_copy(outgoing, landing, receive.at[task]).start()

            return carry

        lax.fori_loop(0, count, body, 0)

    return run


def await_rows(target, receive):
    def body(task, carry):
        lanes = pl.ds(pl.multiple_of(lax.rem(task, PAIRS) * LANES, LANES), LANES)
        landing = target.at[:, task // PAIRS, :, lanes]
        pltpu.make_async_copy(landing, landing, receive.at[task]).wait()
        return carry

    lax.fori_loop(0, TASKS, body, 0)


def forward_kernel(count, piece, qkv, low_col, high_col, taps, mixed_rows, slab, *refs):
    keep = dict(zip(KEPT, refs))
    padded, blended, result, send_one, receive_one, send_two, receive_two = refs[len(KEPT) :]
    me = lax.axis_index("dp")
    task, owns = task_of(me, count)
    greet(count)
    out = scatter_tasks(count, piece, qkv, slab, send_one, receive_one)
    out(False)
    back = return_rows(count, piece, result, mixed_rows, send_two, receive_two)

    @pl.when(owns)
    def _():
        micro, pair = task // PAIRS, lax.rem(task, PAIRS)
        await_slab(count, piece, slab, receive_one)
        attend(slab[0], slab[1], slab[2], low_col[micro], high_col[micro], taps[pair], keep, padded, blended, result.at[0])
        back(False)

    out(True)
    await_rows(mixed_rows, receive_two)

    @pl.when(owns)
    def _():
        back(True)


def backward_kernel(count, piece, grads, low_col, high_col, low_row, high_row, taps, slab, *refs):
    keep = dict(zip(KEPT, refs))
    out_grads, grad_taps, grad_slab, padded, padded_grads, blended, result, send_one, receive_one, send_two, receive_two = refs[len(KEPT) :]
    me = lax.axis_index("dp")
    task, owns = task_of(me, count)
    greet(count)
    out = scatter_tasks(count, piece, grads, grad_slab, send_one, receive_one)
    out(False)
    back = return_rows(count, piece, result, out_grads, send_two, receive_two)
    grad_taps[...] = jnp.zeros(grad_taps.shape, F32)

    @pl.when(owns)
    def _():
        micro, pair = task // PAIRS, lax.rem(task, PAIRS)
        await_slab(count, piece, grad_slab, receive_one)
        attend_back(
            grad_slab[0], slab[0], slab[1], slab[2], low_col[micro], high_col[micro], low_row[micro], high_row[micro],
            taps[pair], keep, padded, padded_grads, blended, result, grad_taps.at[pair],
        )
        back(False)

    out(True)
    await_rows(out_grads, receive_two)

    @pl.when(owns)
    def _():
        back(True)


VMEM = pl.BlockSpec(memory_space=pltpu.VMEM)
DMA = pltpu.SemaphoreType.DMA


def attention_forward(count, qkv, marks, taps, ident):
    piece = qkv.shape[2]
    length = piece * count
    shapes = kept_shapes(length)
    results = pl.pallas_call(
        functools.partial(forward_kernel, count, piece),
        out_shape=[
            jax.ShapeDtypeStruct((1, MICRO, piece, D), BF16),
            jax.ShapeDtypeStruct((3, length, LANES), BF16),
        ]
        + [jax.ShapeDtypeStruct(shapes[name], F32) for name in KEPT],
        in_specs=[VMEM] * 4,
        out_specs=[VMEM] * (2 + len(KEPT)),
        scratch_shapes=[
            pltpu.VMEM((length + LANES, LANES), BF16),
            pltpu.VMEM((length, LANES), F32),
            pltpu.VMEM((1, length, LANES), BF16),
            DMA((TASKS,)),
            DMA((count,)),
            DMA((count,)),
            DMA((TASKS,)),
        ],
        compiler_params=pltpu.CompilerParams(collective_id=ident, has_side_effects=True, vmem_limit_bytes=60 << 20),
        name="attend_forward",
    )(qkv, marks[0], marks[1], taps)
    return results[0][0], results[1:]


def attention_backward(count, grads, marks, taps, kept, ident):
    piece = grads.shape[2]
    length = piece * count
    return pl.pallas_call(
        functools.partial(backward_kernel, count, piece),
        out_shape=[
            jax.ShapeDtypeStruct((3, MICRO, piece, D), BF16),
            jax.ShapeDtypeStruct((PAIRS, 2, 2 * LANES), F32),
        ],
        in_specs=[VMEM] * (7 + len(KEPT)),
        out_specs=[VMEM] * 2,
        scratch_shapes=[
            pltpu.VMEM((1, length, LANES), BF16),
            pltpu.VMEM((length + LANES, LANES), BF16),
            pltpu.VMEM((length + LANES, LANES), BF16),
            pltpu.VMEM((length, LANES), F32),
            pltpu.VMEM((3, length, LANES), BF16),
            DMA((TASKS,)),
            DMA((count,)),
            DMA((count,)),
            DMA((TASKS,)),
        ],
        compiler_params=pltpu.CompilerParams(collective_id=ident, has_side_effects=True, vmem_limit_bytes=60 << 20),
        name="attend_backward",
    )(grads, *marks, taps, *kept)


CHUNK = 48
SLICE = 16


def settle_kernel(
    block_rows, grads_last, grads_first, weights, first, second, small, small_first, small_second,
    grad_out, mean_out, small_out,
    own, got_core, got_y, got_z, inner, step_own, step_got, small_got, small_own, small_step, small_step_got,
    own_sem, core_send, core_got, y_send, y_got, z_send, z_got, inner_sem, rep_send, rep_got, small_send, small_sem, back_send, back_sem, small_rep,
):
    me = lax.axis_index("dp")
    other_rep = 1 - lax.axis_index("rep")
    core, y, z = lax.rem(me, 2), lax.rem(me // 2, 2), me // 4
    devices = 16
    per_layer = block_rows // CHUNK
    chunks = LAYERS * per_layer

    barrier = pltpu.get_barrier_semaphore()

    def signal(step, carry):
        pl.semaphore_signal(barrier, inc=1, device_id={"dp": lax.rem(me + step, devices)}, device_id_type=MESH)
        return carry

    lax.fori_loop(1, devices, signal, 0)
    pl.semaphore_signal(barrier, inc=1, device_id={"rep": other_rep}, device_id_type=MESH)
    pl.semaphore_wait(barrier, devices)

    def to_dp(source, target, send, receive, peer):
        return pltpu.make_async_remote_copy(source, target, send, receive, device_id={"dp": peer}, device_id_type=MESH)

    def to_rep(source, target, send, receive):
        return pltpu.make_async_remote_copy(source, target, send, receive, device_id={"rep": other_rep}, device_id_type=MESH)

    def rows_of(part):
        return pl.ds(pl.multiple_of(part * CHUNK, CHUNK), CHUNK)

    def core_copy(source, chunk, part):
        return to_dp(source.at[:, :, 1 - core, rows_of(part), :], got_core.at[chunk], core_send.at[chunk], core_got.at[chunk], me + 1 - 2 * core)

    def own_copy(source, chunk, part):
        return pltpu.make_async_copy(source.at[:, :, core, rows_of(part), :], own.at[chunk], own_sem.at[chunk])

    for order, source in enumerate((grads_last, grads_first)):

        def begin(part, carry):
            chunk = order * per_layer + part
            core_copy(source, chunk, part).start()
            own_copy(source, chunk, part).start()
            return carry

        lax.fori_loop(0, per_layer, begin, 0)

    def small_copy(step):
        peer = lax.rem(me + step, devices)
        return to_dp(small.at[peer], small_got.at[me], small_send.at[peer], small_sem.at[me], peer)

    def small_begin(step, carry):
        small_copy(step).start()
        return carry

    lax.fori_loop(1, devices, small_begin, 0)

    def y_copy(chunk):
        return to_dp(own.at[chunk, :, 1 - y], got_y.at[chunk], y_send.at[chunk], y_got.at[chunk], me + 2 - 4 * y)

    def z_copy(chunk, hop):
        there = lax.rem(z + hop, 4)
        return to_dp(own.at[chunk, there, y], got_z.at[chunk, hop - 1], z_send.at[chunk, hop - 1], z_got.at[chunk, hop - 1], there * 4 + lax.rem(me, 4))

    def place(chunk):
        return LAYERS - 1 - chunk // per_layer, rows_of(lax.rem(chunk, per_layer))

    def inner_copies(chunk):
        level, rows = place(chunk)
        slot = lax.rem(chunk, 4)
        return [
            pltpu.make_async_copy(array.at[level, rows, :], inner.at[slot, index], inner_sem.at[slot, index])
            for index, array in enumerate((weights, first, second))
        ]

    def rep_copy(chunk):
        return to_rep(step_own.at[chunk], step_got.at[chunk], rep_send.at[chunk], rep_got.at[chunk])

    def change(grad, first_old, second_old):
        new_first = ADAM_ONE * first_old + (1.0 - ADAM_ONE) * grad
        new_second = ADAM_TWO * second_old + (1.0 - ADAM_TWO) * grad * grad
        return new_first * (1.0 / (1.0 - ADAM_ONE**STEP_COUNT)) / (jnp.sqrt(new_second * (1.0 / (1.0 - ADAM_TWO**STEP_COUNT))) + ADAM_EPSILON)

    def stage_core(chunk):
        own_copy(grads_last, chunk, 0).wait()
        core_copy(grads_last, chunk, 0).wait_recv()
        for there in range(4):
            for side in range(2):
                own[chunk, there, side] = own[chunk, there, side] + got_core[chunk, there, side]
        y_copy(chunk).start()
        for copy in inner_copies(chunk):
            copy.start()

    def stage_y(chunk):
        y_copy(chunk).wait_recv()
        for there in range(4):
            own[chunk, there, y] = own[chunk, there, y] + got_y[chunk, there]
        for hop in range(1, 4):
            z_copy(chunk, hop).start()

    def stage_z(chunk):
        for hop in range(1, 4):
            z_copy(chunk, hop).wait_recv()
        for copy in inner_copies(chunk):
            copy.wait()
        total = own[chunk, z, y].astype(F32)
        for hop in range(3):
            total = total + got_z[chunk, hop].astype(F32)
        level, rows = place(chunk)
        grad_out[level, rows, :] = total
        slot = lax.rem(chunk, 4)
        step = change(total, inner[slot, 1], inner[slot, 2]) + WEIGHT_DECAY * inner[slot, 0]
        step_own[chunk] = (LR_INNER * step).astype(BF16)
        rep_copy(chunk).start()

    def stage_rep(chunk):
        rep_copy(chunk).wait_recv()
        level, rows = place(chunk)
        mean_out[level, rows, :] = 0.5 * (step_own[chunk].astype(F32) + step_got[chunk].astype(F32))

    def small_rep_copy():
        return to_rep(small_step, small_step_got, small_rep.at[0], small_rep.at[1])

    def small_back(step):
        peer = lax.rem(me + step, devices)
        return to_dp(small_own, small_out.at[me], back_send.at[peer], back_sem.at[me], peer)

    def small_sum():
        total = small[me]

        def add(step, total):
            peer = lax.rem(me + step, devices)
            pltpu.make_async_copy(small_got.at[peer], small_got.at[peer], small_sem.at[peer]).wait()
            return total + small_got[peer]

        total = lax.fori_loop(1, devices, add, total)
        small_own[0] = total
        small_step[...] = (LR_SMALL * change(total, small_first[me], small_second[me])).astype(BF16)
        small_rep_copy().start()

    def small_spread():
        small_rep_copy().wait_recv()
        small_own[1] = 0.5 * (small_step[...].astype(F32) + small_step_got[...].astype(F32))
        small_out[me] = small_own[...]

        def send(step, carry):
            small_back(step).start()
            return carry

        lax.fori_loop(1, devices, send, 0)

    def turn(now, carry):
        for lag, stage in ((0, stage_core), (2, stage_y), (3, stage_z), (4, stage_rep)):

            @pl.when((now >= lag) & (now < chunks + lag))
            def _():
                stage(now - lag)

        pl.when(now == 2)(small_sum)
        pl.when(now == 5)(small_spread)
        return carry

    lax.fori_loop(0, chunks + 4, turn, 0)

    def drain(chunk, carry):
        core_copy(grads_last, chunk, 0).wait_send()
        y_copy(chunk).wait_send()
        for hop in range(1, 4):
            z_copy(chunk, hop).wait_send()
        rep_copy(chunk).wait_send()
        return carry

    lax.fori_loop(0, chunks, drain, 0)

    def small_drain(step, carry):
        peer = lax.rem(me + step, devices)
        small_copy(step).wait_send()
        small_back(step).wait_send()
        pltpu.make_async_copy(small_own, small_out.at[peer], back_sem.at[peer]).wait()
        return carry

    lax.fori_loop(1, devices, small_drain, 0)
    small_rep_copy().wait_send()


def settle(grads, weights, first, second, small, small_first, small_second):
    block_rows = weights.shape[1]
    chunks = LAYERS * block_rows // CHUNK
    anywhere = pl.BlockSpec(memory_space=pl.ANY)
    devices = 16
    piece = (CHUNK, D)
    return pl.pallas_call(
        functools.partial(settle_kernel, block_rows),
        out_shape=[
            jax.ShapeDtypeStruct(weights.shape, F32),
            jax.ShapeDtypeStruct(weights.shape, F32),
            jax.ShapeDtypeStruct((devices, 2, SLICE, LANES), F32),
        ],
        in_specs=[anywhere] * 5 + [VMEM] * 3,
        out_specs=[VMEM] * 3,
        scratch_shapes=[
            pltpu.VMEM((chunks, 4, 2) + piece, BF16),
            pltpu.VMEM((chunks, 4, 2) + piece, BF16),
            pltpu.VMEM((chunks, 4) + piece, BF16),
            pltpu.VMEM((chunks, 3) + piece, BF16),
            pltpu.VMEM((4, 3) + piece, F32),
            pltpu.VMEM((chunks,) + piece, BF16),
            pltpu.VMEM((chunks,) + piece, BF16),
            pltpu.VMEM((devices, SLICE, LANES), F32),
            pltpu.VMEM((2, SLICE, LANES), F32),
            pltpu.VMEM((SLICE, LANES), BF16),
            pltpu.VMEM((SLICE, LANES), BF16),
            DMA((chunks,)),
            DMA((chunks,)),
            DMA((chunks,)),
            DMA((chunks,)),
            DMA((chunks,)),
            DMA((chunks, 3)),
            DMA((chunks, 3)),
            DMA((4, 3)),
            DMA((chunks,)),
            DMA((chunks,)),
            DMA((devices,)),
            DMA((devices,)),
            DMA((devices,)),
            DMA((devices,)),
            DMA((2,)),
        ],
        compiler_params=pltpu.CompilerParams(collective_id=3, has_side_effects=True, vmem_limit_bytes=63 << 20),
        name="settle",
    )(*[array.reshape(4, 2, 2, block_rows, D) for array in grads], weights, first, second, small, small_first, small_second)


def sliced(array):
    flat = array.reshape(-1)
    return jnp.pad(flat, (0, 16 * SLICE * LANES - flat.shape[0])).reshape(16, SLICE, LANES)


def unsliced(array, shape):
    return array.reshape(-1)[: shape[0] * shape[1]].reshape(shape)


def dense(a, b, dims=NN):
    return mm(a, b, dims)


def layer_norm(values, gain_vec, shift_vec):
    row_mean = jnp.mean(values, axis=-1, keepdims=True)
    centred = values - row_mean
    variance = jnp.mean(centred * centred, axis=-1, keepdims=True)
    return centred * lax.rsqrt(variance + 1e-05) * gain_vec + shift_vec


def unpack(params):
    blocks = [params[index * D : (index + 1) * D] for index in range(8)]
    bias_up = params[8 * D : 8 * D + FF]
    conv_taps = params[8 * D + FF :].reshape(HEADS, TAPS)
    return (blocks, bias_up, conv_taps)


def pair_taps(conv_taps):
    both = jnp.stack([conv_taps.reshape(PAIRS, 2, TAPS), conv_taps[:, ::-1].reshape(PAIRS, 2, TAPS)], axis=1)
    both = both.reshape(PAIRS, 4, TAPS)
    return jnp.pad(both, ((0, 0), (0, 0), (0, 2 * LANES - TAPS)))


def split_rows(rows):
    return rows[: 3 * D].reshape(3, D, D), rows[3 * D : 4 * D], rows[4 * D : 4 * D + FF], rows[4 * D + FF :]


def forward_layer(count, inputs, rows, params, marks, ident):
    piece = inputs.shape[0] // MICRO
    blocks, bias_up, conv_taps = unpack(params)
    proj, out_weight, up_weight, down_weight = split_rows(rows)
    low_in = inputs.astype(BF16)
    bias = jnp.stack([blocks[0], jnp.zeros_like(blocks[0]), blocks[1]])
    qkv = jnp.stack([(dense(low_in, proj[part]) + bias[part]).astype(BF16) for part in range(3)])
    low_comb, kept = attention_forward(count, qkv.reshape(3, MICRO, piece, D), marks, pair_taps(conv_taps), ident)
    low_comb = low_comb.reshape(MICRO * piece, D)
    resid_one = inputs + (dense(low_comb, out_weight) + blocks[2])
    hidden_one = layer_norm(resid_one, blocks[4], blocks[5])
    low_hidden = hidden_one.astype(BF16)
    upward = dense(low_hidden, up_weight, NT) + bias_up
    low_act = jax.nn.gelu(upward).astype(BF16)
    resid_two = hidden_one + (dense(low_act, down_weight) + blocks[3])
    output = layer_norm(resid_two, blocks[6], blocks[7])
    return output, (low_in, kept, low_comb, resid_one, low_hidden, upward, low_act, resid_two)


def backward_layer(count, grad_output, rows, params, marks, state, ident):
    low_in, kept, low_comb, resid_one, low_hidden, upward, low_act, resid_two = state
    total = low_in.shape[0]
    piece = total // MICRO
    blocks, bias_up, conv_taps = unpack(params)
    proj, out_weight, up_weight, down_weight = split_rows(rows)
    _, pull_two = jax.vjp(layer_norm, resid_two, blocks[6], blocks[7])
    grad_two, grad_gain_two, grad_shift_two = pull_two(grad_output)
    low_down = grad_two.astype(BF16)
    grad_bias_down = jnp.sum(low_down.astype(F32), axis=0)
    grad_act = dense(low_down, down_weight, NT)
    _, pull_gelu = jax.vjp(jax.nn.gelu, upward)
    low_up = pull_gelu(grad_act)[0].astype(BF16)
    grad_bias_up = jnp.sum(low_up.astype(F32), axis=0)
    grad_hidden = grad_two + dense(low_up, up_weight)
    _, pull_one = jax.vjp(layer_norm, resid_one, blocks[4], blocks[5])
    grad_one, grad_gain_one, grad_shift_one = pull_one(grad_hidden)
    low_branch = grad_one.astype(BF16)
    grad_bias_out = jnp.sum(low_branch.astype(F32), axis=0)
    grad_comb = dense(low_branch, out_weight, NT).astype(BF16)
    low_grads, grad_taps = attention_backward(count, grad_comb.reshape(1, MICRO, piece, D), marks, pair_taps(conv_taps), kept, ident)
    low_grads = low_grads.reshape(3, total, D)
    grad_bias_q = jnp.sum(low_grads[0].astype(F32), axis=0)
    grad_bias_v = jnp.sum(low_grads[2].astype(F32), axis=0)
    grad_in = grad_one + sum(dense(low_grads[part], proj[part], NT) for part in range(3))
    parts = [dense(low_in, low_grads[part], TN).astype(BF16) for part in range(3)]
    parts = parts + [
        dense(low_comb, low_branch, TN).astype(BF16),
        dense(low_up, low_hidden, TN).astype(BF16),
        dense(low_act, low_down, TN).astype(BF16),
    ]
    grad_small = jnp.concatenate(
        [
            grad_bias_q,
            grad_bias_v,
            grad_bias_out,
            grad_bias_down,
            grad_gain_one,
            grad_shift_one,
            grad_gain_two,
            grad_shift_two,
            grad_bias_up,
            grad_taps[:, :, :TAPS].reshape(-1),
        ]
    )
    return grad_in, jnp.concatenate(parts, axis=0), grad_small


def moments(first, second, grad):
    return ADAM_ONE * first + (1.0 - ADAM_ONE) * grad, ADAM_TWO * second + (1.0 - ADAM_TWO) * grad * grad


def adam(weights, first, second, grad, rate, decay):
    correct_one = 1.0 - ADAM_ONE**STEP_COUNT
    correct_two = 1.0 - ADAM_TWO**STEP_COUNT
    new_first, new_second = moments(first, second, grad)
    step = new_first / correct_one / (jnp.sqrt(new_second / correct_two) + ADAM_EPSILON)
    return new_first, new_second, rate * (step + decay * weights)


def shards(
    hidden,
    bounds,
    cotangent,
    weights,
    small_params,
    first_big,
    second_big,
    first_small,
    second_small,
    outer_big,
    outer_small,
):
    count = lax.axis_size("dp")
    piece = hidden.shape[3]
    total = MICRO * piece
    held = [lax.all_gather(weights[level].astype(BF16), "dp", axis=0, tiled=True) for level in range(LAYERS)]
    edges = bounds[0, :, 0, :]
    low_edges, high_edges = edges[:, :-1], edges[:, 1:]
    marks = (low_edges[:, :, None], high_edges[:, :, None], low_edges[:, None, :], high_edges[:, None, :])
    positions = lax.axis_index("dp") * piece + jnp.arange(piece, dtype=jnp.int32)
    valid = (positions[None, :] < edges[:, -1:]).astype(F32).reshape(total, 1)
    activation = hidden[0, :, 0].reshape(total, D).astype(F32)
    states = []
    for level in range(LAYERS):
        activation, state = forward_layer(count, activation, held[level], small_params[level], marks, 1)
        states.append(state)
    gradient = cotangent[0, :, 0].reshape(total, D).astype(F32) * valid
    grad_parts, small_parts = [None] * LAYERS, [None] * LAYERS
    for level in reversed(range(LAYERS)):
        gradient, grad_rows, small_parts[level] = backward_layer(count, gradient, held[level], small_params[level], marks, states[level], 2)
        grad_parts[level] = grad_rows
    small_parts = jnp.stack(small_parts)
    if count == 16:
        grad_big, mean_big, small_both = settle(
            grad_parts[::-1], weights, first_big[0], second_big[0], sliced(small_parts), sliced(first_small[0]), sliced(second_small[0])
        )
        grad_small, mean_small = [unsliced(small_both[:, which], small_parts.shape) for which in range(2)]
    else:
        grad_big = jnp.stack([lax.psum_scatter(rows, "dp", scatter_dimension=0, tiled=True).astype(F32) for rows in grad_parts])
        grad_small = lax.psum(small_parts, "dp")
        reps = lax.axis_size("rep")
        delta_big = adam(weights, first_big[0], second_big[0], grad_big, LR_INNER, WEIGHT_DECAY)[2]
        delta_small = adam(small_params, first_small[0], second_small[0], grad_small, LR_SMALL, 0.0)[2]
        mean_big = lax.psum(delta_big.astype(BF16), "rep").astype(F32) / reps
        mean_small = lax.psum(delta_small.astype(BF16), "rep").astype(F32) / reps
    new_first, new_second = moments(first_big[0], second_big[0], grad_big)
    new_first_small, new_second_small = moments(first_small[0], second_small[0], grad_small)
    outer_big_new = MOMENTUM * outer_big + mean_big
    outer_small_new = MOMENTUM * outer_small + mean_small
    weights_new = weights - LR_OUTER * (mean_big + MOMENTUM * outer_big_new)
    small_new = small_params - LR_OUTER * (mean_small + MOMENTUM * outer_small_new)
    shape = (1, MICRO, 1, piece, D)
    return (
        activation.reshape(shape),
        gradient.reshape(shape),
        new_first[None],
        new_second[None],
        new_first_small[None],
        new_second_small[None],
        outer_big_new,
        outer_small_new,
        weights_new,
        small_new,
        weights_new.astype(BF16),
    )


def solution(mesh):
    placed = (
        P("rep", None, None, "dp", None),
        P("rep", None, None, None),
        P("rep", None, None, "dp", None),
        P(None, "dp", None),
        P(),
        P("rep", None, "dp", None),
        P("rep", None, "dp", None),
        P("rep", None, None),
        P("rep", None, None),
        P(None, "dp", None),
        P(),
    )
    return jax.shard_map(
        shards,
        mesh=mesh,
        in_specs=placed,
        out_specs=(
            P("rep", None, None, "dp", None),
            P("rep", None, None, "dp", None),
            P("rep", None, "dp", None),
            P("rep", None, "dp", None),
            P("rep", None, None),
            P("rep", None, None),
            P(None, "dp", None),
            P(),
            P(None, "dp", None),
            P(),
            P(None, "dp", None),
        ),
        check_vma=False,
    )
```

```python
import functools

import jax
import jax.numpy as jnp
from jax import lax
from jax.experimental import pallas as pl
from jax.experimental.pallas import tpu as pltpu
from jax.sharding import PartitionSpec as P

D = 768
HEADS = 12
FF = 3072
TAPS = 33
NS_ITERS = 6
LAYERS = 2
MICRO = 2
STEP_COUNT = 5


PRECISE = lax.Precision.HIGHEST
ADAM_ONE = 0.9
ADAM_TWO = 0.95
ADAM_EPSILON = 1e-08
WEIGHT_DECAY = 0.1
LR_INNER = 0.04
LR_SMALL = 0.2
LR_OUTER = 0.7
MOMENTUM = 0.9

HEAD_DIM = 64
MARKS = 64
HALF = TAPS // 2
PAIRS = HEADS // 2
LANES = 128
SCALE = HEAD_DIM**-0.5
NEG = -1e30
MESH = pl.DeviceIdType.MESH
F32 = jnp.float32
BF16 = jnp.bfloat16
NN = (((1,), (0,)), ((), ()))
NT = (((1,), (1,)), ((), ()))
TN = (((0,), (0,)), ((), ()))


def mm(a, b, dims=NN):
    return lax.dot_general(a, b, dims, preferred_element_type=F32)


def halves(a):
    high = a.astype(BF16)
    return high, (a - high.astype(F32)).astype(BF16)


def mm_left(a, b, dims=NN):
    high, rest = halves(a)
    return mm(high, b, dims) + mm(rest, b, dims)


def mm_both(a, b, dims=NN):
    ah, al = halves(a)
    bh, bl = halves(b)
    return mm(ah, bh, dims) + (mm(ah, bl, dims) + mm(al, bh, dims))


def exact(a, b, dims=NN):
    return lax.dot_general(a, b, dims, precision=PRECISE, preferred_element_type=F32)


def iota(shape, dim):
    return lax.broadcasted_iota(jnp.int32, shape, dim)


def diagonal_blocks():
    return (iota((LANES, LANES), 0) < MARKS) == (iota((LANES, LANES), 1) < HEAD_DIM)


def unit():
    return (iota((LANES, LANES), 0) == iota((LANES, LANES), 1)).astype(F32)


def per_head(marks):
    first = iota(marks.shape, 1) < HEAD_DIM
    return jnp.concatenate([jnp.where(first, marks, 0.0), jnp.where(first, 0.0, marks)], axis=0)


def head_sums(a):
    rows, cols = a.shape
    split = a.reshape(2, rows // 2, cols)
    return jnp.broadcast_to(jnp.sum(split, axis=1, keepdims=True), split.shape).reshape(rows, cols)


def head_tops(a):
    rows, cols = a.shape
    split = a.reshape(2, rows // 2, cols)
    return jnp.broadcast_to(jnp.max(split, axis=1, keepdims=True), split.shape).reshape(rows, cols)


def band(taps_row):
    wide = jnp.broadcast_to(taps_row, (LANES, 2 * LANES))
    return pltpu.roll(wide, 0, 1, stride=1, stride_axis=0)


def convolve(padded, bands, length, store):
    first = iota((LANES, LANES), 1) < HEAD_DIM
    pairs = [halves(one) for one in bands]

    def block(at, carry):
        start = pl.multiple_of(at * LANES, LANES)
        window = padded[pl.ds(start, 2 * LANES), :]
        out = [mm(high, window) + mm(rest, window) for high, rest in pairs]
        store(start, jnp.where(first, out[0], out[1]))
        return carry

    lax.fori_loop(0, length // LANES, block, 0)


def attend(queries, keys, values, low_marks, high_marks, taps, keep, padded, blended, result):
    length = queries.shape[0]
    at = iota((MARKS, length), 1)
    member = ((low_marks <= at) & (at < high_marks)).astype(F32).astype(BF16)
    counts = (high_marks - low_marks).astype(F32)
    blocks, eye = diagonal_blocks(), unit()
    q_marks = per_head(mm(member, queries) / counts)
    k_marks = per_head(mm(member, keys) / counts)
    scores = jnp.where(blocks, SCALE * exact(q_marks, k_marks, NT), NEG)
    weights = jnp.exp(scores - jnp.max(scores, axis=1, keepdims=True))
    kernel = weights / jnp.sum(weights, axis=1, keepdims=True)
    total = head_sums(jnp.broadcast_to(jnp.sum(kernel * kernel, axis=1, keepdims=True), kernel.shape))
    inverse = kernel.T / total
    keep["q_marks"][...] = q_marks
    keep["k_marks"][...] = k_marks
    keep["kernel"][...] = kernel
    keep["total"][...] = total
    for sweep in range(NS_ITERS):
        product = exact(kernel, inverse)
        one = 7.0 * eye - product
        two = 15.0 * eye - exact(product, one)
        three = 13.0 * eye - exact(product, two)
        keep["inverse"][sweep] = inverse
        keep["product"][sweep] = product
        keep["two"][sweep] = two
        keep["three"][sweep] = three
        inverse = 0.25 * exact(inverse, three)
    keep["inverse"][NS_ITERS] = inverse
    valid = at[:1] < high_marks[MARKS - 1 :]
    key_scores = jnp.where(valid, SCALE * mm_left(q_marks, keys, NT), NEG)
    key_exp = jnp.where(valid, jnp.exp(key_scores - jnp.max(key_scores, axis=1, keepdims=True)), 0.0)
    key_weights = key_exp / jnp.sum(key_exp, axis=1, keepdims=True)
    keep["key_weights"][...] = key_weights
    summary = jnp.where(blocks, mm_left(key_weights, values), 0.0)
    mixed = exact(inverse, summary)
    keep["summary"][...] = summary
    keep["mixed"][...] = mixed
    token_scores = SCALE * mm_left(k_marks, queries, NT)
    token_exp = jnp.exp(token_scores - head_tops(token_scores))
    token_weights = token_exp / head_sums(token_exp)
    keep["token_weights"][...] = token_weights
    blended[...] = mm_both(token_weights, mixed, TN)
    valid_column = iota((length, 1), 0) < high_marks[MARKS - 1 :]
    padded[0:HALF, :] = jnp.zeros((HALF, LANES), BF16)
    padded[HALF : HALF + length, :] = jnp.where(valid_column, values, jnp.zeros_like(values))
    padded[HALF + length :, :] = jnp.zeros((LANES - HALF, LANES), BF16)

    def store(start, block):
        result[pl.ds(start, LANES), :] = (blended[pl.ds(start, LANES), :] + block).astype(BF16)

    convolve(padded, [band(taps[0:1]), band(taps[1:2])], length, store)


def attend_back(grads, queries, keys, values, low_marks, high_marks, low_row, high_row, taps, keep, padded, padded_grads, blended, result, grad_taps):
    length = grads.shape[0]
    at = iota((length, MARKS), 0)
    member = ((low_row <= at) & (at < high_row)).astype(F32).astype(BF16)
    counts = (high_marks - low_marks).astype(F32)
    blocks, eye = diagonal_blocks(), unit()
    q_marks, k_marks = keep["q_marks"][...], keep["k_marks"][...]
    token_weights, key_weights = keep["token_weights"][...], keep["key_weights"][...]
    summary, mixed = keep["summary"][...], keep["mixed"][...]
    kernel = keep["kernel"][...]
    inverse = keep["inverse"][NS_ITERS]
    grad_mixed = jnp.where(blocks, mm_left(token_weights, grads), 0.0)
    grad_token = token_weights * mm_left(mixed, grads, NT)
    grad_token = SCALE * (grad_token - token_weights * head_sums(grad_token))
    grad_summary = exact(inverse, grad_mixed, TN)
    grad_inverse = exact(grad_mixed, summary, NT)
    grad_kernel = jnp.zeros_like(kernel)
    for sweep in reversed(range(NS_ITERS)):
        before, product = keep["inverse"][sweep], keep["product"][sweep]
        one = 7.0 * eye - product
        two, three = keep["two"][sweep], keep["three"][sweep]
        grad_three = 0.25 * exact(before, grad_inverse, TN)
        grad_two = -exact(product, grad_three, TN)
        grad_one = -exact(product, grad_two, TN)
        grad_product = -(exact(grad_three, two, NT) + exact(grad_two, one, NT) + grad_one)
        grad_kernel = grad_kernel + exact(grad_product, before, NT)
        grad_inverse = 0.25 * exact(grad_inverse, three, NT) + exact(kernel, grad_product, TN)
    total = keep["total"][...]
    turned = grad_inverse.T / total
    weighted = jnp.sum(jnp.where(blocks, turned * kernel, 0.0), axis=1, keepdims=True)
    weighted = head_sums(jnp.broadcast_to(weighted, kernel.shape))
    grad_kernel = grad_kernel + turned - 2.0 * kernel * weighted / total
    grad_scores = SCALE * kernel * (grad_kernel - jnp.sum(kernel * grad_kernel, axis=1, keepdims=True))
    grad_q_marks = exact(grad_scores, k_marks)
    grad_k_marks = exact(grad_scores, q_marks, TN)
    grad_k_marks = grad_k_marks + jnp.where(blocks, mm_left(grad_token, queries), 0.0)
    grad_key = mm_left(grad_summary, values, NT) - jnp.sum(grad_summary * summary, axis=1, keepdims=True)
    grad_key = SCALE * key_weights * grad_key
    grad_q_marks = grad_q_marks + jnp.where(blocks, mm_left(grad_key, keys), 0.0)
    grad_q_marks = (grad_q_marks[:MARKS] + grad_q_marks[MARKS:]) / counts
    grad_k_marks = (grad_k_marks[:MARKS] + grad_k_marks[MARKS:]) / counts
    high, rest = halves(grad_q_marks)
    result[0] = (mm_both(grad_token, k_marks, TN) + mm(member, high) + mm(member, rest)).astype(BF16)
    high, rest = halves(grad_k_marks)
    result[1] = (mm_both(grad_key, q_marks, TN) + mm(member, high) + mm(member, rest)).astype(BF16)
    blended[...] = mm_both(key_weights, grad_summary, TN)
    last = high_marks[MARKS - 1 :]
    valid_column = iota((length, 1), 0) < last
    padded[0:HALF, :] = jnp.zeros((HALF, LANES), BF16)
    padded[HALF : HALF + length, :] = jnp.where(valid_column, values, jnp.zeros_like(values))
    padded[HALF + length :, :] = jnp.zeros((LANES - HALF, LANES), BF16)
    padded_grads[0:HALF, :] = jnp.zeros((HALF, LANES), BF16)
    padded_grads[HALF : HALF + length, :] = grads
    padded_grads[HALF + length :, :] = jnp.zeros((LANES - HALF, LANES), BF16)

    def store(start, block):
        rows = start + iota((LANES, 1), 0)
        total_rows = blended[pl.ds(start, LANES), :] + jnp.where(rows < last, block, 0.0)
        result[2, pl.ds(start, LANES), :] = total_rows.astype(BF16)

    convolve(padded_grads, [band(taps[2:3]), band(taps[3:4])], length, store)
    first = iota((LANES, LANES), 1) < HEAD_DIM

    def block(step, carry):
        start = pl.multiple_of(step * LANES, LANES)
        own = padded_grads[pl.ds(start + HALF, LANES), :]
        window = padded[pl.ds(start, 2 * LANES), :]
        none = jnp.zeros_like(own)
        return (
            carry[0] + mm(jnp.where(first, own, none), window, NT),
            carry[1] + mm(jnp.where(first, none, own), window, NT),
        )

    start_sum = jnp.zeros((LANES, 2 * LANES), F32)
    sums = lax.fori_loop(0, length // LANES, block, (start_sum, start_sum))
    wide = 2 * LANES
    for head in range(2):
        folded = sums[head][0:8]
        for group in range(1, LANES // 8):
            rows = sums[head][8 * group : 8 * group + 8]
            folded = folded + pltpu.roll(rows, wide - 8 * group, 1)
        line = folded[0:1]
        for row in range(1, 8):
            line = line + pltpu.roll(folded[row : row + 1], wide - row, 1)
        grad_taps[head : head + 1, :] = line


TASKS = MICRO * PAIRS
KEPT = ("q_marks", "k_marks", "kernel", "total", "inverse", "product", "two", "three", "key_weights", "summary", "mixed", "token_weights")


def kept_shapes(length):
    square = (LANES, LANES)
    shapes = {name: square for name in KEPT}
    shapes["inverse"] = (NS_ITERS + 1,) + square
    for name in ("product", "two", "three"):
        shapes[name] = (NS_ITERS,) + square
    shapes["key_weights"] = shapes["token_weights"] = (LANES, length)
    return shapes


def owner_of(task, count):
    return task * count // TASKS


def task_of(me, count):
    task = (me * TASKS + count - 1) // count
    return task, owner_of(task, count) == me


def greet(count):
    me = lax.axis_index("dp")
    barrier = pltpu.get_barrier_semaphore()

    def signal(step, carry):
        pl.semaphore_signal(barrier, inc=1, device_id={"dp": lax.rem(me + step, count)}, device_id_type=MESH)
        return carry

    lax.fori_loop(1, count, signal, 0)
    pl.semaphore_wait(barrier, count - 1)


def scatter_tasks(count, piece, source, slab, send, receive):
    me = lax.axis_index("dp")

    def one(step, finish):
        task = lax.rem(task_of(me, count)[0] + step, TASKS)
        owner = owner_of(task, count)
        micro = task // PAIRS
        lanes = pl.ds(pl.multiple_of(lax.rem(task, PAIRS) * LANES, LANES), LANES)
        rows = pl.ds(pl.multiple_of(me * piece, piece), piece)
        outgoing = source.at[:, micro, :, lanes]
        landing = slab.at[:, rows, :]

        @pl.when(owner != me)
        def _():
            copy = pltpu.make_async_remote_copy(outgoing, landing, send.at[task], receive.at[me], device_id={"dp": owner}, device_id_type=MESH)
            if finish:
                copy.wait_send()
            else:
                copy.start()

        @pl.when((owner == me) & (not finish))
        def _():
            pltpu.make_async_copy(outgoing, landing, receive.at[me]).start()

    def run(finish):
        def body(step, carry):
            one(step, finish)
            return carry

        lax.fori_loop(0, TASKS, body, 0)

    return run


def await_slab(count, piece, slab, receive):
    def body(origin, carry):
        landing = slab.at[:, pl.ds(pl.multiple_of(origin * piece, piece), piece), :]
        pltpu.make_async_copy(landing, landing, receive.at[origin]).wait()
        return carry

    lax.fori_loop(0, count, body, 0)


def return_rows(count, piece, result, target, send, receive):
    me = lax.axis_index("dp")
    task = task_of(me, count)[0]
    micro = task // PAIRS
    lanes = pl.ds(pl.multiple_of(lax.rem(task, PAIRS) * LANES, LANES), LANES)

    def run(finish):
        def body(step, carry):
            peer = lax.rem(me + step, count)
            rows = pl.ds(pl.multiple_of(peer * piece, piece), piece)
            outgoing = result.at[:, rows, :]
            landing = target.at[:, micro, :, lanes]

            @pl.when(peer != me)
            def _():
                copy = pltpu.make_async_remote_copy(outgoing, landing, send.at[peer], receive.at[task], device_id={"dp": peer}, device_id_type=MESH)
                if finish:
                    copy.wait_send()
                else:
                    copy.start()

            @pl.when((peer == me) & (not finish))
            def _():
                pltpu.make_async_copy(outgoing, landing, receive.at[task]).start()

            return carry

        lax.fori_loop(0, count, body, 0)

    return run


def await_rows(target, receive):
    def body(task, carry):
        lanes = pl.ds(pl.multiple_of(lax.rem(task, PAIRS) * LANES, LANES), LANES)
        landing = target.at[:, task // PAIRS, :, lanes]
        pltpu.make_async_copy(landing, landing, receive.at[task]).wait()
        return carry

    lax.fori_loop(0, TASKS, body, 0)


def forward_kernel(count, piece, qkv, low_col, high_col, taps, mixed_rows, slab, *refs):
    keep = dict(zip(KEPT, refs))
    padded, blended, result, send_one, receive_one, send_two, receive_two = refs[len(KEPT) :]
    me = lax.axis_index("dp")
    task, owns = task_of(me, count)
    greet(count)
    out = scatter_tasks(count, piece, qkv, slab, send_one, receive_one)
    out(False)
    back = return_rows(count, piece, result, mixed_rows, send_two, receive_two)

    @pl.when(owns)
    def _():
        micro, pair = task // PAIRS, lax.rem(task, PAIRS)
        await_slab(count, piece, slab, receive_one)
        attend(slab[0], slab[1], slab[2], low_col[micro], high_col[micro], taps[pair], keep, padded, blended, result.at[0])
        back(False)

    out(True)
    await_rows(mixed_rows, receive_two)

    @pl.when(owns)
    def _():
        back(True)


def backward_kernel(count, piece, grads, low_col, high_col, low_row, high_row, taps, slab, *refs):
    keep = dict(zip(KEPT, refs))
    out_grads, grad_taps, grad_slab, padded, padded_grads, blended, result, send_one, receive_one, send_two, receive_two = refs[len(KEPT) :]
    me = lax.axis_index("dp")
    task, owns = task_of(me, count)
    greet(count)
    out = scatter_tasks(count, piece, grads, grad_slab, send_one, receive_one)
    out(False)
    back = return_rows(count, piece, result, out_grads, send_two, receive_two)
    grad_taps[...] = jnp.zeros(grad_taps.shape, F32)

    @pl.when(owns)
    def _():
        micro, pair = task // PAIRS, lax.rem(task, PAIRS)
        await_slab(count, piece, grad_slab, receive_one)
        attend_back(
            grad_slab[0], slab[0], slab[1], slab[2], low_col[micro], high_col[micro], low_row[micro], high_row[micro],
            taps[pair], keep, padded, padded_grads, blended, result, grad_taps.at[pair],
        )
        back(False)

    out(True)
    await_rows(out_grads, receive_two)

    @pl.when(owns)
    def _():
        back(True)


VMEM = pl.BlockSpec(memory_space=pltpu.VMEM)
DMA = pltpu.SemaphoreType.DMA


def attention_forward(count, qkv, marks, taps, ident):
    piece = qkv.shape[2]
    length = piece * count
    shapes = kept_shapes(length)
    results = pl.pallas_call(
        functools.partial(forward_kernel, count, piece),
        out_shape=[
            jax.ShapeDtypeStruct((1, MICRO, piece, D), BF16),
            jax.ShapeDtypeStruct((3, length, LANES), BF16),
        ]
        + [jax.ShapeDtypeStruct(shapes[name], F32) for name in KEPT],
        in_specs=[VMEM] * 4,
        out_specs=[VMEM] * (2 + len(KEPT)),
        scratch_shapes=[
            pltpu.VMEM((length + LANES, LANES), BF16),
            pltpu.VMEM((length, LANES), F32),
            pltpu.VMEM((1, length, LANES), BF16),
            DMA((TASKS,)),
            DMA((count,)),
            DMA((count,)),
            DMA((TASKS,)),
        ],
        compiler_params=pltpu.CompilerParams(collective_id=ident, has_side_effects=True, vmem_limit_bytes=60 << 20),
        name="attend_forward",
    )(qkv, marks[0], marks[1], taps)
    return results[0][0], results[1:]


def attention_backward(count, grads, marks, taps, kept, ident):
    piece = grads.shape[2]
    length = piece * count
    return pl.pallas_call(
        functools.partial(backward_kernel, count, piece),
        out_shape=[
            jax.ShapeDtypeStruct((3, MICRO, piece, D), BF16),
            jax.ShapeDtypeStruct((PAIRS, 2, 2 * LANES), F32),
        ],
        in_specs=[VMEM] * (7 + len(KEPT)),
        out_specs=[VMEM] * 2,
        scratch_shapes=[
            pltpu.VMEM((1, length, LANES), BF16),
            pltpu.VMEM((length + LANES, LANES), BF16),
            pltpu.VMEM((length + LANES, LANES), BF16),
            pltpu.VMEM((length, LANES), F32),
            pltpu.VMEM((3, length, LANES), BF16),
            DMA((TASKS,)),
            DMA((count,)),
            DMA((count,)),
            DMA((TASKS,)),
        ],
        compiler_params=pltpu.CompilerParams(collective_id=ident, has_side_effects=True, vmem_limit_bytes=60 << 20),
        name="attend_backward",
    )(grads, *marks, taps, *kept)


def gather_kernel(shard, out, local_sem, z_send, z_got, x_send, x_got, y_send, y_got, core_send, core_got):
    me = lax.axis_index("dp")
    x = lax.axis_index("rep")
    core, y, z = lax.rem(me, 2), lax.rem(me // 2, 2), me // 4
    half = shard.shape[0] // 2
    part = half // 2

    barrier = pltpu.get_barrier_semaphore()

    def peer(axis, sign=1):
        if axis == "x":
            return {"rep": 1 - x}
        if axis == "y":
            return {"dp": me + 2 - 4 * y}
        if axis == "core":
            return {"dp": me + 1 - 2 * core}
        return {"dp": me + 4 * sign}

    for axis in ("x", "y", "core"):
        pl.semaphore_signal(barrier, inc=1, device_id=peer(axis), device_id_type=MESH)
    for sign in (1, -1):

        @pl.when((z + sign >= 0) & (z + sign < 4))
        def _():
            pl.semaphore_signal(barrier, inc=1, device_id=peer("z", sign), device_id_type=MESH)

    pl.semaphore_wait(barrier, 4 + jnp.where((z > 0) & (z < 3), 1, 0))

    def rows(side, sub):
        return pl.ds(pl.multiple_of(side * half + sub * part, part), part)

    def side_rows(side):
        return pl.ds(pl.multiple_of(side * half, half), half)

    def remote(source, target, send, receive, where):
        return pltpu.make_async_remote_copy(source, target, send, receive, device_id=where, device_id_type=MESH)

    def spot(plane, row, side, sub):
        return out.at[plane, row, core, rows(side, sub), :]

    def move(axis, plane, row, side, sub, source=None):
        target = spot(plane, row, side, sub)
        source = target if source is None else source
        if axis == "core":
            return remote(source, target, core_send.at[plane, row, side, sub], core_got, peer("core"))
        send, receive = (x_send, x_got) if axis == "x" else (y_send, y_got)
        return remote(source, target, send.at[plane, row, side, sub], receive.at[plane, row, side, sub], peer(axis))

    def climb(plane, sub, sign, source=None):
        target = spot(plane, y, x, sub)
        way = 0 if sign > 0 else 1
        return remote(target if source is None else source, target, z_send.at[plane, sub, way], z_got.at[plane, sub], peer("z", sign))

    own = pltpu.make_async_copy(shard, out.at[z, y, core], local_sem)
    own.start()
    for sub in range(2):
        for sign in (1, -1):

            @pl.when((z + sign >= 0) & (z + sign < 4))
            def _():
                climb(z, sub, sign, shard.at[rows(x, sub), :]).start()

        move("y", z, y, x, sub, shard.at[rows(x, sub), :]).start()
    for side in range(2):
        for sub in range(2):
            move("core", z, y, side, sub, shard.at[rows(side, sub), :]).start()

    def at_distance(distance, act):
        for sign in (1, -1):
            plane = z - sign * distance

            @pl.when((plane >= 0) & (plane < 4))
            def _():
                act(plane, sign)

    def from_z(plane, sign):
        for sub in range(2):
            climb(plane, sub, sign).wait_recv()

            @pl.when((z + sign >= 0) & (z + sign < 4))
            def _():
                climb(plane, sub, sign).start()

            for axis in ("x", "y", "core"):
                move(axis, plane, y, x, sub).start()

    def take(axis, plane, row, side, sub, onward=None):
        move(axis, plane, row, side, sub).wait_recv()
        if onward is not None:
            move(onward, plane, row, side, sub).start()
        move("core", plane, row, side, sub).start()

    def first_square(plane, sign):
        take("x", plane, y, 1 - x, 0, "y")
        take("y", plane, 1 - y, x, 1, "x")
        take("y", plane, 1 - y, x, 0)
        take("x", plane, y, 1 - x, 1)

    def second_square(plane, sign):
        take("y", plane, 1 - y, 1 - x, 0)
        take("x", plane, 1 - y, 1 - x, 1)

    at_distance(1, from_z)
    for sub in range(2):
        take("y", z, 1 - y, x, sub, "x")
    at_distance(2, from_z)
    at_distance(1, first_square)
    at_distance(3, from_z)
    at_distance(2, first_square)
    for sub in range(2):
        take("x", z, 1 - y, 1 - x, sub)
    at_distance(1, second_square)
    at_distance(3, first_square)
    at_distance(2, second_square)
    at_distance(3, second_square)
    own.wait()

    def finish(plane, sign):
        for sub in range(2):

            @pl.when((z + sign >= 0) & (z + sign < 4))
            def _():
                climb(plane, sub, sign).wait_send()

            move("x", plane, y, x, sub).wait_send()
            move("y", plane, y, x, sub).wait_send()
        move("y", plane, y, 1 - x, 0).wait_send()
        move("x", plane, 1 - y, x, 1).wait_send()

    for distance in (1, 2, 3):
        at_distance(distance, finish)
    for sub in range(2):
        for sign in (1, -1):

            @pl.when((z + sign >= 0) & (z + sign < 4))
            def _():
                climb(z, sub, sign).wait_send()

        move("y", z, y, x, sub).wait_send()
        move("x", z, 1 - y, x, sub).wait_send()

    def core_sent(index, carry):
        plane, row, side, sub = index // 8, lax.rem(index // 4, 2), lax.rem(index // 2, 2), lax.rem(index, 2)
        move("core", plane, row, side, sub).wait_send()
        return carry

    lax.fori_loop(0, 32, core_sent, 0)
    column = out.at[:, :, 1 - core]
    pltpu.make_async_copy(column, column, core_got).wait()


def gather(shard):
    block_rows = shard.shape[0]
    return pl.pallas_call(
        gather_kernel,
        out_shape=jax.ShapeDtypeStruct((4, 2, 2, block_rows, D), BF16),
        in_specs=[VMEM],
        out_specs=pl.BlockSpec(memory_space=pl.ANY),
        scratch_shapes=[
            DMA,
            DMA((4, 2, 2)),
            DMA((4, 2)),
            DMA((4, 2, 2, 2)),
            DMA((4, 2, 2, 2)),
            DMA((4, 2, 2, 2)),
            DMA((4, 2, 2, 2)),
            DMA((4, 2, 2, 2)),
            DMA,
        ],
        compiler_params=pltpu.CompilerParams(collective_id=4, has_side_effects=True),
        name="gather",
    )(shard).reshape(16 * block_rows, D)


CHUNK = 48
SLICE = 16


def settle_kernel(
    block_rows, grads_last, grads_first, weights, first, second, small, small_first, small_second,
    grad_out, mean_out, small_out,
    own, got_core, got_y, got_z, inner, step_own, step_got, small_got, small_own, small_step, small_step_got,
    own_sem, core_send, core_got, y_send, y_got, z_send, z_got, inner_sem, rep_send, rep_got, small_send, small_sem, back_send, back_sem, small_rep,
):
    me = lax.axis_index("dp")
    other_rep = 1 - lax.axis_index("rep")
    core, y, z = lax.rem(me, 2), lax.rem(me // 2, 2), me // 4
    devices = 16
    per_layer = block_rows // CHUNK
    chunks = LAYERS * per_layer

    barrier = pltpu.get_barrier_semaphore()

    def signal(step, carry):
        pl.semaphore_signal(barrier, inc=1, device_id={"dp": lax.rem(me + step, devices)}, device_id_type=MESH)
        return carry

    lax.fori_loop(1, devices, signal, 0)
    pl.semaphore_signal(barrier, inc=1, device_id={"rep": other_rep}, device_id_type=MESH)
    pl.semaphore_wait(barrier, devices)

    def to_dp(source, target, send, receive, peer):
        return pltpu.make_async_remote_copy(source, target, send, receive, device_id={"dp": peer}, device_id_type=MESH)

    def to_rep(source, target, send, receive):
        return pltpu.make_async_remote_copy(source, target, send, receive, device_id={"rep": other_rep}, device_id_type=MESH)

    def rows_of(part):
        return pl.ds(pl.multiple_of(part * CHUNK, CHUNK), CHUNK)

    def core_copy(source, chunk, part):
        return to_dp(source.at[:, :, 1 - core, rows_of(part), :], got_core.at[chunk], core_send.at[chunk], core_got.at[chunk], me + 1 - 2 * core)

    def own_copy(source, chunk, part):
        return pltpu.make_async_copy(source.at[:, :, core, rows_of(part), :], own.at[chunk], own_sem.at[chunk])

    for order, source in enumerate((grads_last, grads_first)):

        def begin(part, carry):
            chunk = order * per_layer + part
            core_copy(source, chunk, part).start()
            own_copy(source, chunk, part).start()
            return carry

        lax.fori_loop(0, per_layer, begin, 0)

    def small_copy(step):
        peer = lax.rem(me + step, devices)
        return to_dp(small.at[peer], small_got.at[me], small_send.at[peer], small_sem.at[me], peer)

    def small_begin(step, carry):
        small_copy(step).start()
        return carry

    lax.fori_loop(1, devices, small_begin, 0)

    def y_copy(chunk):
        return to_dp(own.at[chunk, :, 1 - y], got_y.at[chunk], y_send.at[chunk], y_got.at[chunk], me + 2 - 4 * y)

    def z_copy(chunk, hop):
        there = lax.rem(z + hop, 4)
        return to_dp(own.at[chunk, there, y], got_z.at[chunk, hop - 1], z_send.at[chunk, hop - 1], z_got.at[chunk, hop - 1], there * 4 + lax.rem(me, 4))

    def place(chunk):
        return LAYERS - 1 - chunk // per_layer, rows_of(lax.rem(chunk, per_layer))

    def inner_copies(chunk):
        level, rows = place(chunk)
        slot = lax.rem(chunk, 4)
        return [
            pltpu.make_async_copy(array.at[level, rows, :], inner.at[slot, index], inner_sem.at[slot, index])
            for index, array in enumerate((weights, first, second))
        ]

    def rep_copy(chunk):
        return to_rep(step_own.at[chunk], step_got.at[chunk], rep_send.at[chunk], rep_got.at[chunk])

    def change(grad, first_old, second_old):
        new_first = ADAM_ONE * first_old + (1.0 - ADAM_ONE) * grad
        new_second = ADAM_TWO * second_old + (1.0 - ADAM_TWO) * grad * grad
        return new_first * (1.0 / (1.0 - ADAM_ONE**STEP_COUNT)) / (jnp.sqrt(new_second * (1.0 / (1.0 - ADAM_TWO**STEP_COUNT))) + ADAM_EPSILON)

    def stage_core(chunk):
        own_copy(grads_last, chunk, 0).wait()
        core_copy(grads_last, chunk, 0).wait_recv()
        for there in range(4):
            for side in range(2):
                own[chunk, there, side] = own[chunk, there, side] + got_core[chunk, there, side]
        y_copy(chunk).start()
        for copy in inner_copies(chunk):
            copy.start()

    def stage_y(chunk):
        y_copy(chunk).wait_recv()
        for there in range(4):
            own[chunk, there, y] = own[chunk, there, y] + got_y[chunk, there]
        for hop in range(1, 4):
            z_copy(chunk, hop).start()

    def stage_z(chunk):
        for hop in range(1, 4):
            z_copy(chunk, hop).wait_recv()
        for copy in inner_copies(chunk):
            copy.wait()
        total = own[chunk, z, y].astype(F32)
        for hop in range(3):
            total = total + got_z[chunk, hop].astype(F32)
        level, rows = place(chunk)
        grad_out[level, rows, :] = total
        slot = lax.rem(chunk, 4)
        step = change(total, inner[slot, 1], inner[slot, 2]) + WEIGHT_DECAY * inner[slot, 0]
        step_own[chunk] = (LR_INNER * step).astype(BF16)
        rep_copy(chunk).start()

    def stage_rep(chunk):
        rep_copy(chunk).wait_recv()
        level, rows = place(chunk)
        mean_out[level, rows, :] = 0.5 * (step_own[chunk].astype(F32) + step_got[chunk].astype(F32))

    def small_rep_copy():
        return to_rep(small_step, small_step_got, small_rep.at[0], small_rep.at[1])

    def small_back(step):
        peer = lax.rem(me + step, devices)
        return to_dp(small_own, small_out.at[me], back_send.at[peer], back_sem.at[me], peer)

    def small_sum():
        total = small[me]

        def add(step, total):
            peer = lax.rem(me + step, devices)
            pltpu.make_async_copy(small_got.at[peer], small_got.at[peer], small_sem.at[peer]).wait()
            return total + small_got[peer]

        total = lax.fori_loop(1, devices, add, total)
        small_own[0] = total
        small_step[...] = (LR_SMALL * change(total, small_first[me], small_second[me])).astype(BF16)
        small_rep_copy().start()

    def small_spread():
        small_rep_copy().wait_recv()
        small_own[1] = 0.5 * (small_step[...].astype(F32) + small_step_got[...].astype(F32))
        small_out[me] = small_own[...]

        def send(step, carry):
            small_back(step).start()
            return carry

        lax.fori_loop(1, devices, send, 0)

    def turn(now, carry):
        for lag, stage in ((0, stage_core), (2, stage_y), (3, stage_z), (4, stage_rep)):

            @pl.when((now >= lag) & (now < chunks + lag))
            def _():
                stage(now - lag)

        pl.when(now == 2)(small_sum)
        pl.when(now == 5)(small_spread)
        return carry

    lax.fori_loop(0, chunks + 4, turn, 0)

    def drain(chunk, carry):
        core_copy(grads_last, chunk, 0).wait_send()
        y_copy(chunk).wait_send()
        for hop in range(1, 4):
            z_copy(chunk, hop).wait_send()
        rep_copy(chunk).wait_send()
        return carry

    lax.fori_loop(0, chunks, drain, 0)

    def small_drain(step, carry):
        peer = lax.rem(me + step, devices)
        small_copy(step).wait_send()
        small_back(step).wait_send()
        pltpu.make_async_copy(small_own, small_out.at[peer], back_sem.at[peer]).wait()
        return carry

    lax.fori_loop(1, devices, small_drain, 0)
    small_rep_copy().wait_send()


def settle(grads, weights, first, second, small, small_first, small_second):
    block_rows = weights.shape[1]
    chunks = LAYERS * block_rows // CHUNK
    anywhere = pl.BlockSpec(memory_space=pl.ANY)
    devices = 16
    piece = (CHUNK, D)
    return pl.pallas_call(
        functools.partial(settle_kernel, block_rows),
        out_shape=[
            jax.ShapeDtypeStruct(weights.shape, F32),
            jax.ShapeDtypeStruct(weights.shape, F32),
            jax.ShapeDtypeStruct((devices, 2, SLICE, LANES), F32),
        ],
        in_specs=[anywhere] * 5 + [VMEM] * 3,
        out_specs=[VMEM] * 3,
        scratch_shapes=[
            pltpu.VMEM((chunks, 4, 2) + piece, BF16),
            pltpu.VMEM((chunks, 4, 2) + piece, BF16),
            pltpu.VMEM((chunks, 4) + piece, BF16),
            pltpu.VMEM((chunks, 3) + piece, BF16),
            pltpu.VMEM((4, 3) + piece, F32),
            pltpu.VMEM((chunks,) + piece, BF16),
            pltpu.VMEM((chunks,) + piece, BF16),
            pltpu.VMEM((devices, SLICE, LANES), F32),
            pltpu.VMEM((2, SLICE, LANES), F32),
            pltpu.VMEM((SLICE, LANES), BF16),
            pltpu.VMEM((SLICE, LANES), BF16),
            DMA((chunks,)),
            DMA((chunks,)),
            DMA((chunks,)),
            DMA((chunks,)),
            DMA((chunks,)),
            DMA((chunks, 3)),
            DMA((chunks, 3)),
            DMA((4, 3)),
            DMA((chunks,)),
            DMA((chunks,)),
            DMA((devices,)),
            DMA((devices,)),
            DMA((devices,)),
            DMA((devices,)),
            DMA((2,)),
        ],
        compiler_params=pltpu.CompilerParams(collective_id=3, has_side_effects=True, vmem_limit_bytes=63 << 20),
        name="settle",
    )(*[array.reshape(4, 2, 2, block_rows, D) for array in grads], weights, first, second, small, small_first, small_second)


def sliced(array):
    flat = array.reshape(-1)
    return jnp.pad(flat, (0, 16 * SLICE * LANES - flat.shape[0])).reshape(16, SLICE, LANES)


def unsliced(array, shape):
    return array.reshape(-1)[: shape[0] * shape[1]].reshape(shape)


def dense(a, b, dims=NN):
    return mm(a, b, dims)


def layer_norm(values, gain_vec, shift_vec):
    row_mean = jnp.mean(values, axis=-1, keepdims=True)
    centred = values - row_mean
    variance = jnp.mean(centred * centred, axis=-1, keepdims=True)
    return centred * lax.rsqrt(variance + 1e-05) * gain_vec + shift_vec


def unpack(params):
    blocks = [params[index * D : (index + 1) * D] for index in range(8)]
    bias_up = params[8 * D : 8 * D + FF]
    conv_taps = params[8 * D + FF :].reshape(HEADS, TAPS)
    return (blocks, bias_up, conv_taps)


def pair_taps(conv_taps):
    both = jnp.stack([conv_taps.reshape(PAIRS, 2, TAPS), conv_taps[:, ::-1].reshape(PAIRS, 2, TAPS)], axis=1)
    both = both.reshape(PAIRS, 4, TAPS)
    return jnp.pad(both, ((0, 0), (0, 0), (0, 2 * LANES - TAPS)))


def split_rows(rows):
    return rows[: 3 * D].reshape(3, D, D), rows[3 * D : 4 * D], rows[4 * D : 4 * D + FF], rows[4 * D + FF :]


def forward_layer(count, inputs, rows, params, marks, ident):
    piece = inputs.shape[0] // MICRO
    blocks, bias_up, conv_taps = unpack(params)
    proj, out_weight, up_weight, down_weight = split_rows(rows)
    low_in = inputs.astype(BF16)
    bias = jnp.stack([blocks[0], jnp.zeros_like(blocks[0]), blocks[1]])
    qkv = jnp.stack([(dense(low_in, proj[part]) + bias[part]).astype(BF16) for part in range(3)])
    low_comb, kept = attention_forward(count, qkv.reshape(3, MICRO, piece, D), marks, pair_taps(conv_taps), ident)
    low_comb = low_comb.reshape(MICRO * piece, D)
    resid_one = inputs + (dense(low_comb, out_weight) + blocks[2])
    hidden_one = layer_norm(resid_one, blocks[4], blocks[5])
    low_hidden = hidden_one.astype(BF16)
    upward = dense(low_hidden, up_weight, NT) + bias_up
    low_act = jax.nn.gelu(upward).astype(BF16)
    resid_two = hidden_one + (dense(low_act, down_weight) + blocks[3])
    output = layer_norm(resid_two, blocks[6], blocks[7])
    return output, (low_in, kept, low_comb, resid_one, low_hidden, upward, low_act, resid_two)


def backward_layer(count, grad_output, rows, params, marks, state, ident):
    low_in, kept, low_comb, resid_one, low_hidden, upward, low_act, resid_two = state
    total = low_in.shape[0]
    piece = total // MICRO
    blocks, bias_up, conv_taps = unpack(params)
    proj, out_weight, up_weight, down_weight = split_rows(rows)
    _, pull_two = jax.vjp(layer_norm, resid_two, blocks[6], blocks[7])
    grad_two, grad_gain_two, grad_shift_two = pull_two(grad_output)
    low_down = grad_two.astype(BF16)
    grad_bias_down = jnp.sum(low_down.astype(F32), axis=0)
    grad_act = dense(low_down, down_weight, NT)
    _, pull_gelu = jax.vjp(jax.nn.gelu, upward)
    low_up = pull_gelu(grad_act)[0].astype(BF16)
    grad_bias_up = jnp.sum(low_up.astype(F32), axis=0)
    grad_hidden = grad_two + dense(low_up, up_weight)
    _, pull_one = jax.vjp(layer_norm, resid_one, blocks[4], blocks[5])
    grad_one, grad_gain_one, grad_shift_one = pull_one(grad_hidden)
    low_branch = grad_one.astype(BF16)
    grad_bias_out = jnp.sum(low_branch.astype(F32), axis=0)
    grad_comb = dense(low_branch, out_weight, NT).astype(BF16)
    low_grads, grad_taps = attention_backward(count, grad_comb.reshape(1, MICRO, piece, D), marks, pair_taps(conv_taps), kept, ident)
    low_grads = low_grads.reshape(3, total, D)
    grad_bias_q = jnp.sum(low_grads[0].astype(F32), axis=0)
    grad_bias_v = jnp.sum(low_grads[2].astype(F32), axis=0)
    grad_in = grad_one + sum(dense(low_grads[part], proj[part], NT) for part in range(3))
    parts = [dense(low_in, low_grads[part], TN).astype(BF16) for part in range(3)]
    parts = parts + [
        dense(low_comb, low_branch, TN).astype(BF16),
        dense(low_up, low_hidden, TN).astype(BF16),
        dense(low_act, low_down, TN).astype(BF16),
    ]
    grad_small = jnp.concatenate(
        [
            grad_bias_q,
            grad_bias_v,
            grad_bias_out,
            grad_bias_down,
            grad_gain_one,
            grad_shift_one,
            grad_gain_two,
            grad_shift_two,
            grad_bias_up,
            grad_taps[:, :, :TAPS].reshape(-1),
        ]
    )
    return grad_in, jnp.concatenate(parts, axis=0), grad_small


def moments(first, second, grad):
    return ADAM_ONE * first + (1.0 - ADAM_ONE) * grad, ADAM_TWO * second + (1.0 - ADAM_TWO) * grad * grad


def adam(weights, first, second, grad, rate, decay):
    correct_one = 1.0 - ADAM_ONE**STEP_COUNT
    correct_two = 1.0 - ADAM_TWO**STEP_COUNT
    new_first, new_second = moments(first, second, grad)
    step = new_first / correct_one / (jnp.sqrt(new_second / correct_two) + ADAM_EPSILON)
    return new_first, new_second, rate * (step + decay * weights)


def shards(
    hidden,
    bounds,
    cotangent,
    weights,
    small_params,
    first_big,
    second_big,
    first_small,
    second_small,
    outer_big,
    outer_small,
):
    count = lax.axis_size("dp")
    piece = hidden.shape[3]
    total = MICRO * piece
    low_weights = weights.astype(BF16)
    held = [lax.all_gather(low_weights[level], "dp", axis=0, tiled=True) for level in range(LAYERS)]
    if count == 16:
        held[0] = gather(low_weights[0])
    edges = bounds[0, :, 0, :]
    low_edges, high_edges = edges[:, :-1], edges[:, 1:]
    marks = (low_edges[:, :, None], high_edges[:, :, None], low_edges[:, None, :], high_edges[:, None, :])
    positions = lax.axis_index("dp") * piece + jnp.arange(piece, dtype=jnp.int32)
    valid = (positions[None, :] < edges[:, -1:]).astype(F32).reshape(total, 1)
    activation = hidden[0, :, 0].reshape(total, D).astype(F32)
    states = []
    for level in range(LAYERS):
        activation, state = forward_layer(count, activation, held[level], small_params[level], marks, 1)
        states.append(state)
    gradient = cotangent[0, :, 0].reshape(total, D).astype(F32) * valid
    grad_parts, small_parts = [None] * LAYERS, [None] * LAYERS
    for level in reversed(range(LAYERS)):
        gradient, grad_rows, small_parts[level] = backward_layer(count, gradient, held[level], small_params[level], marks, states[level], 2)
        grad_parts[level] = grad_rows
    small_parts = jnp.stack(small_parts)
    if count == 16:
        grad_big, mean_big, small_both = settle(
            grad_parts[::-1], weights, first_big[0], second_big[0], sliced(small_parts), sliced(first_small[0]), sliced(second_small[0])
        )
        grad_small, mean_small = [unsliced(small_both[:, which], small_parts.shape) for which in range(2)]
    else:
        grad_big = jnp.stack([lax.psum_scatter(rows, "dp", scatter_dimension=0, tiled=True).astype(F32) for rows in grad_parts])
        grad_small = lax.psum(small_parts, "dp")
        reps = lax.axis_size("rep")
        delta_big = adam(weights, first_big[0], second_big[0], grad_big, LR_INNER, WEIGHT_DECAY)[2]
        delta_small = adam(small_params, first_small[0], second_small[0], grad_small, LR_SMALL, 0.0)[2]
        mean_big = lax.psum(delta_big.astype(BF16), "rep").astype(F32) / reps
        mean_small = lax.psum(delta_small.astype(BF16), "rep").astype(F32) / reps
    new_first, new_second = moments(first_big[0], second_big[0], grad_big)
    new_first_small, new_second_small = moments(first_small[0], second_small[0], grad_small)
    outer_big_new = MOMENTUM * outer_big + mean_big
    outer_small_new = MOMENTUM * outer_small + mean_small
    weights_new = weights - LR_OUTER * (mean_big + MOMENTUM * outer_big_new)
    small_new = small_params - LR_OUTER * (mean_small + MOMENTUM * outer_small_new)
    shape = (1, MICRO, 1, piece, D)
    return (
        activation.reshape(shape),
        gradient.reshape(shape),
        new_first[None],
        new_second[None],
        new_first_small[None],
        new_second_small[None],
        outer_big_new,
        outer_small_new,
        weights_new,
        small_new,
        weights_new.astype(BF16),
    )


def solution(mesh):
    placed = (
        P("rep", None, None, "dp", None),
        P("rep", None, None, None),
        P("rep", None, None, "dp", None),
        P(None, "dp", None),
        P(),
        P("rep", None, "dp", None),
        P("rep", None, "dp", None),
        P("rep", None, None),
        P("rep", None, None),
        P(None, "dp", None),
        P(),
    )
    return jax.shard_map(
        shards,
        mesh=mesh,
        in_specs=placed,
        out_specs=(
            P("rep", None, None, "dp", None),
            P("rep", None, None, "dp", None),
            P("rep", None, "dp", None),
            P("rep", None, "dp", None),
            P("rep", None, None),
            P("rep", None, None),
            P(None, "dp", None),
            P(),
            P(None, "dp", None),
            P(),
            P(None, "dp", None),
        ),
        check_vma=False,
    )
```

```python
import functools

import jax
import jax.numpy as jnp
from jax import lax
from jax.experimental import pallas as pl
from jax.experimental.pallas import tpu as pltpu
from jax.sharding import PartitionSpec as P

D = 768
HEADS = 12
FF = 3072
TAPS = 33
NS_ITERS = 6
LAYERS = 2
MICRO = 2
STEP_COUNT = 5


PRECISE = lax.Precision.HIGHEST
ADAM_ONE = 0.9
ADAM_TWO = 0.95
ADAM_EPSILON = 1e-08
WEIGHT_DECAY = 0.1
LR_INNER = 0.04
LR_SMALL = 0.2
LR_OUTER = 0.7
MOMENTUM = 0.9

HEAD_DIM = 64
MARKS = 64
HALF = TAPS // 2
PAIRS = HEADS // 2
LANES = 128
SCALE = HEAD_DIM**-0.5
NEG = -1e30
MESH = pl.DeviceIdType.MESH
F32 = jnp.float32
BF16 = jnp.bfloat16
NN = (((1,), (0,)), ((), ()))
NT = (((1,), (1,)), ((), ()))
TN = (((0,), (0,)), ((), ()))


def mm(a, b, dims=NN):
    return lax.dot_general(a, b, dims, preferred_element_type=F32)


def halves(a):
    high = a.astype(BF16)
    return high, (a - high.astype(F32)).astype(BF16)


def mm_left(a, b, dims=NN):
    high, rest = halves(a)
    return mm(high, b, dims) + mm(rest, b, dims)


def mm_both(a, b, dims=NN):
    ah, al = halves(a)
    bh, bl = halves(b)
    return mm(ah, bh, dims) + (mm(ah, bl, dims) + mm(al, bh, dims))


def exact(a, b, dims=NN):
    return lax.dot_general(a, b, dims, precision=PRECISE, preferred_element_type=F32)


def iota(shape, dim):
    return lax.broadcasted_iota(jnp.int32, shape, dim)


def diagonal_blocks():
    return (iota((LANES, LANES), 0) < MARKS) == (iota((LANES, LANES), 1) < HEAD_DIM)


def unit():
    return (iota((LANES, LANES), 0) == iota((LANES, LANES), 1)).astype(F32)


def per_head(marks):
    first = iota(marks.shape, 1) < HEAD_DIM
    return jnp.concatenate([jnp.where(first, marks, 0.0), jnp.where(first, 0.0, marks)], axis=0)


def head_sums(a):
    rows, cols = a.shape
    split = a.reshape(2, rows // 2, cols)
    return jnp.broadcast_to(jnp.sum(split, axis=1, keepdims=True), split.shape).reshape(rows, cols)


def head_tops(a):
    rows, cols = a.shape
    split = a.reshape(2, rows // 2, cols)
    return jnp.broadcast_to(jnp.max(split, axis=1, keepdims=True), split.shape).reshape(rows, cols)


def band(taps_row):
    wide = jnp.broadcast_to(taps_row, (LANES, 2 * LANES))
    return pltpu.roll(wide, 0, 1, stride=1, stride_axis=0)


def convolve(padded, bands, length, store):
    first = iota((LANES, LANES), 1) < HEAD_DIM
    pairs = [halves(one) for one in bands]

    def block(at, carry):
        start = pl.multiple_of(at * LANES, LANES)
        window = padded[pl.ds(start, 2 * LANES), :]
        out = [mm(high, window) + mm(rest, window) for high, rest in pairs]
        store(start, jnp.where(first, out[0], out[1]))
        return carry

    lax.fori_loop(0, length // LANES, block, 0)


def attend(queries, keys, values, low_marks, high_marks, taps, keep, padded, blended, result):
    length = queries.shape[0]
    at = iota((MARKS, length), 1)
    member = ((low_marks <= at) & (at < high_marks)).astype(F32).astype(BF16)
    counts = (high_marks - low_marks).astype(F32)
    blocks, eye = diagonal_blocks(), unit()
    q_marks = per_head(mm(member, queries) / counts)
    k_marks = per_head(mm(member, keys) / counts)
    scores = jnp.where(blocks, SCALE * exact(q_marks, k_marks, NT), NEG)
    weights = jnp.exp(scores - jnp.max(scores, axis=1, keepdims=True))
    kernel = weights / jnp.sum(weights, axis=1, keepdims=True)
    total = head_sums(jnp.broadcast_to(jnp.sum(kernel * kernel, axis=1, keepdims=True), kernel.shape))
    inverse = kernel.T / total
    keep["q_marks"][...] = q_marks
    keep["k_marks"][...] = k_marks
    keep["kernel"][...] = kernel
    keep["total"][...] = total
    for sweep in range(NS_ITERS):
        product = exact(kernel, inverse)
        one = 7.0 * eye - product
        two = 15.0 * eye - exact(product, one)
        three = 13.0 * eye - exact(product, two)
        keep["inverse"][sweep] = inverse
        keep["product"][sweep] = product
        keep["two"][sweep] = two
        keep["three"][sweep] = three
        inverse = 0.25 * exact(inverse, three)
    keep["inverse"][NS_ITERS] = inverse
    valid = at[:1] < high_marks[MARKS - 1 :]
    key_scores = jnp.where(valid, SCALE * mm_left(q_marks, keys, NT), NEG)
    key_exp = jnp.where(valid, jnp.exp(key_scores - jnp.max(key_scores, axis=1, keepdims=True)), 0.0)
    key_weights = key_exp / jnp.sum(key_exp, axis=1, keepdims=True)
    keep["key_weights"][...] = key_weights
    summary = jnp.where(blocks, mm_left(key_weights, values), 0.0)
    mixed = exact(inverse, summary)
    keep["summary"][...] = summary
    keep["mixed"][...] = mixed
    token_scores = SCALE * mm_left(k_marks, queries, NT)
    token_exp = jnp.exp(token_scores - head_tops(token_scores))
    token_weights = token_exp / head_sums(token_exp)
    keep["token_weights"][...] = token_weights
    blended[...] = mm_both(token_weights, mixed, TN)
    valid_column = iota((length, 1), 0) < high_marks[MARKS - 1 :]
    padded[0:HALF, :] = jnp.zeros((HALF, LANES), BF16)
    padded[HALF : HALF + length, :] = jnp.where(valid_column, values, jnp.zeros_like(values))
    padded[HALF + length :, :] = jnp.zeros((LANES - HALF, LANES), BF16)

    def store(start, block):
        result[pl.ds(start, LANES), :] = (blended[pl.ds(start, LANES), :] + block).astype(BF16)

    convolve(padded, [band(taps[0:1]), band(taps[1:2])], length, store)


def attend_back(grads, queries, keys, values, low_marks, high_marks, low_row, high_row, taps, keep, padded, padded_grads, blended, result, grad_taps):
    length = grads.shape[0]
    at = iota((length, MARKS), 0)
    member = ((low_row <= at) & (at < high_row)).astype(F32).astype(BF16)
    counts = (high_marks - low_marks).astype(F32)
    blocks, eye = diagonal_blocks(), unit()
    q_marks, k_marks = keep["q_marks"][...], keep["k_marks"][...]
    token_weights, key_weights = keep["token_weights"][...], keep["key_weights"][...]
    summary, mixed = keep["summary"][...], keep["mixed"][...]
    kernel = keep["kernel"][...]
    inverse = keep["inverse"][NS_ITERS]
    grad_mixed = jnp.where(blocks, mm_left(token_weights, grads), 0.0)
    grad_token = token_weights * mm_left(mixed, grads, NT)
    grad_token = SCALE * (grad_token - token_weights * head_sums(grad_token))
    grad_summary = exact(inverse, grad_mixed, TN)
    grad_inverse = exact(grad_mixed, summary, NT)
    grad_kernel = jnp.zeros_like(kernel)
    for sweep in reversed(range(NS_ITERS)):
        before, product = keep["inverse"][sweep], keep["product"][sweep]
        one = 7.0 * eye - product
        two, three = keep["two"][sweep], keep["three"][sweep]
        grad_three = 0.25 * exact(before, grad_inverse, TN)
        grad_two = -exact(product, grad_three, TN)
        grad_one = -exact(product, grad_two, TN)
        grad_product = -(exact(grad_three, two, NT) + exact(grad_two, one, NT) + grad_one)
        grad_kernel = grad_kernel + exact(grad_product, before, NT)
        grad_inverse = 0.25 * exact(grad_inverse, three, NT) + exact(kernel, grad_product, TN)
    total = keep["total"][...]
    turned = grad_inverse.T / total
    weighted = jnp.sum(jnp.where(blocks, turned * kernel, 0.0), axis=1, keepdims=True)
    weighted = head_sums(jnp.broadcast_to(weighted, kernel.shape))
    grad_kernel = grad_kernel + turned - 2.0 * kernel * weighted / total
    grad_scores = SCALE * kernel * (grad_kernel - jnp.sum(kernel * grad_kernel, axis=1, keepdims=True))
    grad_q_marks = exact(grad_scores, k_marks)
    grad_k_marks = exact(grad_scores, q_marks, TN)
    grad_k_marks = grad_k_marks + jnp.where(blocks, mm_left(grad_token, queries), 0.0)
    grad_key = mm_left(grad_summary, values, NT) - jnp.sum(grad_summary * summary, axis=1, keepdims=True)
    grad_key = SCALE * key_weights * grad_key
    grad_q_marks = grad_q_marks + jnp.where(blocks, mm_left(grad_key, keys), 0.0)
    grad_q_marks = (grad_q_marks[:MARKS] + grad_q_marks[MARKS:]) / counts
    grad_k_marks = (grad_k_marks[:MARKS] + grad_k_marks[MARKS:]) / counts
    high, rest = halves(grad_q_marks)
    result[0] = (mm_both(grad_token, k_marks, TN) + mm(member, high) + mm(member, rest)).astype(BF16)
    high, rest = halves(grad_k_marks)
    result[1] = (mm_both(grad_key, q_marks, TN) + mm(member, high) + mm(member, rest)).astype(BF16)
    blended[...] = mm_both(key_weights, grad_summary, TN)
    last = high_marks[MARKS - 1 :]
    valid_column = iota((length, 1), 0) < last
    padded[0:HALF, :] = jnp.zeros((HALF, LANES), BF16)
    padded[HALF : HALF + length, :] = jnp.where(valid_column, values, jnp.zeros_like(values))
    padded[HALF + length :, :] = jnp.zeros((LANES - HALF, LANES), BF16)
    padded_grads[0:HALF, :] = jnp.zeros((HALF, LANES), BF16)
    padded_grads[HALF : HALF + length, :] = grads
    padded_grads[HALF + length :, :] = jnp.zeros((LANES - HALF, LANES), BF16)

    def store(start, block):
        rows = start + iota((LANES, 1), 0)
        total_rows = blended[pl.ds(start, LANES), :] + jnp.where(rows < last, block, 0.0)
        result[2, pl.ds(start, LANES), :] = total_rows.astype(BF16)

    convolve(padded_grads, [band(taps[2:3]), band(taps[3:4])], length, store)
    first = iota((LANES, LANES), 1) < HEAD_DIM

    def block(step, carry):
        start = pl.multiple_of(step * LANES, LANES)
        own = padded_grads[pl.ds(start + HALF, LANES), :]
        window = padded[pl.ds(start, 2 * LANES), :]
        none = jnp.zeros_like(own)
        return (
            carry[0] + mm(jnp.where(first, own, none), window, NT),
            carry[1] + mm(jnp.where(first, none, own), window, NT),
        )

    start_sum = jnp.zeros((LANES, 2 * LANES), F32)
    sums = lax.fori_loop(0, length // LANES, block, (start_sum, start_sum))
    wide = 2 * LANES
    for head in range(2):
        folded = sums[head][0:8]
        for group in range(1, LANES // 8):
            rows = sums[head][8 * group : 8 * group + 8]
            folded = folded + pltpu.roll(rows, wide - 8 * group, 1)
        line = folded[0:1]
        for row in range(1, 8):
            line = line + pltpu.roll(folded[row : row + 1], wide - row, 1)
        grad_taps[head : head + 1, :] = line


TASKS = MICRO * PAIRS
KEPT = ("q_marks", "k_marks", "kernel", "total", "inverse", "product", "two", "three", "key_weights", "summary", "mixed", "token_weights")


def kept_shapes(length):
    square = (LANES, LANES)
    shapes = {name: square for name in KEPT}
    shapes["inverse"] = (NS_ITERS + 1,) + square
    for name in ("product", "two", "three"):
        shapes[name] = (NS_ITERS,) + square
    shapes["key_weights"] = shapes["token_weights"] = (LANES, length)
    return shapes


def owner_of(task, count):
    return task * count // TASKS


def task_of(me, count):
    task = (me * TASKS + count - 1) // count
    return task, owner_of(task, count) == me


def greet(count):
    me = lax.axis_index("dp")
    barrier = pltpu.get_barrier_semaphore()

    def signal(step, carry):
        pl.semaphore_signal(barrier, inc=1, device_id={"dp": lax.rem(me + step, count)}, device_id_type=MESH)
        return carry

    lax.fori_loop(1, count, signal, 0)
    pl.semaphore_wait(barrier, count - 1)


def scatter_tasks(count, piece, source, slab, send, receive):
    me = lax.axis_index("dp")

    def one(step, finish):
        task = lax.rem(task_of(me, count)[0] + step, TASKS)
        owner = owner_of(task, count)
        micro = task // PAIRS
        lanes = pl.ds(pl.multiple_of(lax.rem(task, PAIRS) * LANES, LANES), LANES)
        rows = pl.ds(pl.multiple_of(me * piece, piece), piece)
        outgoing = source.at[:, micro, :, lanes]
        landing = slab.at[:, rows, :]

        @pl.when(owner != me)
        def _():
            copy = pltpu.make_async_remote_copy(outgoing, landing, send.at[task], receive.at[me], device_id={"dp": owner}, device_id_type=MESH)
            if finish:
                copy.wait_send()
            else:
                copy.start()

        @pl.when((owner == me) & (not finish))
        def _():
            pltpu.make_async_copy(outgoing, landing, receive.at[me]).start()

    def run(finish):
        def body(step, carry):
            one(step, finish)
            return carry

        lax.fori_loop(0, TASKS, body, 0)

    return run


def await_slab(count, piece, slab, receive):
    def body(origin, carry):
        landing = slab.at[:, pl.ds(pl.multiple_of(origin * piece, piece), piece), :]
        pltpu.make_async_copy(landing, landing, receive.at[origin]).wait()
        return carry

    lax.fori_loop(0, count, body, 0)


def return_rows(count, piece, result, target, send, receive):
    me = lax.axis_index("dp")
    task = task_of(me, count)[0]
    micro = task // PAIRS
    lanes = pl.ds(pl.multiple_of(lax.rem(task, PAIRS) * LANES, LANES), LANES)

    def run(finish):
        def body(step, carry):
            peer = lax.rem(me + step, count)
            rows = pl.ds(pl.multiple_of(peer * piece, piece), piece)
            outgoing = result.at[:, rows, :]
            landing = target.at[:, micro, :, lanes]

            @pl.when(peer != me)
            def _():
                copy = pltpu.make_async_remote_copy(outgoing, landing, send.at[peer], receive.at[task], device_id={"dp": peer}, device_id_type=MESH)
                if finish:
                    copy.wait_send()
                else:
                    copy.start()

            @pl.when((peer == me) & (not finish))
            def _():
                pltpu.make_async_copy(outgoing, landing, receive.at[task]).start()

            return carry

        lax.fori_loop(0, count, body, 0)

    return run


def await_rows(target, receive):
    def body(task, carry):
        lanes = pl.ds(pl.multiple_of(lax.rem(task, PAIRS) * LANES, LANES), LANES)
        landing = target.at[:, task // PAIRS, :, lanes]
        pltpu.make_async_copy(landing, landing, receive.at[task]).wait()
        return carry

    lax.fori_loop(0, TASKS, body, 0)


def forward_kernel(count, piece, qkv, low_col, high_col, taps, mixed_rows, slab, *refs):
    keep = dict(zip(KEPT, refs))
    padded, blended, result, send_one, receive_one, send_two, receive_two = refs[len(KEPT) :]
    me = lax.axis_index("dp")
    task, owns = task_of(me, count)
    greet(count)
    out = scatter_tasks(count, piece, qkv, slab, send_one, receive_one)
    out(False)
    back = return_rows(count, piece, result, mixed_rows, send_two, receive_two)

    @pl.when(owns)
    def _():
        micro, pair = task // PAIRS, lax.rem(task, PAIRS)
        await_slab(count, piece, slab, receive_one)
        attend(slab[0], slab[1], slab[2], low_col[micro], high_col[micro], taps[pair], keep, padded, blended, result.at[0])
        back(False)

    out(True)
    await_rows(mixed_rows, receive_two)

    @pl.when(owns)
    def _():
        back(True)


def backward_kernel(count, piece, grads, low_col, high_col, low_row, high_row, taps, slab, *refs):
    keep = dict(zip(KEPT, refs))
    out_grads, grad_taps, grad_slab, padded, padded_grads, blended, result, send_one, receive_one, send_two, receive_two = refs[len(KEPT) :]
    me = lax.axis_index("dp")
    task, owns = task_of(me, count)
    greet(count)
    out = scatter_tasks(count, piece, grads, grad_slab, send_one, receive_one)
    out(False)
    back = return_rows(count, piece, result, out_grads, send_two, receive_two)
    grad_taps[...] = jnp.zeros(grad_taps.shape, F32)

    @pl.when(owns)
    def _():
        micro, pair = task // PAIRS, lax.rem(task, PAIRS)
        await_slab(count, piece, grad_slab, receive_one)
        attend_back(
            grad_slab[0], slab[0], slab[1], slab[2], low_col[micro], high_col[micro], low_row[micro], high_row[micro],
            taps[pair], keep, padded, padded_grads, blended, result, grad_taps.at[pair],
        )
        back(False)

    out(True)
    await_rows(out_grads, receive_two)

    @pl.when(owns)
    def _():
        back(True)


VMEM = pl.BlockSpec(memory_space=pltpu.VMEM)
DMA = pltpu.SemaphoreType.DMA


def attention_forward(count, qkv, marks, taps, ident):
    piece = qkv.shape[2]
    length = piece * count
    shapes = kept_shapes(length)
    results = pl.pallas_call(
        functools.partial(forward_kernel, count, piece),
        out_shape=[
            jax.ShapeDtypeStruct((1, MICRO, piece, D), BF16),
            jax.ShapeDtypeStruct((3, length, LANES), BF16),
        ]
        + [jax.ShapeDtypeStruct(shapes[name], F32) for name in KEPT],
        in_specs=[VMEM] * 4,
        out_specs=[VMEM] * (2 + len(KEPT)),
        scratch_shapes=[
            pltpu.VMEM((length + LANES, LANES), BF16),
            pltpu.VMEM((length, LANES), F32),
            pltpu.VMEM((1, length, LANES), BF16),
            DMA((TASKS,)),
            DMA((count,)),
            DMA((count,)),
            DMA((TASKS,)),
        ],
        compiler_params=pltpu.CompilerParams(collective_id=ident, has_side_effects=True, vmem_limit_bytes=60 << 20),
        name="attend_forward",
    )(qkv, marks[0], marks[1], taps)
    return results[0][0], results[1:]


def attention_backward(count, grads, marks, taps, kept, ident):
    piece = grads.shape[2]
    length = piece * count
    return pl.pallas_call(
        functools.partial(backward_kernel, count, piece),
        out_shape=[
            jax.ShapeDtypeStruct((3, MICRO, piece, D), BF16),
            jax.ShapeDtypeStruct((PAIRS, 2, 2 * LANES), F32),
        ],
        in_specs=[VMEM] * (7 + len(KEPT)),
        out_specs=[VMEM] * 2,
        scratch_shapes=[
            pltpu.VMEM((1, length, LANES), BF16),
            pltpu.VMEM((length + LANES, LANES), BF16),
            pltpu.VMEM((length + LANES, LANES), BF16),
            pltpu.VMEM((length, LANES), F32),
            pltpu.VMEM((3, length, LANES), BF16),
            DMA((TASKS,)),
            DMA((count,)),
            DMA((count,)),
            DMA((TASKS,)),
        ],
        compiler_params=pltpu.CompilerParams(collective_id=ident, has_side_effects=True, vmem_limit_bytes=60 << 20),
        name="attend_backward",
    )(grads, *marks, taps, *kept)


def gather_kernel(shard, out, local_sem, z_send, z_got, x_send, x_got, y_send, y_got, core_send, core_got):
    me = lax.axis_index("dp")
    x = lax.axis_index("rep")
    core, y, z = lax.rem(me, 2), lax.rem(me // 2, 2), me // 4
    half = shard.shape[0] // 2
    part = half // 2

    barrier = pltpu.get_barrier_semaphore()

    def peer(axis, sign=1):
        if axis == "x":
            return {"rep": 1 - x}
        if axis == "y":
            return {"dp": me + 2 - 4 * y}
        if axis == "core":
            return {"dp": me + 1 - 2 * core}
        return {"dp": me + 4 * sign}

    for axis in ("x", "y", "core"):
        pl.semaphore_signal(barrier, inc=1, device_id=peer(axis), device_id_type=MESH)
    for sign in (1, -1):

        @pl.when((z + sign >= 0) & (z + sign < 4))
        def _():
            pl.semaphore_signal(barrier, inc=1, device_id=peer("z", sign), device_id_type=MESH)

    pl.semaphore_wait(barrier, 4 + jnp.where((z > 0) & (z < 3), 1, 0))

    def rows(side, sub):
        return pl.ds(pl.multiple_of(side * half + sub * part, part), part)

    def side_rows(side):
        return pl.ds(pl.multiple_of(side * half, half), half)

    def remote(source, target, send, receive, where):
        return pltpu.make_async_remote_copy(source, target, send, receive, device_id=where, device_id_type=MESH)

    def spot(plane, row, side, sub):
        return out.at[plane, row, core, rows(side, sub), :]

    def move(axis, plane, row, side, sub, source=None):
        target = spot(plane, row, side, sub)
        source = target if source is None else source
        if axis == "core":
            return remote(source, target, core_send.at[plane, row, side, sub], core_got, peer("core"))
        send, receive = (x_send, x_got) if axis == "x" else (y_send, y_got)
        return remote(source, target, send.at[plane, row, side, sub], receive.at[plane, row, side, sub], peer(axis))

    def climb(plane, sub, sign, source=None):
        target = spot(plane, y, x, sub)
        way = 0 if sign > 0 else 1
        return remote(target if source is None else source, target, z_send.at[plane, sub, way], z_got.at[plane, sub], peer("z", sign))

    own = pltpu.make_async_copy(shard, out.at[z, y, core], local_sem)
    own.start()
    for sub in range(2):
        for sign in (1, -1):

            @pl.when((z + sign >= 0) & (z + sign < 4))
            def _():
                climb(z, sub, sign, shard.at[rows(x, sub), :]).start()

        move("y", z, y, x, sub, shard.at[rows(x, sub), :]).start()
    for side in range(2):
        for sub in range(2):
            move("core", z, y, side, sub, shard.at[rows(side, sub), :]).start()

    def at_distance(distance, act):
        for sign in (1, -1):
            plane = z - sign * distance

            @pl.when((plane >= 0) & (plane < 4))
            def _():
                act(plane, sign)

    def from_z(plane, sign):
        for sub in range(2):
            climb(plane, sub, sign).wait_recv()

            @pl.when((z + sign >= 0) & (z + sign < 4))
            def _():
                climb(plane, sub, sign).start()

            for axis in ("x", "y", "core"):
                move(axis, plane, y, x, sub).start()

    def take(axis, plane, row, side, sub, onward=None):
        move(axis, plane, row, side, sub).wait_recv()
        if onward is not None:
            move(onward, plane, row, side, sub).start()
        move("core", plane, row, side, sub).start()

    def first_square(plane, sign):
        take("x", plane, y, 1 - x, 0, "y")
        take("y", plane, 1 - y, x, 1, "x")
        take("y", plane, 1 - y, x, 0)
        take("x", plane, y, 1 - x, 1)

    def second_square(plane, sign):
        take("y", plane, 1 - y, 1 - x, 0)
        take("x", plane, 1 - y, 1 - x, 1)

    at_distance(1, from_z)
    for sub in range(2):
        take("y", z, 1 - y, x, sub, "x")
    at_distance(2, from_z)
    at_distance(1, first_square)
    at_distance(3, from_z)
    at_distance(2, first_square)
    for sub in range(2):
        take("x", z, 1 - y, 1 - x, sub)
    at_distance(1, second_square)
    at_distance(3, first_square)
    at_distance(2, second_square)
    at_distance(3, second_square)
    own.wait()

    def finish(plane, sign):
        for sub in range(2):

            @pl.when((z + sign >= 0) & (z + sign < 4))
            def _():
                climb(plane, sub, sign).wait_send()

            move("x", plane, y, x, sub).wait_send()
            move("y", plane, y, x, sub).wait_send()
        move("y", plane, y, 1 - x, 0).wait_send()
        move("x", plane, 1 - y, x, 1).wait_send()

    for distance in (1, 2, 3):
        at_distance(distance, finish)
    for sub in range(2):
        for sign in (1, -1):

            @pl.when((z + sign >= 0) & (z + sign < 4))
            def _():
                climb(z, sub, sign).wait_send()

        move("y", z, y, x, sub).wait_send()
        move("x", z, 1 - y, x, sub).wait_send()

    def core_sent(index, carry):
        plane, row, side, sub = index // 8, lax.rem(index // 4, 2), lax.rem(index // 2, 2), lax.rem(index, 2)
        move("core", plane, row, side, sub).wait_send()
        return carry

    lax.fori_loop(0, 32, core_sent, 0)
    column = out.at[:, :, 1 - core]
    pltpu.make_async_copy(column, column, core_got).wait()


def gather(shard):
    block_rows = shard.shape[0]
    return pl.pallas_call(
        gather_kernel,
        out_shape=jax.ShapeDtypeStruct((4, 2, 2, block_rows, D), BF16),
        in_specs=[VMEM],
        out_specs=pl.BlockSpec(memory_space=pl.ANY),
        scratch_shapes=[
            DMA,
            DMA((4, 2, 2)),
            DMA((4, 2)),
            DMA((4, 2, 2, 2)),
            DMA((4, 2, 2, 2)),
            DMA((4, 2, 2, 2)),
            DMA((4, 2, 2, 2)),
            DMA((4, 2, 2, 2)),
            DMA,
        ],
        compiler_params=pltpu.CompilerParams(collective_id=4, has_side_effects=True),
        name="gather",
    )(shard).reshape(16 * block_rows, D)


CHUNK = 48
RING = 8
LINES = 13
MATES = ("low_in", "low_comb", "low_up", "low_act", "low_grads", "low_branch", "low_hidden", "low_down", "gain_one", "shift_one", "gain_two", "shift_two", "taps")


def change(grad, first_old, second_old):
    new_first = ADAM_ONE * first_old + (1.0 - ADAM_ONE) * grad
    new_second = ADAM_TWO * second_old + (1.0 - ADAM_TWO) * grad * grad
    return new_first * (1.0 / (1.0 - ADAM_ONE**STEP_COUNT)) / (jnp.sqrt(new_second * (1.0 / (1.0 - ADAM_TWO**STEP_COUNT))) + ADAM_EPSILON)


def settle_kernel(block_rows, *refs):
    count = len(MATES)
    mates = [dict(zip(MATES, refs[level * count : (level + 1) * count])) for level in range(LAYERS)]
    (
        weights, first, second, small_first, small_second, grad_out, mean_out, small_out,
        turned, right, staged, own, got_core, got_y, got_z, inner, step_own, step_got, small, small_got, small_own, small_step, small_step_got,
        core_send, core_got, y_send, y_got, z_send, z_got, inner_sem, rep_send, rep_got, small_send, small_sem, back_send, back_sem, small_rep,
    ) = refs[LAYERS * count :]
    me = lax.axis_index("dp")
    other_rep = 1 - lax.axis_index("rep")
    core, y, z = lax.rem(me, 2), lax.rem(me // 2, 2), me // 4
    devices = 16
    per_layer = block_rows // CHUNK
    chunks = LAYERS * per_layer

    barrier = pltpu.get_barrier_semaphore()

    def signal(step, carry):
        pl.semaphore_signal(barrier, inc=1, device_id={"dp": lax.rem(me + step, devices)}, device_id_type=MESH)
        return carry

    lax.fori_loop(1, devices, signal, 0)
    pl.semaphore_signal(barrier, inc=1, device_id={"rep": other_rep}, device_id_type=MESH)

    def to_dp(source, target, send, receive, peer):
        return pltpu.make_async_remote_copy(source, target, send, receive, device_id={"dp": peer}, device_id_type=MESH)

    def to_rep(source, target, send, receive):
        return pltpu.make_async_remote_copy(source, target, send, receive, device_id={"rep": other_rep}, device_id_type=MESH)

    def spot(slot):
        return lax.rem(slot, RING)

    features = D * 2 + FF * 2
    for order, level in enumerate(reversed(range(LAYERS))):
        mate = mates[level]
        at = order * features
        for name in MATES[:4]:
            for part in range(mate[name].shape[1] // LANES):
                turned[at : at + LANES, :] = mate[name][:, part * LANES : (part + 1) * LANES].T
                at += LANES
        for part in range(3):
            right[order * 6 + part] = mate["low_grads"][part]
        for part, name in enumerate(MATES[5:8]):
            right[order * 6 + 3 + part] = mate[name][...]

    def put(level, line, row):
        index = level * LINES + line
        small[index // 2, index % 2 : index % 2 + 1, :] = row

    def column_sum(array):
        return jnp.sum(array.astype(F32), axis=0, keepdims=True)

    for level in range(LAYERS):
        mate = mates[level]
        put(level, 0, column_sum(mate["low_grads"][0]))
        put(level, 1, column_sum(mate["low_grads"][2]))
        put(level, 2, column_sum(mate["low_branch"][...]))
        put(level, 3, column_sum(mate["low_down"][...]))
        for line, name in enumerate(MATES[8:12]):
            put(level, 4 + line, mate[name][...])
        for part in range(FF // D):
            put(level, 8 + part, column_sum(mate["low_up"][:, part * D : (part + 1) * D]))
        line = jnp.zeros((1, D), F32)
        for head in range(HEADS):
            taps = jnp.concatenate([mate["taps"][head // 2][head % 2 : head % 2 + 1], jnp.zeros((1, D - 2 * LANES), F32)], axis=1)
            taps = jnp.where(iota((1, D), 1) < TAPS, taps, 0.0)
            line = line + (pltpu.roll(taps, TAPS * head, 1) if head else taps)
        put(level, 12, line)
    for index in range(LAYERS * LINES, 2 * devices):
        small[index // 2, index % 2 : index % 2 + 1, :] = jnp.zeros((1, D), F32)

    pl.semaphore_wait(barrier, devices)

    def small_copy(step):
        peer = lax.rem(me + step, devices)
        return to_dp(small.at[peer], small_got.at[me], small_send.at[peer], small_sem.at[me], peer)

    def small_begin(step, carry):
        small_copy(step).start()
        return carry

    lax.fori_loop(1, devices, small_begin, 0)

    def core_copy(chunk):
        return to_dp(staged.at[lax.rem(chunk, 2)], got_core.at[spot(chunk)], core_send.at[lax.rem(chunk, 2)], core_got.at[spot(chunk)], me + 1 - 2 * core)

    def y_copy(chunk):
        return to_dp(own.at[spot(chunk), :, 1 - y], got_y.at[spot(chunk)], y_send.at[spot(chunk)], y_got.at[spot(chunk)], me + 2 - 4 * y)

    def z_copy(chunk, hop):
        there = lax.rem(z + hop, 4)
        slot = spot(chunk)
        return to_dp(own.at[slot, there, y], got_z.at[slot, hop - 1], z_send.at[slot, hop - 1], z_got.at[slot, hop - 1], there * 4 + lax.rem(me, 4))

    def place(chunk):
        return LAYERS - 1 - chunk // per_layer, pl.ds(pl.multiple_of(lax.rem(chunk, per_layer) * CHUNK, CHUNK), CHUNK)

    def inner_copies(chunk):
        level, rows = place(chunk)
        slot = lax.rem(chunk, 4)
        return [
            pltpu.make_async_copy(array.at[level, rows, :], inner.at[slot, index], inner_sem.at[slot, index])
            for index, array in enumerate((weights, first, second))
        ]

    def rep_copy(chunk):
        return to_rep(step_own.at[spot(chunk)], step_got.at[spot(chunk)], rep_send.at[spot(chunk)], rep_got.at[spot(chunk)])

    def product(chunk, there, row, side):
        order = chunk // per_layer
        block = (there * 2 + row) * 2 + side
        piece = block * per_layer + lax.rem(chunk, per_layer)
        narrow = D // CHUNK
        line = jnp.where(piece < 3 * narrow, lax.rem(piece, narrow), piece - 2 * narrow)
        group = jnp.where(piece < 4 * narrow, piece // narrow, jnp.where(piece < 4 * narrow + FF // CHUNK, 4, 5))
        rows = pl.ds(pl.multiple_of(order * features + line * CHUNK, 16), CHUNK)
        return mm(turned[rows, :], right[order * 6 + group]).astype(BF16)

    def stage_product(chunk):
        for there in range(4):
            for row in range(2):
                staged[lax.rem(chunk, 2), there, row] = product(chunk, there, row, 1 - core)
        core_copy(chunk).start()
        for there in range(4):
            for row in range(2):
                own[spot(chunk), there, row] = product(chunk, there, row, core)

    def stage_core(chunk):
        core_copy(chunk).wait()
        slot = spot(chunk)
        for there in range(4):
            for side in range(2):
                own[slot, there, side] = own[slot, there, side] + got_core[slot, there, side]
        y_copy(chunk).start()

    def stage_y(chunk):
        y_copy(chunk).wait_recv()
        slot = spot(chunk)
        for there in range(4):
            own[slot, there, y] = own[slot, there, y] + got_y[slot, there]
        for hop in range(1, 4):
            z_copy(chunk, hop).start()
        for copy in inner_copies(chunk):
            copy.start()

    def stage_z(chunk):
        y_copy(chunk).wait_send()
        for hop in range(1, 4):
            z_copy(chunk, hop).wait_recv()
        for copy in inner_copies(chunk):
            copy.wait()
        total = own[spot(chunk), z, y].astype(F32)
        for hop in range(3):
            total = total + got_z[spot(chunk), hop].astype(F32)
        level, rows = place(chunk)
        grad_out[level, rows, :] = total
        slot = lax.rem(chunk, 4)
        step = change(total, inner[slot, 1], inner[slot, 2]) + WEIGHT_DECAY * inner[slot, 0]
        step_own[spot(chunk)] = (LR_INNER * step).astype(BF16)
        rep_copy(chunk).start()

    def stage_rep(chunk):
        for hop in range(1, 4):
            z_copy(chunk, hop).wait_send()
        rep_copy(chunk).wait()
        level, rows = place(chunk)
        mean_out[level, rows, :] = 0.5 * (step_own[spot(chunk)].astype(F32) + step_got[spot(chunk)].astype(F32))

    def small_rep_copy():
        return to_rep(small_step, small_step_got, small_rep.at[0], small_rep.at[1])

    def small_back(step):
        peer = lax.rem(me + step, devices)
        return to_dp(small_own, small_out.at[me], back_send.at[peer], back_sem.at[me], peer)

    def small_sum():
        def add(step, total):
            peer = lax.rem(me + step, devices)
            pltpu.make_async_copy(small_got.at[peer], small_got.at[peer], small_sem.at[peer]).wait()
            return total + small_got[peer]

        total = lax.fori_loop(1, devices, add, small[me])
        small_own[0] = total
        small_step[...] = (LR_SMALL * change(total, small_first[me], small_second[me])).astype(BF16)
        small_rep_copy().start()

    def small_spread():
        small_rep_copy().wait_recv()
        small_own[1] = 0.5 * (small_step[...].astype(F32) + small_step_got[...].astype(F32))
        small_out[me] = small_own[...]

        def send(step, carry):
            small_back(step).start()
            return carry

        lax.fori_loop(1, devices, send, 0)

    def turn(now, carry):
        for lag, stage in ((0, stage_product), (1, stage_core), (3, stage_y), (5, stage_z), (7, stage_rep)):

            @pl.when((now >= lag) & (now < chunks + lag))
            def _():
                stage(now - lag)

        pl.when(now == 4)(small_sum)
        pl.when(now == 7)(small_spread)
        return carry

    lax.fori_loop(0, chunks + 7, turn, 0)

    def small_drain(step, carry):
        peer = lax.rem(me + step, devices)
        small_copy(step).wait_send()
        small_back(step).wait_send()
        pltpu.make_async_copy(small_own, small_out.at[peer], back_sem.at[peer]).wait()
        return carry

    lax.fori_loop(1, devices, small_drain, 0)
    small_rep_copy().wait_send()


def settle(mates, weights, first, second, small_first, small_second):
    block_rows = weights.shape[1]
    anywhere = pl.BlockSpec(memory_space=pl.ANY)
    devices = 16
    piece = (CHUNK, D)
    tokens = mates[0]["low_in"].shape[0]
    return pl.pallas_call(
        functools.partial(settle_kernel, block_rows),
        out_shape=[
            jax.ShapeDtypeStruct(weights.shape, F32),
            jax.ShapeDtypeStruct(weights.shape, F32),
            jax.ShapeDtypeStruct((devices, 2, 2, D), F32),
        ],
        in_specs=[VMEM] * (LAYERS * len(MATES)) + [anywhere] * 3 + [VMEM] * 2,
        out_specs=[VMEM] * 3,
        scratch_shapes=[
            pltpu.VMEM((LAYERS * 2 * (D + FF), tokens), BF16),
            pltpu.VMEM((LAYERS * 6, tokens, D), BF16),
            pltpu.VMEM((2, 4, 2) + piece, BF16),
            pltpu.VMEM((RING, 4, 2) + piece, BF16),
            pltpu.VMEM((RING, 4, 2) + piece, BF16),
            pltpu.VMEM((RING, 4) + piece, BF16),
            pltpu.VMEM((RING, 3) + piece, BF16),
            pltpu.VMEM((4, 3) + piece, F32),
            pltpu.VMEM((RING,) + piece, BF16),
            pltpu.VMEM((RING,) + piece, BF16),
            pltpu.VMEM((devices, 2, D), F32),
            pltpu.VMEM((devices, 2, D), F32),
            pltpu.VMEM((2, 2, D), F32),
            pltpu.VMEM((2, D), BF16),
            pltpu.VMEM((2, D), BF16),
            DMA((2,)),
            DMA((RING,)),
            DMA((RING,)),
            DMA((RING,)),
            DMA((RING, 3)),
            DMA((RING, 3)),
            DMA((4, 3)),
            DMA((RING,)),
            DMA((RING,)),
            DMA((devices,)),
            DMA((devices,)),
            DMA((devices,)),
            DMA((devices,)),
            DMA((2,)),
        ],
        compiler_params=pltpu.CompilerParams(collective_id=3, has_side_effects=True, vmem_limit_bytes=63 << 20),
        name="settle",
    )(*[mate[name] for mate in mates for name in MATES], weights, first, second, small_first, small_second)


def sliced(array):
    wide = jnp.pad(array, ((0, 0), (0, LINES * D - array.shape[1]))).reshape(LAYERS * LINES, D)
    return jnp.pad(wide, ((0, 32 - LAYERS * LINES), (0, 0))).reshape(16, 2, D)


def unsliced(array, shape):
    return array.reshape(32, D)[: LAYERS * LINES].reshape(LAYERS, LINES * D)[:, : shape[1]]


def dense(a, b, dims=NN):
    return mm(a, b, dims)


def layer_norm(values, gain_vec, shift_vec):
    row_mean = jnp.mean(values, axis=-1, keepdims=True)
    centred = values - row_mean
    variance = jnp.mean(centred * centred, axis=-1, keepdims=True)
    return centred * lax.rsqrt(variance + 1e-05) * gain_vec + shift_vec


def unpack(params):
    blocks = [params[index * D : (index + 1) * D] for index in range(8)]
    bias_up = params[8 * D : 8 * D + FF]
    conv_taps = params[8 * D + FF :].reshape(HEADS, TAPS)
    return (blocks, bias_up, conv_taps)


def pair_taps(conv_taps):
    both = jnp.stack([conv_taps.reshape(PAIRS, 2, TAPS), conv_taps[:, ::-1].reshape(PAIRS, 2, TAPS)], axis=1)
    both = both.reshape(PAIRS, 4, TAPS)
    return jnp.pad(both, ((0, 0), (0, 0), (0, 2 * LANES - TAPS)))


def split_rows(rows):
    return rows[: 3 * D].reshape(3, D, D), rows[3 * D : 4 * D], rows[4 * D : 4 * D + FF], rows[4 * D + FF :]


def forward_layer(count, inputs, rows, params, marks, ident):
    piece = inputs.shape[0] // MICRO
    blocks, bias_up, conv_taps = unpack(params)
    proj, out_weight, up_weight, down_weight = split_rows(rows)
    low_in = inputs.astype(BF16)
    bias = jnp.stack([blocks[0], jnp.zeros_like(blocks[0]), blocks[1]])
    qkv = jnp.stack([(dense(low_in, proj[part]) + bias[part]).astype(BF16) for part in range(3)])
    low_comb, kept = attention_forward(count, qkv.reshape(3, MICRO, piece, D), marks, pair_taps(conv_taps), ident)
    low_comb = low_comb.reshape(MICRO * piece, D)
    resid_one = inputs + (dense(low_comb, out_weight) + blocks[2])
    hidden_one = layer_norm(resid_one, blocks[4], blocks[5])
    low_hidden = hidden_one.astype(BF16)
    upward = dense(low_hidden, up_weight, NT) + bias_up
    low_act = jax.nn.gelu(upward).astype(BF16)
    resid_two = hidden_one + (dense(low_act, down_weight) + blocks[3])
    output = layer_norm(resid_two, blocks[6], blocks[7])
    return output, (low_in, kept, low_comb, resid_one, low_hidden, upward, low_act, resid_two)


def backward_layer(count, grad_output, rows, params, marks, state, ident):
    low_in, kept, low_comb, resid_one, low_hidden, upward, low_act, resid_two = state
    total = low_in.shape[0]
    piece = total // MICRO
    blocks, bias_up, conv_taps = unpack(params)
    proj, out_weight, up_weight, down_weight = split_rows(rows)
    _, pull_two = jax.vjp(layer_norm, resid_two, blocks[6], blocks[7])
    grad_two, grad_gain_two, grad_shift_two = pull_two(grad_output)
    low_down = grad_two.astype(BF16)
    grad_act = dense(low_down, down_weight, NT)
    _, pull_gelu = jax.vjp(jax.nn.gelu, upward)
    low_up = pull_gelu(grad_act)[0].astype(BF16)
    grad_hidden = grad_two + dense(low_up, up_weight)
    _, pull_one = jax.vjp(layer_norm, resid_one, blocks[4], blocks[5])
    grad_one, grad_gain_one, grad_shift_one = pull_one(grad_hidden)
    low_branch = grad_one.astype(BF16)
    grad_comb = dense(low_branch, out_weight, NT).astype(BF16)
    low_grads, grad_taps = attention_backward(count, grad_comb.reshape(1, MICRO, piece, D), marks, pair_taps(conv_taps), kept, ident)
    low_grads = low_grads.reshape(3, total, D)
    grad_in = grad_one + sum(dense(low_grads[part], proj[part], NT) for part in range(3))
    vectors = [vector.reshape(1, D) for vector in (grad_gain_one, grad_shift_one, grad_gain_two, grad_shift_two)]
    values = (low_in, low_comb, low_up, low_act, low_grads, low_branch, low_hidden, low_down, *vectors, grad_taps)
    return grad_in, dict(zip(MATES, values))


def plain_grads(mate):
    parts = [dense(mate["low_in"], mate["low_grads"][part], TN) for part in range(3)]
    parts = parts + [dense(mate[left], mate[right], TN) for left, right in (("low_comb", "low_branch"), ("low_up", "low_hidden"), ("low_act", "low_down"))]
    sums = [mate["low_grads"][0], mate["low_grads"][2], mate["low_branch"], mate["low_down"]]
    sums = [jnp.sum(one.astype(F32), axis=0) for one in sums]
    sums = sums + [mate[name].reshape(-1) for name in MATES[8:12]]
    sums = sums + [jnp.sum(mate["low_up"].astype(F32), axis=0), mate["taps"][:, :, :TAPS].reshape(-1)]
    return jnp.concatenate(parts, axis=0).astype(BF16), jnp.concatenate(sums)


def moments(first, second, grad):
    return ADAM_ONE * first + (1.0 - ADAM_ONE) * grad, ADAM_TWO * second + (1.0 - ADAM_TWO) * grad * grad


def adam(weights, first, second, grad, rate, decay):
    correct_one = 1.0 - ADAM_ONE**STEP_COUNT
    correct_two = 1.0 - ADAM_TWO**STEP_COUNT
    new_first, new_second = moments(first, second, grad)
    step = new_first / correct_one / (jnp.sqrt(new_second / correct_two) + ADAM_EPSILON)
    return new_first, new_second, rate * (step + decay * weights)


def shards(
    hidden,
    bounds,
    cotangent,
    weights,
    small_params,
    first_big,
    second_big,
    first_small,
    second_small,
    outer_big,
    outer_small,
):
    count = lax.axis_size("dp")
    piece = hidden.shape[3]
    total = MICRO * piece
    low_weights = weights.astype(BF16)
    held = [lax.all_gather(low_weights[level], "dp", axis=0, tiled=True) for level in range(LAYERS)]
    if count == 16:
        held[0] = gather(low_weights[0])
    edges = bounds[0, :, 0, :]
    low_edges, high_edges = edges[:, :-1], edges[:, 1:]
    marks = (low_edges[:, :, None], high_edges[:, :, None], low_edges[:, None, :], high_edges[:, None, :])
    positions = lax.axis_index("dp") * piece + jnp.arange(piece, dtype=jnp.int32)
    valid = (positions[None, :] < edges[:, -1:]).astype(F32).reshape(total, 1)
    activation = hidden[0, :, 0].reshape(total, D).astype(F32)
    states = []
    for level in range(LAYERS):
        activation, state = forward_layer(count, activation, held[level], small_params[level], marks, 1)
        states.append(state)
    gradient = cotangent[0, :, 0].reshape(total, D).astype(F32) * valid
    mates = [None] * LAYERS
    for level in reversed(range(LAYERS)):
        gradient, mates[level] = backward_layer(count, gradient, held[level], small_params[level], marks, states[level], 2)
    if count == 16:
        grad_big, mean_big, small_both = settle(mates, weights, first_big[0], second_big[0], sliced(first_small[0]), sliced(second_small[0]))
        grad_small, mean_small = [unsliced(small_both[:, which], small_params.shape) for which in range(2)]
    else:
        rows, sums = zip(*[plain_grads(mate) for mate in mates])
        grad_big = jnp.stack([lax.psum_scatter(one, "dp", scatter_dimension=0, tiled=True).astype(F32) for one in rows])
        grad_small = lax.psum(jnp.stack(sums), "dp")
        reps = lax.axis_size("rep")
        delta_big = adam(weights, first_big[0], second_big[0], grad_big, LR_INNER, WEIGHT_DECAY)[2]
        delta_small = adam(small_params, first_small[0], second_small[0], grad_small, LR_SMALL, 0.0)[2]
        mean_big = lax.psum(delta_big.astype(BF16), "rep").astype(F32) / reps
        mean_small = lax.psum(delta_small.astype(BF16), "rep").astype(F32) / reps
    new_first, new_second = moments(first_big[0], second_big[0], grad_big)
    new_first_small, new_second_small = moments(first_small[0], second_small[0], grad_small)
    outer_big_new = MOMENTUM * outer_big + mean_big
    outer_small_new = MOMENTUM * outer_small + mean_small
    weights_new = weights - LR_OUTER * (mean_big + MOMENTUM * outer_big_new)
    small_new = small_params - LR_OUTER * (mean_small + MOMENTUM * outer_small_new)
    shape = (1, MICRO, 1, piece, D)
    return (
        activation.reshape(shape),
        gradient.reshape(shape),
        new_first[None],
        new_second[None],
        new_first_small[None],
        new_second_small[None],
        outer_big_new,
        outer_small_new,
        weights_new,
        small_new,
        weights_new.astype(BF16),
    )


def solution(mesh):
    placed = (
        P("rep", None, None, "dp", None),
        P("rep", None, None, None),
        P("rep", None, None, "dp", None),
        P(None, "dp", None),
        P(),
        P("rep", None, "dp", None),
        P("rep", None, "dp", None),
        P("rep", None, None),
        P("rep", None, None),
        P(None, "dp", None),
        P(),
    )
    return jax.shard_map(
        shards,
        mesh=mesh,
        in_specs=placed,
        out_specs=(
            P("rep", None, None, "dp", None),
            P("rep", None, None, "dp", None),
            P("rep", None, "dp", None),
            P("rep", None, "dp", None),
            P("rep", None, None),
            P("rep", None, None),
            P(None, "dp", None),
            P(),
            P(None, "dp", None),
            P(),
            P(None, "dp", None),
        ),
        check_vma=False,
    )
```

```python
import functools

import jax
import jax.numpy as jnp
from jax import lax
from jax.experimental import pallas as pl
from jax.experimental.pallas import tpu as pltpu
from jax.sharding import PartitionSpec as P

D = 768
HEADS = 12
FF = 3072
TAPS = 33
NS_ITERS = 6
LAYERS = 2
MICRO = 2
STEP_COUNT = 5


ADAM_ONE = 0.9
ADAM_TWO = 0.95
ADAM_EPSILON = 1e-08
WEIGHT_DECAY = 0.1
LR_INNER = 0.04
LR_SMALL = 0.2
LR_OUTER = 0.7
MOMENTUM = 0.9

HEAD_DIM = 64
MARKS = 64
HALF = TAPS // 2
PAIRS = HEADS // 2
LINES = 13
TAP_LINE = 12
SMALL = 8 * D + FF + HEADS * TAPS
LANES = 128
SCALE = HEAD_DIM**-0.5
NEG = -1e30
MESH = pl.DeviceIdType.MESH
F32 = jnp.float32
BF16 = jnp.bfloat16
NN = (((1,), (0,)), ((), ()))
NT = (((1,), (1,)), ((), ()))
TN = (((0,), (0,)), ((), ()))


def mm(a, b, dims=NN):
    return lax.dot_general(a, b, dims, preferred_element_type=F32)


def halves(a):
    high = a.astype(BF16)
    return high, (a - high.astype(F32)).astype(BF16)


def mm_left(a, b, dims=NN):
    high, rest = halves(a)
    return mm(high, b, dims) + mm(rest, b, dims)


def mm_both(a, b, dims=NN):
    ah, al = halves(a)
    bh, bl = halves(b)
    return mm(ah, bh, dims) + (mm(ah, bl, dims) + mm(al, bh, dims))


def exact(a, b, dims=NN):
    return mm_both(a, b, dims)


def iota(shape, dim):
    return lax.broadcasted_iota(jnp.int32, shape, dim)


def diagonal_blocks():
    return (iota((LANES, LANES), 0) < MARKS) == (iota((LANES, LANES), 1) < HEAD_DIM)


def unit():
    return (iota((LANES, LANES), 0) == iota((LANES, LANES), 1)).astype(F32)


def per_head(marks):
    first = iota(marks.shape, 1) < HEAD_DIM
    return jnp.concatenate([jnp.where(first, marks, 0.0), jnp.where(first, 0.0, marks)], axis=0)


def head_sums(a):
    rows, cols = a.shape
    split = a.reshape(2, rows // 2, cols)
    return jnp.broadcast_to(jnp.sum(split, axis=1, keepdims=True), split.shape).reshape(rows, cols)


def head_tops(a):
    rows, cols = a.shape
    split = a.reshape(2, rows // 2, cols)
    return jnp.broadcast_to(jnp.max(split, axis=1, keepdims=True), split.shape).reshape(rows, cols)


def head_taps(lines, pair):
    row = jnp.broadcast_to(lines[TAP_LINE : TAP_LINE + 1, :], (8, D))
    rows = []
    for side in range(2):
        turned = pltpu.roll(row, lax.rem(D - TAPS * (2 * pair + side), D), 1)[0:1, : 2 * LANES]
        rows.append(jnp.where(iota((1, 2 * LANES), 1) < TAPS, turned, 0.0))
    return rows


def band(taps_row):
    wide = jnp.broadcast_to(taps_row, (LANES, 2 * LANES))
    return pltpu.roll(wide, 0, 1, stride=1, stride_axis=0)


def band_back(taps_row):
    wide = jnp.broadcast_to(taps_row, (2 * LANES, 2 * LANES))
    return pltpu.roll(wide, 2 * LANES - 2 * HALF, 1, stride=1, stride_axis=0)[:, :LANES].T


def mark_columns(edges):
    low = jnp.broadcast_to(edges, (LANES, LANES)).T[:MARKS, :1]
    high = jnp.broadcast_to(pltpu.roll(edges, LANES - 1, 1), (LANES, LANES)).T[:MARKS, :1]
    return low.astype(jnp.int32), high.astype(jnp.int32)


def mark_rows(edges):
    low, high = edges[:, :MARKS], pltpu.roll(edges, LANES - 1, 1)[:, :MARKS]
    return low.astype(jnp.int32), high.astype(jnp.int32)


def convolve(padded, bands, length, store):
    first = iota((LANES, LANES), 1) < HEAD_DIM
    pairs = [halves(one) for one in bands]

    def block(at, carry):
        start = pl.multiple_of(at * LANES, LANES)
        window = padded[pl.ds(start, 2 * LANES), :]
        out = [mm(high, window) + mm(rest, window) for high, rest in pairs]
        store(start, jnp.where(first, out[0], out[1]))
        return carry

    lax.fori_loop(0, length // LANES, block, 0)


def attend(queries, keys, values, edges, taps, keep, padded, blended, result):
    length = queries.shape[0]
    low_marks, high_marks = mark_columns(edges)
    at = iota((MARKS, length), 1)
    member = ((low_marks <= at) & (at < high_marks)).astype(F32).astype(BF16)
    counts = (high_marks - low_marks).astype(F32)
    blocks, eye = diagonal_blocks(), unit()
    q_marks = per_head(mm(member, queries) / counts)
    k_marks = per_head(mm(member, keys) / counts)
    scores = jnp.where(blocks, SCALE * exact(q_marks, k_marks, NT), NEG)
    weights = jnp.exp(scores - jnp.max(scores, axis=1, keepdims=True))
    kernel = weights / jnp.sum(weights, axis=1, keepdims=True)
    total = head_sums(jnp.broadcast_to(jnp.sum(kernel * kernel, axis=1, keepdims=True), kernel.shape))
    inverse = kernel.T / total
    keep["q_marks"][...] = q_marks
    keep["k_marks"][...] = k_marks
    keep["kernel"][...] = kernel
    keep["total"][...] = total
    for sweep in range(NS_ITERS):
        product = exact(kernel, inverse)
        one = 7.0 * eye - product
        two = 15.0 * eye - exact(product, one)
        three = 13.0 * eye - exact(product, two)
        keep["inverse"][sweep] = inverse
        keep["product"][sweep] = product
        keep["two"][sweep] = two
        keep["three"][sweep] = three
        inverse = 0.25 * exact(inverse, three)
    keep["inverse"][NS_ITERS] = inverse
    valid = at[:1] < high_marks[MARKS - 1 :]
    key_scores = jnp.where(valid, SCALE * mm_left(q_marks, keys, NT), NEG)
    key_exp = jnp.where(valid, jnp.exp(key_scores - jnp.max(key_scores, axis=1, keepdims=True)), 0.0)
    key_weights = key_exp / jnp.sum(key_exp, axis=1, keepdims=True)
    keep["key_weights"][...] = key_weights
    summary = jnp.where(blocks, mm_left(key_weights, values), 0.0)
    mixed = exact(inverse, summary)
    keep["summary"][...] = summary
    keep["mixed"][...] = mixed
    token_scores = SCALE * mm_left(k_marks, queries, NT)
    token_exp = jnp.exp(token_scores - head_tops(token_scores))
    token_weights = token_exp / head_sums(token_exp)
    keep["token_weights"][...] = token_weights
    blended[...] = mm_both(token_weights, mixed, TN)
    valid_column = iota((length, 1), 0) < high_marks[MARKS - 1 :]
    padded[0:HALF, :] = jnp.zeros((HALF, LANES), BF16)
    padded[HALF : HALF + length, :] = jnp.where(valid_column, values, jnp.zeros_like(values))
    padded[HALF + length :, :] = jnp.zeros((LANES - HALF, LANES), BF16)

    def store(start, block):
        result[pl.ds(start, LANES), :] = (blended[pl.ds(start, LANES), :] + block).astype(BF16)

    convolve(padded, [band(one) for one in taps], length, store)


def attend_back(grads, queries, keys, values, edges, taps, keep, padded, padded_grads, blended, result, grad_taps):
    length = grads.shape[0]
    low_marks, high_marks = mark_columns(edges)
    low_row, high_row = mark_rows(edges)
    at = iota((length, MARKS), 0)
    member = ((low_row <= at) & (at < high_row)).astype(F32).astype(BF16)
    counts = (high_marks - low_marks).astype(F32)
    blocks, eye = diagonal_blocks(), unit()
    q_marks, k_marks = keep["q_marks"][...], keep["k_marks"][...]
    token_weights, key_weights = keep["token_weights"][...], keep["key_weights"][...]
    summary, mixed = keep["summary"][...], keep["mixed"][...]
    kernel = keep["kernel"][...]
    inverse = keep["inverse"][NS_ITERS]
    grad_mixed = jnp.where(blocks, mm_left(token_weights, grads), 0.0)
    grad_token = token_weights * mm_left(mixed, grads, NT)
    grad_token = SCALE * (grad_token - token_weights * head_sums(grad_token))
    grad_summary = exact(inverse, grad_mixed, TN)
    grad_inverse = exact(grad_mixed, summary, NT)
    grad_kernel = jnp.zeros_like(kernel)
    for sweep in reversed(range(NS_ITERS)):
        before, product = keep["inverse"][sweep], keep["product"][sweep]
        one = 7.0 * eye - product
        two, three = keep["two"][sweep], keep["three"][sweep]
        grad_three = 0.25 * exact(before, grad_inverse, TN)
        grad_two = -exact(product, grad_three, TN)
        grad_one = -exact(product, grad_two, TN)
        grad_product = -(exact(grad_three, two, NT) + exact(grad_two, one, NT) + grad_one)
        grad_kernel = grad_kernel + exact(grad_product, before, NT)
        grad_inverse = 0.25 * exact(grad_inverse, three, NT) + exact(kernel, grad_product, TN)
    total = keep["total"][...]
    turned = grad_inverse.T / total
    weighted = jnp.sum(jnp.where(blocks, turned * kernel, 0.0), axis=1, keepdims=True)
    weighted = head_sums(jnp.broadcast_to(weighted, kernel.shape))
    grad_kernel = grad_kernel + turned - 2.0 * kernel * weighted / total
    grad_scores = SCALE * kernel * (grad_kernel - jnp.sum(kernel * grad_kernel, axis=1, keepdims=True))
    grad_q_marks = exact(grad_scores, k_marks)
    grad_k_marks = exact(grad_scores, q_marks, TN)
    grad_k_marks = grad_k_marks + jnp.where(blocks, mm_left(grad_token, queries), 0.0)
    grad_key = mm_left(grad_summary, values, NT) - jnp.sum(grad_summary * summary, axis=1, keepdims=True)
    grad_key = SCALE * key_weights * grad_key
    grad_q_marks = grad_q_marks + jnp.where(blocks, mm_left(grad_key, keys), 0.0)
    grad_q_marks = (grad_q_marks[:MARKS] + grad_q_marks[MARKS:]) / counts
    grad_k_marks = (grad_k_marks[:MARKS] + grad_k_marks[MARKS:]) / counts
    high, rest = halves(grad_q_marks)
    result[0] = (mm_both(grad_token, k_marks, TN) + mm(member, high) + mm(member, rest)).astype(BF16)
    high, rest = halves(grad_k_marks)
    result[1] = (mm_both(grad_key, q_marks, TN) + mm(member, high) + mm(member, rest)).astype(BF16)
    blended[...] = mm_both(key_weights, grad_summary, TN)
    last = high_marks[MARKS - 1 :]
    valid_column = iota((length, 1), 0) < last
    padded[0:HALF, :] = jnp.zeros((HALF, LANES), BF16)
    padded[HALF : HALF + length, :] = jnp.where(valid_column, values, jnp.zeros_like(values))
    padded[HALF + length :, :] = jnp.zeros((LANES - HALF, LANES), BF16)
    padded_grads[0:HALF, :] = jnp.zeros((HALF, LANES), BF16)
    padded_grads[HALF : HALF + length, :] = grads
    padded_grads[HALF + length :, :] = jnp.zeros((LANES - HALF, LANES), BF16)

    def store(start, block):
        rows = start + iota((LANES, 1), 0)
        total_rows = blended[pl.ds(start, LANES), :] + jnp.where(rows < last, block, 0.0)
        result[2, pl.ds(start, LANES), :] = total_rows.astype(BF16)

    convolve(padded_grads, [band_back(one) for one in taps], length, store)
    first = iota((LANES, LANES), 1) < HEAD_DIM

    def block(step, carry):
        start = pl.multiple_of(step * LANES, LANES)
        own = padded_grads[pl.ds(start + HALF, LANES), :]
        window = padded[pl.ds(start, 2 * LANES), :]
        none = jnp.zeros_like(own)
        return (
            carry[0] + mm(jnp.where(first, own, none), window, NT),
            carry[1] + mm(jnp.where(first, none, own), window, NT),
        )

    start_sum = jnp.zeros((LANES, 2 * LANES), F32)
    sums = lax.fori_loop(0, length // LANES, block, (start_sum, start_sum))
    wide = 2 * LANES
    for head in range(2):
        folded = sums[head][0:8]
        for group in range(1, LANES // 8):
            rows = sums[head][8 * group : 8 * group + 8]
            folded = folded + pltpu.roll(rows, wide - 8 * group, 1)
        line = folded[0:1]
        for row in range(1, 8):
            line = line + pltpu.roll(folded[row : row + 1], wide - row, 1)
        grad_taps[head : head + 1, :] = line


TASKS = MICRO * PAIRS
KEPT = ("q_marks", "k_marks", "kernel", "total", "inverse", "product", "two", "three", "key_weights", "summary", "mixed", "token_weights")


def kept_shapes(length):
    square = (LANES, LANES)
    shapes = {name: square for name in KEPT}
    shapes["inverse"] = (NS_ITERS + 1,) + square
    for name in ("product", "two", "three"):
        shapes[name] = (NS_ITERS,) + square
    shapes["key_weights"] = shapes["token_weights"] = (LANES, length)
    return shapes


def owner_of(task, count):
    return task * count // TASKS


def task_of(me, count):
    task = (me * TASKS + count - 1) // count
    return task, owner_of(task, count) == me


def greet(count):
    me = lax.axis_index("dp")
    barrier = pltpu.get_barrier_semaphore()

    def signal(step, carry):
        pl.semaphore_signal(barrier, inc=1, device_id={"dp": lax.rem(me + step, count)}, device_id_type=MESH)
        return carry

    lax.fori_loop(1, count, signal, 0)
    pl.semaphore_wait(barrier, count - 1)


def scatter_tasks(count, piece, source, slab, send, receive):
    me = lax.axis_index("dp")

    def one(step, finish):
        task = lax.rem(task_of(me, count)[0] + step, TASKS)
        owner = owner_of(task, count)
        micro = task // PAIRS
        lanes = pl.ds(pl.multiple_of(lax.rem(task, PAIRS) * LANES, LANES), LANES)
        rows = pl.ds(pl.multiple_of(me * piece, piece), piece)
        outgoing = source.at[:, micro, :, lanes]
        landing = slab.at[:, rows, :]

        @pl.when(owner != me)
        def _():
            copy = pltpu.make_async_remote_copy(outgoing, landing, send.at[task], receive.at[me], device_id={"dp": owner}, device_id_type=MESH)
            if finish:
                copy.wait_send()
            else:
                copy.start()

        @pl.when((owner == me) & (not finish))
        def _():
            pltpu.make_async_copy(outgoing, landing, receive.at[me]).start()

    def run(finish):
        def body(step, carry):
            one(step, finish)
            return carry

        lax.fori_loop(0, TASKS, body, 0)

    return run


def await_slab(count, piece, slab, receive):
    def body(origin, carry):
        landing = slab.at[:, pl.ds(pl.multiple_of(origin * piece, piece), piece), :]
        pltpu.make_async_copy(landing, landing, receive.at[origin]).wait()
        return carry

    lax.fori_loop(0, count, body, 0)


def return_rows(count, piece, result, target, send, receive):
    me = lax.axis_index("dp")
    task = task_of(me, count)[0]
    micro = task // PAIRS
    lanes = pl.ds(pl.multiple_of(lax.rem(task, PAIRS) * LANES, LANES), LANES)

    def run(finish):
        def body(step, carry):
            peer = lax.rem(me + step, count)
            rows = pl.ds(pl.multiple_of(peer * piece, piece), piece)
            outgoing = result.at[:, rows, :]
            landing = target.at[:, micro, :, lanes]

            @pl.when(peer != me)
            def _():
                copy = pltpu.make_async_remote_copy(outgoing, landing, send.at[peer], receive.at[task], device_id={"dp": peer}, device_id_type=MESH)
                if finish:
                    copy.wait_send()
                else:
                    copy.start()

            @pl.when((peer == me) & (not finish))
            def _():
                pltpu.make_async_copy(outgoing, landing, receive.at[task]).start()

            return carry

        lax.fori_loop(0, count, body, 0)

    return run


def await_rows(target, receive):
    def body(task, carry):
        lanes = pl.ds(pl.multiple_of(lax.rem(task, PAIRS) * LANES, LANES), LANES)
        landing = target.at[:, task // PAIRS, :, lanes]
        pltpu.make_async_copy(landing, landing, receive.at[task]).wait()
        return carry

    lax.fori_loop(0, TASKS, body, 0)


def forward_kernel(count, piece, qkv, edges, lines, mixed_rows, slab, *refs):
    keep = dict(zip(KEPT, refs))
    padded, blended, result, send_one, receive_one, send_two, receive_two = refs[len(KEPT) :]
    me = lax.axis_index("dp")
    task, owns = task_of(me, count)
    greet(count)
    out = scatter_tasks(count, piece, qkv, slab, send_one, receive_one)
    out(False)
    back = return_rows(count, piece, result, mixed_rows, send_two, receive_two)

    @pl.when(owns)
    def _():
        micro, pair = task // PAIRS, lax.rem(task, PAIRS)
        await_slab(count, piece, slab, receive_one)
        attend(slab[0], slab[1], slab[2], edges[pl.ds(micro, 1), :], head_taps(lines, pair), keep, padded, blended, result.at[0])
        back(False)

    out(True)
    await_rows(mixed_rows, receive_two)

    @pl.when(owns)
    def _():
        back(True)


def backward_kernel(count, piece, grads, edges, lines, slab, *refs):
    keep = dict(zip(KEPT, refs))
    out_grads, grad_taps, grad_slab, padded, padded_grads, blended, result, send_one, receive_one, send_two, receive_two = refs[len(KEPT) :]
    me = lax.axis_index("dp")
    task, owns = task_of(me, count)
    greet(count)
    out = scatter_tasks(count, piece, grads, grad_slab, send_one, receive_one)
    out(False)
    back = return_rows(count, piece, result, out_grads, send_two, receive_two)
    grad_taps[...] = jnp.zeros(grad_taps.shape, F32)

    @pl.when(owns)
    def _():
        micro, pair = task // PAIRS, lax.rem(task, PAIRS)
        await_slab(count, piece, grad_slab, receive_one)
        attend_back(
            grad_slab[0], slab[0], slab[1], slab[2], edges[pl.ds(micro, 1), :], head_taps(lines, pair),
            keep, padded, padded_grads, blended, result, grad_taps.at[pair],
        )
        back(False)

    out(True)
    await_rows(out_grads, receive_two)

    @pl.when(owns)
    def _():
        back(True)


VMEM = pl.BlockSpec(memory_space=pltpu.VMEM)
DMA = pltpu.SemaphoreType.DMA


def attention_forward(count, qkv, edges, lines, ident):
    piece = qkv.shape[2]
    length = piece * count
    shapes = kept_shapes(length)
    results = pl.pallas_call(
        functools.partial(forward_kernel, count, piece),
        out_shape=[
            jax.ShapeDtypeStruct((1, MICRO, piece, D), BF16),
            jax.ShapeDtypeStruct((3, length, LANES), BF16),
        ]
        + [jax.ShapeDtypeStruct(shapes[name], F32) for name in KEPT],
        in_specs=[VMEM] * 3,
        out_specs=[VMEM] * (2 + len(KEPT)),
        scratch_shapes=[
            pltpu.VMEM((length + LANES, LANES), BF16),
            pltpu.VMEM((length, LANES), F32),
            pltpu.VMEM((1, length, LANES), BF16),
            DMA((TASKS,)),
            DMA((count,)),
            DMA((count,)),
            DMA((TASKS,)),
        ],
        compiler_params=pltpu.CompilerParams(collective_id=ident, has_side_effects=True, vmem_limit_bytes=60 << 20),
        name="attend_forward",
    )(qkv, edges, lines)
    return results[0][0], results[1:]


def attention_backward(count, grads, edges, lines, kept, ident):
    piece = grads.shape[2]
    length = piece * count
    return pl.pallas_call(
        functools.partial(backward_kernel, count, piece),
        out_shape=[
            jax.ShapeDtypeStruct((3, MICRO, piece, D), BF16),
            jax.ShapeDtypeStruct((PAIRS, 2, 2 * LANES), F32),
        ],
        in_specs=[VMEM] * (4 + len(KEPT)),
        out_specs=[VMEM] * 2,
        scratch_shapes=[
            pltpu.VMEM((1, length, LANES), BF16),
            pltpu.VMEM((length + LANES, LANES), BF16),
            pltpu.VMEM((length + LANES, LANES), BF16),
            pltpu.VMEM((length, LANES), F32),
            pltpu.VMEM((3, length, LANES), BF16),
            DMA((TASKS,)),
            DMA((count,)),
            DMA((count,)),
            DMA((TASKS,)),
        ],
        compiler_params=pltpu.CompilerParams(collective_id=ident, has_side_effects=True, vmem_limit_bytes=60 << 20),
        name="attend_backward",
    )(grads, edges, lines, *kept)


def arrange(sources, targets):
    params, first, second = sources
    lines, ups, sliced = targets[:LAYERS], targets[LAYERS : 2 * LAYERS], targets[2 * LAYERS :]
    for level in range(LAYERS):
        own = slice(level, level + 1)
        for line in range(TAP_LINE):
            lines[level][line : line + 1, :] = params[own, line * D : (line + 1) * D]
        lines[level][TAP_LINE:, :] = jnp.zeros((16 - TAP_LINE, D), F32)
        lines[level][TAP_LINE : TAP_LINE + 1, : HEADS * TAPS] = params[own, TAP_LINE * D :]
        ups[level][...] = params[own, 8 * D : 8 * D + FF]
    for source, target in zip((first, second), sliced):
        target[LAYERS * LINES // 2 :] = jnp.zeros((16 - LAYERS * LINES // 2, 2, D), F32)
        for level in range(LAYERS):
            own = slice(level, level + 1)
            for line in range(LINES):
                index = level * LINES + line
                spot = slice(index % 2, index % 2 + 1)
                if line < TAP_LINE:
                    target[index // 2, spot, :] = source[own, line * D : (line + 1) * D]
                else:
                    target[index // 2, spot, :] = jnp.zeros((1, D), F32)
                    target[index // 2, spot, : HEADS * TAPS] = source[own, TAP_LINE * D :]


ARRANGED = (
    [jax.ShapeDtypeStruct((16, D), F32)] * LAYERS + [jax.ShapeDtypeStruct((1, FF), F32)] * LAYERS + [jax.ShapeDtypeStruct((16, 2, D), F32)] * 2
)


def arrange_kernel(*refs):
    arrange(refs[:3], refs[3:])


def arranged(*smalls):
    return pl.pallas_call(arrange_kernel, out_shape=ARRANGED, in_specs=[VMEM] * 3, out_specs=[VMEM] * len(ARRANGED), name="arrange")(*smalls)


def gather_kernel(shard, params, first, second, out, *refs):
    targets, refs = refs[: len(ARRANGED)], refs[len(ARRANGED) :]
    gather_body(shard, out, lambda: arrange((params, first, second), targets), *refs)


def gather_body(shard, out, aside, local_sem, z_send, z_got, x_send, x_got, y_send, y_got, core_send, core_got):
    me = lax.axis_index("dp")
    x = lax.axis_index("rep")
    core, y, z = lax.rem(me, 2), lax.rem(me // 2, 2), me // 4
    half = shard.shape[0] // 2
    part = half // 2

    barrier = pltpu.get_barrier_semaphore()

    def peer(axis, sign=1):
        if axis == "x":
            return {"rep": 1 - x}
        if axis == "y":
            return {"dp": me + 2 - 4 * y}
        if axis == "core":
            return {"dp": me + 1 - 2 * core}
        return {"dp": me + 4 * sign}

    for axis in ("x", "y", "core"):
        pl.semaphore_signal(barrier, inc=1, device_id=peer(axis), device_id_type=MESH)
    for sign in (1, -1):

        @pl.when((z + sign >= 0) & (z + sign < 4))
        def _():
            pl.semaphore_signal(barrier, inc=1, device_id=peer("z", sign), device_id_type=MESH)

    pl.semaphore_wait(barrier, 4 + jnp.where((z > 0) & (z < 3), 1, 0))

    def rows(side, sub):
        return pl.ds(pl.multiple_of(side * half + sub * part, part), part)

    def side_rows(side):
        return pl.ds(pl.multiple_of(side * half, half), half)

    def remote(source, target, send, receive, where):
        return pltpu.make_async_remote_copy(source, target, send, receive, device_id=where, device_id_type=MESH)

    def spot(plane, row, side, sub):
        return out.at[plane, row, core, rows(side, sub), :]

    def move(axis, plane, row, side, sub, source=None):
        target = spot(plane, row, side, sub)
        source = target if source is None else source
        if axis == "core":
            return remote(source, target, core_send.at[plane, row, side, sub], core_got, peer("core"))
        send, receive = (x_send, x_got) if axis == "x" else (y_send, y_got)
        return remote(source, target, send.at[plane, row, side, sub], receive.at[plane, row, side, sub], peer(axis))

    def climb(plane, sub, sign, source=None):
        target = spot(plane, y, x, sub)
        way = 0 if sign > 0 else 1
        return remote(target if source is None else source, target, z_send.at[plane, sub, way], z_got.at[plane, sub], peer("z", sign))

    own = pltpu.make_async_copy(shard, out.at[z, y, core], local_sem)
    own.start()
    for sub in range(2):
        for sign in (1, -1):

            @pl.when((z + sign >= 0) & (z + sign < 4))
            def _():
                climb(z, sub, sign, shard.at[rows(x, sub), :]).start()

        move("y", z, y, x, sub, shard.at[rows(x, sub), :]).start()
    for side in range(2):
        for sub in range(2):
            move("core", z, y, side, sub, shard.at[rows(side, sub), :]).start()

    aside()

    def at_distance(distance, act):
        for sign in (1, -1):
            plane = z - sign * distance

            @pl.when((plane >= 0) & (plane < 4))
            def _():
                act(plane, sign)

    def from_z(plane, sign):
        for sub in range(2):
            climb(plane, sub, sign).wait_recv()

            @pl.when((z + sign >= 0) & (z + sign < 4))
            def _():
                climb(plane, sub, sign).start()

            for axis in ("x", "y", "core"):
                move(axis, plane, y, x, sub).start()

    def take(axis, plane, row, side, sub, onward=None):
        move(axis, plane, row, side, sub).wait_recv()
        if onward is not None:
            move(onward, plane, row, side, sub).start()
        move("core", plane, row, side, sub).start()

    def first_square(plane, sign):
        take("x", plane, y, 1 - x, 0, "y")
        take("y", plane, 1 - y, x, 1, "x")
        take("y", plane, 1 - y, x, 0)
        take("x", plane, y, 1 - x, 1)

    def second_square(plane, sign):
        take("y", plane, 1 - y, 1 - x, 0)
        take("x", plane, 1 - y, 1 - x, 1)

    at_distance(1, from_z)
    for sub in range(2):
        take("y", z, 1 - y, x, sub, "x")
    at_distance(2, from_z)
    at_distance(1, first_square)
    at_distance(3, from_z)
    at_distance(2, first_square)
    for sub in range(2):
        take("x", z, 1 - y, 1 - x, sub)
    at_distance(1, second_square)
    at_distance(3, first_square)
    at_distance(2, second_square)
    at_distance(3, second_square)
    own.wait()

    def finish(plane, sign):
        for sub in range(2):

            @pl.when((z + sign >= 0) & (z + sign < 4))
            def _():
                climb(plane, sub, sign).wait_send()

            move("x", plane, y, x, sub).wait_send()
            move("y", plane, y, x, sub).wait_send()
        move("y", plane, y, 1 - x, 0).wait_send()
        move("x", plane, 1 - y, x, 1).wait_send()

    for distance in (1, 2, 3):
        at_distance(distance, finish)
    for sub in range(2):
        for sign in (1, -1):

            @pl.when((z + sign >= 0) & (z + sign < 4))
            def _():
                climb(z, sub, sign).wait_send()

        move("y", z, y, x, sub).wait_send()
        move("x", z, 1 - y, x, sub).wait_send()

    def core_sent(index, carry):
        plane, row, side, sub = index // 8, lax.rem(index // 4, 2), lax.rem(index // 2, 2), lax.rem(index, 2)
        move("core", plane, row, side, sub).wait_send()
        return carry

    lax.fori_loop(0, 32, core_sent, 0)
    column = out.at[:, :, 1 - core]
    pltpu.make_async_copy(column, column, core_got).wait()


def gather(shard, *smalls):
    block_rows = shard.shape[0]
    results = pl.pallas_call(
        gather_kernel,
        out_shape=[jax.ShapeDtypeStruct((4, 2, 2, block_rows, D), BF16)] + ARRANGED,
        in_specs=[VMEM] * 4,
        out_specs=[pl.BlockSpec(memory_space=pl.ANY)] + [VMEM] * len(ARRANGED),
        scratch_shapes=[
            DMA,
            DMA((4, 2, 2)),
            DMA((4, 2)),
            DMA((4, 2, 2, 2)),
            DMA((4, 2, 2, 2)),
            DMA((4, 2, 2, 2)),
            DMA((4, 2, 2, 2)),
            DMA((4, 2, 2, 2)),
            DMA,
        ],
        compiler_params=pltpu.CompilerParams(collective_id=4, has_side_effects=True),
        name="gather",
    )(shard, *smalls)
    return results[0].reshape(16 * block_rows, D), results[1:]


CHUNK = 32
RING = 8
MATES = ("low_in", "low_comb", "low_up", "low_act", "low_grads", "low_branch", "low_hidden", "low_down", "gain_one", "shift_one", "gain_two", "shift_two", "taps")


def change(grad, first_old, second_old):
    new_first = ADAM_ONE * first_old + (1.0 - ADAM_ONE) * grad
    new_second = ADAM_TWO * second_old + (1.0 - ADAM_TWO) * grad * grad
    return new_first * (1.0 / (1.0 - ADAM_ONE**STEP_COUNT)) / (jnp.sqrt(new_second * (1.0 / (1.0 - ADAM_TWO**STEP_COUNT))) + ADAM_EPSILON)


def settle_kernel(block_rows, *refs):
    count = len(MATES)
    mates = [dict(zip(MATES, refs[level * count : (level + 1) * count])) for level in range(LAYERS)]
    (
        weights, first, second, small_first, small_second, grad_out, mean_out, small_out,
        turned, right, staged, own, got_core, got_y, got_z, inner, step_own, step_got, small, small_got, small_own, small_step, small_step_got,
        core_send, core_got, y_send, y_got, z_send, z_got, inner_sem, rep_send, rep_got, small_send, small_sem, back_send, back_sem, small_rep,
    ) = refs[LAYERS * count :]
    me = lax.axis_index("dp")
    other_rep = 1 - lax.axis_index("rep")
    core, y, z = lax.rem(me, 2), lax.rem(me // 2, 2), me // 4
    devices = 16
    per_layer = block_rows // CHUNK
    chunks = LAYERS * per_layer

    barrier = pltpu.get_barrier_semaphore()

    def signal(step, carry):
        pl.semaphore_signal(barrier, inc=1, device_id={"dp": lax.rem(me + step, devices)}, device_id_type=MESH)
        return carry

    lax.fori_loop(1, devices, signal, 0)
    pl.semaphore_signal(barrier, inc=1, device_id={"rep": other_rep}, device_id_type=MESH)

    def to_dp(source, target, send, receive, peer):
        return pltpu.make_async_remote_copy(source, target, send, receive, device_id={"dp": peer}, device_id_type=MESH)

    def to_rep(source, target, send, receive):
        return pltpu.make_async_remote_copy(source, target, send, receive, device_id={"rep": other_rep}, device_id_type=MESH)

    def spot(slot):
        return lax.rem(slot, RING)

    features = D * 2 + FF * 2
    for order, level in enumerate(reversed(range(LAYERS))):
        mate = mates[level]
        at = order * features
        for name in MATES[:4]:
            for part in range(mate[name].shape[1] // LANES):
                turned[at : at + LANES, :] = mate[name][:, part * LANES : (part + 1) * LANES].T
                at += LANES
        for part in range(3):
            right[order * 6 + part] = mate["low_grads"][part]
        for part, name in enumerate(MATES[5:8]):
            right[order * 6 + 3 + part] = mate[name][...]

    def put(level, line, row):
        index = level * LINES + line
        small[index // 2, index % 2 : index % 2 + 1, :] = row

    def column_sum(array):
        return jnp.sum(array.astype(F32), axis=0, keepdims=True)

    for level in range(LAYERS):
        mate = mates[level]
        put(level, 0, column_sum(mate["low_grads"][0]))
        put(level, 1, column_sum(mate["low_grads"][2]))
        put(level, 2, column_sum(mate["low_branch"][...]))
        put(level, 3, column_sum(mate["low_down"][...]))
        for line, name in enumerate(MATES[8:12]):
            put(level, 4 + line, column_sum(mate[name][...]))
        for part in range(FF // D):
            put(level, 8 + part, column_sum(mate["low_up"][:, part * D : (part + 1) * D]))
        line = jnp.zeros((1, D), F32)
        for head in range(HEADS):
            taps = jnp.concatenate([mate["taps"][head // 2][head % 2 : head % 2 + 1], jnp.zeros((1, D - 2 * LANES), F32)], axis=1)
            taps = jnp.where(iota((1, D), 1) < TAPS, taps, 0.0)
            line = line + (pltpu.roll(taps, TAPS * head, 1) if head else taps)
        put(level, 12, line)
    for index in range(LAYERS * LINES, 2 * devices):
        small[index // 2, index % 2 : index % 2 + 1, :] = jnp.zeros((1, D), F32)

    pl.semaphore_wait(barrier, devices)

    def small_copy(step):
        peer = lax.rem(me + step, devices)
        return to_dp(small.at[peer], small_got.at[me], small_send.at[peer], small_sem.at[me], peer)

    def small_begin(step, carry):
        small_copy(step).start()
        return carry

    lax.fori_loop(1, devices, small_begin, 0)

    def core_copy(chunk):
        return to_dp(staged.at[lax.rem(chunk, 2)], got_core.at[spot(chunk)], core_send.at[lax.rem(chunk, 2)], core_got.at[spot(chunk)], me + 1 - 2 * core)

    def y_copy(chunk):
        return to_dp(own.at[spot(chunk), :, 1 - y], got_y.at[spot(chunk)], y_send.at[spot(chunk)], y_got.at[spot(chunk)], me + 2 - 4 * y)

    def z_copy(chunk, hop):
        there = lax.rem(z + hop, 4)
        slot = spot(chunk)
        return to_dp(own.at[slot, there, y], got_z.at[slot, hop - 1], z_send.at[slot, hop - 1], z_got.at[slot, hop - 1], there * 4 + lax.rem(me, 4))

    def place(chunk):
        return LAYERS - 1 - chunk // per_layer, pl.ds(pl.multiple_of(lax.rem(chunk, per_layer) * CHUNK, CHUNK), CHUNK)

    def inner_copies(chunk):
        level, rows = place(chunk)
        slot = lax.rem(chunk, 4)
        return [
            pltpu.make_async_copy(array.at[level, rows, :], inner.at[slot, index], inner_sem.at[slot, index])
            for index, array in enumerate((weights, first, second))
        ]

    def rep_copy(chunk):
        return to_rep(step_own.at[spot(chunk)], step_got.at[spot(chunk)], rep_send.at[spot(chunk)], rep_got.at[spot(chunk)])

    def product(chunk, there, row, side):
        order = chunk // per_layer
        block = (there * 2 + row) * 2 + side
        piece = block * per_layer + lax.rem(chunk, per_layer)
        narrow = D // CHUNK
        line = jnp.where(piece < 3 * narrow, lax.rem(piece, narrow), piece - 2 * narrow)
        group = jnp.where(piece < 4 * narrow, piece // narrow, jnp.where(piece < 4 * narrow + FF // CHUNK, 4, 5))
        rows = pl.ds(pl.multiple_of(order * features + line * CHUNK, 16), CHUNK)
        return mm(turned[rows, :], right[order * 6 + group]).astype(BF16)

    def stage_product(chunk):
        for there in range(4):
            for row in range(2):
                staged[lax.rem(chunk, 2), there, row] = product(chunk, there, row, 1 - core)
        core_copy(chunk).start()
        for there in range(4):
            for row in range(2):
                own[spot(chunk), there, row] = product(chunk, there, row, core)

    def stage_core(chunk):
        core_copy(chunk).wait()
        slot = spot(chunk)
        for there in range(4):
            for side in range(2):
                own[slot, there, side] = own[slot, there, side] + got_core[slot, there, side]
        y_copy(chunk).start()

    def stage_y(chunk):
        y_copy(chunk).wait_recv()
        slot = spot(chunk)
        for there in range(4):
            own[slot, there, y] = own[slot, there, y] + got_y[slot, there]
        for hop in range(1, 4):
            z_copy(chunk, hop).start()
        for copy in inner_copies(chunk):
            copy.start()

    def stage_z(chunk):
        y_copy(chunk).wait_send()
        for hop in range(1, 4):
            z_copy(chunk, hop).wait_recv()
        for copy in inner_copies(chunk):
            copy.wait()
        total = own[spot(chunk), z, y].astype(F32)
        for hop in range(3):
            total = total + got_z[spot(chunk), hop].astype(F32)
        level, rows = place(chunk)
        grad_out[level, rows, :] = total
        slot = lax.rem(chunk, 4)
        step = change(total, inner[slot, 1], inner[slot, 2]) + WEIGHT_DECAY * inner[slot, 0]
        step_own[spot(chunk)] = (LR_INNER * step).astype(BF16)
        rep_copy(chunk).start()

    def stage_rep(chunk):
        for hop in range(1, 4):
            z_copy(chunk, hop).wait_send()
        rep_copy(chunk).wait()
        level, rows = place(chunk)
        mean_out[level, rows, :] = 0.5 * (step_own[spot(chunk)].astype(F32) + step_got[spot(chunk)].astype(F32))

    def small_rep_copy():
        return to_rep(small_step, small_step_got, small_rep.at[0], small_rep.at[1])

    def small_back(step):
        peer = lax.rem(me + step, devices)
        return to_dp(small_own, small_out.at[me], back_send.at[peer], back_sem.at[me], peer)

    def small_sum():
        def add(step, total):
            peer = lax.rem(me + step, devices)
            pltpu.make_async_copy(small_got.at[peer], small_got.at[peer], small_sem.at[peer]).wait()
            return total + small_got[peer]

        total = lax.fori_loop(1, devices, add, small[me])
        small_own[0] = total
        small_step[...] = (LR_SMALL * change(total, small_first[me], small_second[me])).astype(BF16)
        small_rep_copy().start()

    def small_spread():
        small_rep_copy().wait_recv()
        small_own[1] = 0.5 * (small_step[...].astype(F32) + small_step_got[...].astype(F32))
        small_out[me] = small_own[...]

        def send(step, carry):
            small_back(step).start()
            return carry

        lax.fori_loop(1, devices, send, 0)

    def turn(now, carry):
        for lag, stage in ((0, stage_product), (1, stage_core), (3, stage_y), (5, stage_z), (7, stage_rep)):

            @pl.when((now >= lag) & (now < chunks + lag))
            def _():
                stage(now - lag)

        pl.when(now == 4)(small_sum)
        pl.when(now == 7)(small_spread)
        return carry

    lax.fori_loop(0, chunks + 7, turn, 0)

    def small_drain(step, carry):
        peer = lax.rem(me + step, devices)
        small_copy(step).wait_send()
        small_back(step).wait_send()
        pltpu.make_async_copy(small_own, small_out.at[peer], back_sem.at[peer]).wait()
        return carry

    lax.fori_loop(1, devices, small_drain, 0)
    small_rep_copy().wait_send()


def settle(mates, weights, first, second, small_first, small_second):
    block_rows = weights.shape[1]
    anywhere = pl.BlockSpec(memory_space=pl.ANY)
    devices = 16
    piece = (CHUNK, D)
    tokens = mates[0]["low_in"].shape[0]
    return pl.pallas_call(
        functools.partial(settle_kernel, block_rows),
        out_shape=[
            jax.ShapeDtypeStruct(weights.shape, F32),
            jax.ShapeDtypeStruct(weights.shape, F32),
            jax.ShapeDtypeStruct((devices, 2, 2, D), F32),
        ],
        in_specs=[VMEM] * (LAYERS * len(MATES)) + [anywhere] * 3 + [VMEM] * 2,
        out_specs=[VMEM] * 3,
        scratch_shapes=[
            pltpu.VMEM((LAYERS * 2 * (D + FF), tokens), BF16),
            pltpu.VMEM((LAYERS * 6, tokens, D), BF16),
            pltpu.VMEM((2, 4, 2) + piece, BF16),
            pltpu.VMEM((RING, 4, 2) + piece, BF16),
            pltpu.VMEM((RING, 4, 2) + piece, BF16),
            pltpu.VMEM((RING, 4) + piece, BF16),
            pltpu.VMEM((RING, 3) + piece, BF16),
            pltpu.VMEM((4, 3) + piece, F32),
            pltpu.VMEM((RING,) + piece, BF16),
            pltpu.VMEM((RING,) + piece, BF16),
            pltpu.VMEM((devices, 2, D), F32),
            pltpu.VMEM((devices, 2, D), F32),
            pltpu.VMEM((2, 2, D), F32),
            pltpu.VMEM((2, D), BF16),
            pltpu.VMEM((2, D), BF16),
            DMA((2,)),
            DMA((RING,)),
            DMA((RING,)),
            DMA((RING,)),
            DMA((RING, 3)),
            DMA((RING, 3)),
            DMA((4, 3)),
            DMA((RING,)),
            DMA((RING,)),
            DMA((devices,)),
            DMA((devices,)),
            DMA((devices,)),
            DMA((devices,)),
            DMA((2,)),
        ],
        compiler_params=pltpu.CompilerParams(collective_id=3, has_side_effects=True, vmem_limit_bytes=63 << 20),
        name="settle",
    )(*[mate[name] for mate in mates for name in MATES], weights, first, second, small_first, small_second)


def finish_kernel(both, params, outer, first, second, first_new, second_new, outer_new, params_new, grad, mean):
    for level in range(LAYERS):
        for line in range(LINES):
            index = level * LINES + line
            spot = slice(index % 2, index % 2 + 1)
            for which, target in ((0, grad), (1, mean)):
                target[level : level + 1, line * D : (line + 1) * D] = both[index // 2, which, spot, :]
    first_new[...], second_new[...] = moments(first[...], second[...], grad[:, :SMALL])
    momentum = MOMENTUM * outer[...] + mean[:, :SMALL]
    outer_new[...] = momentum
    params_new[...] = params[...] - LR_OUTER * (mean[:, :SMALL] + MOMENTUM * momentum)


def finish(both, params, outer, first, second):
    wide = pltpu.VMEM((LAYERS, LINES * D), F32)
    return pl.pallas_call(
        finish_kernel,
        out_shape=[jax.ShapeDtypeStruct(params.shape, F32)] * 4,
        in_specs=[VMEM] * 5,
        out_specs=[VMEM] * 4,
        scratch_shapes=[wide, wide],
        name="finish",
    )(both, params, outer, first, second)


def dense(a, b, dims=NN):
    return mm(a, b, dims)


def standard(values):
    centred = values - jnp.mean(values, axis=-1, keepdims=True)
    scale = lax.rsqrt(jnp.mean(centred * centred, axis=-1, keepdims=True) + 1e-05)
    return centred * scale, scale


def layer_norm(values, gain, shift):
    return standard(values)[0] * gain + shift


def layer_norm_back(values, gain, grad):
    unit_values, scale = standard(values)
    inner = grad * gain
    along = jnp.mean(inner * unit_values, axis=-1, keepdims=True)
    result = scale * (inner - jnp.mean(inner, axis=-1, keepdims=True) - unit_values * along)
    return result, eighths(grad * unit_values), eighths(grad)


def eighths(rows):
    return jnp.sum(rows.reshape(-1, 8, D), axis=0)


def split_rows(rows):
    return rows[: 3 * D].reshape(3, D, D), rows[3 * D : 4 * D], rows[4 * D : 4 * D + FF], rows[4 * D + FF :]


def forward_layer(count, inputs, rows, small, edges, ident):
    piece = inputs.shape[0] // MICRO
    lines, bias_up = small
    proj, out_weight, up_weight, down_weight = split_rows(rows)
    low_in = inputs.astype(BF16)
    query = (dense(low_in, proj[0]) + lines[0:1]).astype(BF16)
    key = dense(low_in, proj[1]).astype(BF16)
    value = (dense(low_in, proj[2]) + lines[1:2]).astype(BF16)
    qkv = jnp.stack([query, key, value])
    low_comb, kept = attention_forward(count, qkv.reshape(3, MICRO, piece, D), edges, lines, ident)
    low_comb = low_comb.reshape(MICRO * piece, D)
    resid_one = inputs + (dense(low_comb, out_weight) + lines[2:3])
    hidden_one = layer_norm(resid_one, lines[4:5], lines[5:6])
    low_hidden = hidden_one.astype(BF16)
    upward = dense(low_hidden, up_weight, NT) + bias_up
    low_act = jax.nn.gelu(upward).astype(BF16)
    resid_two = hidden_one + (dense(low_act, down_weight) + lines[3:4])
    output = layer_norm(resid_two, lines[6:7], lines[7:8])
    return output, (low_in, kept, low_comb, resid_one, low_hidden, upward, low_act, resid_two)


def backward_layer(count, grad_output, rows, small, edges, state, ident):
    low_in, kept, low_comb, resid_one, low_hidden, upward, low_act, resid_two = state
    total = low_in.shape[0]
    piece = total // MICRO
    lines, _ = small
    proj, out_weight, up_weight, down_weight = split_rows(rows)
    grad_two, grad_gain_two, grad_shift_two = layer_norm_back(resid_two, lines[6:7], grad_output)
    low_down = grad_two.astype(BF16)
    grad_act = dense(low_down, down_weight, NT)
    _, pull_gelu = jax.vjp(jax.nn.gelu, upward)
    low_up = pull_gelu(grad_act)[0].astype(BF16)
    grad_hidden = grad_two + dense(low_up, up_weight)
    grad_one, grad_gain_one, grad_shift_one = layer_norm_back(resid_one, lines[4:5], grad_hidden)
    low_branch = grad_one.astype(BF16)
    grad_comb = dense(low_branch, out_weight, NT).astype(BF16)
    low_grads, grad_taps = attention_backward(count, grad_comb.reshape(1, MICRO, piece, D), edges, lines, kept, ident)
    low_grads = low_grads.reshape(3, total, D)
    grad_in = grad_one + sum(dense(low_grads[part], proj[part], NT) for part in range(3))
    vectors = (grad_gain_one, grad_shift_one, grad_gain_two, grad_shift_two)
    values = (low_in, low_comb, low_up, low_act, low_grads, low_branch, low_hidden, low_down, *vectors, grad_taps)
    return grad_in, dict(zip(MATES, values))


def plain_grads(mate):
    parts = [dense(mate["low_in"], mate["low_grads"][part], TN) for part in range(3)]
    parts = parts + [dense(mate[left], mate[right], TN) for left, right in (("low_comb", "low_branch"), ("low_up", "low_hidden"), ("low_act", "low_down"))]
    sums = [mate["low_grads"][0], mate["low_grads"][2], mate["low_branch"], mate["low_down"]]
    sums = [jnp.sum(one.astype(F32), axis=0) for one in sums]
    sums = sums + [jnp.sum(mate[name], axis=0) for name in MATES[8:12]]
    sums = sums + [jnp.sum(mate["low_up"].astype(F32), axis=0), mate["taps"][:, :, :TAPS].reshape(-1)]
    return jnp.concatenate(parts, axis=0).astype(BF16), jnp.concatenate(sums)


def moments(first, second, grad):
    return ADAM_ONE * first + (1.0 - ADAM_ONE) * grad, ADAM_TWO * second + (1.0 - ADAM_TWO) * grad * grad


def adam(weights, first, second, grad, rate, decay):
    correct_one = 1.0 - ADAM_ONE**STEP_COUNT
    correct_two = 1.0 - ADAM_TWO**STEP_COUNT
    new_first, new_second = moments(first, second, grad)
    step = new_first / correct_one / (jnp.sqrt(new_second / correct_two) + ADAM_EPSILON)
    return new_first, new_second, rate * (step + decay * weights)


def shards(
    hidden,
    bounds,
    cotangent,
    weights,
    small_params,
    first_big,
    second_big,
    first_small,
    second_small,
    outer_big,
    outer_small,
):
    count = lax.axis_size("dp")
    piece = hidden.shape[3]
    total = MICRO * piece
    low_weights = weights.astype(BF16)
    held = [lax.all_gather(low_weights[level], "dp", axis=0, tiled=True) for level in range(LAYERS)]
    if count == 16:
        held[0], prepared = gather(low_weights[0], small_params, first_small[0], second_small[0])
    else:
        prepared = arranged(small_params, first_small[0], second_small[0])
    smalls = [(prepared[level], prepared[LAYERS + level]) for level in range(LAYERS)]
    limits = bounds[0, :, 0, :]
    edges = jnp.pad(limits.astype(F32), ((0, 0), (0, LANES - limits.shape[1])))
    positions = lax.axis_index("dp") * piece + jnp.arange(piece, dtype=jnp.int32)
    valid = (positions[None, :] < limits[:, -1:]).astype(F32).reshape(total, 1)
    activation = hidden[0, :, 0].reshape(total, D).astype(F32)
    states = []
    for level in range(LAYERS):
        activation, state = forward_layer(count, activation, held[level], smalls[level], edges, 1)
        states.append(state)
    gradient = cotangent[0, :, 0].reshape(total, D).astype(F32) * valid
    mates = [None] * LAYERS
    for level in reversed(range(LAYERS)):
        gradient, mates[level] = backward_layer(count, gradient, held[level], smalls[level], edges, states[level], 2)
    if count == 16:
        grad_big, mean_big, small_both = settle(mates, weights, first_big[0], second_big[0], *prepared[2 * LAYERS :])
        new_smalls = finish(small_both, small_params, outer_small, first_small[0], second_small[0])
    else:
        rows, sums = zip(*[plain_grads(mate) for mate in mates])
        grad_big = jnp.stack([lax.psum_scatter(one, "dp", scatter_dimension=0, tiled=True).astype(F32) for one in rows])
        grad_small = lax.psum(jnp.stack(sums), "dp")
        reps = lax.axis_size("rep")
        delta_big = adam(weights, first_big[0], second_big[0], grad_big, LR_INNER, WEIGHT_DECAY)[2]
        delta_small = adam(small_params, first_small[0], second_small[0], grad_small, LR_SMALL, 0.0)[2]
        mean_big = lax.psum(delta_big.astype(BF16), "rep").astype(F32) / reps
        mean_small = lax.psum(delta_small.astype(BF16), "rep").astype(F32) / reps
        momentum = MOMENTUM * outer_small + mean_small
        new_smalls = (*moments(first_small[0], second_small[0], grad_small), momentum, small_params - LR_OUTER * (mean_small + MOMENTUM * momentum))
    new_first, new_second = moments(first_big[0], second_big[0], grad_big)
    new_first_small, new_second_small, outer_small_new, small_new = new_smalls
    outer_big_new = MOMENTUM * outer_big + mean_big
    weights_new = weights - LR_OUTER * (mean_big + MOMENTUM * outer_big_new)
    shape = (1, MICRO, 1, piece, D)
    return (
        activation.reshape(shape),
        gradient.reshape(shape),
        new_first[None],
        new_second[None],
        new_first_small[None],
        new_second_small[None],
        outer_big_new,
        outer_small_new,
        weights_new,
        small_new,
        weights_new.astype(BF16),
    )


def solution(mesh):
    placed = (
        P("rep", None, None, "dp", None),
        P("rep", None, None, None),
        P("rep", None, None, "dp", None),
        P(None, "dp", None),
        P(),
        P("rep", None, "dp", None),
        P("rep", None, "dp", None),
        P("rep", None, None),
        P("rep", None, None),
        P(None, "dp", None),
        P(),
    )
    return jax.shard_map(
        shards,
        mesh=mesh,
        in_specs=placed,
        out_specs=(
            P("rep", None, None, "dp", None),
            P("rep", None, None, "dp", None),
            P("rep", None, "dp", None),
            P("rep", None, "dp", None),
            P("rep", None, None),
            P("rep", None, None),
            P(None, "dp", None),
            P(),
            P(None, "dp", None),
            P(),
            P(None, "dp", None),
        ),
        check_vma=False,
    )
```

```python
import functools

import jax
import jax.numpy as jnp
from jax import lax
from jax.experimental import pallas as pl
from jax.experimental.pallas import tpu as pltpu
from jax.sharding import PartitionSpec as P

D = 768
HEADS = 12
FF = 3072
TAPS = 33
NS_ITERS = 6
LAYERS = 2
MICRO = 2
STEP_COUNT = 5


ADAM_ONE = 0.9
ADAM_TWO = 0.95
ADAM_EPSILON = 1e-08
WEIGHT_DECAY = 0.1
LR_INNER = 0.04
LR_SMALL = 0.2
LR_OUTER = 0.7
MOMENTUM = 0.9

HEAD_DIM = 64
MARKS = 64
HALF = TAPS // 2
PAIRS = HEADS // 2
LINES = 13
TAP_LINE = 12
SMALL = 8 * D + FF + HEADS * TAPS
LANES = 128
SCALE = HEAD_DIM**-0.5
NEG = -1e30
MESH = pl.DeviceIdType.MESH
F32 = jnp.float32
BF16 = jnp.bfloat16
NN = (((1,), (0,)), ((), ()))
NT = (((1,), (1,)), ((), ()))
TN = (((0,), (0,)), ((), ()))


def mm(a, b, dims=NN):
    return lax.dot_general(a, b, dims, preferred_element_type=F32)


def halves(a):
    high = a.astype(BF16)
    return high, (a - high.astype(F32)).astype(BF16)


def mm_left(a, b, dims=NN):
    high, rest = halves(a)
    return mm(high, b, dims) + mm(rest, b, dims)


def mm_both(a, b, dims=NN):
    ah, al = halves(a)
    bh, bl = halves(b)
    return mm(ah, bh, dims) + (mm(ah, bl, dims) + mm(al, bh, dims))


def exact(a, b, dims=NN):
    return mm_both(a, b, dims)


def iota(shape, dim):
    return lax.broadcasted_iota(jnp.int32, shape, dim)


def diagonal_blocks():
    return (iota((LANES, LANES), 0) < MARKS) == (iota((LANES, LANES), 1) < HEAD_DIM)


def unit():
    return (iota((LANES, LANES), 0) == iota((LANES, LANES), 1)).astype(F32)


def per_head(marks):
    first = iota(marks.shape, 1) < HEAD_DIM
    return jnp.concatenate([jnp.where(first, marks, 0.0), jnp.where(first, 0.0, marks)], axis=0)


def head_sums(a):
    rows, cols = a.shape
    split = a.reshape(2, rows // 2, cols)
    return jnp.broadcast_to(jnp.sum(split, axis=1, keepdims=True), split.shape).reshape(rows, cols)


def head_tops(a):
    rows, cols = a.shape
    split = a.reshape(2, rows // 2, cols)
    return jnp.broadcast_to(jnp.max(split, axis=1, keepdims=True), split.shape).reshape(rows, cols)


def head_taps(lines, pair):
    row = jnp.broadcast_to(lines[TAP_LINE : TAP_LINE + 1, :], (8, D))
    rows = []
    for side in range(2):
        turned = pltpu.roll(row, lax.rem(D - TAPS * (2 * pair + side), D), 1)[0:1, : 2 * LANES]
        rows.append(jnp.where(iota((1, 2 * LANES), 1) < TAPS, turned, 0.0))
    return rows


def band(taps_row):
    wide = jnp.broadcast_to(taps_row, (LANES, 2 * LANES))
    return pltpu.roll(wide, 0, 1, stride=1, stride_axis=0)


def band_back(taps_row):
    wide = jnp.broadcast_to(taps_row, (2 * LANES, 2 * LANES))
    return pltpu.roll(wide, 2 * LANES - 2 * HALF, 1, stride=1, stride_axis=0)[:, :LANES].T


def mark_columns(edges):
    low = jnp.broadcast_to(edges, (LANES, LANES)).T[:MARKS, :1]
    high = jnp.broadcast_to(pltpu.roll(edges, LANES - 1, 1), (LANES, LANES)).T[:MARKS, :1]
    return low.astype(jnp.int32), high.astype(jnp.int32)


def mark_rows(edges):
    low, high = edges[:, :MARKS], pltpu.roll(edges, LANES - 1, 1)[:, :MARKS]
    return low.astype(jnp.int32), high.astype(jnp.int32)


def convolve(padded, bands, length, store):
    first = iota((LANES, LANES), 1) < HEAD_DIM
    pairs = [halves(one) for one in bands]

    def block(at, carry):
        start = pl.multiple_of(at * LANES, LANES)
        window = padded[pl.ds(start, 2 * LANES), :]
        out = [mm(high, window) + mm(rest, window) for high, rest in pairs]
        store(start, jnp.where(first, out[0], out[1]))
        return carry

    lax.fori_loop(0, length // LANES, block, 0)


def attend(slab, edges, taps, keep, padded, blended, result):
    length = slab.shape[1]

    def begin():
        low_marks, high_marks = mark_columns(edges())
        at = iota((MARKS, length), 1)
        member = ((low_marks <= at) & (at < high_marks)).astype(F32).astype(BF16)
        counts = (high_marks - low_marks).astype(F32)
        q_marks = per_head(mm(member, slab[0]) / counts)
        k_marks = per_head(mm(member, slab[1]) / counts)
        scores = jnp.where(diagonal_blocks(), SCALE * exact(q_marks, k_marks, NT), NEG)
        weights = jnp.exp(scores - jnp.max(scores, axis=1, keepdims=True))
        kernel = weights / jnp.sum(weights, axis=1, keepdims=True)
        total = head_sums(jnp.broadcast_to(jnp.sum(kernel * kernel, axis=1, keepdims=True), kernel.shape))
        keep["q_marks"][...] = q_marks
        keep["k_marks"][...] = k_marks
        keep["kernel"][...] = kernel
        keep["total"][...] = total
        keep["inverse"][0] = kernel.T / total

    def sweep(at):
        def run():
            eye, inverse = unit(), keep["inverse"][at]
            product = exact(keep["kernel"][...], inverse)
            one = 7.0 * eye - product
            two = 15.0 * eye - exact(product, one)
            three = 13.0 * eye - exact(product, two)
            keep["product"][at] = product
            keep["two"][at] = two
            keep["three"][at] = three
            keep["inverse"][at + 1] = 0.25 * exact(inverse, three)

        return run

    def over_keys():
        valid = iota((1, length), 1) < mark_columns(edges())[1][MARKS - 1 :]
        key_scores = jnp.where(valid, SCALE * mm_left(keep["q_marks"][...], slab[1], NT), NEG)
        key_exp = jnp.where(valid, jnp.exp(key_scores - jnp.max(key_scores, axis=1, keepdims=True)), 0.0)
        key_weights = key_exp / jnp.sum(key_exp, axis=1, keepdims=True)
        keep["key_weights"][...] = key_weights
        keep["summary"][...] = jnp.where(diagonal_blocks(), mm_left(key_weights, slab[2]), 0.0)

    def over_tokens():
        token_scores = SCALE * mm_left(keep["k_marks"][...], slab[0], NT)
        token_exp = jnp.exp(token_scores - head_tops(token_scores))
        keep["token_weights"][...] = token_exp / head_sums(token_exp)

    def close():
        mixed = exact(keep["inverse"][NS_ITERS], keep["summary"][...])
        keep["mixed"][...] = mixed
        blended[...] = mm_both(keep["token_weights"][...], mixed, TN)
        values = slab[2]
        valid_column = iota((length, 1), 0) < mark_columns(edges())[1][MARKS - 1 :]
        padded[0:HALF, :] = jnp.zeros((HALF, LANES), BF16)
        padded[HALF : HALF + length, :] = jnp.where(valid_column, values, jnp.zeros_like(values))
        padded[HALF + length :, :] = jnp.zeros((LANES - HALF, LANES), BF16)

        def store(start, block):
            result[pl.ds(start, LANES), :] = (blended[pl.ds(start, LANES), :] + block).astype(BF16)

        convolve(padded, [band(one) for one in taps()], length, store)

    return [begin] + [sweep(at) for at in range(NS_ITERS)] + [over_keys, over_tokens, close]


def attend_back(grads, queries, keys, values, edges, taps, keep, padded, padded_grads, blended, result, grad_taps):
    length = grads.shape[0]
    low_marks, high_marks = mark_columns(edges)
    low_row, high_row = mark_rows(edges)
    at = iota((length, MARKS), 0)
    member = ((low_row <= at) & (at < high_row)).astype(F32).astype(BF16)
    counts = (high_marks - low_marks).astype(F32)
    blocks, eye = diagonal_blocks(), unit()
    q_marks, k_marks = keep["q_marks"][...], keep["k_marks"][...]
    token_weights, key_weights = keep["token_weights"][...], keep["key_weights"][...]
    summary, mixed = keep["summary"][...], keep["mixed"][...]
    kernel = keep["kernel"][...]
    inverse = keep["inverse"][NS_ITERS]
    grad_mixed = jnp.where(blocks, mm_left(token_weights, grads), 0.0)
    grad_token = token_weights * mm_left(mixed, grads, NT)
    grad_token = SCALE * (grad_token - token_weights * head_sums(grad_token))
    grad_summary = exact(inverse, grad_mixed, TN)
    grad_inverse = exact(grad_mixed, summary, NT)
    grad_kernel = jnp.zeros_like(kernel)
    for sweep in reversed(range(NS_ITERS)):
        before, product = keep["inverse"][sweep], keep["product"][sweep]
        one = 7.0 * eye - product
        two, three = keep["two"][sweep], keep["three"][sweep]
        grad_three = 0.25 * exact(before, grad_inverse, TN)
        grad_two = -exact(product, grad_three, TN)
        grad_one = -exact(product, grad_two, TN)
        grad_product = -(exact(grad_three, two, NT) + exact(grad_two, one, NT) + grad_one)
        grad_kernel = grad_kernel + exact(grad_product, before, NT)
        grad_inverse = 0.25 * exact(grad_inverse, three, NT) + exact(kernel, grad_product, TN)
    total = keep["total"][...]
    turned = grad_inverse.T / total
    weighted = jnp.sum(jnp.where(blocks, turned * kernel, 0.0), axis=1, keepdims=True)
    weighted = head_sums(jnp.broadcast_to(weighted, kernel.shape))
    grad_kernel = grad_kernel + turned - 2.0 * kernel * weighted / total
    grad_scores = SCALE * kernel * (grad_kernel - jnp.sum(kernel * grad_kernel, axis=1, keepdims=True))
    grad_q_marks = exact(grad_scores, k_marks)
    grad_k_marks = exact(grad_scores, q_marks, TN)
    grad_k_marks = grad_k_marks + jnp.where(blocks, mm_left(grad_token, queries), 0.0)
    grad_key = mm_left(grad_summary, values, NT) - jnp.sum(grad_summary * summary, axis=1, keepdims=True)
    grad_key = SCALE * key_weights * grad_key
    grad_q_marks = grad_q_marks + jnp.where(blocks, mm_left(grad_key, keys), 0.0)
    grad_q_marks = (grad_q_marks[:MARKS] + grad_q_marks[MARKS:]) / counts
    grad_k_marks = (grad_k_marks[:MARKS] + grad_k_marks[MARKS:]) / counts
    high, rest = halves(grad_q_marks)
    result[0] = (mm_both(grad_token, k_marks, TN) + mm(member, high) + mm(member, rest)).astype(BF16)
    high, rest = halves(grad_k_marks)
    result[1] = (mm_both(grad_key, q_marks, TN) + mm(member, high) + mm(member, rest)).astype(BF16)
    blended[...] = mm_both(key_weights, grad_summary, TN)
    last = high_marks[MARKS - 1 :]
    valid_column = iota((length, 1), 0) < last
    padded[0:HALF, :] = jnp.zeros((HALF, LANES), BF16)
    padded[HALF : HALF + length, :] = jnp.where(valid_column, values, jnp.zeros_like(values))
    padded[HALF + length :, :] = jnp.zeros((LANES - HALF, LANES), BF16)
    padded_grads[0:HALF, :] = jnp.zeros((HALF, LANES), BF16)
    padded_grads[HALF : HALF + length, :] = grads
    padded_grads[HALF + length :, :] = jnp.zeros((LANES - HALF, LANES), BF16)

    def store(start, block):
        rows = start + iota((LANES, 1), 0)
        total_rows = blended[pl.ds(start, LANES), :] + jnp.where(rows < last, block, 0.0)
        result[2, pl.ds(start, LANES), :] = total_rows.astype(BF16)

    convolve(padded_grads, [band_back(one) for one in taps], length, store)
    first = iota((LANES, LANES), 1) < HEAD_DIM

    def block(step, carry):
        start = pl.multiple_of(step * LANES, LANES)
        own = padded_grads[pl.ds(start + HALF, LANES), :]
        window = padded[pl.ds(start, 2 * LANES), :]
        none = jnp.zeros_like(own)
        return (
            carry[0] + mm(jnp.where(first, own, none), window, NT),
            carry[1] + mm(jnp.where(first, none, own), window, NT),
        )

    start_sum = jnp.zeros((LANES, 2 * LANES), F32)
    sums = lax.fori_loop(0, length // LANES, block, (start_sum, start_sum))
    wide = 2 * LANES
    for head in range(2):
        folded = sums[head][0:8]
        for group in range(1, LANES // 8):
            rows = sums[head][8 * group : 8 * group + 8]
            folded = folded + pltpu.roll(rows, wide - 8 * group, 1)
        line = folded[0:1]
        for row in range(1, 8):
            line = line + pltpu.roll(folded[row : row + 1], wide - row, 1)
        grad_taps[head : head + 1, :] = line


TASKS = MICRO * PAIRS
KEPT = ("q_marks", "k_marks", "kernel", "total", "inverse", "product", "two", "three", "key_weights", "summary", "mixed", "token_weights")


def kept_shapes(length):
    square = (LANES, LANES)
    shapes = {name: square for name in KEPT}
    shapes["inverse"] = (NS_ITERS + 1,) + square
    for name in ("product", "two", "three"):
        shapes[name] = (NS_ITERS,) + square
    shapes["key_weights"] = shapes["token_weights"] = (LANES, length)
    return shapes


def owner_of(task, count):
    return task * count // TASKS


def task_of(me, count):
    task = (me * TASKS + count - 1) // count
    return task, owner_of(task, count) == me


def greet(count, across=False):
    me = lax.axis_index("dp")
    barrier = pltpu.get_barrier_semaphore()
    if across:
        pl.semaphore_signal(barrier, inc=1, device_id={"rep": 1 - lax.axis_index("rep")}, device_id_type=MESH)

    def signal(step, carry):
        pl.semaphore_signal(barrier, inc=1, device_id={"dp": lax.rem(me + step, count)}, device_id_type=MESH)
        return carry

    lax.fori_loop(1, count, signal, 0)
    pl.semaphore_wait(barrier, count if across else count - 1)


def scatter_tasks(count, piece, source, slab, send, receive):
    me = lax.axis_index("dp")

    def one(step, finish):
        task = lax.rem(task_of(me, count)[0] + step, TASKS)
        owner = owner_of(task, count)
        micro = task // PAIRS
        lanes = pl.ds(pl.multiple_of(lax.rem(task, PAIRS) * LANES, LANES), LANES)
        rows = pl.ds(pl.multiple_of(me * piece, piece), piece)
        outgoing = source.at[:, micro, :, lanes]
        landing = slab.at[:, rows, :]

        @pl.when(owner != me)
        def _():
            copy = pltpu.make_async_remote_copy(outgoing, landing, send.at[task], receive.at[me], device_id={"dp": owner}, device_id_type=MESH)
            if finish:
                copy.wait_send()
            else:
                copy.start()

        @pl.when((owner == me) & (not finish))
        def _():
            pltpu.make_async_copy(outgoing, landing, receive.at[me]).start()

    def run(finish):
        def body(step, carry):
            one(step, finish)
            return carry

        lax.fori_loop(0, TASKS, body, 0)

    return run


def await_slab(count, piece, slab, receive):
    def body(origin, carry):
        landing = slab.at[:, pl.ds(pl.multiple_of(origin * piece, piece), piece), :]
        pltpu.make_async_copy(landing, landing, receive.at[origin]).wait()
        return carry

    lax.fori_loop(0, count, body, 0)


def return_rows(count, piece, result, target, send, receive):
    me = lax.axis_index("dp")
    task = task_of(me, count)[0]
    micro = task // PAIRS
    lanes = pl.ds(pl.multiple_of(lax.rem(task, PAIRS) * LANES, LANES), LANES)

    def run(finish):
        def body(step, carry):
            peer = lax.rem(me + step, count)
            rows = pl.ds(pl.multiple_of(peer * piece, piece), piece)
            outgoing = result.at[:, rows, :]
            landing = target.at[:, micro, :, lanes]

            @pl.when(peer != me)
            def _():
                copy = pltpu.make_async_remote_copy(outgoing, landing, send.at[peer], receive.at[task], device_id={"dp": peer}, device_id_type=MESH)
                if finish:
                    copy.wait_send()
                else:
                    copy.start()

            @pl.when((peer == me) & (not finish))
            def _():
                pltpu.make_async_copy(outgoing, landing, receive.at[task]).start()

            return carry

        lax.fori_loop(0, count, body, 0)

    return run


def await_rows(target, receive):
    def body(task, carry):
        lanes = pl.ds(pl.multiple_of(lax.rem(task, PAIRS) * LANES, LANES), LANES)
        landing = target.at[:, task // PAIRS, :, lanes]
        pltpu.make_async_copy(landing, landing, receive.at[task]).wait()
        return carry

    lax.fori_loop(0, TASKS, body, 0)


def forward_kernel(count, piece, spans, qkv, edges, lines, low, mixed_rows, slab, *refs):
    keep = dict(zip(KEPT, refs))
    outs, refs = refs[len(KEPT) : len(KEPT) + len(spans)], refs[len(KEPT) + len(spans) :]
    padded, blended, result, send_one, receive_one, send_two, receive_two = refs[:7]
    begin, steps, finish = spread_all(spans, low, outs, refs[7:])
    me = lax.axis_index("dp")
    task, owns = task_of(me, count)
    micro, pair = task // PAIRS, lax.rem(task, PAIRS)
    greet(count, bool(spans))
    out = scatter_tasks(count, piece, qkv, slab, send_one, receive_one)
    out(False)
    begin()
    back = return_rows(count, piece, result, mixed_rows, send_two, receive_two)
    phases = attend(slab, lambda: edges[pl.ds(micro, 1), :], lambda: head_taps(lines, pair), keep, padded, blended, result.at[0])

    def between(at):
        if at < len(steps):
            steps[at]()

    between(0)
    for at, phase in enumerate(phases):

        @pl.when(owns)
        def _():
            if at == 0:
                await_slab(count, piece, slab, receive_one)
            phase()
            if at == len(phases) - 1:
                back(False)

        if at > 1:
            between(at - 1)
    for at in range(len(phases) - 1, len(steps)):
        between(at)
    finish()
    out(True)
    await_rows(mixed_rows, receive_two)

    @pl.when(owns)
    def _():
        back(True)


def backward_kernel(count, piece, grads, edges, lines, slab, *refs):
    keep = dict(zip(KEPT, refs))
    out_grads, grad_taps, grad_slab, padded, padded_grads, blended, result, send_one, receive_one, send_two, receive_two = refs[len(KEPT) :]
    me = lax.axis_index("dp")
    task, owns = task_of(me, count)
    greet(count)
    out = scatter_tasks(count, piece, grads, grad_slab, send_one, receive_one)
    out(False)
    back = return_rows(count, piece, result, out_grads, send_two, receive_two)
    grad_taps[...] = jnp.zeros(grad_taps.shape, F32)

    @pl.when(owns)
    def _():
        micro, pair = task // PAIRS, lax.rem(task, PAIRS)
        await_slab(count, piece, grad_slab, receive_one)
        attend_back(
            grad_slab[0], slab[0], slab[1], slab[2], edges[pl.ds(micro, 1), :], head_taps(lines, pair),
            keep, padded, padded_grads, blended, result, grad_taps.at[pair],
        )
        back(False)

    out(True)
    await_rows(out_grads, receive_two)

    @pl.when(owns)
    def _():
        back(True)


VMEM = pl.BlockSpec(memory_space=pltpu.VMEM)
DMA = pltpu.SemaphoreType.DMA


def attention_forward(count, qkv, edges, lines, ident, low=None, spans=()):
    piece = qkv.shape[2]
    length = piece * count
    shapes = kept_shapes(length)
    low = lines if low is None else low
    anywhere = pl.BlockSpec(memory_space=pl.ANY)
    results = pl.pallas_call(
        functools.partial(forward_kernel, count, piece, spans),
        out_shape=[
            jax.ShapeDtypeStruct((1, MICRO, piece, D), BF16),
            jax.ShapeDtypeStruct((3, length, LANES), BF16),
        ]
        + [jax.ShapeDtypeStruct(shapes[name], F32) for name in KEPT]
        + [spread_shape(low, span) for span in spans],
        in_specs=[VMEM] * 4,
        out_specs=[VMEM] * (2 + len(KEPT)) + [anywhere] * len(spans),
        scratch_shapes=[
            pltpu.VMEM((length + LANES, LANES), BF16),
            pltpu.VMEM((length, LANES), F32),
            pltpu.VMEM((1, length, LANES), BF16),
            DMA((TASKS,)),
            DMA((count,)),
            DMA((count,)),
            DMA((TASKS,)),
        ]
        + [one for span in spans for one in spread_semaphores(span)],
        compiler_params=pltpu.CompilerParams(collective_id=ident, has_side_effects=True, vmem_limit_bytes=60 << 20),
        name="attend_forward",
    )(qkv, edges, lines, low)
    return results[0][0], results[1 : 2 + len(KEPT)], [flat_rows(one) for one in results[2 + len(KEPT) :]]


def attention_backward(count, grads, edges, lines, kept, ident):
    piece = grads.shape[2]
    length = piece * count
    return pl.pallas_call(
        functools.partial(backward_kernel, count, piece),
        out_shape=[
            jax.ShapeDtypeStruct((3, MICRO, piece, D), BF16),
            jax.ShapeDtypeStruct((PAIRS, 2, 2 * LANES), F32),
        ],
        in_specs=[VMEM] * (4 + len(KEPT)),
        out_specs=[VMEM] * 2,
        scratch_shapes=[
            pltpu.VMEM((1, length, LANES), BF16),
            pltpu.VMEM((length + LANES, LANES), BF16),
            pltpu.VMEM((length + LANES, LANES), BF16),
            pltpu.VMEM((length, LANES), F32),
            pltpu.VMEM((3, length, LANES), BF16),
            DMA((TASKS,)),
            DMA((count,)),
            DMA((count,)),
            DMA((TASKS,)),
        ],
        compiler_params=pltpu.CompilerParams(collective_id=ident, has_side_effects=True, vmem_limit_bytes=60 << 20),
        name="attend_backward",
    )(grads, edges, lines, *kept)


def arrange(sources, targets):
    params, first, second = sources
    lines, ups, sliced = targets[:LAYERS], targets[LAYERS : 2 * LAYERS], targets[2 * LAYERS :]
    for level in range(LAYERS):
        own = slice(level, level + 1)
        for line in range(TAP_LINE):
            lines[level][line : line + 1, :] = params[own, line * D : (line + 1) * D]
        lines[level][TAP_LINE:, :] = jnp.zeros((16 - TAP_LINE, D), F32)
        lines[level][TAP_LINE : TAP_LINE + 1, : HEADS * TAPS] = params[own, TAP_LINE * D :]
        ups[level][...] = params[own, 8 * D : 8 * D + FF]
    for source, target in zip((first, second), sliced):
        target[LAYERS * LINES // 2 :] = jnp.zeros((16 - LAYERS * LINES // 2, 2, D), F32)
        for level in range(LAYERS):
            own = slice(level, level + 1)
            for line in range(LINES):
                index = level * LINES + line
                spot = slice(index % 2, index % 2 + 1)
                if line < TAP_LINE:
                    target[index // 2, spot, :] = source[own, line * D : (line + 1) * D]
                else:
                    target[index // 2, spot, :] = jnp.zeros((1, D), F32)
                    target[index // 2, spot, : HEADS * TAPS] = source[own, TAP_LINE * D :]


ARRANGED = (
    [jax.ShapeDtypeStruct((16, D), F32)] * LAYERS + [jax.ShapeDtypeStruct((1, FF), F32)] * LAYERS + [jax.ShapeDtypeStruct((16, 2, D), F32)] * 2
)


def arrange_kernel(*refs):
    arrange(refs[:3], refs[3:])


def arranged(*smalls):
    return pl.pallas_call(arrange_kernel, out_shape=ARRANGED, in_specs=[VMEM] * 3, out_specs=[VMEM] * len(ARRANGED), name="arrange")(*smalls)


PLANES = 4


def gather_kernel(spans, low, params, first, second, *refs):
    outs, refs = refs[: len(spans)], refs[len(spans) :]
    targets, refs = refs[: len(ARRANGED)], refs[len(ARRANGED) :]
    begin, steps, finish = spread_all(spans, low, outs, refs)
    me, x = lax.axis_index("dp"), lax.axis_index("rep")
    core, y, z = lax.rem(me, 2), lax.rem(me // 2, 2), me // 4
    barrier = pltpu.get_barrier_semaphore()
    for where in ({"rep": 1 - x}, {"dp": me + 2 - 4 * y}, {"dp": me + 1 - 2 * core}):
        pl.semaphore_signal(barrier, inc=1, device_id=where, device_id_type=MESH)
    for sign in (1, -1):

        @pl.when((z + sign >= 0) & (z + sign < PLANES))
        def _():
            pl.semaphore_signal(barrier, inc=1, device_id={"dp": me + 4 * sign}, device_id_type=MESH)

    pl.semaphore_wait(barrier, 4 + jnp.where((z > 0) & (z < PLANES - 1), 1, 0))
    begin()
    arrange((params, first, second), targets)
    for step in steps:
        step()
    finish()


def spread_semaphores(span):
    planes = span[2] - span[1]
    return [DMA, DMA((planes, 2, 2)), DMA((planes, 2))] + [DMA((planes, 2, 2, 2))] * 5 + [DMA]


def spread_shape(low, span):
    return jax.ShapeDtypeStruct((span[2] - span[1], 2, 2) + low.shape[1:], BF16)


def flat_rows(blocks):
    return blocks.reshape(-1, D)


def spread_all(spans, low, outs, semaphores):
    each = len(semaphores) // max(len(spans), 1)
    parts = [
        spread(low.at[level], out, bottom, top, *semaphores[at * each : (at + 1) * each])
        for at, ((level, bottom, top), out) in enumerate(zip(spans, outs))
    ]

    def together(actions):
        def run():
            for action in actions:
                action()

        return run

    steps = [together(actions) for actions in zip(*[part[1] for part in parts])]
    return together([part[0] for part in parts]), steps, together([part[2] for part in parts])


def spread(shard, out, bottom, top, local_sem, z_send, z_got, x_send, x_got, y_send, y_got, core_send, core_got):
    me = lax.axis_index("dp")
    x = lax.axis_index("rep")
    core, y, z = lax.rem(me, 2), lax.rem(me // 2, 2), me // 4
    half = shard.shape[0] // 2
    part = half // 2

    def held(plane):
        return (plane >= bottom) & (plane < top)

    def peer(axis, sign=1):
        if axis == "x":
            return {"rep": 1 - x}
        if axis == "y":
            return {"dp": me + 2 - 4 * y}
        if axis == "core":
            return {"dp": me + 1 - 2 * core}
        return {"dp": me + 4 * sign}

    def rows(side, sub):
        return pl.ds(pl.multiple_of(side * half + sub * part, part), part)

    def remote(source, target, send, receive, where):
        return pltpu.make_async_remote_copy(source, target, send, receive, device_id=where, device_id_type=MESH)

    def spot(plane, row, side, sub):
        return out.at[plane - bottom, row, core, rows(side, sub), :]

    def move(axis, plane, row, side, sub, source=None):
        target = spot(plane, row, side, sub)
        source = target if source is None else source
        at = plane - bottom
        if axis == "core":
            return remote(source, target, core_send.at[at, row, side, sub], core_got, peer("core"))
        send, receive = (x_send, x_got) if axis == "x" else (y_send, y_got)
        return remote(source, target, send.at[at, row, side, sub], receive.at[at, row, side, sub], peer(axis))

    def climb(plane, sub, sign, source=None):
        target = spot(plane, y, x, sub)
        way = 0 if sign > 0 else 1
        at = plane - bottom
        return remote(target if source is None else source, target, z_send.at[at, sub, way], z_got.at[at, sub], peer("z", sign))

    def inside(sign, act):
        pl.when((z + sign >= 0) & (z + sign < PLANES))(act)

    def begin():
        @pl.when(held(z))
        def _():
            pltpu.make_async_copy(shard, out.at[z - bottom, y, core], local_sem).start()
            for sub in range(2):
                for sign in (1, -1):
                    inside(sign, lambda: climb(z, sub, sign, shard.at[rows(x, sub), :]).start())
                move("y", z, y, x, sub, shard.at[rows(x, sub), :]).start()
            for side in range(2):
                for sub in range(2):
                    move("core", z, y, side, sub, shard.at[rows(side, sub), :]).start()

    def at_distance(distance, act):
        for sign in (1, -1):
            plane = z - sign * distance

            @pl.when(held(plane))
            def _():
                act(plane, sign)

    def from_z(plane, sign):
        for sub in range(2):
            climb(plane, sub, sign).wait_recv()
            inside(sign, lambda: climb(plane, sub, sign).start())
            for axis in ("x", "y", "core"):
                move(axis, plane, y, x, sub).start()

    def take(axis, plane, row, side, sub, onward=None):
        move(axis, plane, row, side, sub).wait_recv()
        if onward is not None:
            move(onward, plane, row, side, sub).start()
        move("core", plane, row, side, sub).start()

    def first_square(plane, sign):
        take("x", plane, y, 1 - x, 0, "y")
        take("y", plane, 1 - y, x, 1, "x")
        take("y", plane, 1 - y, x, 0)
        take("x", plane, y, 1 - x, 1)

    def second_square(plane, sign):
        take("y", plane, 1 - y, 1 - x, 0)
        take("x", plane, 1 - y, 1 - x, 1)

    def own_first():
        @pl.when(held(z))
        def _():
            for sub in range(2):
                take("y", z, 1 - y, x, sub, "x")

    def own_last():
        @pl.when(held(z))
        def _():
            for sub in range(2):
                take("x", z, 1 - y, 1 - x, sub)

    def stage(distance, act):
        return lambda: at_distance(distance, act)

    steps = [
        stage(1, from_z), own_first, stage(2, from_z), stage(1, first_square), stage(3, from_z), stage(2, first_square),
        own_last, stage(1, second_square), stage(3, first_square), stage(2, second_square), stage(3, second_square),
    ]

    def sent(plane, sign):
        for sub in range(2):
            inside(sign, lambda: climb(plane, sub, sign).wait_send())
            move("x", plane, y, x, sub).wait_send()
            move("y", plane, y, x, sub).wait_send()
        move("y", plane, y, 1 - x, 0).wait_send()
        move("x", plane, 1 - y, x, 1).wait_send()

    def finish():
        for distance in (1, 2, 3):
            at_distance(distance, sent)

        @pl.when(held(z))
        def _():
            pltpu.make_async_copy(shard, out.at[z - bottom, y, core], local_sem).wait()
            for sub in range(2):
                for sign in (1, -1):
                    inside(sign, lambda: climb(z, sub, sign).wait_send())
                move("y", z, y, x, sub).wait_send()
                move("x", z, 1 - y, x, sub).wait_send()

        def core_sent(index, carry):
            plane, row, side, sub = bottom + index // 8, lax.rem(index // 4, 2), lax.rem(index // 2, 2), lax.rem(index, 2)
            move("core", plane, row, side, sub).wait_send()
            return carry

        lax.fori_loop(0, 8 * (top - bottom), core_sent, 0)
        column = out.at[:, :, 1 - core]
        pltpu.make_async_copy(column, column, core_got).wait()

    return begin, steps, finish


def gather(low, spans, *smalls):
    results = pl.pallas_call(
        functools.partial(gather_kernel, spans),
        out_shape=[spread_shape(low, span) for span in spans] + ARRANGED,
        in_specs=[VMEM] * 4,
        out_specs=[pl.BlockSpec(memory_space=pl.ANY)] * len(spans) + [VMEM] * len(ARRANGED),
        scratch_shapes=[one for span in spans for one in spread_semaphores(span)],
        compiler_params=pltpu.CompilerParams(collective_id=4, has_side_effects=True),
        name="gather",
    )(low, *smalls)
    return [flat_rows(one) for one in results[: len(spans)]], results[len(spans) :]


CHUNK = 32
RING = 8
MATES = ("low_in", "low_comb", "low_up", "low_act", "low_grads", "low_branch", "low_hidden", "low_down", "gain_one", "shift_one", "gain_two", "shift_two", "taps")


def change(grad, first_old, second_old):
    new_first = ADAM_ONE * first_old + (1.0 - ADAM_ONE) * grad
    new_second = ADAM_TWO * second_old + (1.0 - ADAM_TWO) * grad * grad
    return new_first * (1.0 / (1.0 - ADAM_ONE**STEP_COUNT)) / (jnp.sqrt(new_second * (1.0 / (1.0 - ADAM_TWO**STEP_COUNT))) + ADAM_EPSILON)


def settle_kernel(block_rows, *refs):
    count = len(MATES)
    mates = [dict(zip(MATES, refs[level * count : (level + 1) * count])) for level in range(LAYERS)]
    (
        weights, first, second, small_first, small_second, grad_out, mean_out, small_out,
        turned, right, staged, own, got_core, got_y, got_z, inner, step_own, step_got, small, small_got, small_own, small_step, small_step_got,
        core_send, core_got, y_send, y_got, z_send, z_got, inner_sem, rep_send, rep_got, small_send, small_sem, back_send, back_sem, small_rep,
    ) = refs[LAYERS * count :]
    me = lax.axis_index("dp")
    other_rep = 1 - lax.axis_index("rep")
    core, y, z = lax.rem(me, 2), lax.rem(me // 2, 2), me // 4
    devices = 16
    per_layer = block_rows // CHUNK
    chunks = LAYERS * per_layer

    barrier = pltpu.get_barrier_semaphore()

    def signal(step, carry):
        pl.semaphore_signal(barrier, inc=1, device_id={"dp": lax.rem(me + step, devices)}, device_id_type=MESH)
        return carry

    lax.fori_loop(1, devices, signal, 0)
    pl.semaphore_signal(barrier, inc=1, device_id={"rep": other_rep}, device_id_type=MESH)

    def to_dp(source, target, send, receive, peer):
        return pltpu.make_async_remote_copy(source, target, send, receive, device_id={"dp": peer}, device_id_type=MESH)

    def to_rep(source, target, send, receive):
        return pltpu.make_async_remote_copy(source, target, send, receive, device_id={"rep": other_rep}, device_id_type=MESH)

    def spot(slot):
        return lax.rem(slot, RING)

    features = D * 2 + FF * 2
    for order, level in enumerate(reversed(range(LAYERS))):
        mate = mates[level]
        at = order * features
        for name in MATES[:4]:
            for part in range(mate[name].shape[1] // LANES):
                turned[at : at + LANES, :] = mate[name][:, part * LANES : (part + 1) * LANES].T
                at += LANES
        for part in range(3):
            right[order * 6 + part] = mate["low_grads"][part]
        for part, name in enumerate(MATES[5:8]):
            right[order * 6 + 3 + part] = mate[name][...]

    def put(level, line, row):
        index = level * LINES + line
        small[index // 2, index % 2 : index % 2 + 1, :] = row

    def column_sum(array):
        return jnp.sum(array.astype(F32), axis=0, keepdims=True)

    for level in range(LAYERS):
        mate = mates[level]
        put(level, 0, column_sum(mate["low_grads"][0]))
        put(level, 1, column_sum(mate["low_grads"][2]))
        put(level, 2, column_sum(mate["low_branch"][...]))
        put(level, 3, column_sum(mate["low_down"][...]))
        for line, name in enumerate(MATES[8:12]):
            put(level, 4 + line, column_sum(mate[name][...]))
        for part in range(FF // D):
            put(level, 8 + part, column_sum(mate["low_up"][:, part * D : (part + 1) * D]))
        line = jnp.zeros((1, D), F32)
        for head in range(HEADS):
            taps = jnp.concatenate([mate["taps"][head // 2][head % 2 : head % 2 + 1], jnp.zeros((1, D - 2 * LANES), F32)], axis=1)
            taps = jnp.where(iota((1, D), 1) < TAPS, taps, 0.0)
            line = line + (pltpu.roll(taps, TAPS * head, 1) if head else taps)
        put(level, 12, line)
    for index in range(LAYERS * LINES, 2 * devices):
        small[index // 2, index % 2 : index % 2 + 1, :] = jnp.zeros((1, D), F32)

    pl.semaphore_wait(barrier, devices)

    def small_copy(step):
        peer = lax.rem(me + step, devices)
        return to_dp(small.at[peer], small_got.at[me], small_send.at[peer], small_sem.at[me], peer)

    def small_begin(step, carry):
        small_copy(step).start()
        return carry

    lax.fori_loop(1, devices, small_begin, 0)

    def core_copy(chunk):
        return to_dp(staged.at[lax.rem(chunk, 2)], got_core.at[spot(chunk)], core_send.at[lax.rem(chunk, 2)], core_got.at[spot(chunk)], me + 1 - 2 * core)

    def y_copy(chunk):
        return to_dp(own.at[spot(chunk), :, 1 - y], got_y.at[spot(chunk)], y_send.at[spot(chunk)], y_got.at[spot(chunk)], me + 2 - 4 * y)

    def z_copy(chunk, hop):
        there = lax.rem(z + hop, 4)
        slot = spot(chunk)
        return to_dp(own.at[slot, there, y], got_z.at[slot, hop - 1], z_send.at[slot, hop - 1], z_got.at[slot, hop - 1], there * 4 + lax.rem(me, 4))

    def place(chunk):
        return LAYERS - 1 - chunk // per_layer, pl.ds(pl.multiple_of(lax.rem(chunk, per_layer) * CHUNK, CHUNK), CHUNK)

    def inner_copies(chunk):
        level, rows = place(chunk)
        slot = lax.rem(chunk, 4)
        return [
            pltpu.make_async_copy(array.at[level, rows, :], inner.at[slot, index], inner_sem.at[slot, index])
            for index, array in enumerate((weights, first, second))
        ]

    def rep_copy(chunk):
        return to_rep(step_own.at[spot(chunk)], step_got.at[spot(chunk)], rep_send.at[spot(chunk)], rep_got.at[spot(chunk)])

    def product(chunk, there, row, side):
        order = chunk // per_layer
        block = (there * 2 + row) * 2 + side
        piece = block * per_layer + lax.rem(chunk, per_layer)
        narrow = D // CHUNK
        line = jnp.where(piece < 3 * narrow, lax.rem(piece, narrow), piece - 2 * narrow)
        group = jnp.where(piece < 4 * narrow, piece // narrow, jnp.where(piece < 4 * narrow + FF // CHUNK, 4, 5))
        rows = pl.ds(pl.multiple_of(order * features + line * CHUNK, 16), CHUNK)
        return mm(turned[rows, :], right[order * 6 + group]).astype(BF16)

    def stage_product(chunk):
        for there in range(4):
            for row in range(2):
                staged[lax.rem(chunk, 2), there, row] = product(chunk, there, row, 1 - core)
        core_copy(chunk).start()
        for there in range(4):
            for row in range(2):
                own[spot(chunk), there, row] = product(chunk, there, row, core)

    def stage_core(chunk):
        core_copy(chunk).wait()
        slot = spot(chunk)
        for there in range(4):
            for side in range(2):
                own[slot, there, side] = own[slot, there, side] + got_core[slot, there, side]
        y_copy(chunk).start()

    def stage_y(chunk):
        y_copy(chunk).wait_recv()
        slot = spot(chunk)
        for there in range(4):
            own[slot, there, y] = own[slot, there, y] + got_y[slot, there]
        for hop in range(1, 4):
            z_copy(chunk, hop).start()
        for copy in inner_copies(chunk):
            copy.start()

    def stage_z(chunk):
        y_copy(chunk).wait_send()
        for hop in range(1, 4):
            z_copy(chunk, hop).wait_recv()
        for copy in inner_copies(chunk):
            copy.wait()
        total = own[spot(chunk), z, y].astype(F32)
        for hop in range(3):
            total = total + got_z[spot(chunk), hop].astype(F32)
        level, rows = place(chunk)
        grad_out[level, rows, :] = total
        slot = lax.rem(chunk, 4)
        step = change(total, inner[slot, 1], inner[slot, 2]) + WEIGHT_DECAY * inner[slot, 0]
        step_own[spot(chunk)] = (LR_INNER * step).astype(BF16)
        rep_copy(chunk).start()

    def stage_rep(chunk):
        for hop in range(1, 4):
            z_copy(chunk, hop).wait_send()
        rep_copy(chunk).wait()
        level, rows = place(chunk)
        mean_out[level, rows, :] = 0.5 * (step_own[spot(chunk)].astype(F32) + step_got[spot(chunk)].astype(F32))

    def small_rep_copy():
        return to_rep(small_step, small_step_got, small_rep.at[0], small_rep.at[1])

    def small_back(step):
        peer = lax.rem(me + step, devices)
        return to_dp(small_own, small_out.at[me], back_send.at[peer], back_sem.at[me], peer)

    def small_sum():
        def add(step, total):
            peer = lax.rem(me + step, devices)
            pltpu.make_async_copy(small_got.at[peer], small_got.at[peer], small_sem.at[peer]).wait()
            return total + small_got[peer]

        total = lax.fori_loop(1, devices, add, small[me])
        small_own[0] = total
        small_step[...] = (LR_SMALL * change(total, small_first[me], small_second[me])).astype(BF16)
        small_rep_copy().start()

    def small_spread():
        small_rep_copy().wait_recv()
        small_own[1] = 0.5 * (small_step[...].astype(F32) + small_step_got[...].astype(F32))
        small_out[me] = small_own[...]

        def send(step, carry):
            small_back(step).start()
            return carry

        lax.fori_loop(1, devices, send, 0)

    def turn(now, carry):
        for lag, stage in ((0, stage_product), (1, stage_core), (3, stage_y), (5, stage_z), (7, stage_rep)):

            @pl.when((now >= lag) & (now < chunks + lag))
            def _():
                stage(now - lag)

        pl.when(now == 4)(small_sum)
        pl.when(now == 7)(small_spread)
        return carry

    lax.fori_loop(0, chunks + 7, turn, 0)

    def small_drain(step, carry):
        peer = lax.rem(me + step, devices)
        small_copy(step).wait_send()
        small_back(step).wait_send()
        pltpu.make_async_copy(small_own, small_out.at[peer], back_sem.at[peer]).wait()
        return carry

    lax.fori_loop(1, devices, small_drain, 0)
    small_rep_copy().wait_send()


def settle(mates, weights, first, second, small_first, small_second):
    block_rows = weights.shape[1]
    anywhere = pl.BlockSpec(memory_space=pl.ANY)
    devices = 16
    piece = (CHUNK, D)
    tokens = mates[0]["low_in"].shape[0]
    return pl.pallas_call(
        functools.partial(settle_kernel, block_rows),
        out_shape=[
            jax.ShapeDtypeStruct(weights.shape, F32),
            jax.ShapeDtypeStruct(weights.shape, F32),
            jax.ShapeDtypeStruct((devices, 2, 2, D), F32),
        ],
        in_specs=[VMEM] * (LAYERS * len(MATES)) + [anywhere] * 3 + [VMEM] * 2,
        out_specs=[VMEM] * 3,
        scratch_shapes=[
            pltpu.VMEM((LAYERS * 2 * (D + FF), tokens), BF16),
            pltpu.VMEM((LAYERS * 6, tokens, D), BF16),
            pltpu.VMEM((2, 4, 2) + piece, BF16),
            pltpu.VMEM((RING, 4, 2) + piece, BF16),
            pltpu.VMEM((RING, 4, 2) + piece, BF16),
            pltpu.VMEM((RING, 4) + piece, BF16),
            pltpu.VMEM((RING, 3) + piece, BF16),
            pltpu.VMEM((4, 3) + piece, F32),
            pltpu.VMEM((RING,) + piece, BF16),
            pltpu.VMEM((RING,) + piece, BF16),
            pltpu.VMEM((devices, 2, D), F32),
            pltpu.VMEM((devices, 2, D), F32),
            pltpu.VMEM((2, 2, D), F32),
            pltpu.VMEM((2, D), BF16),
            pltpu.VMEM((2, D), BF16),
            DMA((2,)),
            DMA((RING,)),
            DMA((RING,)),
            DMA((RING,)),
            DMA((RING, 3)),
            DMA((RING, 3)),
            DMA((4, 3)),
            DMA((RING,)),
            DMA((RING,)),
            DMA((devices,)),
            DMA((devices,)),
            DMA((devices,)),
            DMA((devices,)),
            DMA((2,)),
        ],
        compiler_params=pltpu.CompilerParams(collective_id=3, has_side_effects=True, vmem_limit_bytes=63 << 20),
        name="settle",
    )(*[mate[name] for mate in mates for name in MATES], weights, first, second, small_first, small_second)


def finish_kernel(both, params, outer, first, second, first_new, second_new, outer_new, params_new, grad, mean):
    for level in range(LAYERS):
        for line in range(LINES):
            index = level * LINES + line
            spot = slice(index % 2, index % 2 + 1)
            for which, target in ((0, grad), (1, mean)):
                target[level : level + 1, line * D : (line + 1) * D] = both[index // 2, which, spot, :]
    first_new[...], second_new[...] = moments(first[...], second[...], grad[:, :SMALL])
    momentum = MOMENTUM * outer[...] + mean[:, :SMALL]
    outer_new[...] = momentum
    params_new[...] = params[...] - LR_OUTER * (mean[:, :SMALL] + MOMENTUM * momentum)


def finish(both, params, outer, first, second):
    wide = pltpu.VMEM((LAYERS, LINES * D), F32)
    return pl.pallas_call(
        finish_kernel,
        out_shape=[jax.ShapeDtypeStruct(params.shape, F32)] * 4,
        in_specs=[VMEM] * 5,
        out_specs=[VMEM] * 4,
        scratch_shapes=[wide, wide],
        name="finish",
    )(both, params, outer, first, second)


def dense(a, b, dims=NN):
    return mm(a, b, dims)


def standard(values):
    centred = values - jnp.mean(values, axis=-1, keepdims=True)
    scale = lax.rsqrt(jnp.mean(centred * centred, axis=-1, keepdims=True) + 1e-05)
    return centred * scale, scale


def layer_norm(values, gain, shift):
    return standard(values)[0] * gain + shift


def layer_norm_back(values, gain, grad):
    unit_values, scale = standard(values)
    inner = grad * gain
    along = jnp.mean(inner * unit_values, axis=-1, keepdims=True)
    result = scale * (inner - jnp.mean(inner, axis=-1, keepdims=True) - unit_values * along)
    return result, eighths(grad * unit_values), eighths(grad)


def eighths(rows):
    return jnp.sum(rows.reshape(-1, 8, D), axis=0)


def split_rows(rest):
    return rest[:D], rest[D : D + FF], rest[D + FF :]


def forward_layer(count, inputs, proj, rest, small, edges, ident, low=None, spans=()):
    piece = inputs.shape[0] // MICRO
    lines, bias_up = small
    proj = proj.reshape(3, D, D)
    low_in = inputs.astype(BF16)
    query = (dense(low_in, proj[0]) + lines[0:1]).astype(BF16)
    key = dense(low_in, proj[1]).astype(BF16)
    value = (dense(low_in, proj[2]) + lines[1:2]).astype(BF16)
    qkv = jnp.stack([query, key, value])
    low_comb, kept, fetched = attention_forward(count, qkv.reshape(3, MICRO, piece, D), edges, lines, ident, low, spans)
    rest = fetched[0] if fetched else rest
    out_weight, up_weight, down_weight = split_rows(rest)
    low_comb = low_comb.reshape(MICRO * piece, D)
    resid_one = inputs + (dense(low_comb, out_weight) + lines[2:3])
    hidden_one = layer_norm(resid_one, lines[4:5], lines[5:6])
    low_hidden = hidden_one.astype(BF16)
    upward = dense(low_hidden, up_weight, NT) + bias_up
    low_act = jax.nn.gelu(upward).astype(BF16)
    resid_two = hidden_one + (dense(low_act, down_weight) + lines[3:4])
    output = layer_norm(resid_two, lines[6:7], lines[7:8])
    return output, (proj, rest, low_in, kept, low_comb, resid_one, low_hidden, upward, low_act, resid_two), fetched[1:]


def backward_layer(count, grad_output, small, edges, state, ident):
    proj, rest, low_in, kept, low_comb, resid_one, low_hidden, upward, low_act, resid_two = state
    total = low_in.shape[0]
    piece = total // MICRO
    lines, _ = small
    out_weight, up_weight, down_weight = split_rows(rest)
    grad_two, grad_gain_two, grad_shift_two = layer_norm_back(resid_two, lines[6:7], grad_output)
    low_down = grad_two.astype(BF16)
    grad_act = dense(low_down, down_weight, NT)
    _, pull_gelu = jax.vjp(jax.nn.gelu, upward)
    low_up = pull_gelu(grad_act)[0].astype(BF16)
    grad_hidden = grad_two + dense(low_up, up_weight)
    grad_one, grad_gain_one, grad_shift_one = layer_norm_back(resid_one, lines[4:5], grad_hidden)
    low_branch = grad_one.astype(BF16)
    grad_comb = dense(low_branch, out_weight, NT).astype(BF16)
    low_grads, grad_taps = attention_backward(count, grad_comb.reshape(1, MICRO, piece, D), edges, lines, kept, ident)
    low_grads = low_grads.reshape(3, total, D)
    grad_in = grad_one + sum(dense(low_grads[part], proj[part], NT) for part in range(3))
    vectors = (grad_gain_one, grad_shift_one, grad_gain_two, grad_shift_two)
    values = (low_in, low_comb, low_up, low_act, low_grads, low_branch, low_hidden, low_down, *vectors, grad_taps)
    return grad_in, dict(zip(MATES, values))


def plain_grads(mate):
    parts = [dense(mate["low_in"], mate["low_grads"][part], TN) for part in range(3)]
    parts = parts + [dense(mate[left], mate[right], TN) for left, right in (("low_comb", "low_branch"), ("low_up", "low_hidden"), ("low_act", "low_down"))]
    sums = [mate["low_grads"][0], mate["low_grads"][2], mate["low_branch"], mate["low_down"]]
    sums = [jnp.sum(one.astype(F32), axis=0) for one in sums]
    sums = sums + [jnp.sum(mate[name], axis=0) for name in MATES[8:12]]
    sums = sums + [jnp.sum(mate["low_up"].astype(F32), axis=0), mate["taps"][:, :, :TAPS].reshape(-1)]
    return jnp.concatenate(parts, axis=0).astype(BF16), jnp.concatenate(sums)


def moments(first, second, grad):
    return ADAM_ONE * first + (1.0 - ADAM_ONE) * grad, ADAM_TWO * second + (1.0 - ADAM_TWO) * grad * grad


def adam(weights, first, second, grad, rate, decay):
    correct_one = 1.0 - ADAM_ONE**STEP_COUNT
    correct_two = 1.0 - ADAM_TWO**STEP_COUNT
    new_first, new_second = moments(first, second, grad)
    step = new_first / correct_one / (jnp.sqrt(new_second / correct_two) + ADAM_EPSILON)
    return new_first, new_second, rate * (step + decay * weights)


def shards(
    hidden,
    bounds,
    cotangent,
    weights,
    small_params,
    first_big,
    second_big,
    first_small,
    second_small,
    outer_big,
    outer_small,
):
    count = lax.axis_size("dp")
    piece = hidden.shape[3]
    total = MICRO * piece
    low_weights = weights.astype(BF16)
    limits = bounds[0, :, 0, :]
    edges = jnp.pad(limits.astype(F32), ((0, 0), (0, LANES - limits.shape[1])))
    positions = lax.axis_index("dp") * piece + lax.broadcasted_iota(jnp.int32, (MICRO, piece, 1), 1)
    valid = positions < limits[:, -1].reshape(MICRO, 1, 1)
    activation = hidden[0, :, 0].reshape(total, D).astype(F32)
    states = [None] * LAYERS
    if count == 16:
        (proj,), prepared = gather(low_weights, ((0, 0, 1),), small_params, first_small[0], second_small[0])
    else:
        prepared = arranged(small_params, first_small[0], second_small[0])
    smalls = [(prepared[level], prepared[LAYERS + level]) for level in range(LAYERS)]
    for level in range(LAYERS):
        if count == 16:
            spans = ((level, 1, PLANES),) + (((level + 1, 0, 1),) if level + 1 < LAYERS else ())
            activation, states[level], more = forward_layer(count, activation, proj, None, smalls[level], edges, 1 + 4 * level, low_weights, spans)
            proj = more[0] if more else None
        else:
            rows = lax.all_gather(low_weights[level], "dp", axis=0, tiled=True)
            activation, states[level], _ = forward_layer(count, activation, rows[: 3 * D], rows[3 * D :], smalls[level], edges, 1)
    gradient = jnp.where(valid, cotangent[0, :, 0].astype(F32), 0.0).reshape(total, D)
    mates = [None] * LAYERS
    for level in reversed(range(LAYERS)):
        gradient, mates[level] = backward_layer(count, gradient, smalls[level], edges, states[level], 2)
    if count == 16:
        grad_big, mean_big, small_both = settle(mates, weights, first_big[0], second_big[0], *prepared[2 * LAYERS :])
        new_smalls = finish(small_both, small_params, outer_small, first_small[0], second_small[0])
    else:
        rows, sums = zip(*[plain_grads(mate) for mate in mates])
        grad_big = jnp.stack([lax.psum_scatter(one, "dp", scatter_dimension=0, tiled=True).astype(F32) for one in rows])
        grad_small = lax.psum(jnp.stack(sums), "dp")
        reps = lax.axis_size("rep")
        delta_big = adam(weights, first_big[0], second_big[0], grad_big, LR_INNER, WEIGHT_DECAY)[2]
        delta_small = adam(small_params, first_small[0], second_small[0], grad_small, LR_SMALL, 0.0)[2]
        mean_big = lax.psum(delta_big.astype(BF16), "rep").astype(F32) / reps
        mean_small = lax.psum(delta_small.astype(BF16), "rep").astype(F32) / reps
        momentum = MOMENTUM * outer_small + mean_small
        new_smalls = (*moments(first_small[0], second_small[0], grad_small), momentum, small_params - LR_OUTER * (mean_small + MOMENTUM * momentum))
    new_first, new_second = moments(first_big[0], second_big[0], grad_big)
    new_first_small, new_second_small, outer_small_new, small_new = new_smalls
    outer_big_new = MOMENTUM * outer_big + mean_big
    weights_new = weights - LR_OUTER * (mean_big + MOMENTUM * outer_big_new)
    shape = (1, MICRO, 1, piece, D)
    return (
        activation.reshape(shape),
        gradient.reshape(shape),
        new_first[None],
        new_second[None],
        new_first_small[None],
        new_second_small[None],
        outer_big_new,
        outer_small_new,
        weights_new,
        small_new,
        weights_new.astype(BF16),
    )


def solution(mesh):
    placed = (
        P("rep", None, None, "dp", None),
        P("rep", None, None, None),
        P("rep", None, None, "dp", None),
        P(None, "dp", None),
        P(),
        P("rep", None, "dp", None),
        P("rep", None, "dp", None),
        P("rep", None, None),
        P("rep", None, None),
        P(None, "dp", None),
        P(),
    )
    return jax.shard_map(
        shards,
        mesh=mesh,
        in_specs=placed,
        out_specs=(
            P("rep", None, None, "dp", None),
            P("rep", None, None, "dp", None),
            P("rep", None, "dp", None),
            P("rep", None, "dp", None),
            P("rep", None, None),
            P("rep", None, None),
            P(None, "dp", None),
            P(),
            P(None, "dp", None),
            P(),
            P(None, "dp", None),
        ),
        check_vma=False,
    )
```

```python
import functools

import jax
import jax.numpy as jnp
from jax import lax
from jax.experimental import pallas as pl
from jax.experimental.pallas import tpu as pltpu
from jax.sharding import PartitionSpec as P

D = 768
HEADS = 12
FF = 3072
TAPS = 33
NS_ITERS = 6
LAYERS = 2
MICRO = 2
STEP_COUNT = 5


ADAM_ONE = 0.9
ADAM_TWO = 0.95
ADAM_EPSILON = 1e-08
WEIGHT_DECAY = 0.1
LR_INNER = 0.04
LR_SMALL = 0.2
LR_OUTER = 0.7
MOMENTUM = 0.9

HEAD_DIM = 64
MARKS = 64
HALF = TAPS // 2
PAIRS = HEADS // 2
LINES = 13
TAP_LINE = 12
SMALL = 8 * D + FF + HEADS * TAPS
LANES = 128
SCALE = HEAD_DIM**-0.5
NEG = -1e30
MESH = pl.DeviceIdType.MESH
F32 = jnp.float32
BF16 = jnp.bfloat16
NN = (((1,), (0,)), ((), ()))
NT = (((1,), (1,)), ((), ()))
TN = (((0,), (0,)), ((), ()))


def mm(a, b, dims=NN):
    return lax.dot_general(a, b, dims, preferred_element_type=F32)


def halves(a):
    high = a.astype(BF16)
    return high, (a - high.astype(F32)).astype(BF16)


def mm_left(a, b, dims=NN):
    high, rest = halves(a)
    return mm(high, b, dims) + mm(rest, b, dims)


def mm_both(a, b, dims=NN):
    ah, al = halves(a)
    bh, bl = halves(b)
    return mm(ah, bh, dims) + (mm(ah, bl, dims) + mm(al, bh, dims))


def exact(a, b, dims=NN):
    return mm_both(a, b, dims)


def iota(shape, dim):
    return lax.broadcasted_iota(jnp.int32, shape, dim)


def diagonal_blocks():
    return (iota((LANES, LANES), 0) < MARKS) == (iota((LANES, LANES), 1) < HEAD_DIM)


def unit():
    return (iota((LANES, LANES), 0) == iota((LANES, LANES), 1)).astype(F32)


def per_head(marks):
    first = iota(marks.shape, 1) < HEAD_DIM
    return jnp.concatenate([jnp.where(first, marks, 0.0), jnp.where(first, 0.0, marks)], axis=0)


def head_sums(a):
    rows, cols = a.shape
    split = a.reshape(2, rows // 2, cols)
    return jnp.broadcast_to(jnp.sum(split, axis=1, keepdims=True), split.shape).reshape(rows, cols)


def head_tops(a):
    rows, cols = a.shape
    split = a.reshape(2, rows // 2, cols)
    return jnp.broadcast_to(jnp.max(split, axis=1, keepdims=True), split.shape).reshape(rows, cols)


def head_taps(lines, pair):
    row = jnp.broadcast_to(lines[TAP_LINE : TAP_LINE + 1, :], (8, D))
    rows = []
    for side in range(2):
        turned = pltpu.roll(row, lax.rem(D - TAPS * (2 * pair + side), D), 1)[0:1, : 2 * LANES]
        rows.append(jnp.where(iota((1, 2 * LANES), 1) < TAPS, turned, 0.0))
    return rows


def band(taps_row):
    wide = jnp.broadcast_to(taps_row, (LANES, 2 * LANES))
    return pltpu.roll(wide, 0, 1, stride=1, stride_axis=0)


def band_back(taps_row):
    wide = jnp.broadcast_to(taps_row, (2 * LANES, 2 * LANES))
    return pltpu.roll(wide, 2 * LANES - 2 * HALF, 1, stride=1, stride_axis=0)[:, :LANES].T


def mark_columns(edges):
    low = jnp.broadcast_to(edges, (LANES, LANES)).T[:MARKS, :1]
    high = jnp.broadcast_to(pltpu.roll(edges, LANES - 1, 1), (LANES, LANES)).T[:MARKS, :1]
    return low.astype(jnp.int32), high.astype(jnp.int32)


def mark_rows(edges):
    low, high = edges[:, :MARKS], pltpu.roll(edges, LANES - 1, 1)[:, :MARKS]
    return low.astype(jnp.int32), high.astype(jnp.int32)


def convolve(padded, bands, length, store):
    first = iota((LANES, LANES), 1) < HEAD_DIM
    pairs = [halves(one) for one in bands]

    def block(at, carry):
        start = pl.multiple_of(at * LANES, LANES)
        window = padded[pl.ds(start, 2 * LANES), :]
        out = [mm(high, window) + mm(rest, window) for high, rest in pairs]
        store(start, jnp.where(first, out[0], out[1]))
        return carry

    lax.fori_loop(0, length // LANES, block, 0)


def put_rows(ref, at, start, rows):
    half = ref.shape[2]
    ref[at, start // half, pl.ds(pl.multiple_of(lax.rem(start, half), LANES), LANES), :] = rows


def whole(ref, at):
    return ref[at].reshape(-1, LANES)


def attend(slab, edges, taps, keep, padded, blended, result):
    length = slab.shape[1] * slab.shape[2]

    def begin():
        low_marks, high_marks = mark_columns(edges())
        at = iota((MARKS, length), 1)
        member = ((low_marks <= at) & (at < high_marks)).astype(F32).astype(BF16)
        counts = (high_marks - low_marks).astype(F32)
        q_marks = per_head(mm(member, whole(slab, 0)) / counts)
        k_marks = per_head(mm(member, whole(slab, 1)) / counts)
        scores = jnp.where(diagonal_blocks(), SCALE * exact(q_marks, k_marks, NT), NEG)
        weights = jnp.exp(scores - jnp.max(scores, axis=1, keepdims=True))
        kernel = weights / jnp.sum(weights, axis=1, keepdims=True)
        total = head_sums(jnp.broadcast_to(jnp.sum(kernel * kernel, axis=1, keepdims=True), kernel.shape))
        keep["q_marks"][...] = q_marks
        keep["k_marks"][...] = k_marks
        keep["kernel"][...] = kernel
        keep["total"][...] = total
        keep["inverse"][0] = kernel.T / total

    def sweep(at):
        def run():
            eye, inverse = unit(), keep["inverse"][at]
            product = exact(keep["kernel"][...], inverse)
            one = 7.0 * eye - product
            two = 15.0 * eye - exact(product, one)
            three = 13.0 * eye - exact(product, two)
            keep["product"][at] = product
            keep["two"][at] = two
            keep["three"][at] = three
            keep["inverse"][at + 1] = 0.25 * exact(inverse, three)

        return run

    def over_keys():
        valid = iota((1, length), 1) < mark_columns(edges())[1][MARKS - 1 :]
        key_scores = jnp.where(valid, SCALE * mm_left(keep["q_marks"][...], whole(slab, 1), NT), NEG)
        key_exp = jnp.where(valid, jnp.exp(key_scores - jnp.max(key_scores, axis=1, keepdims=True)), 0.0)
        key_weights = key_exp / jnp.sum(key_exp, axis=1, keepdims=True)
        keep["key_weights"][...] = key_weights
        keep["summary"][...] = jnp.where(diagonal_blocks(), mm_left(key_weights, whole(slab, 2)), 0.0)

    def over_tokens():
        token_scores = SCALE * mm_left(keep["k_marks"][...], whole(slab, 0), NT)
        token_exp = jnp.exp(token_scores - head_tops(token_scores))
        keep["token_weights"][...] = token_exp / head_sums(token_exp)

    def close():
        mixed = exact(keep["inverse"][NS_ITERS], keep["summary"][...])
        keep["mixed"][...] = mixed
        blended[...] = mm_both(keep["token_weights"][...], mixed, TN)
        values = whole(slab, 2)
        valid_column = iota((length, 1), 0) < mark_columns(edges())[1][MARKS - 1 :]
        padded[0:HALF, :] = jnp.zeros((HALF, LANES), BF16)
        padded[HALF : HALF + length, :] = jnp.where(valid_column, values, jnp.zeros_like(values))
        padded[HALF + length :, :] = jnp.zeros((LANES - HALF, LANES), BF16)

        def store(start, block):
            put_rows(result, 0, start, (blended[pl.ds(start, LANES), :] + block).astype(BF16))

        convolve(padded, [band(one) for one in taps()], length, store)

    return [begin] + [sweep(at) for at in range(NS_ITERS)] + [over_keys, over_tokens, close]


def attend_back(grads, queries, keys, values, edges, taps, keep, padded, padded_grads, blended, result, grad_taps):
    length = grads.shape[0]
    low_marks, high_marks = mark_columns(edges)
    low_row, high_row = mark_rows(edges)
    at = iota((length, MARKS), 0)
    member = ((low_row <= at) & (at < high_row)).astype(F32).astype(BF16)
    counts = (high_marks - low_marks).astype(F32)
    blocks, eye = diagonal_blocks(), unit()
    q_marks, k_marks = keep["q_marks"][...], keep["k_marks"][...]
    token_weights, key_weights = keep["token_weights"][...], keep["key_weights"][...]
    summary, mixed = keep["summary"][...], keep["mixed"][...]
    kernel = keep["kernel"][...]
    inverse = keep["inverse"][NS_ITERS]
    grad_mixed = jnp.where(blocks, mm_left(token_weights, grads), 0.0)
    grad_token = token_weights * mm_left(mixed, grads, NT)
    grad_token = SCALE * (grad_token - token_weights * head_sums(grad_token))
    grad_summary = exact(inverse, grad_mixed, TN)
    grad_inverse = exact(grad_mixed, summary, NT)
    grad_kernel = jnp.zeros_like(kernel)
    for sweep in reversed(range(NS_ITERS)):
        before, product = keep["inverse"][sweep], keep["product"][sweep]
        one = 7.0 * eye - product
        two, three = keep["two"][sweep], keep["three"][sweep]
        grad_three = 0.25 * exact(before, grad_inverse, TN)
        grad_two = -exact(product, grad_three, TN)
        grad_one = -exact(product, grad_two, TN)
        grad_product = -(exact(grad_three, two, NT) + exact(grad_two, one, NT) + grad_one)
        grad_kernel = grad_kernel + exact(grad_product, before, NT)
        grad_inverse = 0.25 * exact(grad_inverse, three, NT) + exact(kernel, grad_product, TN)
    total = keep["total"][...]
    turned = grad_inverse.T / total
    weighted = jnp.sum(jnp.where(blocks, turned * kernel, 0.0), axis=1, keepdims=True)
    weighted = head_sums(jnp.broadcast_to(weighted, kernel.shape))
    grad_kernel = grad_kernel + turned - 2.0 * kernel * weighted / total
    grad_scores = SCALE * kernel * (grad_kernel - jnp.sum(kernel * grad_kernel, axis=1, keepdims=True))
    grad_q_marks = exact(grad_scores, k_marks)
    grad_k_marks = exact(grad_scores, q_marks, TN)
    grad_k_marks = grad_k_marks + jnp.where(blocks, mm_left(grad_token, queries), 0.0)
    grad_key = mm_left(grad_summary, values, NT) - jnp.sum(grad_summary * summary, axis=1, keepdims=True)
    grad_key = SCALE * key_weights * grad_key
    grad_q_marks = grad_q_marks + jnp.where(blocks, mm_left(grad_key, keys), 0.0)
    grad_q_marks = (grad_q_marks[:MARKS] + grad_q_marks[MARKS:]) / counts
    grad_k_marks = (grad_k_marks[:MARKS] + grad_k_marks[MARKS:]) / counts
    high, rest = halves(grad_q_marks)
    result[0] = (mm_both(grad_token, k_marks, TN) + mm(member, high) + mm(member, rest)).astype(BF16).reshape(result.shape[1:])
    high, rest = halves(grad_k_marks)
    result[1] = (mm_both(grad_key, q_marks, TN) + mm(member, high) + mm(member, rest)).astype(BF16).reshape(result.shape[1:])
    blended[...] = mm_both(key_weights, grad_summary, TN)
    last = high_marks[MARKS - 1 :]
    valid_column = iota((length, 1), 0) < last
    padded[0:HALF, :] = jnp.zeros((HALF, LANES), BF16)
    padded[HALF : HALF + length, :] = jnp.where(valid_column, values, jnp.zeros_like(values))
    padded[HALF + length :, :] = jnp.zeros((LANES - HALF, LANES), BF16)
    padded_grads[0:HALF, :] = jnp.zeros((HALF, LANES), BF16)
    padded_grads[HALF : HALF + length, :] = grads
    padded_grads[HALF + length :, :] = jnp.zeros((LANES - HALF, LANES), BF16)

    def store(start, block):
        rows = start + iota((LANES, 1), 0)
        total_rows = blended[pl.ds(start, LANES), :] + jnp.where(rows < last, block, 0.0)
        put_rows(result, 2, start, total_rows.astype(BF16))

    convolve(padded_grads, [band_back(one) for one in taps], length, store)
    first = iota((LANES, LANES), 1) < HEAD_DIM

    def block(step, carry):
        start = pl.multiple_of(step * LANES, LANES)
        own = padded_grads[pl.ds(start + HALF, LANES), :]
        window = padded[pl.ds(start, 2 * LANES), :]
        none = jnp.zeros_like(own)
        return (
            carry[0] + mm(jnp.where(first, own, none), window, NT),
            carry[1] + mm(jnp.where(first, none, own), window, NT),
        )

    start_sum = jnp.zeros((LANES, 2 * LANES), F32)
    sums = lax.fori_loop(0, length // LANES, block, (start_sum, start_sum))
    wide = 2 * LANES
    for head in range(2):
        folded = sums[head][0:8]
        for group in range(1, LANES // 8):
            rows = sums[head][8 * group : 8 * group + 8]
            folded = folded + pltpu.roll(rows, wide - 8 * group, 1)
        line = folded[0:1]
        for row in range(1, 8):
            line = line + pltpu.roll(folded[row : row + 1], wide - row, 1)
        grad_taps[head : head + 1, :] = line


KEPT = ("q_marks", "k_marks", "kernel", "total", "inverse", "product", "two", "three", "key_weights", "summary", "mixed", "token_weights")


def kept_shapes(length):
    square = (LANES, LANES)
    shapes = {name: square for name in KEPT}
    shapes["inverse"] = (NS_ITERS + 1,) + square
    for name in ("product", "two", "three"):
        shapes[name] = (NS_ITERS,) + square
    shapes["key_weights"] = shapes["token_weights"] = (LANES, length)
    return shapes


class Layout:
    def __init__(self, count):
        self.count = count
        self.groups = MICRO if count == 16 else 1
        self.members = count // self.groups
        self.tasks = PAIRS * MICRO // self.groups

    def place(self):
        me = lax.axis_index("dp")
        self.me, self.group, self.index = me, me // self.members, lax.rem(me, self.members)
        self.task = (self.index * self.tasks + self.members - 1) // self.members
        self.owns = self.owner(self.task) == self.index
        self.micro = self.micro_of(self.task)
        self.pair = lax.rem(self.task, PAIRS)
        return self

    def owner(self, task):
        return task * self.members // self.tasks

    def micro_of(self, task):
        return self.group if self.groups > 1 else task // PAIRS

    def device(self, index):
        return {"dp": self.group * self.members + index}

    def block(self, array, task):
        lanes = pl.ds(pl.multiple_of(lax.rem(task, PAIRS) * LANES, LANES), LANES)
        return array.at[:, :, :, lanes] if self.groups > 1 else array.at[:, pl.ds(task // PAIRS, 1), :, lanes]

    def rows(self, slab, index, piece):
        return slab.at[:, :, pl.ds(pl.multiple_of(index * piece, piece), piece), :]

    def mate(self):
        return {"dp": lax.rem(self.me + self.members, self.count)}


def greet(at, everyone=False, mate=False):
    barrier = pltpu.get_barrier_semaphore()
    size, index = (at.count, at.me) if everyone else (at.members, at.index)
    if everyone:
        pl.semaphore_signal(barrier, inc=1, device_id={"rep": 1 - lax.axis_index("rep")}, device_id_type=MESH)
    if mate:
        pl.semaphore_signal(barrier, inc=1, device_id=at.mate(), device_id_type=MESH)

    def signal(step, carry):
        other = lax.rem(index + step, size)
        pl.semaphore_signal(barrier, inc=1, device_id={"dp": other} if everyone else at.device(other), device_id_type=MESH)
        return carry

    lax.fori_loop(1, size, signal, 0)
    pl.semaphore_wait(barrier, size - 1 + int(everyone) + int(mate))


def scatter_tasks(at, piece, source, slab, send, receive):
    def one(step, finish):
        task = lax.rem(at.task + step, at.tasks)
        owner = at.owner(task)
        outgoing, landing = at.block(source, task), at.rows(slab, at.index, piece)

        @pl.when(owner != at.index)
        def _():
            copy = pltpu.make_async_remote_copy(
                outgoing, landing, send.at[task], receive.at[at.index], device_id=at.device(owner), device_id_type=MESH
            )
            if finish:
                copy.wait_send()
            else:
                copy.start()

        @pl.when((owner == at.index) & (not finish))
        def _():
            pltpu.make_async_copy(outgoing, landing, receive.at[at.index]).start()

    def run(finish):
        def body(step, carry):
            one(step, finish)
            return carry

        lax.fori_loop(0, at.tasks, body, 0)

    return run


def await_slab(at, piece, slab, receive):
    def body(origin, carry):
        landing = at.rows(slab, origin, piece)
        pltpu.make_async_copy(landing, landing, receive.at[origin]).wait()
        return carry

    lax.fori_loop(0, at.members, body, 0)


def return_rows(at, piece, result, target, send, receive):
    def run(finish):
        def body(step, carry):
            peer = lax.rem(at.index + step, at.members)
            outgoing, landing = at.rows(result, peer, piece), at.block(target, at.task)

            @pl.when(peer != at.index)
            def _():
                copy = pltpu.make_async_remote_copy(
                    outgoing, landing, send.at[peer], receive.at[at.task], device_id=at.device(peer), device_id_type=MESH
                )
                if finish:
                    copy.wait_send()
                else:
                    copy.start()

            @pl.when((peer == at.index) & (not finish))
            def _():
                pltpu.make_async_copy(outgoing, landing, receive.at[at.task]).start()

            return carry

        lax.fori_loop(0, at.members, body, 0)

    return run


def await_rows(at, target, receive):
    def body(task, carry):
        landing = at.block(target, task)
        pltpu.make_async_copy(landing, landing, receive.at[task]).wait()
        return carry

    lax.fori_loop(0, at.tasks, body, 0)


def swap(at, source, target, send, receive):
    return pltpu.make_async_remote_copy(
        source.at[1 - at.group], target.at[at.group], send, receive, device_id=at.mate(), device_id_type=MESH
    )


def forward_kernel(count, piece, spans, qkv, edges, lines, low, mixed_rows, slab, *refs):
    keep = dict(zip(KEPT, refs))
    outs, refs = refs[len(KEPT) : len(KEPT) + len(spans)], refs[len(KEPT) + len(spans) :]
    padded, blended, result, send_one, receive_one, send_two, receive_two = refs[:7]
    begin, steps, finish = spread_all(spans, low, outs, refs[7:])
    at = Layout(count).place()
    greet(at, bool(spans))
    out = scatter_tasks(at, piece, qkv, slab, send_one, receive_one)
    out(False)
    begin()
    back = return_rows(at, piece, result, mixed_rows, send_two, receive_two)
    phases = attend(slab, lambda: edges[pl.ds(at.micro, 1), :], lambda: head_taps(lines, at.pair), keep, padded, blended, result)

    def between(turn):
        if turn < len(steps):
            steps[turn]()

    between(0)
    for turn, phase in enumerate(phases):

        @pl.when(at.owns)
        def _():
            if turn == 0:
                await_slab(at, piece, slab, receive_one)
            phase()
            if turn == len(phases) - 1:
                back(False)

        if turn > 1:
            between(turn - 1)
    for turn in range(len(phases) - 1, len(steps)):
        between(turn)
    finish()
    out(True)
    await_rows(at, mixed_rows, receive_two)

    @pl.when(at.owns)
    def _():
        back(True)


def backward_kernel(count, piece, carries, grads, edges, lines, *refs):
    carried, refs = refs[:carries], refs[carries:]
    slab, refs = refs[0], refs[1:]
    keep = dict(zip(KEPT, refs))
    out_grads, grad_taps, refs = refs[len(KEPT)], refs[len(KEPT) + 1], refs[len(KEPT) + 2 :]
    swapped, refs = refs[:carries], refs[carries:]
    grad_slab, padded, padded_grads, blended, result, send_one, receive_one, send_two, receive_two, send_swap, receive_swap = refs
    at = Layout(count).place()
    greet(at, mate=bool(carries))
    out = scatter_tasks(at, piece, grads, grad_slab, send_one, receive_one)
    out(False)
    swaps = [swap(at, one, two, send_swap, receive_swap) for one, two in zip(carried, swapped)]
    for one, source, target in zip(swaps, carried, swapped):
        one.start()
        target[pl.ds(at.group, 1)] = source[pl.ds(at.group, 1)]
    back = return_rows(at, piece, result, out_grads, send_two, receive_two)
    grad_taps[...] = jnp.zeros(grad_taps.shape, F32)

    @pl.when(at.owns)
    def _():
        await_slab(at, piece, grad_slab, receive_one)
        attend_back(
            whole(grad_slab, 0), whole(slab, 0), whole(slab, 1), whole(slab, 2), edges[pl.ds(at.micro, 1), :], head_taps(lines, at.pair),
            keep, padded, padded_grads, blended, result, grad_taps.at[at.pair],
        )
        back(False)

    out(True)
    await_rows(at, out_grads, receive_two)
    for one in swaps:
        one.wait()

    @pl.when(at.owns)
    def _():
        back(True)


VMEM = pl.BlockSpec(memory_space=pltpu.VMEM)
DMA = pltpu.SemaphoreType.DMA


def attention_forward(count, qkv, edges, lines, ident, low=None, spans=()):
    piece = qkv.shape[2]
    length = piece * count
    shapes = kept_shapes(length)
    low = low if spans else lines
    at = Layout(count)
    halved = (at.groups, length // at.groups, LANES)
    anywhere = pl.BlockSpec(memory_space=pl.ANY)
    results = pl.pallas_call(
        functools.partial(forward_kernel, count, piece, spans),
        out_shape=[
            jax.ShapeDtypeStruct((1, MICRO, piece, D), BF16),
            jax.ShapeDtypeStruct((3,) + halved, BF16),
        ]
        + [jax.ShapeDtypeStruct(shapes[name], F32) for name in KEPT]
        + [spread_shape(low, span) for span in spans],
        in_specs=[VMEM] * 4,
        out_specs=[VMEM] * (2 + len(KEPT)) + [anywhere] * len(spans),
        scratch_shapes=[
            pltpu.VMEM((length + LANES, LANES), BF16),
            pltpu.VMEM((length, LANES), F32),
            pltpu.VMEM((1,) + halved, BF16),
            DMA((at.tasks,)),
            DMA((at.members,)),
            DMA((at.members,)),
            DMA((at.tasks,)),
        ]
        + [one for span in spans for one in spread_semaphores(span)],
        compiler_params=pltpu.CompilerParams(collective_id=ident, has_side_effects=True, vmem_limit_bytes=60 << 20),
        name="attend_forward",
    )(qkv, edges, lines, low)
    return results[0][0], results[1 : 2 + len(KEPT)], [flat_rows(one) for one in results[2 + len(KEPT) :]]


def attention_backward(count, grads, edges, lines, kept, ident, carried=()):
    piece = grads.shape[2]
    length = piece * count
    at = Layout(count)
    halved = (at.groups, length // at.groups, LANES)
    results = pl.pallas_call(
        functools.partial(backward_kernel, count, piece, len(carried)),
        out_shape=[
            jax.ShapeDtypeStruct((3, MICRO, piece, D), BF16),
            jax.ShapeDtypeStruct((PAIRS, 2, 2 * LANES), F32),
        ]
        + [jax.ShapeDtypeStruct(one.shape, one.dtype) for one in carried],
        in_specs=[VMEM] * (4 + len(carried) + len(KEPT)),
        out_specs=[VMEM] * (2 + len(carried)),
        scratch_shapes=[
            pltpu.VMEM((1,) + halved, BF16),
            pltpu.VMEM((length + LANES, LANES), BF16),
            pltpu.VMEM((length + LANES, LANES), BF16),
            pltpu.VMEM((length, LANES), F32),
            pltpu.VMEM((3,) + halved, BF16),
            DMA((at.tasks,)),
            DMA((at.members,)),
            DMA((at.members,)),
            DMA((at.tasks,)),
            DMA,
            DMA,
        ],
        compiler_params=pltpu.CompilerParams(collective_id=ident, has_side_effects=True, vmem_limit_bytes=60 << 20),
        name="attend_backward",
    )(grads, edges, lines, *carried, *kept)
    return results[0], results[1], results[2:]


def arrange(sources, targets):
    params, first, second = sources
    lines, ups, sliced = targets[:LAYERS], targets[LAYERS : 2 * LAYERS], targets[2 * LAYERS :]
    for level in range(LAYERS):
        own = slice(level, level + 1)
        for line in range(TAP_LINE):
            lines[level][line : line + 1, :] = params[own, line * D : (line + 1) * D]
        lines[level][TAP_LINE:, :] = jnp.zeros((16 - TAP_LINE, D), F32)
        lines[level][TAP_LINE : TAP_LINE + 1, : HEADS * TAPS] = params[own, TAP_LINE * D :]
        ups[level][...] = params[own, 8 * D : 8 * D + FF]
    for source, target in zip((first, second), sliced):
        target[LAYERS * LINES // 2 :] = jnp.zeros((16 - LAYERS * LINES // 2, 2, D), F32)
        for level in range(LAYERS):
            own = slice(level, level + 1)
            for line in range(LINES):
                index = level * LINES + line
                spot = slice(index % 2, index % 2 + 1)
                if line < TAP_LINE:
                    target[index // 2, spot, :] = source[own, line * D : (line + 1) * D]
                else:
                    target[index // 2, spot, :] = jnp.zeros((1, D), F32)
                    target[index // 2, spot, : HEADS * TAPS] = source[own, TAP_LINE * D :]


ARRANGED = (
    [jax.ShapeDtypeStruct((16, D), F32)] * LAYERS + [jax.ShapeDtypeStruct((1, FF), F32)] * LAYERS + [jax.ShapeDtypeStruct((16, 2, D), F32)] * 2
)


def arrange_kernel(*refs):
    arrange(refs[:3], refs[3:])


def arranged(*smalls):
    return pl.pallas_call(arrange_kernel, out_shape=ARRANGED, in_specs=[VMEM] * 3, out_specs=[VMEM] * len(ARRANGED), name="arrange")(*smalls)


PLANES = 4
SUBS = 2
EVEN, ODD = range(0, SUBS, 2), range(1, SUBS, 2)


def gather_kernel(spans, low, params, first, second, hidden, cotangent, *refs):
    outs, refs = refs[: len(spans)], refs[len(spans) :]
    targets, refs = refs[: len(ARRANGED)], refs[len(ARRANGED) :]
    swapped, swap_sems, refs = refs[:2], refs[2], refs[3:]
    begin, steps, finish = spread_all(spans, low, outs, refs)
    at = Layout(16).place()
    me, x = lax.axis_index("dp"), lax.axis_index("rep")
    core, y, z = lax.rem(me, 2), lax.rem(me // 2, 2), me // 4
    barrier = pltpu.get_barrier_semaphore()
    for where in ({"rep": 1 - x}, {"dp": me + 2 - 4 * y}, {"dp": me + 1 - 2 * core}, at.mate()):
        pl.semaphore_signal(barrier, inc=1, device_id=where, device_id_type=MESH)
    for sign in (1, -1):

        @pl.when((z + sign >= 0) & (z + sign < PLANES))
        def _():
            pl.semaphore_signal(barrier, inc=1, device_id={"dp": me + 4 * sign}, device_id_type=MESH)

    pl.semaphore_wait(barrier, 5 + jnp.where((z > 0) & (z < PLANES - 1), 1, 0))
    begin()
    swaps = [swap(at, one, two, swap_sems.at[0, which], swap_sems.at[1, which]) for which, (one, two) in enumerate(zip((hidden, cotangent), swapped))]
    for one, source, target in zip(swaps, (hidden, cotangent), swapped):
        one.start()
        target[pl.ds(at.group, 1)] = source[pl.ds(at.group, 1)]
    arrange((params, first, second), targets)
    for step in steps:
        step()
    finish()
    for one in swaps:
        one.wait()


def spread_semaphores(span):
    planes = span[2] - span[1]
    return [DMA, DMA((planes, SUBS, 2)), DMA((planes, SUBS))] + [DMA((planes, 2, 2, SUBS))] * 5 + [DMA]


def spread_shape(low, span):
    return jax.ShapeDtypeStruct((span[2] - span[1], 2, 2) + low.shape[1:], BF16)


def flat_rows(blocks):
    return blocks.reshape(-1, D)


def spread_all(spans, low, outs, semaphores):
    each = len(semaphores) // max(len(spans), 1)
    parts = [
        spread(low.at[level], out, bottom, top, *semaphores[at * each : (at + 1) * each])
        for at, ((level, bottom, top), out) in enumerate(zip(spans, outs))
    ]

    def together(actions):
        def run():
            for action in actions:
                action()

        return run

    steps = [together(actions) for actions in zip(*[part[1] for part in parts])]
    return together([part[0] for part in parts]), steps, together([part[2] for part in parts])


def spread(shard, out, bottom, top, local_sem, z_send, z_got, x_send, x_got, y_send, y_got, core_send, core_got):
    me = lax.axis_index("dp")
    x = lax.axis_index("rep")
    core, y, z = lax.rem(me, 2), lax.rem(me // 2, 2), me // 4
    half = shard.shape[0] // 2
    part = half // SUBS

    def held(plane):
        return (plane >= bottom) & (plane < top)

    def peer(axis, sign=1):
        if axis == "x":
            return {"rep": 1 - x}
        if axis == "y":
            return {"dp": me + 2 - 4 * y}
        if axis == "core":
            return {"dp": me + 1 - 2 * core}
        return {"dp": me + 4 * sign}

    def rows(side, sub):
        return pl.ds(pl.multiple_of(side * half + sub * part, part), part)

    def remote(source, target, send, receive, where):
        return pltpu.make_async_remote_copy(source, target, send, receive, device_id=where, device_id_type=MESH)

    def spot(plane, row, side, sub):
        return out.at[plane - bottom, row, core, rows(side, sub), :]

    def move(axis, plane, row, side, sub, source=None):
        target = spot(plane, row, side, sub)
        source = target if source is None else source
        at = plane - bottom
        if axis == "core":
            return remote(source, target, core_send.at[at, row, side, sub], core_got, peer("core"))
        send, receive = (x_send, x_got) if axis == "x" else (y_send, y_got)
        return remote(source, target, send.at[at, row, side, sub], receive.at[at, row, side, sub], peer(axis))

    def climb(plane, sub, sign, source=None):
        target = spot(plane, y, x, sub)
        way = 0 if sign > 0 else 1
        at = plane - bottom
        return remote(target if source is None else source, target, z_send.at[at, sub, way], z_got.at[at, sub], peer("z", sign))

    def inside(sign, act):
        pl.when((z + sign >= 0) & (z + sign < PLANES))(act)

    def begin():
        @pl.when(held(z))
        def _():
            pltpu.make_async_copy(shard, out.at[z - bottom, y, core], local_sem).start()
            for sub in range(SUBS):
                for sign in (1, -1):
                    inside(sign, lambda: climb(z, sub, sign, shard.at[rows(x, sub), :]).start())
                move("y", z, y, x, sub, shard.at[rows(x, sub), :]).start()
            for side in range(2):
                for sub in range(SUBS):
                    move("core", z, y, side, sub, shard.at[rows(side, sub), :]).start()

    def at_distance(distance, act):
        for sign in (1, -1):
            plane = z - sign * distance

            @pl.when(held(plane))
            def _():
                act(plane, sign)

    def from_z(plane, sign):
        for sub in range(SUBS):
            climb(plane, sub, sign).wait_recv()
            inside(sign, lambda: climb(plane, sub, sign).start())
            for axis in ("x", "y", "core"):
                move(axis, plane, y, x, sub).start()

    def take(axis, plane, row, side, sub, onward=None):
        move(axis, plane, row, side, sub).wait_recv()
        if onward is not None:
            move(onward, plane, row, side, sub).start()
        move("core", plane, row, side, sub).start()

    def first_square(plane, sign):
        for even, odd in zip(EVEN, ODD):
            take("x", plane, y, 1 - x, even, "y")
            take("y", plane, 1 - y, x, odd, "x")
            take("y", plane, 1 - y, x, even)
            take("x", plane, y, 1 - x, odd)

    def second_square(plane, sign):
        for even, odd in zip(EVEN, ODD):
            take("y", plane, 1 - y, 1 - x, even)
            take("x", plane, 1 - y, 1 - x, odd)

    def own_first():
        @pl.when(held(z))
        def _():
            for sub in range(SUBS):
                take("y", z, 1 - y, x, sub, "x")

    def own_last():
        @pl.when(held(z))
        def _():
            for sub in range(SUBS):
                take("x", z, 1 - y, 1 - x, sub)

    def stage(distance, act):
        return lambda: at_distance(distance, act)

    steps = [
        stage(1, from_z), own_first, stage(2, from_z), stage(1, first_square), stage(3, from_z), stage(2, first_square),
        own_last, stage(1, second_square), stage(3, first_square), stage(2, second_square), stage(3, second_square),
    ]

    def sent(plane, sign):
        for sub in range(SUBS):
            inside(sign, lambda: climb(plane, sub, sign).wait_send())
            move("x", plane, y, x, sub).wait_send()
            move("y", plane, y, x, sub).wait_send()
        for even, odd in zip(EVEN, ODD):
            move("y", plane, y, 1 - x, even).wait_send()
            move("x", plane, 1 - y, x, odd).wait_send()

    def finish():
        for distance in (1, 2, 3):
            at_distance(distance, sent)

        @pl.when(held(z))
        def _():
            pltpu.make_async_copy(shard, out.at[z - bottom, y, core], local_sem).wait()
            for sub in range(SUBS):
                for sign in (1, -1):
                    inside(sign, lambda: climb(z, sub, sign).wait_send())
                move("y", z, y, x, sub).wait_send()
                move("x", z, 1 - y, x, sub).wait_send()

        def core_sent(index, carry):
            plane, row = bottom + index // (4 * SUBS), lax.rem(index // (2 * SUBS), 2)
            side, sub = lax.rem(index // SUBS, 2), lax.rem(index, SUBS)
            move("core", plane, row, side, sub).wait_send()
            return carry

        lax.fori_loop(0, 4 * SUBS * (top - bottom), core_sent, 0)
        column = out.at[:, :, 1 - core]
        pltpu.make_async_copy(column, column, core_got).wait()

    return begin, steps, finish


def gather(low, spans, hidden, cotangent, *smalls):
    results = pl.pallas_call(
        functools.partial(gather_kernel, spans),
        out_shape=[spread_shape(low, span) for span in spans] + ARRANGED + [jax.ShapeDtypeStruct(hidden.shape, BF16)] * 2,
        in_specs=[VMEM] * 6,
        out_specs=[pl.BlockSpec(memory_space=pl.ANY)] * len(spans) + [VMEM] * (len(ARRANGED) + 2),
        scratch_shapes=[DMA((2, 2))] + [one for span in spans for one in spread_semaphores(span)],
        compiler_params=pltpu.CompilerParams(collective_id=4, has_side_effects=True),
        name="gather",
    )(low, *smalls, hidden, cotangent)
    return [flat_rows(one) for one in results[: len(spans)]], results[len(spans) : -2], results[-2:]


CHUNK = 32
RING = 8
MATES = ("low_in", "low_comb", "low_up", "low_act", "low_grads", "low_branch", "low_hidden", "low_down", "gain_one", "shift_one", "gain_two", "shift_two", "taps")


def change(grad, first_old, second_old):
    new_first = ADAM_ONE * first_old + (1.0 - ADAM_ONE) * grad
    new_second = ADAM_TWO * second_old + (1.0 - ADAM_TWO) * grad * grad
    return new_first * (1.0 / (1.0 - ADAM_ONE**STEP_COUNT)) / (jnp.sqrt(new_second * (1.0 / (1.0 - ADAM_TWO**STEP_COUNT))) + ADAM_EPSILON)


def settle_kernel(block_rows, *refs):
    count = len(MATES)
    mates = [dict(zip(MATES, refs[level * count : (level + 1) * count])) for level in range(LAYERS)]
    (
        weights, first, second, small_first, small_second, grad_in, grad_out, mean_out, small_out, grad_in_out,
        turned, right, staged, own, got_core, got_y, got_z, inner, step_own, step_got, small, small_got, small_own, small_step, small_step_got,
        core_send, core_got, y_send, y_got, z_send, z_got, inner_sem, rep_send, rep_got, small_send, small_sem, back_send, back_sem, small_rep, swap_sems,
    ) = refs[LAYERS * count :]
    me = lax.axis_index("dp")
    other_rep = 1 - lax.axis_index("rep")
    core, y, z = lax.rem(me, 2), lax.rem(me // 2, 2), me // 4
    devices = 16
    per_layer = block_rows // CHUNK
    chunks = LAYERS * per_layer

    barrier = pltpu.get_barrier_semaphore()

    def signal(step, carry):
        pl.semaphore_signal(barrier, inc=1, device_id={"dp": lax.rem(me + step, devices)}, device_id_type=MESH)
        return carry

    lax.fori_loop(1, devices, signal, 0)
    pl.semaphore_signal(barrier, inc=1, device_id={"rep": other_rep}, device_id_type=MESH)

    def to_dp(source, target, send, receive, peer):
        return pltpu.make_async_remote_copy(source, target, send, receive, device_id={"dp": peer}, device_id_type=MESH)

    def to_rep(source, target, send, receive):
        return pltpu.make_async_remote_copy(source, target, send, receive, device_id={"rep": other_rep}, device_id_type=MESH)

    def spot(slot):
        return lax.rem(slot, RING)

    features = D * 2 + FF * 2
    for order, level in enumerate(reversed(range(LAYERS))):
        mate = mates[level]
        at = order * features
        for name in MATES[:4]:
            for part in range(mate[name].shape[1] // LANES):
                turned[at : at + LANES, :] = mate[name][:, part * LANES : (part + 1) * LANES].T
                at += LANES
        for part in range(3):
            right[order * 6 + part] = mate["low_grads"][part]
        for part, name in enumerate(MATES[5:8]):
            right[order * 6 + 3 + part] = mate[name][...]

    def put(level, line, row):
        index = level * LINES + line
        small[index // 2, index % 2 : index % 2 + 1, :] = row

    def column_sum(array):
        return jnp.sum(array.astype(F32), axis=0, keepdims=True)

    for level in range(LAYERS):
        mate = mates[level]
        put(level, 0, column_sum(mate["low_grads"][0]))
        put(level, 1, column_sum(mate["low_grads"][2]))
        put(level, 2, column_sum(mate["low_branch"][...]))
        put(level, 3, column_sum(mate["low_down"][...]))
        for line, name in enumerate(MATES[8:12]):
            put(level, 4 + line, column_sum(mate[name][...]))
        for part in range(FF // D):
            put(level, 8 + part, column_sum(mate["low_up"][:, part * D : (part + 1) * D]))
        line = jnp.zeros((1, D), F32)
        for head in range(HEADS):
            taps = jnp.concatenate([mate["taps"][head // 2][head % 2 : head % 2 + 1], jnp.zeros((1, D - 2 * LANES), F32)], axis=1)
            taps = jnp.where(iota((1, D), 1) < TAPS, taps, 0.0)
            line = line + (pltpu.roll(taps, TAPS * head, 1) if head else taps)
        put(level, 12, line)
    for index in range(LAYERS * LINES, 2 * devices):
        small[index // 2, index % 2 : index % 2 + 1, :] = jnp.zeros((1, D), F32)

    pl.semaphore_wait(barrier, devices)

    at_layout = Layout(16).place()
    swapping = swap(at_layout, grad_in, grad_in_out, swap_sems.at[0], swap_sems.at[1])
    swapping.start()
    grad_in_out[pl.ds(at_layout.group, 1)] = grad_in[pl.ds(at_layout.group, 1)]

    def small_copy(step):
        peer = lax.rem(me + step, devices)
        return to_dp(small.at[peer], small_got.at[me], small_send.at[peer], small_sem.at[me], peer)

    def small_begin(step, carry):
        small_copy(step).start()
        return carry

    lax.fori_loop(1, devices, small_begin, 0)

    def core_copy(chunk):
        return to_dp(staged.at[lax.rem(chunk, 2)], got_core.at[spot(chunk)], core_send.at[lax.rem(chunk, 2)], core_got.at[spot(chunk)], me + 1 - 2 * core)

    def y_copy(chunk):
        return to_dp(own.at[spot(chunk), :, 1 - y], got_y.at[spot(chunk)], y_send.at[spot(chunk)], y_got.at[spot(chunk)], me + 2 - 4 * y)

    def z_copy(chunk, hop):
        there = lax.rem(z + hop, 4)
        slot = spot(chunk)
        return to_dp(own.at[slot, there, y], got_z.at[slot, hop - 1], z_send.at[slot, hop - 1], z_got.at[slot, hop - 1], there * 4 + lax.rem(me, 4))

    def place(chunk):
        return LAYERS - 1 - chunk // per_layer, pl.ds(pl.multiple_of(lax.rem(chunk, per_layer) * CHUNK, CHUNK), CHUNK)

    def inner_copies(chunk):
        level, rows = place(chunk)
        slot = lax.rem(chunk, 4)
        return [
            pltpu.make_async_copy(array.at[level, rows, :], inner.at[slot, index], inner_sem.at[slot, index])
            for index, array in enumerate((weights, first, second))
        ]

    def rep_copy(chunk):
        return to_rep(step_own.at[spot(chunk)], step_got.at[spot(chunk)], rep_send.at[spot(chunk)], rep_got.at[spot(chunk)])

    def product(chunk, there, row, side):
        order = chunk // per_layer
        block = (there * 2 + row) * 2 + side
        piece = block * per_layer + lax.rem(chunk, per_layer)
        narrow = D // CHUNK
        line = jnp.where(piece < 3 * narrow, lax.rem(piece, narrow), piece - 2 * narrow)
        group = jnp.where(piece < 4 * narrow, piece // narrow, jnp.where(piece < 4 * narrow + FF // CHUNK, 4, 5))
        rows = pl.ds(pl.multiple_of(order * features + line * CHUNK, 16), CHUNK)
        return mm(turned[rows, :], right[order * 6 + group]).astype(BF16)

    def stage_product(chunk):
        for there in range(4):
            for row in range(2):
                staged[lax.rem(chunk, 2), there, row] = product(chunk, there, row, 1 - core)
        core_copy(chunk).start()
        for there in range(4):
            for row in range(2):
                own[spot(chunk), there, row] = product(chunk, there, row, core)

    def stage_core(chunk):
        core_copy(chunk).wait()
        slot = spot(chunk)
        for there in range(4):
            for side in range(2):
                own[slot, there, side] = own[slot, there, side] + got_core[slot, there, side]
        y_copy(chunk).start()

    def stage_y(chunk):
        y_copy(chunk).wait_recv()
        slot = spot(chunk)
        for there in range(4):
            own[slot, there, y] = own[slot, there, y] + got_y[slot, there]
        for hop in range(1, 4):
            z_copy(chunk, hop).start()
        for copy in inner_copies(chunk):
            copy.start()

    def stage_z(chunk):
        y_copy(chunk).wait_send()
        for hop in range(1, 4):
            z_copy(chunk, hop).wait_recv()
        for copy in inner_copies(chunk):
            copy.wait()
        total = own[spot(chunk), z, y].astype(F32)
        for hop in range(3):
            total = total + got_z[spot(chunk), hop].astype(F32)
        level, rows = place(chunk)
        grad_out[level, rows, :] = total
        slot = lax.rem(chunk, 4)
        step = change(total, inner[slot, 1], inner[slot, 2]) + WEIGHT_DECAY * inner[slot, 0]
        step_own[spot(chunk)] = (LR_INNER * step).astype(BF16)
        rep_copy(chunk).start()

    def stage_rep(chunk):
        for hop in range(1, 4):
            z_copy(chunk, hop).wait_send()
        rep_copy(chunk).wait()
        level, rows = place(chunk)
        mean_out[level, rows, :] = 0.5 * (step_own[spot(chunk)].astype(F32) + step_got[spot(chunk)].astype(F32))

    def small_rep_copy():
        return to_rep(small_step, small_step_got, small_rep.at[0], small_rep.at[1])

    def small_back(step):
        peer = lax.rem(me + step, devices)
        return to_dp(small_own, small_out.at[me], back_send.at[peer], back_sem.at[me], peer)

    def small_sum():
        def add(step, total):
            peer = lax.rem(me + step, devices)
            pltpu.make_async_copy(small_got.at[peer], small_got.at[peer], small_sem.at[peer]).wait()
            return total + small_got[peer]

        total = lax.fori_loop(1, devices, add, small[me])
        small_own[0] = total
        small_step[...] = (LR_SMALL * change(total, small_first[me], small_second[me])).astype(BF16)
        small_rep_copy().start()

    def small_spread():
        small_rep_copy().wait_recv()
        small_own[1] = 0.5 * (small_step[...].astype(F32) + small_step_got[...].astype(F32))
        small_out[me] = small_own[...]

        def send(step, carry):
            small_back(step).start()
            return carry

        lax.fori_loop(1, devices, send, 0)

    def turn(now, carry):
        for lag, stage in ((0, stage_product), (1, stage_core), (3, stage_y), (5, stage_z), (7, stage_rep)):

            @pl.when((now >= lag) & (now < chunks + lag))
            def _():
                stage(now - lag)

        pl.when(now == 4)(small_sum)
        pl.when(now == 7)(small_spread)
        return carry

    lax.fori_loop(0, chunks + 7, turn, 0)

    def small_drain(step, carry):
        peer = lax.rem(me + step, devices)
        small_copy(step).wait_send()
        small_back(step).wait_send()
        pltpu.make_async_copy(small_own, small_out.at[peer], back_sem.at[peer]).wait()
        return carry

    lax.fori_loop(1, devices, small_drain, 0)
    small_rep_copy().wait_send()
    swapping.wait()


def settle(mates, weights, first, second, small_first, small_second, grad_in):
    block_rows = weights.shape[1]
    anywhere = pl.BlockSpec(memory_space=pl.ANY)
    devices = 16
    piece = (CHUNK, D)
    tokens = mates[0]["low_in"].shape[0]
    return pl.pallas_call(
        functools.partial(settle_kernel, block_rows),
        out_shape=[
            jax.ShapeDtypeStruct(weights.shape, F32),
            jax.ShapeDtypeStruct(weights.shape, F32),
            jax.ShapeDtypeStruct((devices, 2, 2, D), F32),
            jax.ShapeDtypeStruct(grad_in.shape, F32),
        ],
        in_specs=[VMEM] * (LAYERS * len(MATES)) + [anywhere] * 3 + [VMEM] * 3,
        out_specs=[VMEM] * 4,
        scratch_shapes=[
            pltpu.VMEM((LAYERS * 2 * (D + FF), tokens), BF16),
            pltpu.VMEM((LAYERS * 6, tokens, D), BF16),
            pltpu.VMEM((2, 4, 2) + piece, BF16),
            pltpu.VMEM((RING, 4, 2) + piece, BF16),
            pltpu.VMEM((RING, 4, 2) + piece, BF16),
            pltpu.VMEM((RING, 4) + piece, BF16),
            pltpu.VMEM((RING, 3) + piece, BF16),
            pltpu.VMEM((4, 3) + piece, F32),
            pltpu.VMEM((RING,) + piece, BF16),
            pltpu.VMEM((RING,) + piece, BF16),
            pltpu.VMEM((devices, 2, D), F32),
            pltpu.VMEM((devices, 2, D), F32),
            pltpu.VMEM((2, 2, D), F32),
            pltpu.VMEM((2, D), BF16),
            pltpu.VMEM((2, D), BF16),
            DMA((2,)),
            DMA((RING,)),
            DMA((RING,)),
            DMA((RING,)),
            DMA((RING, 3)),
            DMA((RING, 3)),
            DMA((4, 3)),
            DMA((RING,)),
            DMA((RING,)),
            DMA((devices,)),
            DMA((devices,)),
            DMA((devices,)),
            DMA((devices,)),
            DMA((2,)),
            DMA((2,)),
        ],
        compiler_params=pltpu.CompilerParams(collective_id=3, has_side_effects=True, vmem_limit_bytes=63 << 20),
        name="settle",
    )(*[mate[name] for mate in mates for name in MATES], weights, first, second, small_first, small_second, grad_in)


def finish_kernel(both, params, outer, first, second, first_new, second_new, outer_new, params_new, grad, mean):
    for level in range(LAYERS):
        for line in range(LINES):
            index = level * LINES + line
            spot = slice(index % 2, index % 2 + 1)
            for which, target in ((0, grad), (1, mean)):
                target[level : level + 1, line * D : (line + 1) * D] = both[index // 2, which, spot, :]
    first_new[...], second_new[...] = moments(first[...], second[...], grad[:, :SMALL])
    momentum = MOMENTUM * outer[...] + mean[:, :SMALL]
    outer_new[...] = momentum
    params_new[...] = params[...] - LR_OUTER * (mean[:, :SMALL] + MOMENTUM * momentum)


def finish(both, params, outer, first, second):
    wide = pltpu.VMEM((LAYERS, LINES * D), F32)
    return pl.pallas_call(
        finish_kernel,
        out_shape=[jax.ShapeDtypeStruct(params.shape, F32)] * 4,
        in_specs=[VMEM] * 5,
        out_specs=[VMEM] * 4,
        scratch_shapes=[wide, wide],
        name="finish",
    )(both, params, outer, first, second)


def dense(a, b, dims=NN):
    return mm(a, b, dims)


def standard(values):
    centred = values - jnp.mean(values, axis=-1, keepdims=True)
    scale = lax.rsqrt(jnp.mean(centred * centred, axis=-1, keepdims=True) + 1e-05)
    return centred * scale, scale


def layer_norm(values, gain, shift):
    return standard(values)[0] * gain + shift


def layer_norm_back(values, gain, grad):
    unit_values, scale = standard(values)
    inner = grad * gain
    along = jnp.mean(inner * unit_values, axis=-1, keepdims=True)
    result = scale * (inner - jnp.mean(inner, axis=-1, keepdims=True) - unit_values * along)
    return result, eighths(grad * unit_values), eighths(grad)


def eighths(rows):
    return jnp.sum(rows.reshape(-1, 8, D), axis=0)


def split_rows(rest):
    return rest[:D], rest[D : D + FF], rest[D + FF :]


def forward_layer(count, inputs, proj, rest, small, edges, ident, low=None, spans=()):
    piece = inputs.shape[0] // MICRO
    lines, bias_up = small
    proj = proj.reshape(3, D, D)
    low_in = inputs.astype(BF16)
    query = (dense(low_in, proj[0]) + lines[0:1]).astype(BF16)
    key = dense(low_in, proj[1]).astype(BF16)
    value = (dense(low_in, proj[2]) + lines[1:2]).astype(BF16)
    qkv = jnp.stack([query, key, value])
    low_comb, kept, fetched = attention_forward(count, qkv.reshape(3, MICRO, piece, D), edges, lines, ident, low, spans)
    out_weight, up_weight, down_weight = split_rows(rest)
    low_comb = low_comb.reshape(MICRO * piece, D)
    resid_one = inputs + (dense(low_comb, out_weight) + lines[2:3])
    hidden_one = layer_norm(resid_one, lines[4:5], lines[5:6])
    low_hidden = hidden_one.astype(BF16)
    upward = dense(low_hidden, up_weight, NT) + bias_up
    low_act = jax.nn.gelu(upward).astype(BF16)
    resid_two = hidden_one + (dense(low_act, down_weight) + lines[3:4])
    output = layer_norm(resid_two, lines[6:7], lines[7:8])
    return output, (proj, rest, low_in, kept, low_comb, resid_one, low_hidden, upward, low_act, resid_two), fetched


def backward_layer(count, grad_output, small, edges, state, ident, carried=()):
    proj, rest, low_in, kept, low_comb, resid_one, low_hidden, upward, low_act, resid_two = state
    total = low_in.shape[0]
    piece = total // MICRO
    lines, _ = small
    out_weight, up_weight, down_weight = split_rows(rest)
    grad_two, grad_gain_two, grad_shift_two = layer_norm_back(resid_two, lines[6:7], grad_output)
    low_down = grad_two.astype(BF16)
    grad_act = dense(low_down, down_weight, NT)
    _, pull_gelu = jax.vjp(jax.nn.gelu, upward)
    low_up = pull_gelu(grad_act)[0].astype(BF16)
    grad_hidden = grad_two + dense(low_up, up_weight)
    grad_one, grad_gain_one, grad_shift_one = layer_norm_back(resid_one, lines[4:5], grad_hidden)
    low_branch = grad_one.astype(BF16)
    grad_comb = dense(low_branch, out_weight, NT).astype(BF16)
    low_grads, grad_taps, swapped = attention_backward(count, grad_comb.reshape(1, MICRO, piece, D), edges, lines, kept, ident, carried)
    low_grads = low_grads.reshape(3, total, D)
    grad_in = grad_one + sum(dense(low_grads[part], proj[part], NT) for part in range(3))
    vectors = (grad_gain_one, grad_shift_one, grad_gain_two, grad_shift_two)
    values = (low_in, low_comb, low_up, low_act, low_grads, low_branch, low_hidden, low_down, *vectors, grad_taps)
    return grad_in, dict(zip(MATES, values)), swapped


def plain_grads(mate):
    parts = [dense(mate["low_in"], mate["low_grads"][part], TN) for part in range(3)]
    parts = parts + [dense(mate[left], mate[right], TN) for left, right in (("low_comb", "low_branch"), ("low_up", "low_hidden"), ("low_act", "low_down"))]
    sums = [mate["low_grads"][0], mate["low_grads"][2], mate["low_branch"], mate["low_down"]]
    sums = [jnp.sum(one.astype(F32), axis=0) for one in sums]
    sums = sums + [jnp.sum(mate[name], axis=0) for name in MATES[8:12]]
    sums = sums + [jnp.sum(mate["low_up"].astype(F32), axis=0), mate["taps"][:, :, :TAPS].reshape(-1)]
    return jnp.concatenate(parts, axis=0).astype(BF16), jnp.concatenate(sums)


def moments(first, second, grad):
    return ADAM_ONE * first + (1.0 - ADAM_ONE) * grad, ADAM_TWO * second + (1.0 - ADAM_TWO) * grad * grad


def adam(weights, first, second, grad, rate, decay):
    correct_one = 1.0 - ADAM_ONE**STEP_COUNT
    correct_two = 1.0 - ADAM_TWO**STEP_COUNT
    new_first, new_second = moments(first, second, grad)
    step = new_first / correct_one / (jnp.sqrt(new_second / correct_two) + ADAM_EPSILON)
    return new_first, new_second, rate * (step + decay * weights)


def shards(
    hidden,
    bounds,
    cotangent,
    weights,
    small_params,
    first_big,
    second_big,
    first_small,
    second_small,
    outer_big,
    outer_small,
):
    count = lax.axis_size("dp")
    piece = hidden.shape[3]
    total = MICRO * piece
    low_weights = weights.astype(BF16)
    limits = bounds[0, :, 0, :]
    edges = jnp.pad(limits.astype(F32), ((0, 0), (0, LANES - limits.shape[1])))
    own_hidden, own_cotangent = hidden[0, :, 0], cotangent[0, :, 0]
    me = lax.axis_index("dp")
    start, last = me * piece, limits[:, -1].reshape(MICRO, 1, 1)
    if count == 16:
        (rows,), prepared, (own_hidden, own_cotangent) = gather(
            low_weights, ((0, 0, PLANES),), own_hidden, own_cotangent, small_params, first_small[0], second_small[0]
        )
        half = count // MICRO
        start = (lax.broadcasted_iota(jnp.int32, (MICRO, 1, 1), 0) * half + lax.rem(me, half)) * piece
        last = jnp.where(me < half, limits[0, -1], limits[1, -1])
    else:
        prepared = arranged(small_params, first_small[0], second_small[0])
    positions = start + lax.broadcasted_iota(jnp.int32, (MICRO, piece, 1), 1)
    valid = positions < last
    activation = own_hidden.reshape(total, D).astype(F32)
    states = [None] * LAYERS
    smalls = [(prepared[level], prepared[LAYERS + level]) for level in range(LAYERS)]
    for level in range(LAYERS):
        if count == 16:
            spans = ((level + 1, 0, PLANES),) if level + 1 < LAYERS else ()
            activation, states[level], more = forward_layer(
                count, activation, rows[: 3 * D], rows[3 * D :], smalls[level], edges, 1 + 4 * level, low_weights, spans
            )
            rows = more[0] if more else None
        else:
            rows = lax.all_gather(low_weights[level], "dp", axis=0, tiled=True)
            activation, states[level], _ = forward_layer(count, activation, rows[: 3 * D], rows[3 * D :], smalls[level], edges, 1)
    gradient = jnp.where(valid, own_cotangent.astype(F32), 0.0).reshape(total, D)
    mates = [None] * LAYERS
    for level in reversed(range(LAYERS)):
        carried = (activation.reshape(MICRO, piece, D),) if count == 16 and level == LAYERS - 1 else ()
        gradient, mates[level], swapped = backward_layer(count, gradient, smalls[level], edges, states[level], 2 + 4 * level, carried)
        activation = swapped[0] if carried else activation
    if count == 16:
        grad_big, mean_big, small_both, gradient = settle(
            mates, weights, first_big[0], second_big[0], *prepared[2 * LAYERS :], gradient.reshape(MICRO, piece, D)
        )
        new_smalls = finish(small_both, small_params, outer_small, first_small[0], second_small[0])
    else:
        rows, sums = zip(*[plain_grads(mate) for mate in mates])
        grad_big = jnp.stack([lax.psum_scatter(one, "dp", scatter_dimension=0, tiled=True).astype(F32) for one in rows])
        grad_small = lax.psum(jnp.stack(sums), "dp")
        reps = lax.axis_size("rep")
        delta_big = adam(weights, first_big[0], second_big[0], grad_big, LR_INNER, WEIGHT_DECAY)[2]
        delta_small = adam(small_params, first_small[0], second_small[0], grad_small, LR_SMALL, 0.0)[2]
        mean_big = lax.psum(delta_big.astype(BF16), "rep").astype(F32) / reps
        mean_small = lax.psum(delta_small.astype(BF16), "rep").astype(F32) / reps
        momentum = MOMENTUM * outer_small + mean_small
        new_smalls = (*moments(first_small[0], second_small[0], grad_small), momentum, small_params - LR_OUTER * (mean_small + MOMENTUM * momentum))
    new_first, new_second = moments(first_big[0], second_big[0], grad_big)
    new_first_small, new_second_small, outer_small_new, small_new = new_smalls
    outer_big_new = MOMENTUM * outer_big + mean_big
    weights_new = weights - LR_OUTER * (mean_big + MOMENTUM * outer_big_new)
    shape = (1, MICRO, 1, piece, D)
    return (
        activation.reshape(shape),
        gradient.reshape(shape),
        new_first[None],
        new_second[None],
        new_first_small[None],
        new_second_small[None],
        outer_big_new,
        outer_small_new,
        weights_new,
        small_new,
        weights_new.astype(BF16),
    )


def solution(mesh):
    placed = (
        P("rep", None, None, "dp", None),
        P("rep", None, None, None),
        P("rep", None, None, "dp", None),
        P(None, "dp", None),
        P(),
        P("rep", None, "dp", None),
        P("rep", None, "dp", None),
        P("rep", None, None),
        P("rep", None, None),
        P(None, "dp", None),
        P(),
    )
    return jax.shard_map(
        shards,
        mesh=mesh,
        in_specs=placed,
        out_specs=(
            P("rep", None, None, "dp", None),
            P("rep", None, None, "dp", None),
            P("rep", None, "dp", None),
            P("rep", None, "dp", None),
            P("rep", None, None),
            P("rep", None, None),
            P(None, "dp", None),
            P(),
            P(None, "dp", None),
            P(),
            P(None, "dp", None),
        ),
        check_vma=False,
    )
```

```python
import functools

import jax
import jax.numpy as jnp
from jax import lax
from jax.experimental import pallas as pl
from jax.experimental.pallas import tpu as pltpu
from jax.sharding import PartitionSpec as P

D = 768
HEADS = 12
FF = 3072
TAPS = 33
NS_ITERS = 6
LAYERS = 2
MICRO = 2
STEP_COUNT = 5


ADAM_ONE = 0.9
ADAM_TWO = 0.95
ADAM_EPSILON = 1e-08
WEIGHT_DECAY = 0.1
LR_INNER = 0.04
LR_SMALL = 0.2
LR_OUTER = 0.7
MOMENTUM = 0.9

HEAD_DIM = 64
MARKS = 64
HALF = TAPS // 2
PAIRS = HEADS // 2
LINES = 13
TAP_LINE = 12
SMALL = 8 * D + FF + HEADS * TAPS
LANES = 128
SCALE = HEAD_DIM**-0.5
NEG = -1e30
MESH = pl.DeviceIdType.MESH
F32 = jnp.float32
BF16 = jnp.bfloat16
NN = (((1,), (0,)), ((), ()))
NT = (((1,), (1,)), ((), ()))
TN = (((0,), (0,)), ((), ()))


def mm(a, b, dims=NN):
    return lax.dot_general(a, b, dims, preferred_element_type=F32)


def halves(a):
    high = a.astype(BF16)
    return high, (a - high.astype(F32)).astype(BF16)


def mm_left(a, b, dims=NN):
    high, rest = halves(a)
    return mm(high, b, dims) + mm(rest, b, dims)


def mm_both(a, b, dims=NN):
    ah, al = halves(a)
    bh, bl = halves(b)
    return mm(ah, bh, dims) + (mm(ah, bl, dims) + mm(al, bh, dims))


def exact(a, b, dims=NN):
    return mm_both(a, b, dims)


def iota(shape, dim):
    return lax.broadcasted_iota(jnp.int32, shape, dim)


def diagonal_blocks():
    return (iota((LANES, LANES), 0) < MARKS) == (iota((LANES, LANES), 1) < HEAD_DIM)


def unit():
    return (iota((LANES, LANES), 0) == iota((LANES, LANES), 1)).astype(F32)


def per_head(marks):
    first = iota(marks.shape, 1) < HEAD_DIM
    return jnp.concatenate([jnp.where(first, marks, 0.0), jnp.where(first, 0.0, marks)], axis=0)


def head_sums(a):
    rows, cols = a.shape
    split = a.reshape(2, rows // 2, cols)
    return jnp.broadcast_to(jnp.sum(split, axis=1, keepdims=True), split.shape).reshape(rows, cols)


def head_tops(a):
    rows, cols = a.shape
    split = a.reshape(2, rows // 2, cols)
    return jnp.broadcast_to(jnp.max(split, axis=1, keepdims=True), split.shape).reshape(rows, cols)


def head_taps(lines, pair):
    row = jnp.broadcast_to(lines[TAP_LINE : TAP_LINE + 1, :], (8, D))
    rows = []
    for side in range(2):
        turned = pltpu.roll(row, lax.rem(D - TAPS * (2 * pair + side), D), 1)[0:1, : 2 * LANES]
        rows.append(jnp.where(iota((1, 2 * LANES), 1) < TAPS, turned, 0.0))
    return rows


def band(taps_row):
    wide = jnp.broadcast_to(taps_row, (LANES, 2 * LANES))
    return pltpu.roll(wide, 0, 1, stride=1, stride_axis=0)


def band_back(taps_row):
    wide = jnp.broadcast_to(taps_row, (2 * LANES, 2 * LANES))
    return pltpu.roll(wide, 2 * LANES - 2 * HALF, 1, stride=1, stride_axis=0)[:, :LANES].T


def mark_columns(edges):
    low = jnp.broadcast_to(edges, (LANES, LANES)).T[:MARKS, :1]
    high = jnp.broadcast_to(pltpu.roll(edges, LANES - 1, 1), (LANES, LANES)).T[:MARKS, :1]
    return low.astype(jnp.int32), high.astype(jnp.int32)


def mark_rows(edges):
    low, high = edges[:, :MARKS], pltpu.roll(edges, LANES - 1, 1)[:, :MARKS]
    return low.astype(jnp.int32), high.astype(jnp.int32)


def convolve(padded, bands, length, store):
    first = iota((LANES, LANES), 1) < HEAD_DIM
    pairs = [halves(one) for one in bands]

    def block(at, carry):
        start = pl.multiple_of(at * LANES, LANES)
        window = padded[pl.ds(start, 2 * LANES), :]
        out = [mm(high, window) + mm(rest, window) for high, rest in pairs]
        store(start, jnp.where(first, out[0], out[1]))
        return carry

    lax.fori_loop(0, length // LANES, block, 0)


def put_rows(ref, at, start, rows):
    half = ref.shape[2]
    ref[at, start // half, pl.ds(pl.multiple_of(lax.rem(start, half), LANES), LANES), :] = rows


def whole(ref, at):
    return ref[at].reshape(-1, LANES)


def attend(slab, edges, taps, keep, padded, blended, result):
    length = slab.shape[1] * slab.shape[2]

    def begin():
        low_marks, high_marks = mark_columns(edges())
        at = iota((MARKS, length), 1)
        member = ((low_marks <= at) & (at < high_marks)).astype(F32).astype(BF16)
        counts = (high_marks - low_marks).astype(F32)
        q_marks = per_head(mm(member, whole(slab, 0)) / counts)
        k_marks = per_head(mm(member, whole(slab, 1)) / counts)
        scores = jnp.where(diagonal_blocks(), SCALE * exact(q_marks, k_marks, NT), NEG)
        weights = jnp.exp(scores - jnp.max(scores, axis=1, keepdims=True))
        kernel = weights / jnp.sum(weights, axis=1, keepdims=True)
        total = head_sums(jnp.broadcast_to(jnp.sum(kernel * kernel, axis=1, keepdims=True), kernel.shape))
        keep["q_marks"][...] = q_marks
        keep["k_marks"][...] = k_marks
        keep["kernel"][...] = kernel
        keep["total"][...] = total
        keep["inverse"][0] = kernel.T / total

    def sweep(at):
        def run():
            eye, inverse = unit(), keep["inverse"][at]
            product = exact(keep["kernel"][...], inverse)
            one = 7.0 * eye - product
            two = 15.0 * eye - exact(product, one)
            three = 13.0 * eye - exact(product, two)
            keep["product"][at] = product
            keep["two"][at] = two
            keep["three"][at] = three
            keep["inverse"][at + 1] = 0.25 * exact(inverse, three)

        return run

    def over_keys():
        valid = iota((1, length), 1) < mark_columns(edges())[1][MARKS - 1 :]
        key_scores = jnp.where(valid, SCALE * mm_left(keep["q_marks"][...], whole(slab, 1), NT), NEG)
        key_exp = jnp.where(valid, jnp.exp(key_scores - jnp.max(key_scores, axis=1, keepdims=True)), 0.0)
        key_weights = key_exp / jnp.sum(key_exp, axis=1, keepdims=True)
        keep["key_weights"][...] = key_weights
        keep["summary"][...] = jnp.where(diagonal_blocks(), mm_left(key_weights, whole(slab, 2)), 0.0)

    def over_tokens():
        token_scores = SCALE * mm_left(keep["k_marks"][...], whole(slab, 0), NT)
        token_exp = jnp.exp(token_scores - head_tops(token_scores))
        keep["token_weights"][...] = token_exp / head_sums(token_exp)

    def close():
        mixed = exact(keep["inverse"][NS_ITERS], keep["summary"][...])
        keep["mixed"][...] = mixed
        blended[...] = mm_both(keep["token_weights"][...], mixed, TN)
        values = whole(slab, 2)
        valid_column = iota((length, 1), 0) < mark_columns(edges())[1][MARKS - 1 :]
        padded[0:HALF, :] = jnp.zeros((HALF, LANES), BF16)
        padded[HALF : HALF + length, :] = jnp.where(valid_column, values, jnp.zeros_like(values))
        padded[HALF + length :, :] = jnp.zeros((LANES - HALF, LANES), BF16)

        def store(start, block):
            put_rows(result, 0, start, (blended[pl.ds(start, LANES), :] + block).astype(BF16))

        convolve(padded, [band(one) for one in taps()], length, store)

    return [begin] + [sweep(at) for at in range(NS_ITERS)] + [over_keys, over_tokens, close]


def attend_back(grads, queries, keys, values, edges, taps, keep, padded, padded_grads, blended, result, grad_taps):
    length = grads.shape[0]
    low_marks, high_marks = mark_columns(edges)
    low_row, high_row = mark_rows(edges)
    at = iota((length, MARKS), 0)
    member = ((low_row <= at) & (at < high_row)).astype(F32).astype(BF16)
    counts = (high_marks - low_marks).astype(F32)
    blocks, eye = diagonal_blocks(), unit()
    q_marks, k_marks = keep["q_marks"][...], keep["k_marks"][...]
    token_weights, key_weights = keep["token_weights"][...], keep["key_weights"][...]
    summary, mixed = keep["summary"][...], keep["mixed"][...]
    kernel = keep["kernel"][...]
    inverse = keep["inverse"][NS_ITERS]
    grad_mixed = jnp.where(blocks, mm_left(token_weights, grads), 0.0)
    grad_token = token_weights * mm_left(mixed, grads, NT)
    grad_token = SCALE * (grad_token - token_weights * head_sums(grad_token))
    grad_summary = exact(inverse, grad_mixed, TN)
    grad_inverse = exact(grad_mixed, summary, NT)
    grad_kernel = jnp.zeros_like(kernel)
    for sweep in reversed(range(NS_ITERS)):
        before, product = keep["inverse"][sweep], keep["product"][sweep]
        one = 7.0 * eye - product
        two, three = keep["two"][sweep], keep["three"][sweep]
        grad_three = 0.25 * exact(before, grad_inverse, TN)
        grad_two = -exact(product, grad_three, TN)
        grad_one = -exact(product, grad_two, TN)
        grad_product = -(exact(grad_three, two, NT) + exact(grad_two, one, NT) + grad_one)
        grad_kernel = grad_kernel + exact(grad_product, before, NT)
        grad_inverse = 0.25 * exact(grad_inverse, three, NT) + exact(kernel, grad_product, TN)
    total = keep["total"][...]
    turned = grad_inverse.T / total
    weighted = jnp.sum(jnp.where(blocks, turned * kernel, 0.0), axis=1, keepdims=True)
    weighted = head_sums(jnp.broadcast_to(weighted, kernel.shape))
    grad_kernel = grad_kernel + turned - 2.0 * kernel * weighted / total
    grad_scores = SCALE * kernel * (grad_kernel - jnp.sum(kernel * grad_kernel, axis=1, keepdims=True))
    grad_q_marks = exact(grad_scores, k_marks)
    grad_k_marks = exact(grad_scores, q_marks, TN)
    grad_k_marks = grad_k_marks + jnp.where(blocks, mm_left(grad_token, queries), 0.0)
    grad_key = mm_left(grad_summary, values, NT) - jnp.sum(grad_summary * summary, axis=1, keepdims=True)
    grad_key = SCALE * key_weights * grad_key
    grad_q_marks = grad_q_marks + jnp.where(blocks, mm_left(grad_key, keys), 0.0)
    grad_q_marks = (grad_q_marks[:MARKS] + grad_q_marks[MARKS:]) / counts
    grad_k_marks = (grad_k_marks[:MARKS] + grad_k_marks[MARKS:]) / counts
    high, rest = halves(grad_q_marks)
    result[0] = (mm_both(grad_token, k_marks, TN) + mm(member, high) + mm(member, rest)).astype(BF16).reshape(result.shape[1:])
    high, rest = halves(grad_k_marks)
    result[1] = (mm_both(grad_key, q_marks, TN) + mm(member, high) + mm(member, rest)).astype(BF16).reshape(result.shape[1:])
    blended[...] = mm_both(key_weights, grad_summary, TN)
    last = high_marks[MARKS - 1 :]
    valid_column = iota((length, 1), 0) < last
    padded[0:HALF, :] = jnp.zeros((HALF, LANES), BF16)
    padded[HALF : HALF + length, :] = jnp.where(valid_column, values, jnp.zeros_like(values))
    padded[HALF + length :, :] = jnp.zeros((LANES - HALF, LANES), BF16)
    padded_grads[0:HALF, :] = jnp.zeros((HALF, LANES), BF16)
    padded_grads[HALF : HALF + length, :] = grads
    padded_grads[HALF + length :, :] = jnp.zeros((LANES - HALF, LANES), BF16)

    def store(start, block):
        rows = start + iota((LANES, 1), 0)
        total_rows = blended[pl.ds(start, LANES), :] + jnp.where(rows < last, block, 0.0)
        put_rows(result, 2, start, total_rows.astype(BF16))

    convolve(padded_grads, [band_back(one) for one in taps], length, store)
    first = iota((LANES, LANES), 1) < HEAD_DIM

    def block(step, carry):
        start = pl.multiple_of(step * LANES, LANES)
        own = padded_grads[pl.ds(start + HALF, LANES), :]
        window = padded[pl.ds(start, 2 * LANES), :]
        none = jnp.zeros_like(own)
        return (
            carry[0] + mm(jnp.where(first, own, none), window, NT),
            carry[1] + mm(jnp.where(first, none, own), window, NT),
        )

    start_sum = jnp.zeros((LANES, 2 * LANES), F32)
    sums = lax.fori_loop(0, length // LANES, block, (start_sum, start_sum))
    wide = 2 * LANES
    for head in range(2):
        folded = sums[head][0:8]
        for group in range(1, LANES // 8):
            rows = sums[head][8 * group : 8 * group + 8]
            folded = folded + pltpu.roll(rows, wide - 8 * group, 1)
        line = folded[0:1]
        for row in range(1, 8):
            line = line + pltpu.roll(folded[row : row + 1], wide - row, 1)
        grad_taps[head : head + 1, :] = line


KEPT = ("q_marks", "k_marks", "kernel", "total", "inverse", "product", "two", "three", "key_weights", "summary", "mixed", "token_weights")


def kept_shapes(length):
    square = (LANES, LANES)
    shapes = {name: square for name in KEPT}
    shapes["inverse"] = (NS_ITERS + 1,) + square
    for name in ("product", "two", "three"):
        shapes[name] = (NS_ITERS,) + square
    shapes["key_weights"] = shapes["token_weights"] = (LANES, length)
    return shapes


class Layout:
    def __init__(self, count):
        self.count = count
        self.groups = MICRO if count == 16 else 1
        self.members = count // self.groups
        self.tasks = PAIRS * MICRO // self.groups

    def place(self):
        me = lax.axis_index("dp")
        self.me, self.group, self.index = me, me // self.members, lax.rem(me, self.members)
        self.task = (self.index * self.tasks + self.members - 1) // self.members
        self.owns = self.owner(self.task) == self.index
        self.micro = self.micro_of(self.task)
        self.pair = lax.rem(self.task, PAIRS)
        return self

    def owner(self, task):
        return task * self.members // self.tasks

    def micro_of(self, task):
        return self.group if self.groups > 1 else task // PAIRS

    def device(self, index):
        return {"dp": self.group * self.members + index}

    def block(self, array, task):
        lanes = pl.ds(pl.multiple_of(lax.rem(task, PAIRS) * LANES, LANES), LANES)
        return array.at[:, :, :, lanes] if self.groups > 1 else array.at[:, pl.ds(task // PAIRS, 1), :, lanes]

    def rows(self, slab, index, piece):
        return slab.at[:, :, pl.ds(pl.multiple_of(index * piece, piece), piece), :]

    def mate(self):
        return {"dp": lax.rem(self.me + self.members, self.count)}


def greet(at, everyone=False, mate=False):
    barrier = pltpu.get_barrier_semaphore()
    size, index = (at.count, at.me) if everyone else (at.members, at.index)
    if everyone:
        pl.semaphore_signal(barrier, inc=1, device_id={"rep": 1 - lax.axis_index("rep")}, device_id_type=MESH)
    if mate:
        pl.semaphore_signal(barrier, inc=1, device_id=at.mate(), device_id_type=MESH)

    def signal(step, carry):
        other = lax.rem(index + step, size)
        pl.semaphore_signal(barrier, inc=1, device_id={"dp": other} if everyone else at.device(other), device_id_type=MESH)
        return carry

    lax.fori_loop(1, size, signal, 0)
    pl.semaphore_wait(barrier, size - 1 + int(everyone) + int(mate))


def scatter_tasks(at, piece, source, slab, send, receive):
    def one(step, finish):
        task = lax.rem(at.task + step, at.tasks)
        owner = at.owner(task)
        outgoing, landing = at.block(source, task), at.rows(slab, at.index, piece)

        @pl.when(owner != at.index)
        def _():
            copy = pltpu.make_async_remote_copy(
                outgoing, landing, send.at[task], receive.at[at.index], device_id=at.device(owner), device_id_type=MESH
            )
            if finish:
                copy.wait_send()
            else:
                copy.start()

        @pl.when((owner == at.index) & (not finish))
        def _():
            pltpu.make_async_copy(outgoing, landing, receive.at[at.index]).start()

    def run(finish):
        def body(step, carry):
            one(step, finish)
            return carry

        lax.fori_loop(0, at.tasks, body, 0)

    return run


def await_slab(at, piece, slab, receive):
    def body(origin, carry):
        landing = at.rows(slab, origin, piece)
        pltpu.make_async_copy(landing, landing, receive.at[origin]).wait()
        return carry

    lax.fori_loop(0, at.members, body, 0)


def return_rows(at, piece, result, target, send, receive):
    def run(finish):
        def body(step, carry):
            peer = lax.rem(at.index + step, at.members)
            outgoing, landing = at.rows(result, peer, piece), at.block(target, at.task)

            @pl.when(peer != at.index)
            def _():
                copy = pltpu.make_async_remote_copy(
                    outgoing, landing, send.at[peer], receive.at[at.task], device_id=at.device(peer), device_id_type=MESH
                )
                if finish:
                    copy.wait_send()
                else:
                    copy.start()

            @pl.when((peer == at.index) & (not finish))
            def _():
                pltpu.make_async_copy(outgoing, landing, receive.at[at.task]).start()

            return carry

        lax.fori_loop(0, at.members, body, 0)

    return run


def await_rows(at, target, receive):
    def body(task, carry):
        landing = at.block(target, task)
        pltpu.make_async_copy(landing, landing, receive.at[task]).wait()
        return carry

    lax.fori_loop(0, at.tasks, body, 0)


def swap(at, source, target, send, receive):
    return pltpu.make_async_remote_copy(
        source.at[1 - at.group], target.at[at.group], send, receive, device_id=at.mate(), device_id_type=MESH
    )


def forward_kernel(count, piece, spans, qkv, edges, lines, low, mixed_rows, slab, *refs):
    keep = dict(zip(KEPT, refs))
    outs, refs = refs[len(KEPT) : len(KEPT) + len(spans)], refs[len(KEPT) + len(spans) :]
    padded, blended, result, send_one, receive_one, send_two, receive_two = refs[:7]
    begin, steps, finish = spread_all(spans, low, outs, refs[7:])
    at = Layout(count).place()
    greet(at, bool(spans))
    out = scatter_tasks(at, piece, qkv, slab, send_one, receive_one)
    out(False)
    begin()
    back = return_rows(at, piece, result, mixed_rows, send_two, receive_two)
    phases = attend(slab, lambda: edges[pl.ds(at.micro, 1), :], lambda: head_taps(lines, at.pair), keep, padded, blended, result)

    def between(turn):
        if turn < len(steps):
            steps[turn]()

    between(0)
    for turn, phase in enumerate(phases):

        @pl.when(at.owns)
        def _():
            if turn == 0:
                await_slab(at, piece, slab, receive_one)
            phase()
            if turn == len(phases) - 1:
                back(False)

        if turn > 1:
            between(turn - 1)
    for turn in range(len(phases) - 1, len(steps)):
        between(turn)
    finish()
    out(True)
    await_rows(at, mixed_rows, receive_two)

    @pl.when(at.owns)
    def _():
        back(True)


def backward_kernel(count, piece, carries, grads, edges, lines, *refs):
    carried, refs = refs[:carries], refs[carries:]
    slab, refs = refs[0], refs[1:]
    keep = dict(zip(KEPT, refs))
    out_grads, grad_taps, refs = refs[len(KEPT)], refs[len(KEPT) + 1], refs[len(KEPT) + 2 :]
    swapped, refs = refs[:carries], refs[carries:]
    grad_slab, padded, padded_grads, blended, result, send_one, receive_one, send_two, receive_two, send_swap, receive_swap = refs
    at = Layout(count).place()
    greet(at, mate=bool(carries))
    out = scatter_tasks(at, piece, grads, grad_slab, send_one, receive_one)
    out(False)
    swaps = [swap(at, one, two, send_swap, receive_swap) for one, two in zip(carried, swapped)]
    for one, source, target in zip(swaps, carried, swapped):
        one.start()
        target[pl.ds(at.group, 1)] = source[pl.ds(at.group, 1)]
    back = return_rows(at, piece, result, out_grads, send_two, receive_two)
    grad_taps[...] = jnp.zeros(grad_taps.shape, F32)

    @pl.when(at.owns)
    def _():
        await_slab(at, piece, grad_slab, receive_one)
        attend_back(
            whole(grad_slab, 0), whole(slab, 0), whole(slab, 1), whole(slab, 2), edges[pl.ds(at.micro, 1), :], head_taps(lines, at.pair),
            keep, padded, padded_grads, blended, result, grad_taps.at[at.pair],
        )
        back(False)

    out(True)
    await_rows(at, out_grads, receive_two)
    for one in swaps:
        one.wait()

    @pl.when(at.owns)
    def _():
        back(True)


VMEM = pl.BlockSpec(memory_space=pltpu.VMEM)
DMA = pltpu.SemaphoreType.DMA


def attention_forward(count, qkv, edges, lines, ident, low=None, spans=()):
    piece = qkv.shape[2]
    length = piece * count
    shapes = kept_shapes(length)
    low = low if spans else lines
    at = Layout(count)
    halved = (at.groups, length // at.groups, LANES)
    anywhere = pl.BlockSpec(memory_space=pl.ANY)
    results = pl.pallas_call(
        functools.partial(forward_kernel, count, piece, spans),
        out_shape=[
            jax.ShapeDtypeStruct((1, MICRO, piece, D), BF16),
            jax.ShapeDtypeStruct((3,) + halved, BF16),
        ]
        + [jax.ShapeDtypeStruct(shapes[name], F32) for name in KEPT]
        + [spread_shape(low, span) for span in spans],
        in_specs=[VMEM] * 4,
        out_specs=[VMEM] * (2 + len(KEPT)) + [anywhere] * len(spans),
        scratch_shapes=[
            pltpu.VMEM((length + LANES, LANES), BF16),
            pltpu.VMEM((length, LANES), F32),
            pltpu.VMEM((1,) + halved, BF16),
            DMA((at.tasks,)),
            DMA((at.members,)),
            DMA((at.members,)),
            DMA((at.tasks,)),
        ]
        + [one for span in spans for one in spread_semaphores(span)],
        compiler_params=pltpu.CompilerParams(collective_id=ident, has_side_effects=True, vmem_limit_bytes=60 << 20),
        name="attend_forward",
    )(qkv, edges, lines, low)
    return results[0][0], results[1 : 2 + len(KEPT)], [flat_rows(one) for one in results[2 + len(KEPT) :]]


def attention_backward(count, grads, edges, lines, kept, ident, carried=()):
    piece = grads.shape[2]
    length = piece * count
    at = Layout(count)
    halved = (at.groups, length // at.groups, LANES)
    results = pl.pallas_call(
        functools.partial(backward_kernel, count, piece, len(carried)),
        out_shape=[
            jax.ShapeDtypeStruct((3, MICRO, piece, D), BF16),
            jax.ShapeDtypeStruct((PAIRS, 2, 2 * LANES), F32),
        ]
        + [jax.ShapeDtypeStruct(one.shape, one.dtype) for one in carried],
        in_specs=[VMEM] * (4 + len(carried) + len(KEPT)),
        out_specs=[VMEM] * (2 + len(carried)),
        scratch_shapes=[
            pltpu.VMEM((1,) + halved, BF16),
            pltpu.VMEM((length + LANES, LANES), BF16),
            pltpu.VMEM((length + LANES, LANES), BF16),
            pltpu.VMEM((length, LANES), F32),
            pltpu.VMEM((3,) + halved, BF16),
            DMA((at.tasks,)),
            DMA((at.members,)),
            DMA((at.members,)),
            DMA((at.tasks,)),
            DMA,
            DMA,
        ],
        compiler_params=pltpu.CompilerParams(collective_id=ident, has_side_effects=True, vmem_limit_bytes=60 << 20),
        name="attend_backward",
    )(grads, edges, lines, *carried, *kept)
    return results[0], results[1], results[2:]


def arrange(sources, targets):
    params, first, second = sources
    lines, ups, sliced = targets[:LAYERS], targets[LAYERS : 2 * LAYERS], targets[2 * LAYERS :]
    for level in range(LAYERS):
        own = slice(level, level + 1)
        for line in range(TAP_LINE):
            lines[level][line : line + 1, :] = params[own, line * D : (line + 1) * D]
        lines[level][TAP_LINE:, :] = jnp.zeros((16 - TAP_LINE, D), F32)
        lines[level][TAP_LINE : TAP_LINE + 1, : HEADS * TAPS] = params[own, TAP_LINE * D :]
        ups[level][...] = params[own, 8 * D : 8 * D + FF]
    for source, target in zip((first, second), sliced):
        target[LAYERS * LINES // 2 :] = jnp.zeros((16 - LAYERS * LINES // 2, 2, D), F32)
        for level in range(LAYERS):
            own = slice(level, level + 1)
            for line in range(LINES):
                index = level * LINES + line
                spot = slice(index % 2, index % 2 + 1)
                if line < TAP_LINE:
                    target[index // 2, spot, :] = source[own, line * D : (line + 1) * D]
                else:
                    target[index // 2, spot, :] = jnp.zeros((1, D), F32)
                    target[index // 2, spot, : HEADS * TAPS] = source[own, TAP_LINE * D :]


ARRANGED = (
    [jax.ShapeDtypeStruct((16, D), F32)] * LAYERS + [jax.ShapeDtypeStruct((1, FF), F32)] * LAYERS + [jax.ShapeDtypeStruct((16, 2, D), F32)] * 2
)


def arrange_kernel(*refs):
    arrange(refs[:3], refs[3:])


def arranged(*smalls):
    return pl.pallas_call(arrange_kernel, out_shape=ARRANGED, in_specs=[VMEM] * 3, out_specs=[VMEM] * len(ARRANGED), name="arrange")(*smalls)


PLANES = 4
SUBS = 2
EVEN, ODD = range(0, SUBS, 2), range(1, SUBS, 2)


def gather_kernel(spans, low, params, first, second, hidden, cotangent, *refs):
    outs, refs = refs[: len(spans)], refs[len(spans) :]
    targets, refs = refs[: len(ARRANGED)], refs[len(ARRANGED) :]
    swapped, swap_sems, refs = refs[:2], refs[2], refs[3:]
    begin, steps, finish = spread_all(spans, low, outs, refs)
    at = Layout(16).place()
    me, x = lax.axis_index("dp"), lax.axis_index("rep")
    core, y, z = lax.rem(me, 2), lax.rem(me // 2, 2), me // 4
    barrier = pltpu.get_barrier_semaphore()
    for where in ({"rep": 1 - x}, {"dp": me + 2 - 4 * y}, {"dp": me + 1 - 2 * core}, at.mate()):
        pl.semaphore_signal(barrier, inc=1, device_id=where, device_id_type=MESH)
    for sign in (1, -1):

        @pl.when((z + sign >= 0) & (z + sign < PLANES))
        def _():
            pl.semaphore_signal(barrier, inc=1, device_id={"dp": me + 4 * sign}, device_id_type=MESH)

    pl.semaphore_wait(barrier, 5 + jnp.where((z > 0) & (z < PLANES - 1), 1, 0))
    begin()
    swaps = [swap(at, one, two, swap_sems.at[0, which], swap_sems.at[1, which]) for which, (one, two) in enumerate(zip((hidden, cotangent), swapped))]
    for one, source, target in zip(swaps, (hidden, cotangent), swapped):
        one.start()
        target[pl.ds(at.group, 1)] = source[pl.ds(at.group, 1)]
    arrange((params, first, second), targets)
    for step in steps:
        step()
    finish()
    for one in swaps:
        one.wait()


def spread_semaphores(span):
    planes = span[2] - span[1]
    return [DMA, DMA((planes, SUBS, 2)), DMA((planes, SUBS))] + [DMA((planes, 2, 2, SUBS))] * 5 + [DMA]


def spread_shape(low, span):
    return jax.ShapeDtypeStruct((span[2] - span[1], 2, 2) + low.shape[1:], BF16)


def flat_rows(blocks):
    return blocks.reshape(-1, D)


def spread_all(spans, low, outs, semaphores):
    each = len(semaphores) // max(len(spans), 1)
    parts = [
        spread(low.at[level], out, bottom, top, *semaphores[at * each : (at + 1) * each])
        for at, ((level, bottom, top), out) in enumerate(zip(spans, outs))
    ]

    def together(actions):
        def run():
            for action in actions:
                action()

        return run

    steps = [together(actions) for actions in zip(*[part[1] for part in parts])]
    return together([part[0] for part in parts]), steps, together([part[2] for part in parts])


def spread(shard, out, bottom, top, local_sem, z_send, z_got, x_send, x_got, y_send, y_got, core_send, core_got):
    me = lax.axis_index("dp")
    x = lax.axis_index("rep")
    core, y, z = lax.rem(me, 2), lax.rem(me // 2, 2), me // 4
    half = shard.shape[0] // 2
    part = half // SUBS

    def held(plane):
        return (plane >= bottom) & (plane < top)

    def peer(axis, sign=1):
        if axis == "x":
            return {"rep": 1 - x}
        if axis == "y":
            return {"dp": me + 2 - 4 * y}
        if axis == "core":
            return {"dp": me + 1 - 2 * core}
        return {"dp": me + 4 * sign}

    def rows(side, sub):
        return pl.ds(pl.multiple_of(side * half + sub * part, part), part)

    def remote(source, target, send, receive, where):
        return pltpu.make_async_remote_copy(source, target, send, receive, device_id=where, device_id_type=MESH)

    def spot(plane, row, side, sub):
        return out.at[plane - bottom, row, core, rows(side, sub), :]

    def move(axis, plane, row, side, sub, source=None):
        target = spot(plane, row, side, sub)
        source = target if source is None else source
        at = plane - bottom
        if axis == "core":
            return remote(source, target, core_send.at[at, row, side, sub], core_got, peer("core"))
        send, receive = (x_send, x_got) if axis == "x" else (y_send, y_got)
        return remote(source, target, send.at[at, row, side, sub], receive.at[at, row, side, sub], peer(axis))

    def climb(plane, sub, sign, source=None):
        target = spot(plane, y, x, sub)
        way = 0 if sign > 0 else 1
        at = plane - bottom
        return remote(target if source is None else source, target, z_send.at[at, sub, way], z_got.at[at, sub], peer("z", sign))

    def inside(sign, act):
        pl.when((z + sign >= 0) & (z + sign < PLANES))(act)

    def begin():
        @pl.when(held(z))
        def _():
            pltpu.make_async_copy(shard, out.at[z - bottom, y, core], local_sem).start()
            for sub in range(SUBS):
                for sign in (1, -1):
                    inside(sign, lambda: climb(z, sub, sign, shard.at[rows(x, sub), :]).start())
                move("y", z, y, x, sub, shard.at[rows(x, sub), :]).start()
            for side in range(2):
                for sub in range(SUBS):
                    move("core", z, y, side, sub, shard.at[rows(side, sub), :]).start()

    def at_distance(distance, act):
        for sign in (1, -1):
            plane = z - sign * distance

            @pl.when(held(plane))
            def _():
                act(plane, sign)

    def from_z(plane, sign):
        for sub in range(SUBS):
            climb(plane, sub, sign).wait_recv()
            inside(sign, lambda: climb(plane, sub, sign).start())
            for axis in ("x", "y", "core"):
                move(axis, plane, y, x, sub).start()

    def take(axis, plane, row, side, sub, onward=None):
        move(axis, plane, row, side, sub).wait_recv()
        if onward is not None:
            move(onward, plane, row, side, sub).start()
        move("core", plane, row, side, sub).start()

    def first_square(plane, sign):
        for even, odd in zip(EVEN, ODD):
            take("x", plane, y, 1 - x, even, "y")
            take("y", plane, 1 - y, x, odd, "x")
            take("y", plane, 1 - y, x, even)
            take("x", plane, y, 1 - x, odd)

    def second_square(plane, sign):
        for even, odd in zip(EVEN, ODD):
            take("y", plane, 1 - y, 1 - x, even)
            take("x", plane, 1 - y, 1 - x, odd)

    def own_first():
        @pl.when(held(z))
        def _():
            for sub in range(SUBS):
                take("y", z, 1 - y, x, sub, "x")

    def own_last():
        @pl.when(held(z))
        def _():
            for sub in range(SUBS):
                take("x", z, 1 - y, 1 - x, sub)

    def stage(distance, act):
        return lambda: at_distance(distance, act)

    steps = [
        stage(1, from_z), own_first, stage(2, from_z), stage(1, first_square), stage(3, from_z), stage(2, first_square),
        own_last, stage(1, second_square), stage(3, first_square), stage(2, second_square), stage(3, second_square),
    ]

    def sent(plane, sign):
        for sub in range(SUBS):
            inside(sign, lambda: climb(plane, sub, sign).wait_send())
            move("x", plane, y, x, sub).wait_send()
            move("y", plane, y, x, sub).wait_send()
        for even, odd in zip(EVEN, ODD):
            move("y", plane, y, 1 - x, even).wait_send()
            move("x", plane, 1 - y, x, odd).wait_send()

    def finish():
        for distance in (1, 2, 3):
            at_distance(distance, sent)

        @pl.when(held(z))
        def _():
            pltpu.make_async_copy(shard, out.at[z - bottom, y, core], local_sem).wait()
            for sub in range(SUBS):
                for sign in (1, -1):
                    inside(sign, lambda: climb(z, sub, sign).wait_send())
                move("y", z, y, x, sub).wait_send()
                move("x", z, 1 - y, x, sub).wait_send()

        def core_sent(index, carry):
            plane, row = bottom + index // (4 * SUBS), lax.rem(index // (2 * SUBS), 2)
            side, sub = lax.rem(index // SUBS, 2), lax.rem(index, SUBS)
            move("core", plane, row, side, sub).wait_send()
            return carry

        lax.fori_loop(0, 4 * SUBS * (top - bottom), core_sent, 0)
        column = out.at[:, :, 1 - core]
        pltpu.make_async_copy(column, column, core_got).wait()

    return begin, steps, finish


def gather(low, spans, hidden, cotangent, *smalls):
    results = pl.pallas_call(
        functools.partial(gather_kernel, spans),
        out_shape=[spread_shape(low, span) for span in spans] + ARRANGED + [jax.ShapeDtypeStruct(hidden.shape, BF16)] * 2,
        in_specs=[VMEM] * 6,
        out_specs=[pl.BlockSpec(memory_space=pl.ANY)] * len(spans) + [VMEM] * (len(ARRANGED) + 2),
        scratch_shapes=[DMA((2, 2))] + [one for span in spans for one in spread_semaphores(span)],
        compiler_params=pltpu.CompilerParams(collective_id=4, has_side_effects=True),
        name="gather",
    )(low, *smalls, hidden, cotangent)
    return [flat_rows(one) for one in results[: len(spans)]], results[len(spans) : -2], results[-2:]


CHUNK = 32
RING = 12
CYCLE = 6
MATES = ("low_in", "low_comb", "low_up", "low_act", "low_grads", "low_branch", "low_hidden", "low_down", "gain_one", "shift_one", "gain_two", "shift_two", "taps")


def change(grad, first_old, second_old):
    new_first = ADAM_ONE * first_old + (1.0 - ADAM_ONE) * grad
    new_second = ADAM_TWO * second_old + (1.0 - ADAM_TWO) * grad * grad
    return new_first * (1.0 / (1.0 - ADAM_ONE**STEP_COUNT)) / (jnp.sqrt(new_second * (1.0 / (1.0 - ADAM_TWO**STEP_COUNT))) + ADAM_EPSILON)


def settle_kernel(block_rows, *refs):
    count = len(MATES)
    mates = [dict(zip(MATES, refs[level * count : (level + 1) * count])) for level in range(LAYERS)]
    (
        weights, first, second, small_first, small_second, grad_in, grad_out, mean_out, small_out, grad_in_out,
        turned, right, staged, own, got_core, got_y, got_near, got_far, inner, step_own, step_got, small, small_got, small_own, small_step, small_step_got,
        core_send, core_got, y_send, y_got, near_send, near_got, far_send, far_got, inner_sem, rep_send, rep_got, small_send, small_sem, back_send, back_sem, small_rep, swap_sems,
    ) = refs[LAYERS * count :]
    me = lax.axis_index("dp")
    other_rep = 1 - lax.axis_index("rep")
    core, y, z = lax.rem(me, 2), lax.rem(me // 2, 2), me // 4
    devices = 16
    per_layer = block_rows // CHUNK
    chunks = LAYERS * per_layer

    barrier = pltpu.get_barrier_semaphore()

    def signal(step, carry):
        pl.semaphore_signal(barrier, inc=1, device_id={"dp": lax.rem(me + step, devices)}, device_id_type=MESH)
        return carry

    lax.fori_loop(1, devices, signal, 0)
    pl.semaphore_signal(barrier, inc=1, device_id={"rep": other_rep}, device_id_type=MESH)

    def to_dp(source, target, send, receive, peer):
        return pltpu.make_async_remote_copy(source, target, send, receive, device_id={"dp": peer}, device_id_type=MESH)

    def to_rep(source, target, send, receive):
        return pltpu.make_async_remote_copy(source, target, send, receive, device_id={"rep": other_rep}, device_id_type=MESH)

    def spot(slot):
        return lax.rem(slot, RING)

    features = D * 2 + FF * 2
    for order, level in enumerate(reversed(range(LAYERS))):
        mate = mates[level]
        at = order * features
        for name in MATES[:4]:
            for part in range(mate[name].shape[1] // LANES):
                turned[at : at + LANES, :] = mate[name][:, part * LANES : (part + 1) * LANES].T
                at += LANES
        for part in range(3):
            right[order * 6 + part] = mate["low_grads"][part]
        for part, name in enumerate(MATES[5:8]):
            right[order * 6 + 3 + part] = mate[name][...]

    def put(level, line, row):
        index = level * LINES + line
        small[index // 2, index % 2 : index % 2 + 1, :] = row

    def column_sum(array):
        return jnp.sum(array.astype(F32), axis=0, keepdims=True)

    for level in range(LAYERS):
        mate = mates[level]
        put(level, 0, column_sum(mate["low_grads"][0]))
        put(level, 1, column_sum(mate["low_grads"][2]))
        put(level, 2, column_sum(mate["low_branch"][...]))
        put(level, 3, column_sum(mate["low_down"][...]))
        for line, name in enumerate(MATES[8:12]):
            put(level, 4 + line, column_sum(mate[name][...]))
        for part in range(FF // D):
            put(level, 8 + part, column_sum(mate["low_up"][:, part * D : (part + 1) * D]))
        line = jnp.zeros((1, D), F32)
        for head in range(HEADS):
            taps = jnp.concatenate([mate["taps"][head // 2][head % 2 : head % 2 + 1], jnp.zeros((1, D - 2 * LANES), F32)], axis=1)
            taps = jnp.where(iota((1, D), 1) < TAPS, taps, 0.0)
            line = line + (pltpu.roll(taps, TAPS * head, 1) if head else taps)
        put(level, 12, line)
    for index in range(LAYERS * LINES, 2 * devices):
        small[index // 2, index % 2 : index % 2 + 1, :] = jnp.zeros((1, D), F32)

    pl.semaphore_wait(barrier, devices)

    at_layout = Layout(16).place()
    swapping = swap(at_layout, grad_in, grad_in_out, swap_sems.at[0], swap_sems.at[1])
    swapping.start()
    grad_in_out[pl.ds(at_layout.group, 1)] = grad_in[pl.ds(at_layout.group, 1)]

    def small_copy(step):
        peer = lax.rem(me + step, devices)
        return to_dp(small.at[peer], small_got.at[me], small_send.at[peer], small_sem.at[me], peer)

    def small_begin(step, carry):
        small_copy(step).start()
        return carry

    lax.fori_loop(1, devices, small_begin, 0)

    def core_copy(chunk):
        return to_dp(staged.at[lax.rem(chunk, 2)], got_core.at[spot(chunk)], core_send.at[lax.rem(chunk, 2)], core_got.at[spot(chunk)], me + 1 - 2 * core)

    near, far = z + 1 - 2 * lax.rem(z, 2), 3 - z

    def plane_device(plane):
        return plane * 4 + lax.rem(me, 4)

    def y_copy(chunk, full):
        slot = spot(chunk)
        source, target = (own.at[slot, :, 1 - y], got_y.at[slot]) if full else (own.at[slot, z, 1 - y], got_y.at[slot, 0])
        return to_dp(source, target, y_send.at[slot], y_got.at[slot], me + 2 - 4 * y)

    def near_copy(chunk, which, full):
        slot, block = spot(chunk), 3 - near if which else near
        source, target = (own.at[slot, block], got_near.at[slot, which]) if full else (own.at[slot, block, y], got_near.at[slot, which, 0])
        return to_dp(source, target, near_send.at[slot, which], near_got.at[slot, which], plane_device(near))

    def far_copy(chunk, full):
        slot = spot(chunk)
        source, target = (own.at[slot, far], got_far.at[slot]) if full else (own.at[slot, far, y], got_far.at[slot, 0])
        return to_dp(source, target, far_send.at[slot], far_got.at[slot], plane_device(far))

    def by_order(chunk, y_first, z_first):
        turn_z = lax.rem(chunk, CYCLE) == CYCLE // 2
        pl.when(jnp.logical_not(turn_z))(y_first)
        pl.when(turn_z)(z_first)

    def place(chunk):
        return LAYERS - 1 - chunk // per_layer, pl.ds(pl.multiple_of(lax.rem(chunk, per_layer) * CHUNK, CHUNK), CHUNK)

    def inner_copies(chunk):
        level, rows = place(chunk)
        slot = lax.rem(chunk, 4)
        return [
            pltpu.make_async_copy(array.at[level, rows, :], inner.at[slot, index], inner_sem.at[slot, index])
            for index, array in enumerate((weights, first, second))
        ]

    def rep_copy(chunk):
        return to_rep(step_own.at[spot(chunk)], step_got.at[spot(chunk)], rep_send.at[spot(chunk)], rep_got.at[spot(chunk)])

    def product(chunk, there, row, side):
        order = chunk // per_layer
        block = (there * 2 + row) * 2 + side
        piece = block * per_layer + lax.rem(chunk, per_layer)
        narrow = D // CHUNK
        line = jnp.where(piece < 3 * narrow, lax.rem(piece, narrow), piece - 2 * narrow)
        group = jnp.where(piece < 4 * narrow, piece // narrow, jnp.where(piece < 4 * narrow + FF // CHUNK, 4, 5))
        rows = pl.ds(pl.multiple_of(order * features + line * CHUNK, 16), CHUNK)
        return mm(turned[rows, :], right[order * 6 + group]).astype(BF16)

    def stage_product(chunk):
        for there in range(4):
            for row in range(2):
                staged[lax.rem(chunk, 2), there, row] = product(chunk, there, row, 1 - core)
        core_copy(chunk).start()
        for there in range(4):
            for row in range(2):
                own[spot(chunk), there, row] = product(chunk, there, row, core)

    def stage_core(chunk):
        core_copy(chunk).wait()
        slot = spot(chunk)
        for there in range(4):
            for side in range(2):
                own[slot, there, side] = own[slot, there, side] + got_core[slot, there, side]

        def z_first():
            for which in range(2):
                near_copy(chunk, which, True).start()

        by_order(chunk, lambda: y_copy(chunk, True).start(), z_first)

    def stage_second(chunk):
        slot = spot(chunk)

        def y_first():
            y_copy(chunk, True).wait()
            for there in range(4):
                own[slot, there, y] = own[slot, there, y] + got_y[slot, there]
            for which in range(2):
                near_copy(chunk, which, False).start()

        def z_first():
            for which in range(2):
                near_copy(chunk, which, True).wait()
            for row in range(2):
                own[slot, far, row] = own[slot, far, row] + got_near[slot, 1, row]
                own[slot, z, row] = own[slot, z, row] + got_near[slot, 0, row]
            far_copy(chunk, True).start()

        by_order(chunk, y_first, z_first)

    def stage_third(chunk):
        slot = spot(chunk)

        def y_first():
            for which in range(2):
                near_copy(chunk, which, False).wait()
            own[slot, far, y] = own[slot, far, y] + got_near[slot, 1, 0]
            own[slot, z, y] = own[slot, z, y] + got_near[slot, 0, 0]
            far_copy(chunk, False).start()

        def z_first():
            far_copy(chunk, True).wait()
            for row in range(2):
                own[slot, z, row] = own[slot, z, row] + got_far[slot, row]
            y_copy(chunk, False).start()

        by_order(chunk, y_first, z_first)
        for copy in inner_copies(chunk):
            copy.start()

    def stage_last(chunk):
        for copy in inner_copies(chunk):
            copy.wait()
        by_order(chunk, lambda: far_copy(chunk, False).wait(), lambda: y_copy(chunk, False).wait())
        slot = spot(chunk)
        turn_z = lax.rem(chunk, CYCLE) == CYCLE // 2
        total = own[slot, z, y].astype(F32) + jnp.where(turn_z, got_y[slot, 0].astype(F32), got_far[slot, 0].astype(F32))
        level, rows = place(chunk)
        grad_out[level, rows, :] = total
        slot = lax.rem(chunk, 4)
        step = change(total, inner[slot, 1], inner[slot, 2]) + WEIGHT_DECAY * inner[slot, 0]
        step_own[spot(chunk)] = (LR_INNER * step).astype(BF16)
        rep_copy(chunk).start()

    def stage_rep(chunk):
        rep_copy(chunk).wait()
        level, rows = place(chunk)
        mean_out[level, rows, :] = 0.5 * (step_own[spot(chunk)].astype(F32) + step_got[spot(chunk)].astype(F32))

    def small_rep_copy():
        return to_rep(small_step, small_step_got, small_rep.at[0], small_rep.at[1])

    def small_back(step):
        peer = lax.rem(me + step, devices)
        return to_dp(small_own, small_out.at[me], back_send.at[peer], back_sem.at[me], peer)

    def small_sum():
        def add(step, total):
            peer = lax.rem(me + step, devices)
            pltpu.make_async_copy(small_got.at[peer], small_got.at[peer], small_sem.at[peer]).wait()
            return total + small_got[peer]

        total = lax.fori_loop(1, devices, add, small[me])
        small_own[0] = total
        small_step[...] = (LR_SMALL * change(total, small_first[me], small_second[me])).astype(BF16)
        small_rep_copy().start()

    def small_spread():
        small_rep_copy().wait_recv()
        small_own[1] = 0.5 * (small_step[...].astype(F32) + small_step_got[...].astype(F32))
        small_out[me] = small_own[...]

        def send(step, carry):
            small_back(step).start()
            return carry

        lax.fori_loop(1, devices, send, 0)

    def turn(now, carry):
        for lag, stage in ((0, stage_product), (1, stage_core), (3, stage_second), (5, stage_third), (7, stage_last), (9, stage_rep)):

            @pl.when((now >= lag) & (now < chunks + lag))
            def _():
                stage(now - lag)

        pl.when(now == 4)(small_sum)
        pl.when(now == 7)(small_spread)
        return carry

    lax.fori_loop(0, chunks + 9, turn, 0)

    def small_drain(step, carry):
        peer = lax.rem(me + step, devices)
        small_copy(step).wait_send()
        small_back(step).wait_send()
        pltpu.make_async_copy(small_own, small_out.at[peer], back_sem.at[peer]).wait()
        return carry

    lax.fori_loop(1, devices, small_drain, 0)
    small_rep_copy().wait_send()
    swapping.wait()


def settle(mates, weights, first, second, small_first, small_second, grad_in):
    block_rows = weights.shape[1]
    anywhere = pl.BlockSpec(memory_space=pl.ANY)
    devices = 16
    piece = (CHUNK, D)
    tokens = mates[0]["low_in"].shape[0]
    return pl.pallas_call(
        functools.partial(settle_kernel, block_rows),
        out_shape=[
            jax.ShapeDtypeStruct(weights.shape, F32),
            jax.ShapeDtypeStruct(weights.shape, F32),
            jax.ShapeDtypeStruct((devices, 2, 2, D), F32),
            jax.ShapeDtypeStruct(grad_in.shape, F32),
        ],
        in_specs=[VMEM] * (LAYERS * len(MATES)) + [anywhere] * 3 + [VMEM] * 3,
        out_specs=[VMEM] * 4,
        scratch_shapes=[
            pltpu.VMEM((LAYERS * 2 * (D + FF), tokens), BF16),
            pltpu.VMEM((LAYERS * 6, tokens, D), BF16),
            pltpu.VMEM((2, 4, 2) + piece, BF16),
            pltpu.VMEM((RING, 4, 2) + piece, BF16),
            pltpu.VMEM((RING, 4, 2) + piece, BF16),
            pltpu.VMEM((RING, 4) + piece, BF16),
            pltpu.VMEM((RING, 2, 2) + piece, BF16),
            pltpu.VMEM((RING, 2) + piece, BF16),
            pltpu.VMEM((4, 3) + piece, F32),
            pltpu.VMEM((RING,) + piece, BF16),
            pltpu.VMEM((RING,) + piece, BF16),
            pltpu.VMEM((devices, 2, D), F32),
            pltpu.VMEM((devices, 2, D), F32),
            pltpu.VMEM((2, 2, D), F32),
            pltpu.VMEM((2, D), BF16),
            pltpu.VMEM((2, D), BF16),
            DMA((2,)),
            DMA((RING,)),
            DMA((RING,)),
            DMA((RING,)),
            DMA((RING, 2)),
            DMA((RING, 2)),
            DMA((RING,)),
            DMA((RING,)),
            DMA((4, 3)),
            DMA((RING,)),
            DMA((RING,)),
            DMA((devices,)),
            DMA((devices,)),
            DMA((devices,)),
            DMA((devices,)),
            DMA((2,)),
            DMA((2,)),
        ],
        compiler_params=pltpu.CompilerParams(collective_id=3, has_side_effects=True, vmem_limit_bytes=63 << 20),
        name="settle",
    )(*[mate[name] for mate in mates for name in MATES], weights, first, second, small_first, small_second, grad_in)


def finish_kernel(both, params, outer, first, second, first_new, second_new, outer_new, params_new, grad, mean):
    for level in range(LAYERS):
        for line in range(LINES):
            index = level * LINES + line
            spot = slice(index % 2, index % 2 + 1)
            for which, target in ((0, grad), (1, mean)):
                target[level : level + 1, line * D : (line + 1) * D] = both[index // 2, which, spot, :]
    first_new[...], second_new[...] = moments(first[...], second[...], grad[:, :SMALL])
    momentum = MOMENTUM * outer[...] + mean[:, :SMALL]
    outer_new[...] = momentum
    params_new[...] = params[...] - LR_OUTER * (mean[:, :SMALL] + MOMENTUM * momentum)


def finish(both, params, outer, first, second):
    wide = pltpu.VMEM((LAYERS, LINES * D), F32)
    return pl.pallas_call(
        finish_kernel,
        out_shape=[jax.ShapeDtypeStruct(params.shape, F32)] * 4,
        in_specs=[VMEM] * 5,
        out_specs=[VMEM] * 4,
        scratch_shapes=[wide, wide],
        name="finish",
    )(both, params, outer, first, second)


def dense(a, b, dims=NN):
    return mm(a, b, dims)


def standard(values):
    centred = values - jnp.mean(values, axis=-1, keepdims=True)
    scale = lax.rsqrt(jnp.mean(centred * centred, axis=-1, keepdims=True) + 1e-05)
    return centred * scale, scale


def layer_norm(values, gain, shift):
    return standard(values)[0] * gain + shift


def layer_norm_back(values, gain, grad):
    unit_values, scale = standard(values)
    inner = grad * gain
    along = jnp.mean(inner * unit_values, axis=-1, keepdims=True)
    result = scale * (inner - jnp.mean(inner, axis=-1, keepdims=True) - unit_values * along)
    return result, eighths(grad * unit_values), eighths(grad)


def eighths(rows):
    return jnp.sum(rows.reshape(-1, 8, D), axis=0)


def split_rows(rest):
    return rest[:D], rest[D : D + FF], rest[D + FF :]


def forward_layer(count, inputs, proj, rest, small, edges, ident, low=None, spans=()):
    piece = inputs.shape[0] // MICRO
    lines, bias_up = small
    proj = proj.reshape(3, D, D)
    low_in = inputs.astype(BF16)
    query = (dense(low_in, proj[0]) + lines[0:1]).astype(BF16)
    key = dense(low_in, proj[1]).astype(BF16)
    value = (dense(low_in, proj[2]) + lines[1:2]).astype(BF16)
    qkv = jnp.stack([query, key, value])
    low_comb, kept, fetched = attention_forward(count, qkv.reshape(3, MICRO, piece, D), edges, lines, ident, low, spans)
    out_weight, up_weight, down_weight = split_rows(rest)
    low_comb = low_comb.reshape(MICRO * piece, D)
    resid_one = inputs + (dense(low_comb, out_weight) + lines[2:3])
    hidden_one = layer_norm(resid_one, lines[4:5], lines[5:6])
    low_hidden = hidden_one.astype(BF16)
    upward = dense(low_hidden, up_weight, NT) + bias_up
    low_act = jax.nn.gelu(upward).astype(BF16)
    resid_two = hidden_one + (dense(low_act, down_weight) + lines[3:4])
    output = layer_norm(resid_two, lines[6:7], lines[7:8])
    return output, (proj, rest, low_in, kept, low_comb, resid_one, low_hidden, upward, low_act, resid_two), fetched


def backward_layer(count, grad_output, small, edges, state, ident, carried=()):
    proj, rest, low_in, kept, low_comb, resid_one, low_hidden, upward, low_act, resid_two = state
    total = low_in.shape[0]
    piece = total // MICRO
    lines, _ = small
    out_weight, up_weight, down_weight = split_rows(rest)
    grad_two, grad_gain_two, grad_shift_two = layer_norm_back(resid_two, lines[6:7], grad_output)
    low_down = grad_two.astype(BF16)
    grad_act = dense(low_down, down_weight, NT)
    _, pull_gelu = jax.vjp(jax.nn.gelu, upward)
    low_up = pull_gelu(grad_act)[0].astype(BF16)
    grad_hidden = grad_two + dense(low_up, up_weight)
    grad_one, grad_gain_one, grad_shift_one = layer_norm_back(resid_one, lines[4:5], grad_hidden)
    low_branch = grad_one.astype(BF16)
    grad_comb = dense(low_branch, out_weight, NT).astype(BF16)
    low_grads, grad_taps, swapped = attention_backward(count, grad_comb.reshape(1, MICRO, piece, D), edges, lines, kept, ident, carried)
    low_grads = low_grads.reshape(3, total, D)
    grad_in = grad_one + sum(dense(low_grads[part], proj[part], NT) for part in range(3))
    vectors = (grad_gain_one, grad_shift_one, grad_gain_two, grad_shift_two)
    values = (low_in, low_comb, low_up, low_act, low_grads, low_branch, low_hidden, low_down, *vectors, grad_taps)
    return grad_in, dict(zip(MATES, values)), swapped


def plain_grads(mate):
    parts = [dense(mate["low_in"], mate["low_grads"][part], TN) for part in range(3)]
    parts = parts + [dense(mate[left], mate[right], TN) for left, right in (("low_comb", "low_branch"), ("low_up", "low_hidden"), ("low_act", "low_down"))]
    sums = [mate["low_grads"][0], mate["low_grads"][2], mate["low_branch"], mate["low_down"]]
    sums = [jnp.sum(one.astype(F32), axis=0) for one in sums]
    sums = sums + [jnp.sum(mate[name], axis=0) for name in MATES[8:12]]
    sums = sums + [jnp.sum(mate["low_up"].astype(F32), axis=0), mate["taps"][:, :, :TAPS].reshape(-1)]
    return jnp.concatenate(parts, axis=0).astype(BF16), jnp.concatenate(sums)


def moments(first, second, grad):
    return ADAM_ONE * first + (1.0 - ADAM_ONE) * grad, ADAM_TWO * second + (1.0 - ADAM_TWO) * grad * grad


def adam(weights, first, second, grad, rate, decay):
    correct_one = 1.0 - ADAM_ONE**STEP_COUNT
    correct_two = 1.0 - ADAM_TWO**STEP_COUNT
    new_first, new_second = moments(first, second, grad)
    step = new_first / correct_one / (jnp.sqrt(new_second / correct_two) + ADAM_EPSILON)
    return new_first, new_second, rate * (step + decay * weights)


def shards(
    hidden,
    bounds,
    cotangent,
    weights,
    small_params,
    first_big,
    second_big,
    first_small,
    second_small,
    outer_big,
    outer_small,
):
    count = lax.axis_size("dp")
    piece = hidden.shape[3]
    total = MICRO * piece
    low_weights = weights.astype(BF16)
    limits = bounds[0, :, 0, :]
    edges = jnp.pad(limits.astype(F32), ((0, 0), (0, LANES - limits.shape[1])))
    own_hidden, own_cotangent = hidden[0, :, 0], cotangent[0, :, 0]
    me = lax.axis_index("dp")
    start, last = me * piece, limits[:, -1].reshape(MICRO, 1, 1)
    if count == 16:
        (proj, rest), prepared, (own_hidden, own_cotangent) = gather(
            low_weights, ((0, 0, 1), (0, 1, PLANES)), own_hidden, own_cotangent, small_params, first_small[0], second_small[0]
        )
        half = count // MICRO
        start = (lax.broadcasted_iota(jnp.int32, (MICRO, 1, 1), 0) * half + lax.rem(me, half)) * piece
        last = jnp.where(me < half, limits[0, -1], limits[1, -1])
    else:
        prepared = arranged(small_params, first_small[0], second_small[0])
    positions = start + lax.broadcasted_iota(jnp.int32, (MICRO, piece, 1), 1)
    valid = positions < last
    activation = own_hidden.reshape(total, D).astype(F32)
    states = [None] * LAYERS
    smalls = [(prepared[level], prepared[LAYERS + level]) for level in range(LAYERS)]
    for level in range(LAYERS):
        if count == 16:
            spans = ((level + 1, 0, 1), (level + 1, 1, PLANES)) if level + 1 < LAYERS else ()
            activation, states[level], more = forward_layer(
                count, activation, proj, rest, smalls[level], edges, 1 + 4 * level, low_weights, spans
            )
            proj, rest = more or (None, None)
        else:
            rows = lax.all_gather(low_weights[level], "dp", axis=0, tiled=True)
            activation, states[level], _ = forward_layer(count, activation, rows[: 3 * D], rows[3 * D :], smalls[level], edges, 1)
    gradient = jnp.where(valid, own_cotangent.astype(F32), 0.0).reshape(total, D)
    mates = [None] * LAYERS
    for level in reversed(range(LAYERS)):
        carried = (activation.reshape(MICRO, piece, D),) if count == 16 and level == LAYERS - 1 else ()
        gradient, mates[level], swapped = backward_layer(count, gradient, smalls[level], edges, states[level], 2 + 4 * level, carried)
        activation = swapped[0] if carried else activation
    if count == 16:
        grad_big, mean_big, small_both, gradient = settle(
            mates, weights, first_big[0], second_big[0], *prepared[2 * LAYERS :], gradient.reshape(MICRO, piece, D)
        )
        new_smalls = finish(small_both, small_params, outer_small, first_small[0], second_small[0])
    else:
        rows, sums = zip(*[plain_grads(mate) for mate in mates])
        grad_big = jnp.stack([lax.psum_scatter(one, "dp", scatter_dimension=0, tiled=True).astype(F32) for one in rows])
        grad_small = lax.psum(jnp.stack(sums), "dp")
        reps = lax.axis_size("rep")
        delta_big = adam(weights, first_big[0], second_big[0], grad_big, LR_INNER, WEIGHT_DECAY)[2]
        delta_small = adam(small_params, first_small[0], second_small[0], grad_small, LR_SMALL, 0.0)[2]
        mean_big = lax.psum(delta_big.astype(BF16), "rep").astype(F32) / reps
        mean_small = lax.psum(delta_small.astype(BF16), "rep").astype(F32) / reps
        momentum = MOMENTUM * outer_small + mean_small
        new_smalls = (*moments(first_small[0], second_small[0], grad_small), momentum, small_params - LR_OUTER * (mean_small + MOMENTUM * momentum))
    new_first, new_second = moments(first_big[0], second_big[0], grad_big)
    new_first_small, new_second_small, outer_small_new, small_new = new_smalls
    outer_big_new = MOMENTUM * outer_big + mean_big
    weights_new = weights - LR_OUTER * (mean_big + MOMENTUM * outer_big_new)
    shape = (1, MICRO, 1, piece, D)
    return (
        activation.reshape(shape),
        gradient.reshape(shape),
        new_first[None],
        new_second[None],
        new_first_small[None],
        new_second_small[None],
        outer_big_new,
        outer_small_new,
        weights_new,
        small_new,
        weights_new.astype(BF16),
    )


def solution(mesh):
    placed = (
        P("rep", None, None, "dp", None),
        P("rep", None, None, None),
        P("rep", None, None, "dp", None),
        P(None, "dp", None),
        P(),
        P("rep", None, "dp", None),
        P("rep", None, "dp", None),
        P("rep", None, None),
        P("rep", None, None),
        P(None, "dp", None),
        P(),
    )
    return jax.shard_map(
        shards,
        mesh=mesh,
        in_specs=placed,
        out_specs=(
            P("rep", None, None, "dp", None),
            P("rep", None, None, "dp", None),
            P("rep", None, "dp", None),
            P("rep", None, "dp", None),
            P("rep", None, None),
            P("rep", None, None),
            P(None, "dp", None),
            P(),
            P(None, "dp", None),
            P(),
            P(None, "dp", None),
        ),
        check_vma=False,
    )
```

```python
import functools

import jax
import jax.numpy as jnp
from jax import lax
from jax.experimental import pallas as pl
from jax.experimental.pallas import tpu as pltpu
from jax.sharding import PartitionSpec as P

D = 768
HEADS = 12
FF = 3072
TAPS = 33
NS_ITERS = 6
LAYERS = 2
MICRO = 2
STEP_COUNT = 5


ADAM_ONE = 0.9
ADAM_TWO = 0.95
ADAM_EPSILON = 1e-08
WEIGHT_DECAY = 0.1
LR_INNER = 0.04
LR_SMALL = 0.2
LR_OUTER = 0.7
MOMENTUM = 0.9

HEAD_DIM = 64
MARKS = 64
HALF = TAPS // 2
PAIRS = HEADS // 2
LINES = 13
TAP_LINE = 12
SMALL = 8 * D + FF + HEADS * TAPS
LANES = 128
SCALE = HEAD_DIM**-0.5
NEG = -1e30
MESH = pl.DeviceIdType.MESH
F32 = jnp.float32
BF16 = jnp.bfloat16
NN = (((1,), (0,)), ((), ()))
NT = (((1,), (1,)), ((), ()))
TN = (((0,), (0,)), ((), ()))


def mm(a, b, dims=NN):
    return lax.dot_general(a, b, dims, preferred_element_type=F32)


def halves(a):
    high = a.astype(BF16)
    return high, (a - high.astype(F32)).astype(BF16)


def mm_left(a, b, dims=NN):
    high, rest = halves(a)
    return mm(high, b, dims) + mm(rest, b, dims)


def mm_both(a, b, dims=NN):
    ah, al = halves(a)
    bh, bl = halves(b)
    return mm(ah, bh, dims) + (mm(ah, bl, dims) + mm(al, bh, dims))


def exact(a, b, dims=NN):
    return mm_both(a, b, dims)


def iota(shape, dim):
    return lax.broadcasted_iota(jnp.int32, shape, dim)


def diagonal_blocks():
    return (iota((LANES, LANES), 0) < MARKS) == (iota((LANES, LANES), 1) < HEAD_DIM)


def unit():
    return (iota((LANES, LANES), 0) == iota((LANES, LANES), 1)).astype(F32)


def per_head(marks):
    first = iota(marks.shape, 1) < HEAD_DIM
    return jnp.concatenate([jnp.where(first, marks, 0.0), jnp.where(first, 0.0, marks)], axis=0)


def head_sums(a):
    rows, cols = a.shape
    split = a.reshape(2, rows // 2, cols)
    return jnp.broadcast_to(jnp.sum(split, axis=1, keepdims=True), split.shape).reshape(rows, cols)


def head_tops(a):
    rows, cols = a.shape
    split = a.reshape(2, rows // 2, cols)
    return jnp.broadcast_to(jnp.max(split, axis=1, keepdims=True), split.shape).reshape(rows, cols)


def head_taps(lines, pair):
    row = jnp.broadcast_to(lines[TAP_LINE : TAP_LINE + 1, :], (8, D))
    rows = []
    for side in range(2):
        turned = pltpu.roll(row, lax.rem(D - TAPS * (2 * pair + side), D), 1)[0:1, : 2 * LANES]
        rows.append(jnp.where(iota((1, 2 * LANES), 1) < TAPS, turned, 0.0))
    return rows


def band(taps_row):
    wide = jnp.broadcast_to(taps_row, (LANES, 2 * LANES))
    return pltpu.roll(wide, 0, 1, stride=1, stride_axis=0)


def band_back(taps_row):
    wide = jnp.broadcast_to(taps_row, (2 * LANES, 2 * LANES))
    return pltpu.roll(wide, 2 * LANES - 2 * HALF, 1, stride=1, stride_axis=0)[:, :LANES].T


def mark_columns(edges):
    low = jnp.broadcast_to(edges, (LANES, LANES)).T[:MARKS, :1]
    high = jnp.broadcast_to(pltpu.roll(edges, LANES - 1, 1), (LANES, LANES)).T[:MARKS, :1]
    return low.astype(jnp.int32), high.astype(jnp.int32)


def mark_rows(edges):
    low, high = edges[:, :MARKS], pltpu.roll(edges, LANES - 1, 1)[:, :MARKS]
    return low.astype(jnp.int32), high.astype(jnp.int32)


def convolve(padded, bands, length, store):
    first = iota((LANES, LANES), 1) < HEAD_DIM
    pairs = [halves(one) for one in bands]

    def block(at, carry):
        start = pl.multiple_of(at * LANES, LANES)
        window = padded[pl.ds(start, 2 * LANES), :]
        out = [mm(high, window) + mm(rest, window) for high, rest in pairs]
        store(start, jnp.where(first, out[0], out[1]))
        return carry

    lax.fori_loop(0, length // LANES, block, 0)


def put_rows(ref, at, start, rows):
    half = ref.shape[2]
    ref[at, start // half, pl.ds(pl.multiple_of(lax.rem(start, half), LANES), LANES), :] = rows


def whole(ref, at):
    return ref[at].reshape(-1, LANES)


def attend(slab, edges, taps, keep, padded, blended, result):
    length = slab.shape[1] * slab.shape[2]

    def begin():
        low_marks, high_marks = mark_columns(edges())
        at = iota((MARKS, length), 1)
        member = ((low_marks <= at) & (at < high_marks)).astype(F32).astype(BF16)
        counts = (high_marks - low_marks).astype(F32)
        q_marks = per_head(mm(member, whole(slab, 0)) / counts)
        k_marks = per_head(mm(member, whole(slab, 1)) / counts)
        scores = jnp.where(diagonal_blocks(), SCALE * exact(q_marks, k_marks, NT), NEG)
        weights = jnp.exp(scores - jnp.max(scores, axis=1, keepdims=True))
        kernel = weights / jnp.sum(weights, axis=1, keepdims=True)
        total = head_sums(jnp.broadcast_to(jnp.sum(kernel * kernel, axis=1, keepdims=True), kernel.shape))
        keep["q_marks"][...] = q_marks
        keep["k_marks"][...] = k_marks
        keep["kernel"][...] = kernel
        keep["total"][...] = total
        keep["inverse"][0] = kernel.T / total

    def sweep(at):
        def run():
            eye, inverse = unit(), keep["inverse"][at]
            product = exact(keep["kernel"][...], inverse)
            one = 7.0 * eye - product
            two = 15.0 * eye - exact(product, one)
            three = 13.0 * eye - exact(product, two)
            keep["product"][at] = product
            keep["two"][at] = two
            keep["three"][at] = three
            keep["inverse"][at + 1] = 0.25 * exact(inverse, three)

        return run

    def over_keys():
        valid = iota((1, length), 1) < mark_columns(edges())[1][MARKS - 1 :]
        key_scores = jnp.where(valid, SCALE * mm_left(keep["q_marks"][...], whole(slab, 1), NT), NEG)
        key_exp = jnp.where(valid, jnp.exp(key_scores - jnp.max(key_scores, axis=1, keepdims=True)), 0.0)
        key_weights = key_exp / jnp.sum(key_exp, axis=1, keepdims=True)
        keep["key_weights"][...] = key_weights
        keep["summary"][...] = jnp.where(diagonal_blocks(), mm_left(key_weights, whole(slab, 2)), 0.0)

    def over_tokens():
        token_scores = SCALE * mm_left(keep["k_marks"][...], whole(slab, 0), NT)
        token_exp = jnp.exp(token_scores - head_tops(token_scores))
        keep["token_weights"][...] = token_exp / head_sums(token_exp)

    def close():
        mixed = exact(keep["inverse"][NS_ITERS], keep["summary"][...])
        keep["mixed"][...] = mixed
        blended[...] = mm_both(keep["token_weights"][...], mixed, TN)
        values = whole(slab, 2)
        valid_column = iota((length, 1), 0) < mark_columns(edges())[1][MARKS - 1 :]
        padded[0:HALF, :] = jnp.zeros((HALF, LANES), BF16)
        padded[HALF : HALF + length, :] = jnp.where(valid_column, values, jnp.zeros_like(values))
        padded[HALF + length :, :] = jnp.zeros((LANES - HALF, LANES), BF16)

        def store(start, block):
            put_rows(result, 0, start, (blended[pl.ds(start, LANES), :] + block).astype(BF16))

        convolve(padded, [band(one) for one in taps()], length, store)

    return [begin] + [sweep(at) for at in range(NS_ITERS)] + [over_keys, over_tokens, close]


def attend_back(grads, queries, keys, values, edges, taps, keep, padded, padded_grads, blended, result, grad_taps):
    length = grads.shape[0]
    low_marks, high_marks = mark_columns(edges)
    low_row, high_row = mark_rows(edges)
    at = iota((length, MARKS), 0)
    member = ((low_row <= at) & (at < high_row)).astype(F32).astype(BF16)
    counts = (high_marks - low_marks).astype(F32)
    blocks, eye = diagonal_blocks(), unit()
    q_marks, k_marks = keep["q_marks"][...], keep["k_marks"][...]
    token_weights, key_weights = keep["token_weights"][...], keep["key_weights"][...]
    summary, mixed = keep["summary"][...], keep["mixed"][...]
    kernel = keep["kernel"][...]
    inverse = keep["inverse"][NS_ITERS]
    grad_mixed = jnp.where(blocks, mm_left(token_weights, grads), 0.0)
    grad_token = token_weights * mm_left(mixed, grads, NT)
    grad_token = SCALE * (grad_token - token_weights * head_sums(grad_token))
    grad_summary = exact(inverse, grad_mixed, TN)
    grad_inverse = exact(grad_mixed, summary, NT)
    grad_kernel = jnp.zeros_like(kernel)
    for sweep in reversed(range(NS_ITERS)):
        before, product = keep["inverse"][sweep], keep["product"][sweep]
        one = 7.0 * eye - product
        two, three = keep["two"][sweep], keep["three"][sweep]
        grad_three = 0.25 * exact(before, grad_inverse, TN)
        grad_two = -exact(product, grad_three, TN)
        grad_one = -exact(product, grad_two, TN)
        grad_product = -(exact(grad_three, two, NT) + exact(grad_two, one, NT) + grad_one)
        grad_kernel = grad_kernel + exact(grad_product, before, NT)
        grad_inverse = 0.25 * exact(grad_inverse, three, NT) + exact(kernel, grad_product, TN)
    total = keep["total"][...]
    turned = grad_inverse.T / total
    weighted = jnp.sum(jnp.where(blocks, turned * kernel, 0.0), axis=1, keepdims=True)
    weighted = head_sums(jnp.broadcast_to(weighted, kernel.shape))
    grad_kernel = grad_kernel + turned - 2.0 * kernel * weighted / total
    grad_scores = SCALE * kernel * (grad_kernel - jnp.sum(kernel * grad_kernel, axis=1, keepdims=True))
    grad_q_marks = exact(grad_scores, k_marks)
    grad_k_marks = exact(grad_scores, q_marks, TN)
    grad_k_marks = grad_k_marks + jnp.where(blocks, mm_left(grad_token, queries), 0.0)
    grad_key = mm_left(grad_summary, values, NT) - jnp.sum(grad_summary * summary, axis=1, keepdims=True)
    grad_key = SCALE * key_weights * grad_key
    grad_q_marks = grad_q_marks + jnp.where(blocks, mm_left(grad_key, keys), 0.0)
    grad_q_marks = (grad_q_marks[:MARKS] + grad_q_marks[MARKS:]) / counts
    grad_k_marks = (grad_k_marks[:MARKS] + grad_k_marks[MARKS:]) / counts
    high, rest = halves(grad_q_marks)
    result[0] = (mm_both(grad_token, k_marks, TN) + mm(member, high) + mm(member, rest)).astype(BF16).reshape(result.shape[1:])
    high, rest = halves(grad_k_marks)
    result[1] = (mm_both(grad_key, q_marks, TN) + mm(member, high) + mm(member, rest)).astype(BF16).reshape(result.shape[1:])
    blended[...] = mm_both(key_weights, grad_summary, TN)
    last = high_marks[MARKS - 1 :]
    valid_column = iota((length, 1), 0) < last
    padded[0:HALF, :] = jnp.zeros((HALF, LANES), BF16)
    padded[HALF : HALF + length, :] = jnp.where(valid_column, values, jnp.zeros_like(values))
    padded[HALF + length :, :] = jnp.zeros((LANES - HALF, LANES), BF16)
    padded_grads[0:HALF, :] = jnp.zeros((HALF, LANES), BF16)
    padded_grads[HALF : HALF + length, :] = grads
    padded_grads[HALF + length :, :] = jnp.zeros((LANES - HALF, LANES), BF16)

    def store(start, block):
        rows = start + iota((LANES, 1), 0)
        total_rows = blended[pl.ds(start, LANES), :] + jnp.where(rows < last, block, 0.0)
        put_rows(result, 2, start, total_rows.astype(BF16))

    convolve(padded_grads, [band_back(one) for one in taps], length, store)
    first = iota((LANES, LANES), 1) < HEAD_DIM

    def block(step, carry):
        start = pl.multiple_of(step * LANES, LANES)
        own = padded_grads[pl.ds(start + HALF, LANES), :]
        window = padded[pl.ds(start, 2 * LANES), :]
        none = jnp.zeros_like(own)
        return (
            carry[0] + mm(jnp.where(first, own, none), window, NT),
            carry[1] + mm(jnp.where(first, none, own), window, NT),
        )

    start_sum = jnp.zeros((LANES, 2 * LANES), F32)
    sums = lax.fori_loop(0, length // LANES, block, (start_sum, start_sum))
    wide = 2 * LANES
    for head in range(2):
        folded = sums[head][0:8]
        for group in range(1, LANES // 8):
            rows = sums[head][8 * group : 8 * group + 8]
            folded = folded + pltpu.roll(rows, wide - 8 * group, 1)
        line = folded[0:1]
        for row in range(1, 8):
            line = line + pltpu.roll(folded[row : row + 1], wide - row, 1)
        grad_taps[head : head + 1, :] = line


KEPT = ("q_marks", "k_marks", "kernel", "total", "inverse", "product", "two", "three", "key_weights", "summary", "mixed", "token_weights")


def kept_shapes(length):
    square = (LANES, LANES)
    shapes = {name: square for name in KEPT}
    shapes["inverse"] = (NS_ITERS + 1,) + square
    for name in ("product", "two", "three"):
        shapes[name] = (NS_ITERS,) + square
    shapes["key_weights"] = shapes["token_weights"] = (LANES, length)
    return shapes


class Layout:
    def __init__(self, count):
        self.count = count
        self.groups = MICRO if count == 16 else 1
        self.members = count // self.groups
        self.tasks = PAIRS * MICRO // self.groups

    def place(self):
        me = lax.axis_index("dp")
        self.me, self.group, self.index = me, me // self.members, lax.rem(me, self.members)
        self.task = (self.index * self.tasks + self.members - 1) // self.members
        self.owns = self.owner(self.task) == self.index
        self.micro = self.micro_of(self.task)
        self.pair = lax.rem(self.task, PAIRS)
        return self

    def owner(self, task):
        return task * self.members // self.tasks

    def micro_of(self, task):
        return self.group if self.groups > 1 else task // PAIRS

    def device(self, index):
        return {"dp": self.group * self.members + index}

    def block(self, array, task):
        lanes = pl.ds(pl.multiple_of(lax.rem(task, PAIRS) * LANES, LANES), LANES)
        return array.at[:, :, :, lanes] if self.groups > 1 else array.at[:, pl.ds(task // PAIRS, 1), :, lanes]

    def rows(self, slab, index, piece):
        return slab.at[:, :, pl.ds(pl.multiple_of(index * piece, piece), piece), :]

    def mate(self):
        return {"dp": lax.rem(self.me + self.members, self.count)}


def greet(at, everyone=False, mate=False):
    barrier = pltpu.get_barrier_semaphore()
    size, index = (at.count, at.me) if everyone else (at.members, at.index)
    if everyone:
        pl.semaphore_signal(barrier, inc=1, device_id={"rep": 1 - lax.axis_index("rep")}, device_id_type=MESH)
    if mate:
        pl.semaphore_signal(barrier, inc=1, device_id=at.mate(), device_id_type=MESH)

    def signal(step, carry):
        other = lax.rem(index + step, size)
        pl.semaphore_signal(barrier, inc=1, device_id={"dp": other} if everyone else at.device(other), device_id_type=MESH)
        return carry

    lax.fori_loop(1, size, signal, 0)
    pl.semaphore_wait(barrier, size - 1 + int(everyone) + int(mate))


def scatter_tasks(at, piece, source, slab, send, receive):
    def one(step, finish):
        task = lax.rem(at.task + step, at.tasks)
        owner = at.owner(task)
        outgoing, landing = at.block(source, task), at.rows(slab, at.index, piece)

        @pl.when(owner != at.index)
        def _():
            copy = pltpu.make_async_remote_copy(
                outgoing, landing, send.at[task], receive.at[at.index], device_id=at.device(owner), device_id_type=MESH
            )
            if finish:
                copy.wait_send()
            else:
                copy.start()

        @pl.when((owner == at.index) & (not finish))
        def _():
            pltpu.make_async_copy(outgoing, landing, receive.at[at.index]).start()

    def run(finish):
        def body(step, carry):
            one(step, finish)
            return carry

        lax.fori_loop(0, at.tasks, body, 0)

    return run


def await_slab(at, piece, slab, receive):
    def body(origin, carry):
        landing = at.rows(slab, origin, piece)
        pltpu.make_async_copy(landing, landing, receive.at[origin]).wait()
        return carry

    lax.fori_loop(0, at.members, body, 0)


def return_rows(at, piece, result, target, send, receive):
    def run(finish):
        def body(step, carry):
            peer = lax.rem(at.index + step, at.members)
            outgoing, landing = at.rows(result, peer, piece), at.block(target, at.task)

            @pl.when(peer != at.index)
            def _():
                copy = pltpu.make_async_remote_copy(
                    outgoing, landing, send.at[peer], receive.at[at.task], device_id=at.device(peer), device_id_type=MESH
                )
                if finish:
                    copy.wait_send()
                else:
                    copy.start()

            @pl.when((peer == at.index) & (not finish))
            def _():
                pltpu.make_async_copy(outgoing, landing, receive.at[at.task]).start()

            return carry

        lax.fori_loop(0, at.members, body, 0)

    return run


def await_rows(at, target, receive):
    def body(task, carry):
        landing = at.block(target, task)
        pltpu.make_async_copy(landing, landing, receive.at[task]).wait()
        return carry

    lax.fori_loop(0, at.tasks, body, 0)


def swap(at, source, target, send, receive):
    return pltpu.make_async_remote_copy(
        source.at[1 - at.group], target.at[at.group], send, receive, device_id=at.mate(), device_id_type=MESH
    )


def forward_kernel(count, piece, spans, qkv, edges, lines, low, mixed_rows, slab, *refs):
    keep = dict(zip(KEPT, refs))
    outs, refs = refs[len(KEPT) : len(KEPT) + len(spans)], refs[len(KEPT) + len(spans) :]
    padded, blended, result, send_one, receive_one, send_two, receive_two = refs[:7]
    begin, steps, finish = spread_all(spans, low, outs, refs[7:])
    at = Layout(count).place()
    greet(at, bool(spans))
    out = scatter_tasks(at, piece, qkv, slab, send_one, receive_one)
    out(False)
    begin()
    back = return_rows(at, piece, result, mixed_rows, send_two, receive_two)
    phases = attend(slab, lambda: edges[pl.ds(at.micro, 1), :], lambda: head_taps(lines, at.pair), keep, padded, blended, result)

    def between(turn):
        if turn < len(steps):
            steps[turn]()

    between(0)
    for turn, phase in enumerate(phases):

        @pl.when(at.owns)
        def _():
            if turn == 0:
                await_slab(at, piece, slab, receive_one)
            phase()
            if turn == len(phases) - 1:
                back(False)

        if turn > 1:
            between(turn - 1)
    for turn in range(len(phases) - 1, len(steps)):
        between(turn)
    finish()
    out(True)
    await_rows(at, mixed_rows, receive_two)

    @pl.when(at.owns)
    def _():
        back(True)


def backward_kernel(count, piece, carries, grads, edges, lines, *refs):
    carried, refs = refs[:carries], refs[carries:]
    slab, refs = refs[0], refs[1:]
    keep = dict(zip(KEPT, refs))
    out_grads, grad_taps, refs = refs[len(KEPT)], refs[len(KEPT) + 1], refs[len(KEPT) + 2 :]
    swapped, refs = refs[:carries], refs[carries:]
    grad_slab, padded, padded_grads, blended, result, send_one, receive_one, send_two, receive_two, send_swap, receive_swap = refs
    at = Layout(count).place()
    greet(at, mate=bool(carries))
    out = scatter_tasks(at, piece, grads, grad_slab, send_one, receive_one)
    out(False)
    swaps = [swap(at, one, two, send_swap, receive_swap) for one, two in zip(carried, swapped)]
    for one, source, target in zip(swaps, carried, swapped):
        one.start()
        target[pl.ds(at.group, 1)] = source[pl.ds(at.group, 1)]
    back = return_rows(at, piece, result, out_grads, send_two, receive_two)
    grad_taps[...] = jnp.zeros(grad_taps.shape, F32)

    @pl.when(at.owns)
    def _():
        await_slab(at, piece, grad_slab, receive_one)
        attend_back(
            whole(grad_slab, 0), whole(slab, 0), whole(slab, 1), whole(slab, 2), edges[pl.ds(at.micro, 1), :], head_taps(lines, at.pair),
            keep, padded, padded_grads, blended, result, grad_taps.at[at.pair],
        )
        back(False)

    out(True)
    await_rows(at, out_grads, receive_two)
    for one in swaps:
        one.wait()

    @pl.when(at.owns)
    def _():
        back(True)


VMEM = pl.BlockSpec(memory_space=pltpu.VMEM)
DMA = pltpu.SemaphoreType.DMA


def attention_forward(count, qkv, edges, lines, ident, low=None, spans=()):
    piece = qkv.shape[2]
    length = piece * count
    shapes = kept_shapes(length)
    low = low if spans else lines
    at = Layout(count)
    halved = (at.groups, length // at.groups, LANES)
    anywhere = pl.BlockSpec(memory_space=pl.ANY)
    results = pl.pallas_call(
        functools.partial(forward_kernel, count, piece, spans),
        out_shape=[
            jax.ShapeDtypeStruct((1, MICRO, piece, D), BF16),
            jax.ShapeDtypeStruct((3,) + halved, BF16),
        ]
        + [jax.ShapeDtypeStruct(shapes[name], F32) for name in KEPT]
        + [spread_shape(low, span) for span in spans],
        in_specs=[VMEM] * 4,
        out_specs=[VMEM] * (2 + len(KEPT)) + [anywhere] * len(spans),
        scratch_shapes=[
            pltpu.VMEM((length + LANES, LANES), BF16),
            pltpu.VMEM((length, LANES), F32),
            pltpu.VMEM((1,) + halved, BF16),
            DMA((at.tasks,)),
            DMA((at.members,)),
            DMA((at.members,)),
            DMA((at.tasks,)),
        ]
        + [one for span in spans for one in spread_semaphores(span)],
        compiler_params=pltpu.CompilerParams(collective_id=ident, has_side_effects=True, vmem_limit_bytes=60 << 20),
        name="attend_forward",
    )(qkv, edges, lines, low)
    return results[0][0], results[1 : 2 + len(KEPT)], [flat_rows(one) for one in results[2 + len(KEPT) :]]


def attention_backward(count, grads, edges, lines, kept, ident, carried=()):
    piece = grads.shape[2]
    length = piece * count
    at = Layout(count)
    halved = (at.groups, length // at.groups, LANES)
    results = pl.pallas_call(
        functools.partial(backward_kernel, count, piece, len(carried)),
        out_shape=[
            jax.ShapeDtypeStruct((3, MICRO, piece, D), BF16),
            jax.ShapeDtypeStruct((PAIRS, 2, 2 * LANES), F32),
        ]
        + [jax.ShapeDtypeStruct(one.shape, one.dtype) for one in carried],
        in_specs=[VMEM] * (4 + len(carried) + len(KEPT)),
        out_specs=[VMEM] * (2 + len(carried)),
        scratch_shapes=[
            pltpu.VMEM((1,) + halved, BF16),
            pltpu.VMEM((length + LANES, LANES), BF16),
            pltpu.VMEM((length + LANES, LANES), BF16),
            pltpu.VMEM((length, LANES), F32),
            pltpu.VMEM((3,) + halved, BF16),
            DMA((at.tasks,)),
            DMA((at.members,)),
            DMA((at.members,)),
            DMA((at.tasks,)),
            DMA,
            DMA,
        ],
        compiler_params=pltpu.CompilerParams(collective_id=ident, has_side_effects=True, vmem_limit_bytes=60 << 20),
        name="attend_backward",
    )(grads, edges, lines, *carried, *kept)
    return results[0], results[1], results[2:]


def arrange(sources, targets):
    params, first, second = sources
    lines, ups, sliced = targets[:LAYERS], targets[LAYERS : 2 * LAYERS], targets[2 * LAYERS :]
    for level in range(LAYERS):
        own = slice(level, level + 1)
        for line in range(TAP_LINE):
            lines[level][line : line + 1, :] = params[own, line * D : (line + 1) * D]
        lines[level][TAP_LINE:, :] = jnp.zeros((16 - TAP_LINE, D), F32)
        lines[level][TAP_LINE : TAP_LINE + 1, : HEADS * TAPS] = params[own, TAP_LINE * D :]
        ups[level][...] = params[own, 8 * D : 8 * D + FF]
    for source, target in zip((first, second), sliced):
        target[LAYERS * LINES // 2 :] = jnp.zeros((16 - LAYERS * LINES // 2, 2, D), F32)
        for level in range(LAYERS):
            own = slice(level, level + 1)
            for line in range(LINES):
                index = level * LINES + line
                spot = slice(index % 2, index % 2 + 1)
                if line < TAP_LINE:
                    target[index // 2, spot, :] = source[own, line * D : (line + 1) * D]
                else:
                    target[index // 2, spot, :] = jnp.zeros((1, D), F32)
                    target[index // 2, spot, : HEADS * TAPS] = source[own, TAP_LINE * D :]


ARRANGED = (
    [jax.ShapeDtypeStruct((16, D), F32)] * LAYERS + [jax.ShapeDtypeStruct((1, FF), F32)] * LAYERS + [jax.ShapeDtypeStruct((16, 2, D), F32)] * 2
)


def arrange_kernel(*refs):
    arrange(refs[:3], refs[3:])


def arranged(*smalls):
    return pl.pallas_call(arrange_kernel, out_shape=ARRANGED, in_specs=[VMEM] * 3, out_specs=[VMEM] * len(ARRANGED), name="arrange")(*smalls)


PLANES = 4
SUBS = 2
EVEN, ODD = range(0, SUBS, 2), range(1, SUBS, 2)


def gather_kernel(spans, low, params, first, second, hidden, cotangent, *refs):
    outs, refs = refs[: len(spans)], refs[len(spans) :]
    targets, refs = refs[: len(ARRANGED)], refs[len(ARRANGED) :]
    swapped, swap_sems, refs = refs[:2], refs[2], refs[3:]
    begin, steps, finish = spread_all(spans, low, outs, refs)
    at = Layout(16).place()
    me, x = lax.axis_index("dp"), lax.axis_index("rep")
    core, y, z = lax.rem(me, 2), lax.rem(me // 2, 2), me // 4
    barrier = pltpu.get_barrier_semaphore()
    for where in ({"rep": 1 - x}, {"dp": me + 2 - 4 * y}, {"dp": me + 1 - 2 * core}, at.mate()):
        pl.semaphore_signal(barrier, inc=1, device_id=where, device_id_type=MESH)
    for sign in (1, -1):

        @pl.when((z + sign >= 0) & (z + sign < PLANES))
        def _():
            pl.semaphore_signal(barrier, inc=1, device_id={"dp": me + 4 * sign}, device_id_type=MESH)

    pl.semaphore_wait(barrier, 5 + jnp.where((z > 0) & (z < PLANES - 1), 1, 0))
    begin()
    swaps = [swap(at, one, two, swap_sems.at[0, which], swap_sems.at[1, which]) for which, (one, two) in enumerate(zip((hidden, cotangent), swapped))]
    for one, source, target in zip(swaps, (hidden, cotangent), swapped):
        one.start()
        target[pl.ds(at.group, 1)] = source[pl.ds(at.group, 1)]
    arrange((params, first, second), targets)
    for step in steps:
        step()
    finish()
    for one in swaps:
        one.wait()


def spread_semaphores(span):
    planes = span[2] - span[1]
    return [DMA, DMA((planes, SUBS, 2)), DMA((planes, SUBS))] + [DMA((planes, 2, 2, SUBS))] * 5 + [DMA]


def spread_shape(low, span):
    return jax.ShapeDtypeStruct((span[2] - span[1], 2, 2) + low.shape[1:], BF16)


def flat_rows(blocks):
    return blocks.reshape(-1, D)


def spread_all(spans, low, outs, semaphores):
    each = len(semaphores) // max(len(spans), 1)
    parts = [
        spread(low.at[level], out, bottom, top, *semaphores[at * each : (at + 1) * each])
        for at, ((level, bottom, top), out) in enumerate(zip(spans, outs))
    ]

    def together(actions):
        def run():
            for action in actions:
                action()

        return run

    steps = [together(actions) for actions in zip(*[part[1] for part in parts])]
    return together([part[0] for part in parts]), steps, together([part[2] for part in parts])


def spread(shard, out, bottom, top, local_sem, z_send, z_got, x_send, x_got, y_send, y_got, core_send, core_got):
    me = lax.axis_index("dp")
    x = lax.axis_index("rep")
    core, y, z = lax.rem(me, 2), lax.rem(me // 2, 2), me // 4
    half = shard.shape[0] // 2
    part = half // SUBS

    def held(plane):
        return (plane >= bottom) & (plane < top)

    def peer(axis, sign=1):
        if axis == "x":
            return {"rep": 1 - x}
        if axis == "y":
            return {"dp": me + 2 - 4 * y}
        if axis == "core":
            return {"dp": me + 1 - 2 * core}
        return {"dp": me + 4 * sign}

    def rows(side, sub):
        return pl.ds(pl.multiple_of(side * half + sub * part, part), part)

    def remote(source, target, send, receive, where):
        return pltpu.make_async_remote_copy(source, target, send, receive, device_id=where, device_id_type=MESH)

    def spot(plane, row, side, sub):
        return out.at[plane - bottom, row, core, rows(side, sub), :]

    def move(axis, plane, row, side, sub, source=None):
        target = spot(plane, row, side, sub)
        source = target if source is None else source
        at = plane - bottom
        if axis == "core":
            return remote(source, target, core_send.at[at, row, side, sub], core_got, peer("core"))
        send, receive = (x_send, x_got) if axis == "x" else (y_send, y_got)
        return remote(source, target, send.at[at, row, side, sub], receive.at[at, row, side, sub], peer(axis))

    def climb(plane, sub, sign, source=None):
        target = spot(plane, y, x, sub)
        way = 0 if sign > 0 else 1
        at = plane - bottom
        return remote(target if source is None else source, target, z_send.at[at, sub, way], z_got.at[at, sub], peer("z", sign))

    def inside(sign, act):
        pl.when((z + sign >= 0) & (z + sign < PLANES))(act)

    def begin():
        @pl.when(held(z))
        def _():
            pltpu.make_async_copy(shard, out.at[z - bottom, y, core], local_sem).start()
            for sub in range(SUBS):
                for sign in (1, -1):
                    inside(sign, lambda: climb(z, sub, sign, shard.at[rows(x, sub), :]).start())
                move("y", z, y, x, sub, shard.at[rows(x, sub), :]).start()
            for side in range(2):
                for sub in range(SUBS):
                    move("core", z, y, side, sub, shard.at[rows(side, sub), :]).start()

    def at_distance(distance, act):
        for sign in (1, -1):
            plane = z - sign * distance

            @pl.when(held(plane))
            def _():
                act(plane, sign)

    def from_z(plane, sign):
        for sub in range(SUBS):
            climb(plane, sub, sign).wait_recv()
            inside(sign, lambda: climb(plane, sub, sign).start())
            for axis in ("x", "y", "core"):
                move(axis, plane, y, x, sub).start()

    def take(axis, plane, row, side, sub, onward=None):
        move(axis, plane, row, side, sub).wait_recv()
        if onward is not None:
            move(onward, plane, row, side, sub).start()
        move("core", plane, row, side, sub).start()

    def first_square(plane, sign):
        for even, odd in zip(EVEN, ODD):
            take("x", plane, y, 1 - x, even, "y")
            take("y", plane, 1 - y, x, odd, "x")
            take("y", plane, 1 - y, x, even)
            take("x", plane, y, 1 - x, odd)

    def second_square(plane, sign):
        for even, odd in zip(EVEN, ODD):
            take("y", plane, 1 - y, 1 - x, even)
            take("x", plane, 1 - y, 1 - x, odd)

    def own_first():
        @pl.when(held(z))
        def _():
            for sub in range(SUBS):
                take("y", z, 1 - y, x, sub, "x")

    def own_last():
        @pl.when(held(z))
        def _():
            for sub in range(SUBS):
                take("x", z, 1 - y, 1 - x, sub)

    def stage(distance, act):
        return lambda: at_distance(distance, act)

    steps = [
        stage(1, from_z), own_first, stage(2, from_z), stage(1, first_square), stage(3, from_z), stage(2, first_square),
        own_last, stage(1, second_square), stage(3, first_square), stage(2, second_square), stage(3, second_square),
    ]

    def sent(plane, sign):
        for sub in range(SUBS):
            inside(sign, lambda: climb(plane, sub, sign).wait_send())
            move("x", plane, y, x, sub).wait_send()
            move("y", plane, y, x, sub).wait_send()
        for even, odd in zip(EVEN, ODD):
            move("y", plane, y, 1 - x, even).wait_send()
            move("x", plane, 1 - y, x, odd).wait_send()

    def finish():
        for distance in (1, 2, 3):
            at_distance(distance, sent)

        @pl.when(held(z))
        def _():
            pltpu.make_async_copy(shard, out.at[z - bottom, y, core], local_sem).wait()
            for sub in range(SUBS):
                for sign in (1, -1):
                    inside(sign, lambda: climb(z, sub, sign).wait_send())
                move("y", z, y, x, sub).wait_send()
                move("x", z, 1 - y, x, sub).wait_send()

        def core_sent(index, carry):
            plane, row = bottom + index // (4 * SUBS), lax.rem(index // (2 * SUBS), 2)
            side, sub = lax.rem(index // SUBS, 2), lax.rem(index, SUBS)
            move("core", plane, row, side, sub).wait_send()
            return carry

        lax.fori_loop(0, 4 * SUBS * (top - bottom), core_sent, 0)
        column = out.at[:, :, 1 - core]
        pltpu.make_async_copy(column, column, core_got).wait()

    return begin, steps, finish


def gather(low, spans, hidden, cotangent, *smalls):
    results = pl.pallas_call(
        functools.partial(gather_kernel, spans),
        out_shape=[spread_shape(low, span) for span in spans] + ARRANGED + [jax.ShapeDtypeStruct(hidden.shape, BF16)] * 2,
        in_specs=[VMEM] * 6,
        out_specs=[pl.BlockSpec(memory_space=pl.ANY)] * len(spans) + [VMEM] * (len(ARRANGED) + 2),
        scratch_shapes=[DMA((2, 2))] + [one for span in spans for one in spread_semaphores(span)],
        compiler_params=pltpu.CompilerParams(collective_id=4, has_side_effects=True),
        name="gather",
    )(low, *smalls, hidden, cotangent)
    return [flat_rows(one) for one in results[: len(spans)]], results[len(spans) : -2], results[-2:]


CHUNK = 32
RING = 12
CYCLE = 6
MATES = ("low_in", "low_comb", "low_up", "low_act", "low_grads", "low_branch", "low_hidden", "low_down", "gain_one", "shift_one", "gain_two", "shift_two", "taps")
LATE = ("low_grads", "taps")


def change(grad, first_old, second_old):
    new_first = ADAM_ONE * first_old + (1.0 - ADAM_ONE) * grad
    new_second = ADAM_TWO * second_old + (1.0 - ADAM_TWO) * grad * grad
    return new_first * (1.0 / (1.0 - ADAM_ONE**STEP_COUNT)) / (jnp.sqrt(new_second * (1.0 / (1.0 - ADAM_TWO**STEP_COUNT))) + ADAM_EPSILON)


def settle_kernel(block_rows, tokens, *refs):
    early = [name for name in MATES if name not in LATE]
    mates = [dict(zip(early, refs)), dict(zip(MATES, refs[len(early) :]))]
    refs = refs[len(early) + len(MATES) :]
    grads, edges, lines, proj, grad_one, slab = refs[:6]
    keep = dict(zip(KEPT, refs[6:]))
    refs = refs[6 + len(KEPT) :]
    (
        weights, first, second, small_first, small_second, grad_out, mean_out, small_out, grad_in_out,
        turned, right, staged, own, got_core, got_y, got_near, got_far, inner, step_own, step_got, small, small_got, small_own, small_step, small_step_got,
        core_send, core_got, y_send, y_got, near_send, near_got, far_send, far_got, inner_sem, rep_send, rep_got, small_send, small_sem, back_send, back_sem, small_rep, swap_sems,
        low_grads, taps, grad_slab, padded, padded_grads, blended, result, grad_in, send_one, receive_one, send_two, receive_two,
    ) = refs
    mates[0].update(low_grads=low_grads, taps=taps)
    piece = grads.shape[2]
    me = lax.axis_index("dp")
    other_rep = 1 - lax.axis_index("rep")
    core, y, z = lax.rem(me, 2), lax.rem(me // 2, 2), me // 4
    devices = 16
    per_layer = block_rows // CHUNK
    chunks = LAYERS * per_layer

    barrier = pltpu.get_barrier_semaphore()

    def signal(step, carry):
        pl.semaphore_signal(barrier, inc=1, device_id={"dp": lax.rem(me + step, devices)}, device_id_type=MESH)
        return carry

    lax.fori_loop(1, devices, signal, 0)
    pl.semaphore_signal(barrier, inc=1, device_id={"rep": other_rep}, device_id_type=MESH)

    def to_dp(source, target, send, receive, peer):
        return pltpu.make_async_remote_copy(source, target, send, receive, device_id={"dp": peer}, device_id_type=MESH)

    def to_rep(source, target, send, receive):
        return pltpu.make_async_remote_copy(source, target, send, receive, device_id={"rep": other_rep}, device_id_type=MESH)

    def spot(slot):
        return lax.rem(slot, RING)

    features = D * 2 + FF * 2

    def prepare(level):
        order = LAYERS - 1 - level
        mate, at = mates[level], order * features
        for name in MATES[:4]:
            for part in range(mate[name].shape[1] // LANES):
                turned[at : at + LANES, :] = mate[name][:, part * LANES : (part + 1) * LANES].T
                at += LANES
        for part in range(3):
            right[order * 6 + part] = mate["low_grads"][part].reshape(tokens, D)
        for part, name in enumerate(MATES[5:8]):
            right[order * 6 + 3 + part] = mate[name][...]

    prepare(LAYERS - 1)

    def put(level, line, row):
        index = level * LINES + line
        small[index // 2, index % 2 : index % 2 + 1, :] = row

    def column_sum(array):
        return jnp.sum(array.astype(F32), axis=0, keepdims=True)

    def small_rows():
        for level in range(LAYERS):
            mate = mates[level]
            put(level, 0, column_sum(right[(LAYERS - 1 - level) * 6]))
            put(level, 1, column_sum(right[(LAYERS - 1 - level) * 6 + 2]))
            put(level, 2, column_sum(mate["low_branch"][...]))
            put(level, 3, column_sum(mate["low_down"][...]))
            for line, name in enumerate(MATES[8:12]):
                put(level, 4 + line, column_sum(mate[name][...]))
            for part in range(FF // D):
                put(level, 8 + part, column_sum(mate["low_up"][:, part * D : (part + 1) * D]))
            line = jnp.zeros((1, D), F32)
            for head in range(HEADS):
                taps = jnp.concatenate([mate["taps"][head // 2][head % 2 : head % 2 + 1], jnp.zeros((1, D - 2 * LANES), F32)], axis=1)
                taps = jnp.where(iota((1, D), 1) < TAPS, taps, 0.0)
                line = line + (pltpu.roll(taps, TAPS * head, 1) if head else taps)
            put(level, 12, line)
        for index in range(LAYERS * LINES, 2 * devices):
            small[index // 2, index % 2 : index % 2 + 1, :] = jnp.zeros((1, D), F32)

    pl.semaphore_wait(barrier, devices)

    at = Layout(16).place()
    out = scatter_tasks(at, piece, grads, grad_slab, send_one, receive_one)
    back = return_rows(at, piece, result, low_grads, send_two, receive_two)
    swapping = swap(at, grad_in, grad_in_out, swap_sems.at[0], swap_sems.at[1])
    out(False)

    def attention():
        taps[...] = jnp.zeros(taps.shape, F32)

        @pl.when(at.owns)
        def _():
            await_slab(at, piece, grad_slab, receive_one)
            attend_back(
                whole(grad_slab, 0), whole(slab, 0), whole(slab, 1), whole(slab, 2), edges[pl.ds(at.micro, 1), :], head_taps(lines, at.pair),
                keep, padded, padded_grads, blended, result, taps.at[at.pair],
            )
            back(False)

    def collect():
        out(True)
        await_rows(at, low_grads, receive_two)
        pl.when(at.owns)(lambda: back(True))

    def input_grads():
        total = grad_one[...]
        for part in range(3):
            total = total + mm(low_grads[part].reshape(tokens, D), proj[part], NT)
        grad_in[...] = total.reshape(grad_in.shape)
        swapping.start()
        grad_in_out[pl.ds(at.group, 1)] = grad_in[pl.ds(at.group, 1)]

    def small_copy(step):
        peer = lax.rem(me + step, devices)
        return to_dp(small.at[peer], small_got.at[me], small_send.at[peer], small_sem.at[me], peer)

    def small_begin(step, carry):
        small_copy(step).start()
        return carry

    def small_start():
        small_rows()
        lax.fori_loop(1, devices, small_begin, 0)

    def core_copy(chunk):
        return to_dp(staged.at[lax.rem(chunk, 2)], got_core.at[spot(chunk)], core_send.at[lax.rem(chunk, 2)], core_got.at[spot(chunk)], me + 1 - 2 * core)

    near, far = z + 1 - 2 * lax.rem(z, 2), 3 - z

    def plane_device(plane):
        return plane * 4 + lax.rem(me, 4)

    def y_copy(chunk, full):
        slot = spot(chunk)
        source, target = (own.at[slot, :, 1 - y], got_y.at[slot]) if full else (own.at[slot, z, 1 - y], got_y.at[slot, 0])
        return to_dp(source, target, y_send.at[slot], y_got.at[slot], me + 2 - 4 * y)

    def near_copy(chunk, which, full):
        slot, block = spot(chunk), 3 - near if which else near
        source, target = (own.at[slot, block], got_near.at[slot, which]) if full else (own.at[slot, block, y], got_near.at[slot, which, 0])
        return to_dp(source, target, near_send.at[slot, which], near_got.at[slot, which], plane_device(near))

    def far_copy(chunk, full):
        slot = spot(chunk)
        source, target = (own.at[slot, far], got_far.at[slot]) if full else (own.at[slot, far, y], got_far.at[slot, 0])
        return to_dp(source, target, far_send.at[slot], far_got.at[slot], plane_device(far))

    def by_order(chunk, y_first, z_first):
        turn_z = lax.rem(chunk, CYCLE) == CYCLE // 2
        pl.when(jnp.logical_not(turn_z))(y_first)
        pl.when(turn_z)(z_first)

    def place(chunk):
        return LAYERS - 1 - chunk // per_layer, pl.ds(pl.multiple_of(lax.rem(chunk, per_layer) * CHUNK, CHUNK), CHUNK)

    def inner_copies(chunk):
        level, rows = place(chunk)
        slot = lax.rem(chunk, 4)
        return [
            pltpu.make_async_copy(array.at[level, rows, :], inner.at[slot, index], inner_sem.at[slot, index])
            for index, array in enumerate((weights, first, second))
        ]

    def rep_copy(chunk):
        return to_rep(step_own.at[spot(chunk)], step_got.at[spot(chunk)], rep_send.at[spot(chunk)], rep_got.at[spot(chunk)])

    def product(chunk, there, row, side):
        order = chunk // per_layer
        block = (there * 2 + row) * 2 + side
        piece = block * per_layer + lax.rem(chunk, per_layer)
        narrow = D // CHUNK
        line = jnp.where(piece < 3 * narrow, lax.rem(piece, narrow), piece - 2 * narrow)
        group = jnp.where(piece < 4 * narrow, piece // narrow, jnp.where(piece < 4 * narrow + FF // CHUNK, 4, 5))
        rows = pl.ds(pl.multiple_of(order * features + line * CHUNK, 16), CHUNK)
        return mm(turned[rows, :], right[order * 6 + group]).astype(BF16)

    def stage_product(chunk):
        for there in range(4):
            for row in range(2):
                staged[lax.rem(chunk, 2), there, row] = product(chunk, there, row, 1 - core)
        core_copy(chunk).start()
        for there in range(4):
            for row in range(2):
                own[spot(chunk), there, row] = product(chunk, there, row, core)

    def stage_core(chunk):
        core_copy(chunk).wait()
        slot = spot(chunk)
        for there in range(4):
            for side in range(2):
                own[slot, there, side] = own[slot, there, side] + got_core[slot, there, side]

        def z_first():
            for which in range(2):
                near_copy(chunk, which, True).start()

        by_order(chunk, lambda: y_copy(chunk, True).start(), z_first)

    def stage_second(chunk):
        slot = spot(chunk)

        def y_first():
            y_copy(chunk, True).wait()
            for there in range(4):
                own[slot, there, y] = own[slot, there, y] + got_y[slot, there]
            for which in range(2):
                near_copy(chunk, which, False).start()

        def z_first():
            for which in range(2):
                near_copy(chunk, which, True).wait()
            for row in range(2):
                own[slot, far, row] = own[slot, far, row] + got_near[slot, 1, row]
                own[slot, z, row] = own[slot, z, row] + got_near[slot, 0, row]
            far_copy(chunk, True).start()

        by_order(chunk, y_first, z_first)

    def stage_third(chunk):
        slot = spot(chunk)

        def y_first():
            for which in range(2):
                near_copy(chunk, which, False).wait()
            own[slot, far, y] = own[slot, far, y] + got_near[slot, 1, 0]
            own[slot, z, y] = own[slot, z, y] + got_near[slot, 0, 0]
            far_copy(chunk, False).start()

        def z_first():
            far_copy(chunk, True).wait()
            for row in range(2):
                own[slot, z, row] = own[slot, z, row] + got_far[slot, row]
            y_copy(chunk, False).start()

        by_order(chunk, y_first, z_first)
        for copy in inner_copies(chunk):
            copy.start()

    def stage_last(chunk):
        for copy in inner_copies(chunk):
            copy.wait()
        by_order(chunk, lambda: far_copy(chunk, False).wait(), lambda: y_copy(chunk, False).wait())
        slot = spot(chunk)
        turn_z = lax.rem(chunk, CYCLE) == CYCLE // 2
        total = own[slot, z, y].astype(F32) + jnp.where(turn_z, got_y[slot, 0].astype(F32), got_far[slot, 0].astype(F32))
        level, rows = place(chunk)
        grad_out[level, rows, :] = total
        slot = lax.rem(chunk, 4)
        step = change(total, inner[slot, 1], inner[slot, 2]) + WEIGHT_DECAY * inner[slot, 0]
        step_own[spot(chunk)] = (LR_INNER * step).astype(BF16)
        rep_copy(chunk).start()

    def stage_rep(chunk):
        rep_copy(chunk).wait()
        level, rows = place(chunk)
        mean_out[level, rows, :] = 0.5 * (step_own[spot(chunk)].astype(F32) + step_got[spot(chunk)].astype(F32))

    def small_rep_copy():
        return to_rep(small_step, small_step_got, small_rep.at[0], small_rep.at[1])

    def small_back(step):
        peer = lax.rem(me + step, devices)
        return to_dp(small_own, small_out.at[me], back_send.at[peer], back_sem.at[me], peer)

    def small_sum():
        def add(step, total):
            peer = lax.rem(me + step, devices)
            pltpu.make_async_copy(small_got.at[peer], small_got.at[peer], small_sem.at[peer]).wait()
            return total + small_got[peer]

        total = lax.fori_loop(1, devices, add, small[me])
        small_own[0] = total
        small_step[...] = (LR_SMALL * change(total, small_first[me], small_second[me])).astype(BF16)
        small_rep_copy().start()

    def small_spread():
        small_rep_copy().wait_recv()
        small_own[1] = 0.5 * (small_step[...].astype(F32) + small_step_got[...].astype(F32))
        small_out[me] = small_own[...]

        def send(step, carry):
            small_back(step).start()
            return carry

        lax.fori_loop(1, devices, send, 0)

    def turn(now, carry):
        for lag, stage in ((0, stage_product), (1, stage_core), (3, stage_second), (5, stage_third), (7, stage_last), (9, stage_rep)):

            @pl.when((now >= lag) & (now < chunks + lag))
            def _():
                stage(now - lag)

        for when, act in (
            (2, attention), (6, collect), (7, lambda: prepare(0)), (8, input_grads), (9, small_start), (13, small_sum), (16, small_spread),
        ):
            pl.when(now == when)(act)
        return carry

    lax.fori_loop(0, chunks + 9, turn, 0)

    def small_drain(step, carry):
        peer = lax.rem(me + step, devices)
        small_copy(step).wait_send()
        small_back(step).wait_send()
        pltpu.make_async_copy(small_own, small_out.at[peer], back_sem.at[peer]).wait()
        return carry

    lax.fori_loop(1, devices, small_drain, 0)
    small_rep_copy().wait_send()
    swapping.wait()


def settle(mates, attention, weights, first, second, small_first, small_second):
    block_rows = weights.shape[1]
    anywhere = pl.BlockSpec(memory_space=pl.ANY)
    devices = 16
    piece = (CHUNK, D)
    tokens = mates[0]["low_in"].shape[0]
    share = attention[0].shape[2]
    at = Layout(devices)
    length = share * devices
    halved = (at.groups, length // at.groups, LANES)
    early = [mates[0][name] for name in MATES if name not in LATE] + [mates[1][name] for name in MATES] + list(attention)
    return pl.pallas_call(
        functools.partial(settle_kernel, block_rows, tokens),
        out_shape=[
            jax.ShapeDtypeStruct(weights.shape, F32),
            jax.ShapeDtypeStruct(weights.shape, F32),
            jax.ShapeDtypeStruct((devices, 2, 2, D), F32),
            jax.ShapeDtypeStruct((MICRO, share, D), F32),
        ],
        in_specs=[VMEM] * len(early) + [anywhere] * 3 + [VMEM] * 2,
        out_specs=[VMEM] * 4,
        scratch_shapes=[
            pltpu.VMEM((LAYERS * 2 * (D + FF), tokens), BF16),
            pltpu.VMEM((LAYERS * 6, tokens, D), BF16),
            pltpu.VMEM((2, 4, 2) + piece, BF16),
            pltpu.VMEM((RING, 4, 2) + piece, BF16),
            pltpu.VMEM((RING, 4, 2) + piece, BF16),
            pltpu.VMEM((RING, 4) + piece, BF16),
            pltpu.VMEM((RING, 2, 2) + piece, BF16),
            pltpu.VMEM((RING, 2) + piece, BF16),
            pltpu.VMEM((4, 3) + piece, F32),
            pltpu.VMEM((RING,) + piece, BF16),
            pltpu.VMEM((RING,) + piece, BF16),
            pltpu.VMEM((devices, 2, D), F32),
            pltpu.VMEM((devices, 2, D), F32),
            pltpu.VMEM((2, 2, D), F32),
            pltpu.VMEM((2, D), BF16),
            pltpu.VMEM((2, D), BF16),
            DMA((2,)),
            DMA((RING,)),
            DMA((RING,)),
            DMA((RING,)),
            DMA((RING, 2)),
            DMA((RING, 2)),
            DMA((RING,)),
            DMA((RING,)),
            DMA((4, 3)),
            DMA((RING,)),
            DMA((RING,)),
            DMA((devices,)),
            DMA((devices,)),
            DMA((devices,)),
            DMA((devices,)),
            DMA((2,)),
            DMA((2,)),
            pltpu.VMEM((3, MICRO, share, D), BF16),
            pltpu.VMEM((PAIRS, 2, 2 * LANES), F32),
            pltpu.VMEM((1,) + halved, BF16),
            pltpu.VMEM((length + LANES, LANES), BF16),
            pltpu.VMEM((length + LANES, LANES), BF16),
            pltpu.VMEM((length, LANES), F32),
            pltpu.VMEM((3,) + halved, BF16),
            pltpu.VMEM((MICRO, share, D), F32),
            DMA((at.tasks,)),
            DMA((at.members,)),
            DMA((at.members,)),
            DMA((at.tasks,)),
        ],
        compiler_params=pltpu.CompilerParams(collective_id=3, has_side_effects=True, vmem_limit_bytes=63 << 20),
        name="settle",
    )(*early, weights, first, second, small_first, small_second)


def finish_kernel(both, params, outer, first, second, first_new, second_new, outer_new, params_new, grad, mean):
    for level in range(LAYERS):
        for line in range(LINES):
            index = level * LINES + line
            spot = slice(index % 2, index % 2 + 1)
            for which, target in ((0, grad), (1, mean)):
                target[level : level + 1, line * D : (line + 1) * D] = both[index // 2, which, spot, :]
    first_new[...], second_new[...] = moments(first[...], second[...], grad[:, :SMALL])
    momentum = MOMENTUM * outer[...] + mean[:, :SMALL]
    outer_new[...] = momentum
    params_new[...] = params[...] - LR_OUTER * (mean[:, :SMALL] + MOMENTUM * momentum)


def finish(both, params, outer, first, second):
    wide = pltpu.VMEM((LAYERS, LINES * D), F32)
    return pl.pallas_call(
        finish_kernel,
        out_shape=[jax.ShapeDtypeStruct(params.shape, F32)] * 4,
        in_specs=[VMEM] * 5,
        out_specs=[VMEM] * 4,
        scratch_shapes=[wide, wide],
        name="finish",
    )(both, params, outer, first, second)


def dense(a, b, dims=NN):
    return mm(a, b, dims)


def standard(values):
    centred = values - jnp.mean(values, axis=-1, keepdims=True)
    scale = lax.rsqrt(jnp.mean(centred * centred, axis=-1, keepdims=True) + 1e-05)
    return centred * scale, scale


def layer_norm(values, gain, shift):
    return standard(values)[0] * gain + shift


def layer_norm_back(values, gain, grad):
    unit_values, scale = standard(values)
    inner = grad * gain
    along = jnp.mean(inner * unit_values, axis=-1, keepdims=True)
    result = scale * (inner - jnp.mean(inner, axis=-1, keepdims=True) - unit_values * along)
    return result, eighths(grad * unit_values), eighths(grad)


def eighths(rows):
    return jnp.sum(rows.reshape(-1, 8, D), axis=0)


def split_rows(rest):
    return rest[:D], rest[D : D + FF], rest[D + FF :]


def forward_layer(count, inputs, proj, rest, small, edges, ident, low=None, spans=()):
    piece = inputs.shape[0] // MICRO
    lines, bias_up = small
    proj = proj.reshape(3, D, D)
    low_in = inputs.astype(BF16)
    query = (dense(low_in, proj[0]) + lines[0:1]).astype(BF16)
    key = dense(low_in, proj[1]).astype(BF16)
    value = (dense(low_in, proj[2]) + lines[1:2]).astype(BF16)
    qkv = jnp.stack([query, key, value])
    low_comb, kept, fetched = attention_forward(count, qkv.reshape(3, MICRO, piece, D), edges, lines, ident, low, spans)
    out_weight, up_weight, down_weight = split_rows(rest)
    low_comb = low_comb.reshape(MICRO * piece, D)
    resid_one = inputs + (dense(low_comb, out_weight) + lines[2:3])
    hidden_one = layer_norm(resid_one, lines[4:5], lines[5:6])
    low_hidden = hidden_one.astype(BF16)
    upward = dense(low_hidden, up_weight, NT) + bias_up
    low_act = jax.nn.gelu(upward).astype(BF16)
    resid_two = hidden_one + (dense(low_act, down_weight) + lines[3:4])
    output = layer_norm(resid_two, lines[6:7], lines[7:8])
    return output, (proj, rest, low_in, kept, low_comb, resid_one, low_hidden, upward, low_act, resid_two), fetched


def backward_layer(count, grad_output, small, edges, state, ident, carried=(), later=False):
    proj, rest, low_in, kept, low_comb, resid_one, low_hidden, upward, low_act, resid_two = state
    total = low_in.shape[0]
    piece = total // MICRO
    lines, _ = small
    out_weight, up_weight, down_weight = split_rows(rest)
    grad_two, grad_gain_two, grad_shift_two = layer_norm_back(resid_two, lines[6:7], grad_output)
    low_down = grad_two.astype(BF16)
    grad_act = dense(low_down, down_weight, NT)
    _, pull_gelu = jax.vjp(jax.nn.gelu, upward)
    low_up = pull_gelu(grad_act)[0].astype(BF16)
    grad_hidden = grad_two + dense(low_up, up_weight)
    grad_one, grad_gain_one, grad_shift_one = layer_norm_back(resid_one, lines[4:5], grad_hidden)
    low_branch = grad_one.astype(BF16)
    grad_comb = dense(low_branch, out_weight, NT).astype(BF16)
    vectors = (grad_gain_one, grad_shift_one, grad_gain_two, grad_shift_two)
    if later:
        names = [name for name in MATES if name not in LATE]
        values = (low_in, low_comb, low_up, low_act, low_branch, low_hidden, low_down, *vectors)
        return None, dict(zip(names, values)), (grad_comb.reshape(1, MICRO, piece, D), edges, lines, proj, grad_one, *kept)
    low_grads, grad_taps, swapped = attention_backward(count, grad_comb.reshape(1, MICRO, piece, D), edges, lines, kept, ident, carried)
    low_grads = low_grads.reshape(3, total, D)
    grad_in = grad_one + sum(dense(low_grads[part], proj[part], NT) for part in range(3))
    values = (low_in, low_comb, low_up, low_act, low_grads, low_branch, low_hidden, low_down, *vectors, grad_taps)
    return grad_in, dict(zip(MATES, values)), swapped


def plain_grads(mate):
    parts = [dense(mate["low_in"], mate["low_grads"][part], TN) for part in range(3)]
    parts = parts + [dense(mate[left], mate[right], TN) for left, right in (("low_comb", "low_branch"), ("low_up", "low_hidden"), ("low_act", "low_down"))]
    sums = [mate["low_grads"][0], mate["low_grads"][2], mate["low_branch"], mate["low_down"]]
    sums = [jnp.sum(one.astype(F32), axis=0) for one in sums]
    sums = sums + [jnp.sum(mate[name], axis=0) for name in MATES[8:12]]
    sums = sums + [jnp.sum(mate["low_up"].astype(F32), axis=0), mate["taps"][:, :, :TAPS].reshape(-1)]
    return jnp.concatenate(parts, axis=0).astype(BF16), jnp.concatenate(sums)


def moments(first, second, grad):
    return ADAM_ONE * first + (1.0 - ADAM_ONE) * grad, ADAM_TWO * second + (1.0 - ADAM_TWO) * grad * grad


def adam(weights, first, second, grad, rate, decay):
    correct_one = 1.0 - ADAM_ONE**STEP_COUNT
    correct_two = 1.0 - ADAM_TWO**STEP_COUNT
    new_first, new_second = moments(first, second, grad)
    step = new_first / correct_one / (jnp.sqrt(new_second / correct_two) + ADAM_EPSILON)
    return new_first, new_second, rate * (step + decay * weights)


def shards(
    hidden,
    bounds,
    cotangent,
    weights,
    small_params,
    first_big,
    second_big,
    first_small,
    second_small,
    outer_big,
    outer_small,
):
    count = lax.axis_size("dp")
    piece = hidden.shape[3]
    total = MICRO * piece
    low_weights = weights.astype(BF16)
    limits = bounds[0, :, 0, :]
    edges = jnp.pad(limits.astype(F32), ((0, 0), (0, LANES - limits.shape[1])))
    own_hidden, own_cotangent = hidden[0, :, 0], cotangent[0, :, 0]
    me = lax.axis_index("dp")
    start, last = me * piece, limits[:, -1].reshape(MICRO, 1, 1)
    if count == 16:
        (proj, rest), prepared, (own_hidden, own_cotangent) = gather(
            low_weights, ((0, 0, 1), (0, 1, PLANES)), own_hidden, own_cotangent, small_params, first_small[0], second_small[0]
        )
        half = count // MICRO
        start = (lax.broadcasted_iota(jnp.int32, (MICRO, 1, 1), 0) * half + lax.rem(me, half)) * piece
        last = jnp.where(me < half, limits[0, -1], limits[1, -1])
    else:
        prepared = arranged(small_params, first_small[0], second_small[0])
    positions = start + lax.broadcasted_iota(jnp.int32, (MICRO, piece, 1), 1)
    valid = positions < last
    activation = own_hidden.reshape(total, D).astype(F32)
    states = [None] * LAYERS
    smalls = [(prepared[level], prepared[LAYERS + level]) for level in range(LAYERS)]
    for level in range(LAYERS):
        if count == 16:
            spans = ((level + 1, 0, 1), (level + 1, 1, PLANES)) if level + 1 < LAYERS else ()
            activation, states[level], more = forward_layer(
                count, activation, proj, rest, smalls[level], edges, 1 + 4 * level, low_weights, spans
            )
            proj, rest = more or (None, None)
        else:
            rows = lax.all_gather(low_weights[level], "dp", axis=0, tiled=True)
            activation, states[level], _ = forward_layer(count, activation, rows[: 3 * D], rows[3 * D :], smalls[level], edges, 1)
    gradient = jnp.where(valid, own_cotangent.astype(F32), 0.0).reshape(total, D)
    mates = [None] * LAYERS
    for level in reversed(range(LAYERS)):
        carried = (activation.reshape(MICRO, piece, D),) if count == 16 and level == LAYERS - 1 else ()
        later = count == 16 and level == 0
        gradient, mates[level], swapped = backward_layer(count, gradient, smalls[level], edges, states[level], 2 + 4 * level, carried, later)
        activation = swapped[0] if carried else activation
    if count == 16:
        grad_big, mean_big, small_both, gradient = settle(
            mates, swapped, weights, first_big[0], second_big[0], *prepared[2 * LAYERS :]
        )
        new_smalls = finish(small_both, small_params, outer_small, first_small[0], second_small[0])
    else:
        rows, sums = zip(*[plain_grads(mate) for mate in mates])
        grad_big = jnp.stack([lax.psum_scatter(one, "dp", scatter_dimension=0, tiled=True).astype(F32) for one in rows])
        grad_small = lax.psum(jnp.stack(sums), "dp")
        reps = lax.axis_size("rep")
        delta_big = adam(weights, first_big[0], second_big[0], grad_big, LR_INNER, WEIGHT_DECAY)[2]
        delta_small = adam(small_params, first_small[0], second_small[0], grad_small, LR_SMALL, 0.0)[2]
        mean_big = lax.psum(delta_big.astype(BF16), "rep").astype(F32) / reps
        mean_small = lax.psum(delta_small.astype(BF16), "rep").astype(F32) / reps
        momentum = MOMENTUM * outer_small + mean_small
        new_smalls = (*moments(first_small[0], second_small[0], grad_small), momentum, small_params - LR_OUTER * (mean_small + MOMENTUM * momentum))
    new_first, new_second = moments(first_big[0], second_big[0], grad_big)
    new_first_small, new_second_small, outer_small_new, small_new = new_smalls
    outer_big_new = MOMENTUM * outer_big + mean_big
    weights_new = weights - LR_OUTER * (mean_big + MOMENTUM * outer_big_new)
    shape = (1, MICRO, 1, piece, D)
    return (
        activation.reshape(shape),
        gradient.reshape(shape),
        new_first[None],
        new_second[None],
        new_first_small[None],
        new_second_small[None],
        outer_big_new,
        outer_small_new,
        weights_new,
        small_new,
        weights_new.astype(BF16),
    )


def solution(mesh):
    placed = (
        P("rep", None, None, "dp", None),
        P("rep", None, None, None),
        P("rep", None, None, "dp", None),
        P(None, "dp", None),
        P(),
        P("rep", None, "dp", None),
        P("rep", None, "dp", None),
        P("rep", None, None),
        P("rep", None, None),
        P(None, "dp", None),
        P(),
    )
    return jax.shard_map(
        shards,
        mesh=mesh,
        in_specs=placed,
        out_specs=(
            P("rep", None, None, "dp", None),
            P("rep", None, None, "dp", None),
            P("rep", None, "dp", None),
            P("rep", None, "dp", None),
            P("rep", None, None),
            P("rep", None, None),
            P(None, "dp", None),
            P(),
            P(None, "dp", None),
            P(),
            P(None, "dp", None),
        ),
        check_vma=False,
    )
```

```python
import functools

import jax
import jax.numpy as jnp
from jax import lax
from jax.experimental import pallas as pl
from jax.experimental.pallas import tpu as pltpu
from jax.sharding import PartitionSpec as P

D = 768
HEADS = 12
FF = 3072
TAPS = 33
NS_ITERS = 6
LAYERS = 2
MICRO = 2
STEP_COUNT = 5


ADAM_ONE = 0.9
ADAM_TWO = 0.95
ADAM_EPSILON = 1e-08
WEIGHT_DECAY = 0.1
LR_INNER = 0.04
LR_SMALL = 0.2
LR_OUTER = 0.7
MOMENTUM = 0.9

HEAD_DIM = 64
MARKS = 64
HALF = TAPS // 2
PAIRS = HEADS // 2
LINES = 13
TAP_LINE = 12
SMALL = 8 * D + FF + HEADS * TAPS
LANES = 128
SCALE = HEAD_DIM**-0.5
NEG = -1e30
MESH = pl.DeviceIdType.MESH
F32 = jnp.float32
BF16 = jnp.bfloat16
NN = (((1,), (0,)), ((), ()))
NT = (((1,), (1,)), ((), ()))
TN = (((0,), (0,)), ((), ()))


def mm(a, b, dims=NN):
    return lax.dot_general(a, b, dims, preferred_element_type=F32)


def halves(a):
    high = a.astype(BF16)
    return high, (a - high.astype(F32)).astype(BF16)


def mm_left(a, b, dims=NN):
    high, rest = halves(a)
    return mm(high, b, dims) + mm(rest, b, dims)


def mm_both(a, b, dims=NN):
    ah, al = halves(a)
    bh, bl = halves(b)
    return mm(ah, bh, dims) + (mm(ah, bl, dims) + mm(al, bh, dims))


def exact(a, b, dims=NN):
    return mm_both(a, b, dims)


def sweep_all(body, carry, rolled):
    if rolled:
        return lax.fori_loop(0, NS_ITERS, body, carry)
    for step in range(NS_ITERS):
        carry = body(step, carry)
    return carry


def iota(shape, dim):
    return lax.broadcasted_iota(jnp.int32, shape, dim)


def diagonal_blocks():
    return (iota((LANES, LANES), 0) < MARKS) == (iota((LANES, LANES), 1) < HEAD_DIM)


def unit():
    return (iota((LANES, LANES), 0) == iota((LANES, LANES), 1)).astype(F32)


def per_head(marks):
    first = iota(marks.shape, 1) < HEAD_DIM
    return jnp.concatenate([jnp.where(first, marks, 0.0), jnp.where(first, 0.0, marks)], axis=0)


def head_sums(a):
    rows, cols = a.shape
    split = a.reshape(2, rows // 2, cols)
    return jnp.broadcast_to(jnp.sum(split, axis=1, keepdims=True), split.shape).reshape(rows, cols)


def head_tops(a):
    rows, cols = a.shape
    split = a.reshape(2, rows // 2, cols)
    return jnp.broadcast_to(jnp.max(split, axis=1, keepdims=True), split.shape).reshape(rows, cols)


def head_taps(lines, pair):
    row = jnp.broadcast_to(lines[TAP_LINE : TAP_LINE + 1, :], (8, D))
    rows = []
    for side in range(2):
        turned = pltpu.roll(row, lax.rem(D - TAPS * (2 * pair + side), D), 1)[0:1, : 2 * LANES]
        rows.append(jnp.where(iota((1, 2 * LANES), 1) < TAPS, turned, 0.0))
    return rows


def band(taps_row):
    wide = jnp.broadcast_to(taps_row, (LANES, 2 * LANES))
    return pltpu.roll(wide, 0, 1, stride=1, stride_axis=0)


def band_back(taps_row):
    wide = jnp.broadcast_to(taps_row, (2 * LANES, 2 * LANES))
    return pltpu.roll(wide, 2 * LANES - 2 * HALF, 1, stride=1, stride_axis=0)[:, :LANES].T


def mark_columns(edges):
    low = jnp.broadcast_to(edges, (LANES, LANES)).T[:MARKS, :1]
    high = jnp.broadcast_to(pltpu.roll(edges, LANES - 1, 1), (LANES, LANES)).T[:MARKS, :1]
    return low.astype(jnp.int32), high.astype(jnp.int32)


def mark_rows(edges):
    low, high = edges[:, :MARKS], pltpu.roll(edges, LANES - 1, 1)[:, :MARKS]
    return low.astype(jnp.int32), high.astype(jnp.int32)


def convolve(padded, bands, length, store):
    first = iota((LANES, LANES), 1) < HEAD_DIM
    pairs = [halves(one) for one in bands]

    def block(at, carry):
        start = pl.multiple_of(at * LANES, LANES)
        window = padded[pl.ds(start, 2 * LANES), :]
        out = [mm(high, window) + mm(rest, window) for high, rest in pairs]
        store(start, jnp.where(first, out[0], out[1]))
        return carry

    lax.fori_loop(0, length // LANES, block, 0)


def put_rows(ref, at, start, rows):
    half = ref.shape[2]
    ref[at, start // half, pl.ds(pl.multiple_of(lax.rem(start, half), LANES), LANES), :] = rows


def whole(ref, at):
    return ref[at].reshape(-1, LANES)


def attend(slab, edges, taps, keep, padded, blended, result):
    length = slab.shape[1] * slab.shape[2]

    def begin():
        low_marks, high_marks = mark_columns(edges())
        at = iota((MARKS, length), 1)
        member = ((low_marks <= at) & (at < high_marks)).astype(F32).astype(BF16)
        counts = (high_marks - low_marks).astype(F32)
        q_marks = per_head(mm(member, whole(slab, 0)) / counts)
        k_marks = per_head(mm(member, whole(slab, 1)) / counts)
        scores = jnp.where(diagonal_blocks(), SCALE * exact(q_marks, k_marks, NT), NEG)
        weights = jnp.exp(scores - jnp.max(scores, axis=1, keepdims=True))
        kernel = weights / jnp.sum(weights, axis=1, keepdims=True)
        total = head_sums(jnp.broadcast_to(jnp.sum(kernel * kernel, axis=1, keepdims=True), kernel.shape))
        keep["q_marks"][...] = q_marks
        keep["k_marks"][...] = k_marks
        keep["kernel"][...] = kernel
        keep["total"][...] = total
        keep["inverse"][0] = kernel.T / total

    def sweeps():
        def run(at, carry):
            eye, inverse = unit(), keep["inverse"][at]
            product = exact(keep["kernel"][...], inverse)
            one = 7.0 * eye - product
            two = 15.0 * eye - exact(product, one)
            three = 13.0 * eye - exact(product, two)
            keep["product"][at] = product
            keep["two"][at] = two
            keep["three"][at] = three
            keep["inverse"][at + 1] = 0.25 * exact(inverse, three)
            return carry

        sweep_all(run, 0, length <= 8 * LANES)

    def over_keys():
        valid = iota((1, length), 1) < mark_columns(edges())[1][MARKS - 1 :]
        key_scores = jnp.where(valid, SCALE * mm_left(keep["q_marks"][...], whole(slab, 1), NT), NEG)
        key_exp = jnp.where(valid, jnp.exp(key_scores - jnp.max(key_scores, axis=1, keepdims=True)), 0.0)
        key_weights = key_exp / jnp.sum(key_exp, axis=1, keepdims=True)
        keep["key_weights"][...] = key_weights
        keep["summary"][...] = jnp.where(diagonal_blocks(), mm_left(key_weights, whole(slab, 2)), 0.0)

    def over_tokens():
        token_scores = SCALE * mm_left(keep["k_marks"][...], whole(slab, 0), NT)
        token_exp = jnp.exp(token_scores - head_tops(token_scores))
        keep["token_weights"][...] = token_exp / head_sums(token_exp)

    def close():
        mixed = exact(keep["inverse"][NS_ITERS], keep["summary"][...])
        keep["mixed"][...] = mixed
        blended[...] = mm_both(keep["token_weights"][...], mixed, TN)
        values = whole(slab, 2)
        valid_column = iota((length, 1), 0) < mark_columns(edges())[1][MARKS - 1 :]
        padded[0:HALF, :] = jnp.zeros((HALF, LANES), BF16)
        padded[HALF : HALF + length, :] = jnp.where(valid_column, values, jnp.zeros_like(values))
        padded[HALF + length :, :] = jnp.zeros((LANES - HALF, LANES), BF16)

        def store(start, block):
            put_rows(result, 0, start, (blended[pl.ds(start, LANES), :] + block).astype(BF16))

        convolve(padded, [band(one) for one in taps()], length, store)

    return [begin, sweeps, over_keys, over_tokens, close]


def attend_back(grads, queries, keys, values, edges, taps, keep, padded, padded_grads, blended, result, grad_taps):
    length = grads.shape[0]
    low_marks, high_marks = mark_columns(edges)
    low_row, high_row = mark_rows(edges)
    at = iota((length, MARKS), 0)
    member = ((low_row <= at) & (at < high_row)).astype(F32).astype(BF16)
    counts = (high_marks - low_marks).astype(F32)
    blocks, eye = diagonal_blocks(), unit()
    q_marks, k_marks = keep["q_marks"][...], keep["k_marks"][...]
    token_weights, key_weights = keep["token_weights"][...], keep["key_weights"][...]
    summary, mixed = keep["summary"][...], keep["mixed"][...]
    kernel = keep["kernel"][...]
    inverse = keep["inverse"][NS_ITERS]
    grad_mixed = jnp.where(blocks, mm_left(token_weights, grads), 0.0)
    grad_token = token_weights * mm_left(mixed, grads, NT)
    grad_token = SCALE * (grad_token - token_weights * head_sums(grad_token))
    grad_summary = exact(inverse, grad_mixed, TN)
    grad_inverse = exact(grad_mixed, summary, NT)

    def sweep_back(step, carry):
        grad_kernel, grad_inverse = carry
        sweep = NS_ITERS - 1 - step
        before, product = keep["inverse"][sweep], keep["product"][sweep]
        one = 7.0 * eye - product
        two, three = keep["two"][sweep], keep["three"][sweep]
        grad_three = 0.25 * exact(before, grad_inverse, TN)
        grad_two = -exact(product, grad_three, TN)
        grad_one = -exact(product, grad_two, TN)
        grad_product = -(exact(grad_three, two, NT) + exact(grad_two, one, NT) + grad_one)
        grad_kernel = grad_kernel + exact(grad_product, before, NT)
        grad_inverse = 0.25 * exact(grad_inverse, three, NT) + exact(kernel, grad_product, TN)
        return grad_kernel, grad_inverse

    grad_kernel, grad_inverse = sweep_all(sweep_back, (jnp.zeros_like(kernel), grad_inverse), length <= 8 * LANES)
    total = keep["total"][...]
    turned = grad_inverse.T / total
    weighted = jnp.sum(jnp.where(blocks, turned * kernel, 0.0), axis=1, keepdims=True)
    weighted = head_sums(jnp.broadcast_to(weighted, kernel.shape))
    grad_kernel = grad_kernel + turned - 2.0 * kernel * weighted / total
    grad_scores = SCALE * kernel * (grad_kernel - jnp.sum(kernel * grad_kernel, axis=1, keepdims=True))
    grad_q_marks = exact(grad_scores, k_marks)
    grad_k_marks = exact(grad_scores, q_marks, TN)
    grad_k_marks = grad_k_marks + jnp.where(blocks, mm_left(grad_token, queries), 0.0)
    grad_key = mm_left(grad_summary, values, NT) - jnp.sum(grad_summary * summary, axis=1, keepdims=True)
    grad_key = SCALE * key_weights * grad_key
    grad_q_marks = grad_q_marks + jnp.where(blocks, mm_left(grad_key, keys), 0.0)
    grad_q_marks = (grad_q_marks[:MARKS] + grad_q_marks[MARKS:]) / counts
    grad_k_marks = (grad_k_marks[:MARKS] + grad_k_marks[MARKS:]) / counts
    high, rest = halves(grad_q_marks)
    result[0] = (mm_both(grad_token, k_marks, TN) + mm(member, high) + mm(member, rest)).astype(BF16).reshape(result.shape[1:])
    high, rest = halves(grad_k_marks)
    result[1] = (mm_both(grad_key, q_marks, TN) + mm(member, high) + mm(member, rest)).astype(BF16).reshape(result.shape[1:])
    blended[...] = mm_both(key_weights, grad_summary, TN)
    last = high_marks[MARKS - 1 :]
    valid_column = iota((length, 1), 0) < last
    padded[0:HALF, :] = jnp.zeros((HALF, LANES), BF16)
    padded[HALF : HALF + length, :] = jnp.where(valid_column, values, jnp.zeros_like(values))
    padded[HALF + length :, :] = jnp.zeros((LANES - HALF, LANES), BF16)
    padded_grads[0:HALF, :] = jnp.zeros((HALF, LANES), BF16)
    padded_grads[HALF : HALF + length, :] = grads
    padded_grads[HALF + length :, :] = jnp.zeros((LANES - HALF, LANES), BF16)

    def store(start, block):
        rows = start + iota((LANES, 1), 0)
        total_rows = blended[pl.ds(start, LANES), :] + jnp.where(rows < last, block, 0.0)
        put_rows(result, 2, start, total_rows.astype(BF16))

    convolve(padded_grads, [band_back(one) for one in taps], length, store)
    first = iota((LANES, LANES), 1) < HEAD_DIM

    def block(step, carry):
        start = pl.multiple_of(step * LANES, LANES)
        own = padded_grads[pl.ds(start + HALF, LANES), :]
        window = padded[pl.ds(start, 2 * LANES), :]
        none = jnp.zeros_like(own)
        return (
            carry[0] + mm(jnp.where(first, own, none), window, NT),
            carry[1] + mm(jnp.where(first, none, own), window, NT),
        )

    start_sum = jnp.zeros((LANES, 2 * LANES), F32)
    sums = lax.fori_loop(0, length // LANES, block, (start_sum, start_sum))
    wide = 2 * LANES
    for head in range(2):
        folded = sums[head][0:8]
        for group in range(1, LANES // 8):
            rows = sums[head][8 * group : 8 * group + 8]
            folded = folded + pltpu.roll(rows, wide - 8 * group, 1)
        line = folded[0:1]
        for row in range(1, 8):
            line = line + pltpu.roll(folded[row : row + 1], wide - row, 1)
        grad_taps[head : head + 1, :] = line


KEPT = ("q_marks", "k_marks", "kernel", "total", "inverse", "product", "two", "three", "key_weights", "summary", "mixed", "token_weights")


def kept_shapes(length):
    square = (LANES, LANES)
    shapes = {name: square for name in KEPT}
    shapes["inverse"] = (NS_ITERS + 1,) + square
    for name in ("product", "two", "three"):
        shapes[name] = (NS_ITERS,) + square
    shapes["key_weights"] = shapes["token_weights"] = (LANES, length)
    return shapes


class Layout:
    def __init__(self, count):
        self.count = count
        self.groups = MICRO if count == 16 else 1
        self.members = count // self.groups
        self.tasks = PAIRS * MICRO // self.groups

    def place(self):
        me = lax.axis_index("dp")
        self.me, self.group, self.index = me, me // self.members, lax.rem(me, self.members)
        self.task = (self.index * self.tasks + self.members - 1) // self.members
        if self.groups > 1:
            self.task = jnp.where(self.index < 3, self.index, jnp.where(self.index < 6, 3, self.index - 2))
        self.owns = self.owner(self.task) == self.index
        self.micro = self.micro_of(self.task)
        self.pair = lax.rem(self.task, PAIRS)
        return self

    def owner(self, task):
        if self.groups > 1:
            return jnp.where(task < 3, task, jnp.where(task < 4, 4, task + 2))
        return task * self.members // self.tasks

    def micro_of(self, task):
        return self.group if self.groups > 1 else task // PAIRS

    def device(self, index):
        return {"dp": self.group * self.members + index}

    def block(self, array, task):
        lanes = pl.ds(pl.multiple_of(lax.rem(task, PAIRS) * LANES, LANES), LANES)
        return array.at[:, :, :, lanes] if self.groups > 1 else array.at[:, pl.ds(task // PAIRS, 1), :, lanes]

    def rows(self, slab, index, piece):
        return slab.at[:, :, pl.ds(pl.multiple_of(index * piece, piece), piece), :]

    def mate(self):
        return {"dp": lax.rem(self.me + self.members, self.count)}


def greet(at, everyone=False, mate=False):
    barrier = pltpu.get_barrier_semaphore()
    size, index = (at.count, at.me) if everyone else (at.members, at.index)
    if everyone:
        pl.semaphore_signal(barrier, inc=1, device_id={"rep": 1 - lax.axis_index("rep")}, device_id_type=MESH)
    if mate:
        pl.semaphore_signal(barrier, inc=1, device_id=at.mate(), device_id_type=MESH)

    def signal(step, carry):
        other = lax.rem(index + step, size)
        pl.semaphore_signal(barrier, inc=1, device_id={"dp": other} if everyone else at.device(other), device_id_type=MESH)
        return carry

    lax.fori_loop(1, size, signal, 0)
    pl.semaphore_wait(barrier, size - 1 + int(everyone) + int(mate))


def scatter_tasks(at, piece, source, slab, send, receive):
    def one(step, finish):
        task = lax.rem(at.task + step, at.tasks)
        owner = at.owner(task)
        outgoing, landing = at.block(source, task), at.rows(slab, at.index, piece)

        @pl.when(owner != at.index)
        def _():
            copy = pltpu.make_async_remote_copy(
                outgoing, landing, send.at[task], receive.at[at.index], device_id=at.device(owner), device_id_type=MESH
            )
            if finish:
                copy.wait_send()
            else:
                copy.start()

        @pl.when((owner == at.index) & (not finish))
        def _():
            pltpu.make_async_copy(outgoing, landing, receive.at[at.index]).start()

    def run(finish):
        def body(step, carry):
            one(step, finish)
            return carry

        lax.fori_loop(0, at.tasks, body, 0)

    return run


def await_slab(at, piece, slab, receive):
    def body(origin, carry):
        landing = at.rows(slab, origin, piece)
        pltpu.make_async_copy(landing, landing, receive.at[origin]).wait()
        return carry

    lax.fori_loop(0, at.members, body, 0)


def return_rows(at, piece, result, target, send, receive):
    def run(finish):
        def body(step, carry):
            peer = lax.rem(at.index + step, at.members)
            outgoing, landing = at.rows(result, peer, piece), at.block(target, at.task)

            @pl.when(peer != at.index)
            def _():
                copy = pltpu.make_async_remote_copy(
                    outgoing, landing, send.at[peer], receive.at[at.task], device_id=at.device(peer), device_id_type=MESH
                )
                if finish:
                    copy.wait_send()
                else:
                    copy.start()

            @pl.when((peer == at.index) & (not finish))
            def _():
                pltpu.make_async_copy(outgoing, landing, receive.at[at.task]).start()

            return carry

        lax.fori_loop(0, at.members, body, 0)

    return run


def await_rows(at, target, receive):
    def body(task, carry):
        landing = at.block(target, task)
        pltpu.make_async_copy(landing, landing, receive.at[task]).wait()
        return carry

    lax.fori_loop(0, at.tasks, body, 0)


def swap(at, source, target, send, receive):
    return pltpu.make_async_remote_copy(
        source.at[1 - at.group], target.at[at.group], send, receive, device_id=at.mate(), device_id_type=MESH
    )


def forward_kernel(count, piece, spans, qkv, edges, lines, low, mixed_rows, slab, *refs):
    keep = dict(zip(KEPT, refs))
    outs, refs = refs[len(KEPT) : len(KEPT) + len(spans)], refs[len(KEPT) + len(spans) :]
    padded, blended, result, send_one, receive_one, send_two, receive_two = refs[:7]
    begin, steps, finish = spread_all(spans, low, outs, refs[7:])
    at = Layout(count).place()
    greet(at, bool(spans))
    out = scatter_tasks(at, piece, qkv, slab, send_one, receive_one)
    out(False)
    begin()
    back = return_rows(at, piece, result, mixed_rows, send_two, receive_two)
    phases = attend(slab, lambda: edges[pl.ds(at.micro, 1), :], lambda: head_taps(lines, at.pair), keep, padded, blended, result)

    def between(turn):
        if turn < len(steps):
            steps[turn]()

    between(0)
    for turn, phase in enumerate(phases):

        @pl.when(at.owns)
        def _():
            if turn == 0:
                await_slab(at, piece, slab, receive_one)
            phase()
            if turn == len(phases) - 1:
                back(False)

        if turn > 1:
            between(turn - 1)
    for turn in range(len(phases) - 1, len(steps)):
        between(turn)
    finish()
    out(True)
    await_rows(at, mixed_rows, receive_two)

    @pl.when(at.owns)
    def _():
        back(True)


def backward_kernel(count, piece, carries, grads, edges, lines, *refs):
    carried, refs = refs[:carries], refs[carries:]
    slab, refs = refs[0], refs[1:]
    keep = dict(zip(KEPT, refs))
    out_grads, grad_taps, refs = refs[len(KEPT)], refs[len(KEPT) + 1], refs[len(KEPT) + 2 :]
    swapped, refs = refs[:carries], refs[carries:]
    grad_slab, padded, padded_grads, blended, result, send_one, receive_one, send_two, receive_two, send_swap, receive_swap = refs
    at = Layout(count).place()
    greet(at, mate=bool(carries))
    out = scatter_tasks(at, piece, grads, grad_slab, send_one, receive_one)
    out(False)
    swaps = [swap(at, one, two, send_swap, receive_swap) for one, two in zip(carried, swapped)]
    for one, source, target in zip(swaps, carried, swapped):
        one.start()
        target[pl.ds(at.group, 1)] = source[pl.ds(at.group, 1)]
    back = return_rows(at, piece, result, out_grads, send_two, receive_two)
    grad_taps[...] = jnp.zeros(grad_taps.shape, F32)

    @pl.when(at.owns)
    def _():
        await_slab(at, piece, grad_slab, receive_one)
        attend_back(
            whole(grad_slab, 0), whole(slab, 0), whole(slab, 1), whole(slab, 2), edges[pl.ds(at.micro, 1), :], head_taps(lines, at.pair),
            keep, padded, padded_grads, blended, result, grad_taps.at[at.pair],
        )
        back(False)

    out(True)
    await_rows(at, out_grads, receive_two)
    for one in swaps:
        one.wait()

    @pl.when(at.owns)
    def _():
        back(True)


VMEM = pl.BlockSpec(memory_space=pltpu.VMEM)
DMA = pltpu.SemaphoreType.DMA


def attention_forward(count, qkv, edges, lines, ident, low=None, spans=()):
    piece = qkv.shape[2]
    length = piece * count
    shapes = kept_shapes(length)
    low = low if spans else lines
    at = Layout(count)
    halved = (at.groups, length // at.groups, LANES)
    anywhere = pl.BlockSpec(memory_space=pl.ANY)
    results = pl.pallas_call(
        functools.partial(forward_kernel, count, piece, spans),
        out_shape=[
            jax.ShapeDtypeStruct((1, MICRO, piece, D), BF16),
            jax.ShapeDtypeStruct((3,) + halved, BF16),
        ]
        + [jax.ShapeDtypeStruct(shapes[name], F32) for name in KEPT]
        + [spread_shape(low, span) for span in spans],
        in_specs=[VMEM] * 4,
        out_specs=[VMEM] * (2 + len(KEPT)) + [anywhere] * len(spans),
        scratch_shapes=[
            pltpu.VMEM((length + LANES, LANES), BF16),
            pltpu.VMEM((length, LANES), F32),
            pltpu.VMEM((1,) + halved, BF16),
            DMA((at.tasks,)),
            DMA((at.members,)),
            DMA((at.members,)),
            DMA((at.tasks,)),
        ]
        + [one for span in spans for one in spread_semaphores(span)],
        compiler_params=pltpu.CompilerParams(collective_id=ident, has_side_effects=True, vmem_limit_bytes=60 << 20),
        name="attend_forward",
    )(qkv, edges, lines, low)
    return results[0][0], results[1 : 2 + len(KEPT)], [flat_rows(one) for one in results[2 + len(KEPT) :]]


def attention_backward(count, grads, edges, lines, kept, ident, carried=()):
    piece = grads.shape[2]
    length = piece * count
    at = Layout(count)
    halved = (at.groups, length // at.groups, LANES)
    results = pl.pallas_call(
        functools.partial(backward_kernel, count, piece, len(carried)),
        out_shape=[
            jax.ShapeDtypeStruct((3, MICRO, piece, D), BF16),
            jax.ShapeDtypeStruct((PAIRS, 2, 2 * LANES), F32),
        ]
        + [jax.ShapeDtypeStruct(one.shape, one.dtype) for one in carried],
        in_specs=[VMEM] * (4 + len(carried) + len(KEPT)),
        out_specs=[VMEM] * (2 + len(carried)),
        scratch_shapes=[
            pltpu.VMEM((1,) + halved, BF16),
            pltpu.VMEM((length + LANES, LANES), BF16),
            pltpu.VMEM((length + LANES, LANES), BF16),
            pltpu.VMEM((length, LANES), F32),
            pltpu.VMEM((3,) + halved, BF16),
            DMA((at.tasks,)),
            DMA((at.members,)),
            DMA((at.members,)),
            DMA((at.tasks,)),
            DMA,
            DMA,
        ],
        compiler_params=pltpu.CompilerParams(collective_id=ident, has_side_effects=True, vmem_limit_bytes=60 << 20),
        name="attend_backward",
    )(grads, edges, lines, *carried, *kept)
    return results[0], results[1], results[2:]


def arrange(sources, targets):
    params, first, second = sources
    lines, ups, sliced = targets[:LAYERS], targets[LAYERS : 2 * LAYERS], targets[2 * LAYERS :]
    for level in range(LAYERS):
        own = slice(level, level + 1)
        for line in range(TAP_LINE):
            lines[level][line : line + 1, :] = params[own, line * D : (line + 1) * D]
        lines[level][TAP_LINE:, :] = jnp.zeros((16 - TAP_LINE, D), F32)
        lines[level][TAP_LINE : TAP_LINE + 1, : HEADS * TAPS] = params[own, TAP_LINE * D :]
        ups[level][...] = params[own, 8 * D : 8 * D + FF]
    for source, target in zip((first, second), sliced):
        target[LAYERS * LINES // 2 :] = jnp.zeros((16 - LAYERS * LINES // 2, 2, D), F32)
        for level in range(LAYERS):
            own = slice(level, level + 1)
            for line in range(LINES):
                index = level * LINES + line
                spot = slice(index % 2, index % 2 + 1)
                if line < TAP_LINE:
                    target[index // 2, spot, :] = source[own, line * D : (line + 1) * D]
                else:
                    target[index // 2, spot, :] = jnp.zeros((1, D), F32)
                    target[index // 2, spot, : HEADS * TAPS] = source[own, TAP_LINE * D :]


ARRANGED = (
    [jax.ShapeDtypeStruct((16, D), F32)] * LAYERS + [jax.ShapeDtypeStruct((1, FF), F32)] * LAYERS + [jax.ShapeDtypeStruct((16, 2, D), F32)] * 2
)


def arrange_kernel(*refs):
    arrange(refs[:3], refs[3:])


def arranged(*smalls):
    return pl.pallas_call(arrange_kernel, out_shape=ARRANGED, in_specs=[VMEM] * 3, out_specs=[VMEM] * len(ARRANGED), name="arrange")(*smalls)


PLANES = 4
SUBS = 2
EVEN, ODD = range(0, SUBS, 2), range(1, SUBS, 2)


def gather_kernel(spans, low, params, first, second, hidden, cotangent, *refs):
    outs, refs = refs[: len(spans)], refs[len(spans) :]
    targets, refs = refs[: len(ARRANGED)], refs[len(ARRANGED) :]
    swapped, swap_sems, refs = refs[:2], refs[2], refs[3:]
    begin, steps, finish = spread_all(spans, low, outs, refs)
    at = Layout(16).place()
    me, x = lax.axis_index("dp"), lax.axis_index("rep")
    core, y, z = lax.rem(me, 2), lax.rem(me // 2, 2), me // 4
    barrier = pltpu.get_barrier_semaphore()
    for where in ({"rep": 1 - x}, {"dp": me + 2 - 4 * y}, {"dp": me + 1 - 2 * core}, at.mate()):
        pl.semaphore_signal(barrier, inc=1, device_id=where, device_id_type=MESH)
    for sign in (1, -1):

        @pl.when((z + sign >= 0) & (z + sign < PLANES))
        def _():
            pl.semaphore_signal(barrier, inc=1, device_id={"dp": me + 4 * sign}, device_id_type=MESH)

    pl.semaphore_wait(barrier, 5 + jnp.where((z > 0) & (z < PLANES - 1), 1, 0))
    begin()
    swaps = [swap(at, one, two, swap_sems.at[0, which], swap_sems.at[1, which]) for which, (one, two) in enumerate(zip((hidden, cotangent), swapped))]
    for one, source, target in zip(swaps, (hidden, cotangent), swapped):
        one.start()
        target[pl.ds(at.group, 1)] = source[pl.ds(at.group, 1)]
    arrange((params, first, second), targets)
    for step in steps:
        step()
    finish()
    for one in swaps:
        one.wait()


def spread_semaphores(span):
    planes = span[2] - span[1]
    return [DMA, DMA((planes, SUBS, 2)), DMA((planes, SUBS))] + [DMA((planes, 2, 2, SUBS))] * 5 + [DMA]


def spread_shape(low, span):
    return jax.ShapeDtypeStruct((span[2] - span[1], 2, 2) + low.shape[1:], BF16)


def flat_rows(blocks):
    return blocks.reshape(-1, D)


def spread_all(spans, low, outs, semaphores):
    each = len(semaphores) // max(len(spans), 1)
    parts = [
        spread(low.at[level], out, bottom, top, *semaphores[at * each : (at + 1) * each])
        for at, ((level, bottom, top), out) in enumerate(zip(spans, outs))
    ]

    def together(actions):
        def run():
            for action in actions:
                action()

        return run

    steps = [together(actions) for actions in zip(*[part[1] for part in parts])]
    return together([part[0] for part in parts]), steps, together([part[2] for part in parts])


def spread(shard, out, bottom, top, local_sem, z_send, z_got, x_send, x_got, y_send, y_got, core_send, core_got):
    me = lax.axis_index("dp")
    x = lax.axis_index("rep")
    core, y, z = lax.rem(me, 2), lax.rem(me // 2, 2), me // 4
    half = shard.shape[0] // 2
    part = half // SUBS

    def held(plane):
        return (plane >= bottom) & (plane < top)

    def peer(axis, sign=1):
        if axis == "x":
            return {"rep": 1 - x}
        if axis == "y":
            return {"dp": me + 2 - 4 * y}
        if axis == "core":
            return {"dp": me + 1 - 2 * core}
        return {"dp": me + 4 * sign}

    def rows(side, sub):
        return pl.ds(pl.multiple_of(side * half + sub * part, part), part)

    def remote(source, target, send, receive, where):
        return pltpu.make_async_remote_copy(source, target, send, receive, device_id=where, device_id_type=MESH)

    def spot(plane, row, side, sub):
        return out.at[plane - bottom, row, core, rows(side, sub), :]

    def move(axis, plane, row, side, sub, source=None):
        target = spot(plane, row, side, sub)
        source = target if source is None else source
        at = plane - bottom
        if axis == "core":
            return remote(source, target, core_send.at[at, row, side, sub], core_got, peer("core"))
        send, receive = (x_send, x_got) if axis == "x" else (y_send, y_got)
        return remote(source, target, send.at[at, row, side, sub], receive.at[at, row, side, sub], peer(axis))

    def climb(plane, sub, sign, source=None):
        target = spot(plane, y, x, sub)
        way = (1 - sign) // 2
        at = plane - bottom
        return remote(target if source is None else source, target, z_send.at[at, sub, way], z_got.at[at, sub], peer("z", sign))

    def inside(sign, act):
        pl.when((z + sign >= 0) & (z + sign < PLANES))(act)

    def begin():
        @pl.when(held(z))
        def _():
            pltpu.make_async_copy(shard, out.at[z - bottom, y, core], local_sem).start()
            for sub in range(SUBS):
                for sign in (1, -1):
                    inside(sign, lambda: climb(z, sub, sign, shard.at[rows(x, sub), :]).start())
                move("y", z, y, x, sub, shard.at[rows(x, sub), :]).start()
            for side in range(2):
                for sub in range(SUBS):
                    move("core", z, y, side, sub, shard.at[rows(side, sub), :]).start()

    def at_distance(distance, act):
        def side(step, carry):
            sign = 1 - 2 * step
            plane = z - sign * distance
            pl.when(held(plane))(lambda: act(plane, sign))
            return carry

        lax.fori_loop(0, 2, side, 0)

    def for_subs(act):
        def one(sub, carry):
            act(sub)
            return carry

        lax.fori_loop(0, SUBS, one, 0)

    def from_z(plane, sign):
        def one(sub):
            climb(plane, sub, sign).wait_recv()
            inside(sign, lambda: climb(plane, sub, sign).start())
            for axis in ("x", "y", "core"):
                move(axis, plane, y, x, sub).start()

        for_subs(one)

    def take(axis, plane, row, side, sub, onward=None):
        move(axis, plane, row, side, sub).wait_recv()
        if onward is not None:
            move(onward, plane, row, side, sub).start()
        move("core", plane, row, side, sub).start()

    def first_square(plane, sign):
        for even, odd in zip(EVEN, ODD):
            take("x", plane, y, 1 - x, even, "y")
            take("y", plane, 1 - y, x, odd, "x")
            take("y", plane, 1 - y, x, even)
            take("x", plane, y, 1 - x, odd)

    def second_square(plane, sign):
        for even, odd in zip(EVEN, ODD):
            take("y", plane, 1 - y, 1 - x, even)
            take("x", plane, 1 - y, 1 - x, odd)

    def own_first():
        @pl.when(held(z))
        def _():
            for sub in range(SUBS):
                take("y", z, 1 - y, x, sub, "x")

    def own_last():
        @pl.when(held(z))
        def _():
            for sub in range(SUBS):
                take("x", z, 1 - y, 1 - x, sub)

    def stage(distance, act):
        return lambda: at_distance(distance, act)

    steps = [
        stage(1, from_z), own_first, stage(2, from_z), stage(1, first_square), stage(3, from_z), stage(2, first_square),
        own_last, stage(1, second_square), stage(3, first_square), stage(2, second_square), stage(3, second_square),
    ]

    def sent(plane, sign):
        def one(sub):
            inside(sign, lambda: climb(plane, sub, sign).wait_send())
            move("x", plane, y, x, sub).wait_send()
            move("y", plane, y, x, sub).wait_send()

        for_subs(one)
        for even, odd in zip(EVEN, ODD):
            move("y", plane, y, 1 - x, even).wait_send()
            move("x", plane, 1 - y, x, odd).wait_send()

    def finish():
        def distant(distance, carry):
            at_distance(distance, sent)
            return carry

        lax.fori_loop(1, 4, distant, 0)

        @pl.when(held(z))
        def _():
            pltpu.make_async_copy(shard, out.at[z - bottom, y, core], local_sem).wait()
            for sub in range(SUBS):
                for sign in (1, -1):
                    inside(sign, lambda: climb(z, sub, sign).wait_send())
                move("y", z, y, x, sub).wait_send()
                move("x", z, 1 - y, x, sub).wait_send()

        def core_sent(index, carry):
            plane, row = bottom + index // (4 * SUBS), lax.rem(index // (2 * SUBS), 2)
            side, sub = lax.rem(index // SUBS, 2), lax.rem(index, SUBS)
            move("core", plane, row, side, sub).wait_send()
            return carry

        lax.fori_loop(0, 4 * SUBS * (top - bottom), core_sent, 0)
        column = out.at[:, :, 1 - core]
        pltpu.make_async_copy(column, column, core_got).wait()

    return begin, steps, finish


def gather(low, spans, hidden, cotangent, *smalls):
    results = pl.pallas_call(
        functools.partial(gather_kernel, spans),
        out_shape=[spread_shape(low, span) for span in spans] + ARRANGED + [jax.ShapeDtypeStruct(hidden.shape, BF16)] * 2,
        in_specs=[VMEM] * 6,
        out_specs=[pl.BlockSpec(memory_space=pl.ANY)] * len(spans) + [VMEM] * (len(ARRANGED) + 2),
        scratch_shapes=[DMA((2, 2))] + [one for span in spans for one in spread_semaphores(span)],
        compiler_params=pltpu.CompilerParams(collective_id=4, has_side_effects=True),
        name="gather",
    )(low, *smalls, hidden, cotangent)
    return [flat_rows(one) for one in results[: len(spans)]], results[len(spans) : -2], results[-2:]


CHUNK = 32
RING = 12
CYCLE = 6
MATES = ("low_in", "low_comb", "low_up", "low_act", "low_grads", "low_branch", "low_hidden", "low_down", "gain_one", "shift_one", "gain_two", "shift_two", "taps")
LATE = ("low_grads", "taps")


def change(grad, first_old, second_old):
    new_first = ADAM_ONE * first_old + (1.0 - ADAM_ONE) * grad
    new_second = ADAM_TWO * second_old + (1.0 - ADAM_TWO) * grad * grad
    return new_first * (1.0 / (1.0 - ADAM_ONE**STEP_COUNT)) / (jnp.sqrt(new_second * (1.0 / (1.0 - ADAM_TWO**STEP_COUNT))) + ADAM_EPSILON)


def settle_kernel(block_rows, tokens, *refs):
    early = [name for name in MATES if name not in LATE]
    mates = [dict(zip(early, refs)), dict(zip(MATES, refs[len(early) :]))]
    refs = refs[len(early) + len(MATES) :]
    grads, edges, lines, proj, grad_one, slab = refs[:6]
    keep = dict(zip(KEPT, refs[6:]))
    refs = refs[6 + len(KEPT) :]
    (
        weights, first, second, small_first, small_second, grad_out, mean_out, small_out, grad_in_out,
        turned, right, staged, own, got_core, got_y, got_near, got_far, inner, step_own, step_got, small, small_got, small_own, small_step, small_step_got,
        core_send, core_got, y_send, y_got, near_send, near_got, far_send, far_got, inner_sem, rep_send, rep_got, small_send, small_sem, back_send, back_sem, small_rep, swap_sems,
        low_grads, taps, grad_slab, padded, padded_grads, blended, result, grad_in, send_one, receive_one, send_two, receive_two,
    ) = refs
    mates[0].update(low_grads=low_grads, taps=taps)
    piece = grads.shape[2]
    me = lax.axis_index("dp")
    other_rep = 1 - lax.axis_index("rep")
    core, y, z = lax.rem(me, 2), lax.rem(me // 2, 2), me // 4
    devices = 16
    per_layer = block_rows // CHUNK
    chunks = LAYERS * per_layer

    barrier = pltpu.get_barrier_semaphore()

    def signal(step, carry):
        pl.semaphore_signal(barrier, inc=1, device_id={"dp": lax.rem(me + step, devices)}, device_id_type=MESH)
        return carry

    lax.fori_loop(1, devices, signal, 0)
    pl.semaphore_signal(barrier, inc=1, device_id={"rep": other_rep}, device_id_type=MESH)

    def to_dp(source, target, send, receive, peer):
        return pltpu.make_async_remote_copy(source, target, send, receive, device_id={"dp": peer}, device_id_type=MESH)

    def to_rep(source, target, send, receive):
        return pltpu.make_async_remote_copy(source, target, send, receive, device_id={"rep": other_rep}, device_id_type=MESH)

    def spot(slot):
        return lax.rem(slot, RING)

    features = D * 2 + FF * 2

    def prepare(level):
        order = LAYERS - 1 - level
        mate, at = mates[level], order * features
        for name in MATES[:4]:
            source, base = mate[name], at

            def transpose(step, carry):
                for part in range(D // LANES):
                    lanes = pl.multiple_of(step * D + part * LANES, LANES)
                    turned[pl.ds(pl.multiple_of(base + lanes, LANES), LANES), :] = source[:, pl.ds(lanes, LANES)].T
                return carry

            lax.fori_loop(0, source.shape[1] // D, transpose, 0)
            at += source.shape[1]
        for part in range(3):
            right[order * 6 + part] = mate["low_grads"][part].reshape(tokens, D)
        for part, name in enumerate(MATES[5:8]):
            right[order * 6 + 3 + part] = mate[name][...]

    prepare(LAYERS - 1)

    def put(level, line, row):
        index = level * LINES + line
        small[index // 2, index % 2 : index % 2 + 1, :] = row

    def column_sum(array):
        return jnp.sum(array.astype(F32), axis=0, keepdims=True)

    def small_rows():
        for level in range(LAYERS):
            mate = mates[level]
            put(level, 0, column_sum(right[(LAYERS - 1 - level) * 6]))
            put(level, 1, column_sum(right[(LAYERS - 1 - level) * 6 + 2]))
            put(level, 2, column_sum(mate["low_branch"][...]))
            put(level, 3, column_sum(mate["low_down"][...]))
            for line, name in enumerate(MATES[8:12]):
                put(level, 4 + line, column_sum(mate[name][...]))
            for part in range(FF // D):
                put(level, 8 + part, column_sum(mate["low_up"][:, part * D : (part + 1) * D]))
            line = jnp.zeros((1, D), F32)
            for head in range(HEADS):
                taps = jnp.concatenate([mate["taps"][head // 2][head % 2 : head % 2 + 1], jnp.zeros((1, D - 2 * LANES), F32)], axis=1)
                taps = jnp.where(iota((1, D), 1) < TAPS, taps, 0.0)
                line = line + (pltpu.roll(taps, TAPS * head, 1) if head else taps)
            put(level, 12, line)
        for index in range(LAYERS * LINES, 2 * devices):
            small[index // 2, index % 2 : index % 2 + 1, :] = jnp.zeros((1, D), F32)

    pl.semaphore_wait(barrier, devices)

    at = Layout(16).place()
    out = scatter_tasks(at, piece, grads, grad_slab, send_one, receive_one)
    back = return_rows(at, piece, result, low_grads, send_two, receive_two)
    swapping = swap(at, grad_in, grad_in_out, swap_sems.at[0], swap_sems.at[1])
    out(False)

    def attention():
        taps[...] = jnp.zeros(taps.shape, F32)

        @pl.when(at.owns)
        def _():
            await_slab(at, piece, grad_slab, receive_one)
            attend_back(
                whole(grad_slab, 0), whole(slab, 0), whole(slab, 1), whole(slab, 2), edges[pl.ds(at.micro, 1), :], head_taps(lines, at.pair),
                keep, padded, padded_grads, blended, result, taps.at[at.pair],
            )
            back(False)

    def collect():
        out(True)
        await_rows(at, low_grads, receive_two)
        pl.when(at.owns)(lambda: back(True))

    def input_grads():
        total = grad_one[...]
        for part in range(3):
            total = total + mm(low_grads[part].reshape(tokens, D), proj[part], NT)
        grad_in[...] = total.reshape(grad_in.shape)
        swapping.start()
        grad_in_out[pl.ds(at.group, 1)] = grad_in[pl.ds(at.group, 1)]

    def small_copy(step):
        peer = lax.rem(me + step, devices)
        return to_dp(small.at[peer], small_got.at[me], small_send.at[peer], small_sem.at[me], peer)

    def small_begin(step, carry):
        small_copy(step).start()
        return carry

    def small_start():
        small_rows()
        lax.fori_loop(1, devices, small_begin, 0)

    def core_copy(chunk):
        return to_dp(staged.at[lax.rem(chunk, 2)], got_core.at[spot(chunk)], core_send.at[lax.rem(chunk, 2)], core_got.at[spot(chunk)], me + 1 - 2 * core)

    near, far = z + 1 - 2 * lax.rem(z, 2), 3 - z

    def plane_device(plane):
        return plane * 4 + lax.rem(me, 4)

    def y_copy(chunk, full):
        slot = spot(chunk)
        source, target = (own.at[slot, :, 1 - y], got_y.at[slot]) if full else (own.at[slot, z, 1 - y], got_y.at[slot, 0])
        return to_dp(source, target, y_send.at[slot], y_got.at[slot], me + 2 - 4 * y)

    def near_copy(chunk, which, full):
        slot, block = spot(chunk), 3 - near if which else near
        source, target = (own.at[slot, block], got_near.at[slot, which]) if full else (own.at[slot, block, y], got_near.at[slot, which, 0])
        return to_dp(source, target, near_send.at[slot, which], near_got.at[slot, which], plane_device(near))

    def far_copy(chunk, full):
        slot = spot(chunk)
        source, target = (own.at[slot, far], got_far.at[slot]) if full else (own.at[slot, far, y], got_far.at[slot, 0])
        return to_dp(source, target, far_send.at[slot], far_got.at[slot], plane_device(far))

    def by_order(chunk, y_first, z_first):
        turn_z = lax.rem(chunk, CYCLE) == CYCLE // 2
        pl.when(jnp.logical_not(turn_z))(y_first)
        pl.when(turn_z)(z_first)

    def place(chunk):
        return LAYERS - 1 - chunk // per_layer, pl.ds(pl.multiple_of(lax.rem(chunk, per_layer) * CHUNK, CHUNK), CHUNK)

    def inner_copies(chunk):
        level, rows = place(chunk)
        slot = lax.rem(chunk, 4)
        return [
            pltpu.make_async_copy(array.at[level, rows, :], inner.at[slot, index], inner_sem.at[slot, index])
            for index, array in enumerate((weights, first, second))
        ]

    def rep_copy(chunk):
        return to_rep(step_own.at[spot(chunk)], step_got.at[spot(chunk)], rep_send.at[spot(chunk)], rep_got.at[spot(chunk)])

    def product(chunk, there, row, side):
        order = chunk // per_layer
        block = (there * 2 + row) * 2 + side
        piece = block * per_layer + lax.rem(chunk, per_layer)
        narrow = D // CHUNK
        line = jnp.where(piece < 3 * narrow, lax.rem(piece, narrow), piece - 2 * narrow)
        group = jnp.where(piece < 4 * narrow, piece // narrow, jnp.where(piece < 4 * narrow + FF // CHUNK, 4, 5))
        rows = pl.ds(pl.multiple_of(order * features + line * CHUNK, 16), CHUNK)
        return mm(turned[rows, :], right[order * 6 + group]).astype(BF16)

    def stage_product(chunk):
        for there in range(4):
            for row in range(2):
                staged[lax.rem(chunk, 2), there, row] = product(chunk, there, row, 1 - core)
        core_copy(chunk).start()
        for there in range(4):
            for row in range(2):
                own[spot(chunk), there, row] = product(chunk, there, row, core)

    def stage_core(chunk):
        core_copy(chunk).wait()
        slot = spot(chunk)
        for there in range(4):
            for side in range(2):
                own[slot, there, side] = own[slot, there, side] + got_core[slot, there, side]

        def z_first():
            for which in range(2):
                near_copy(chunk, which, True).start()

        by_order(chunk, lambda: y_copy(chunk, True).start(), z_first)

    def stage_second(chunk):
        slot = spot(chunk)

        def y_first():
            y_copy(chunk, True).wait()
            for there in range(4):
                own[slot, there, y] = own[slot, there, y] + got_y[slot, there]
            for which in range(2):
                near_copy(chunk, which, False).start()

        def z_first():
            for which in range(2):
                near_copy(chunk, which, True).wait()
            for row in range(2):
                own[slot, far, row] = own[slot, far, row] + got_near[slot, 1, row]
                own[slot, z, row] = own[slot, z, row] + got_near[slot, 0, row]
            far_copy(chunk, True).start()

        by_order(chunk, y_first, z_first)

    def stage_third(chunk):
        slot = spot(chunk)

        def y_first():
            for which in range(2):
                near_copy(chunk, which, False).wait()
            own[slot, far, y] = own[slot, far, y] + got_near[slot, 1, 0]
            own[slot, z, y] = own[slot, z, y] + got_near[slot, 0, 0]
            far_copy(chunk, False).start()

        def z_first():
            far_copy(chunk, True).wait()
            for row in range(2):
                own[slot, z, row] = own[slot, z, row] + got_far[slot, row]
            y_copy(chunk, False).start()

        by_order(chunk, y_first, z_first)
        for copy in inner_copies(chunk):
            copy.start()

    def stage_last(chunk):
        for copy in inner_copies(chunk):
            copy.wait()
        by_order(chunk, lambda: far_copy(chunk, False).wait(), lambda: y_copy(chunk, False).wait())
        slot = spot(chunk)
        turn_z = lax.rem(chunk, CYCLE) == CYCLE // 2
        total = own[slot, z, y].astype(F32) + jnp.where(turn_z, got_y[slot, 0].astype(F32), got_far[slot, 0].astype(F32))
        level, rows = place(chunk)
        grad_out[level, rows, :] = total
        slot = lax.rem(chunk, 4)
        step = change(total, inner[slot, 1], inner[slot, 2]) + WEIGHT_DECAY * inner[slot, 0]
        step_own[spot(chunk)] = (LR_INNER * step).astype(BF16)
        rep_copy(chunk).start()

    def stage_rep(chunk):
        rep_copy(chunk).wait()
        level, rows = place(chunk)
        mean_out[level, rows, :] = 0.5 * (step_own[spot(chunk)].astype(F32) + step_got[spot(chunk)].astype(F32))

    def small_rep_copy():
        return to_rep(small_step, small_step_got, small_rep.at[0], small_rep.at[1])

    def small_back(step):
        peer = lax.rem(me + step, devices)
        return to_dp(small_own, small_out.at[me], back_send.at[peer], back_sem.at[me], peer)

    def small_sum():
        def add(step, total):
            peer = lax.rem(me + step, devices)
            pltpu.make_async_copy(small_got.at[peer], small_got.at[peer], small_sem.at[peer]).wait()
            return total + small_got[peer]

        total = lax.fori_loop(1, devices, add, small[me])
        small_own[0] = total
        small_step[...] = (LR_SMALL * change(total, small_first[me], small_second[me])).astype(BF16)
        small_rep_copy().start()

    def small_spread():
        small_rep_copy().wait_recv()
        small_own[1] = 0.5 * (small_step[...].astype(F32) + small_step_got[...].astype(F32))
        small_out[me] = small_own[...]

        def send(step, carry):
            small_back(step).start()
            return carry

        lax.fori_loop(1, devices, send, 0)

    def turn(now, carry):
        for lag, stage in ((0, stage_product), (1, stage_core), (3, stage_second), (5, stage_third), (7, stage_last), (9, stage_rep)):

            @pl.when((now >= lag) & (now < chunks + lag))
            def _():
                stage(now - lag)

        for when, act in (
            (2, attention), (6, collect), (7, lambda: prepare(0)), (8, input_grads), (9, small_start), (13, small_sum), (16, small_spread),
        ):
            pl.when(now == when)(act)
        return carry

    lax.fori_loop(0, chunks + 9, turn, 0)

    def small_drain(step, carry):
        peer = lax.rem(me + step, devices)
        small_copy(step).wait_send()
        small_back(step).wait_send()
        pltpu.make_async_copy(small_own, small_out.at[peer], back_sem.at[peer]).wait()
        return carry

    lax.fori_loop(1, devices, small_drain, 0)
    small_rep_copy().wait_send()
    swapping.wait()


def settle(mates, attention, weights, first, second, small_first, small_second):
    block_rows = weights.shape[1]
    anywhere = pl.BlockSpec(memory_space=pl.ANY)
    devices = 16
    piece = (CHUNK, D)
    tokens = mates[0]["low_in"].shape[0]
    share = attention[0].shape[2]
    at = Layout(devices)
    length = share * devices
    halved = (at.groups, length // at.groups, LANES)
    early = [mates[0][name] for name in MATES if name not in LATE] + [mates[1][name] for name in MATES] + list(attention)
    return pl.pallas_call(
        functools.partial(settle_kernel, block_rows, tokens),
        out_shape=[
            jax.ShapeDtypeStruct(weights.shape, F32),
            jax.ShapeDtypeStruct(weights.shape, F32),
            jax.ShapeDtypeStruct((devices, 2, 2, D), F32),
            jax.ShapeDtypeStruct((MICRO, share, D), F32),
        ],
        in_specs=[VMEM] * len(early) + [anywhere] * 3 + [VMEM] * 2,
        out_specs=[VMEM] * 4,
        scratch_shapes=[
            pltpu.VMEM((LAYERS * 2 * (D + FF), tokens), BF16),
            pltpu.VMEM((LAYERS * 6, tokens, D), BF16),
            pltpu.VMEM((2, 4, 2) + piece, BF16),
            pltpu.VMEM((RING, 4, 2) + piece, BF16),
            pltpu.VMEM((RING, 4, 2) + piece, BF16),
            pltpu.VMEM((RING, 4) + piece, BF16),
            pltpu.VMEM((RING, 2, 2) + piece, BF16),
            pltpu.VMEM((RING, 2) + piece, BF16),
            pltpu.VMEM((4, 3) + piece, F32),
            pltpu.VMEM((RING,) + piece, BF16),
            pltpu.VMEM((RING,) + piece, BF16),
            pltpu.VMEM((devices, 2, D), F32),
            pltpu.VMEM((devices, 2, D), F32),
            pltpu.VMEM((2, 2, D), F32),
            pltpu.VMEM((2, D), BF16),
            pltpu.VMEM((2, D), BF16),
            DMA((2,)),
            DMA((RING,)),
            DMA((RING,)),
            DMA((RING,)),
            DMA((RING, 2)),
            DMA((RING, 2)),
            DMA((RING,)),
            DMA((RING,)),
            DMA((4, 3)),
            DMA((RING,)),
            DMA((RING,)),
            DMA((devices,)),
            DMA((devices,)),
            DMA((devices,)),
            DMA((devices,)),
            DMA((2,)),
            DMA((2,)),
            pltpu.VMEM((3, MICRO, share, D), BF16),
            pltpu.VMEM((PAIRS, 2, 2 * LANES), F32),
            pltpu.VMEM((1,) + halved, BF16),
            pltpu.VMEM((length + LANES, LANES), BF16),
            pltpu.VMEM((length + LANES, LANES), BF16),
            pltpu.VMEM((length, LANES), F32),
            pltpu.VMEM((3,) + halved, BF16),
            pltpu.VMEM((MICRO, share, D), F32),
            DMA((at.tasks,)),
            DMA((at.members,)),
            DMA((at.members,)),
            DMA((at.tasks,)),
        ],
        compiler_params=pltpu.CompilerParams(collective_id=3, has_side_effects=True, vmem_limit_bytes=63 << 20),
        name="settle",
    )(*early, weights, first, second, small_first, small_second)


def finish_kernel(both, params, outer, first, second, first_new, second_new, outer_new, params_new, grad, mean):
    for level in range(LAYERS):
        for line in range(LINES):
            index = level * LINES + line
            spot = slice(index % 2, index % 2 + 1)
            for which, target in ((0, grad), (1, mean)):
                target[level : level + 1, line * D : (line + 1) * D] = both[index // 2, which, spot, :]
    first_new[...], second_new[...] = moments(first[...], second[...], grad[:, :SMALL])
    momentum = MOMENTUM * outer[...] + mean[:, :SMALL]
    outer_new[...] = momentum
    params_new[...] = params[...] - LR_OUTER * (mean[:, :SMALL] + MOMENTUM * momentum)


def finish(both, params, outer, first, second):
    wide = pltpu.VMEM((LAYERS, LINES * D), F32)
    return pl.pallas_call(
        finish_kernel,
        out_shape=[jax.ShapeDtypeStruct(params.shape, F32)] * 4,
        in_specs=[VMEM] * 5,
        out_specs=[VMEM] * 4,
        scratch_shapes=[wide, wide],
        name="finish",
    )(both, params, outer, first, second)


def dense(a, b, dims=NN):
    return mm(a, b, dims)


def standard(values):
    centred = values - jnp.mean(values, axis=-1, keepdims=True)
    scale = lax.rsqrt(jnp.mean(centred * centred, axis=-1, keepdims=True) + 1e-05)
    return centred * scale, scale


def layer_norm(values, gain, shift):
    return standard(values)[0] * gain + shift


def layer_norm_back(values, gain, grad):
    unit_values, scale = standard(values)
    inner = grad * gain
    along = jnp.mean(inner * unit_values, axis=-1, keepdims=True)
    result = scale * (inner - jnp.mean(inner, axis=-1, keepdims=True) - unit_values * along)
    return result, eighths(grad * unit_values), eighths(grad)


def eighths(rows):
    return jnp.sum(rows.reshape(-1, 8, D), axis=0)


def split_rows(rest):
    return rest[:D], rest[D : D + FF], rest[D + FF :]


def forward_layer(count, inputs, proj, rest, small, edges, ident, low=None, spans=()):
    piece = inputs.shape[0] // MICRO
    lines, bias_up = small
    proj = proj.reshape(3, D, D)
    low_in = inputs.astype(BF16)
    query = (dense(low_in, proj[0]) + lines[0:1]).astype(BF16)
    key = dense(low_in, proj[1]).astype(BF16)
    value = (dense(low_in, proj[2]) + lines[1:2]).astype(BF16)
    qkv = jnp.stack([query, key, value])
    low_comb, kept, fetched = attention_forward(count, qkv.reshape(3, MICRO, piece, D), edges, lines, ident, low, spans)
    out_weight, up_weight, down_weight = split_rows(rest)
    low_comb = low_comb.reshape(MICRO * piece, D)
    resid_one = inputs + (dense(low_comb, out_weight) + lines[2:3])
    hidden_one = layer_norm(resid_one, lines[4:5], lines[5:6])
    low_hidden = hidden_one.astype(BF16)
    upward = dense(low_hidden, up_weight, NT) + bias_up
    low_act = jax.nn.gelu(upward).astype(BF16)
    resid_two = hidden_one + (dense(low_act, down_weight) + lines[3:4])
    output = layer_norm(resid_two, lines[6:7], lines[7:8])
    return output, (proj, rest, low_in, kept, low_comb, resid_one, low_hidden, upward, low_act, resid_two), fetched


def backward_layer(count, grad_output, small, edges, state, ident, carried=(), later=False):
    proj, rest, low_in, kept, low_comb, resid_one, low_hidden, upward, low_act, resid_two = state
    total = low_in.shape[0]
    piece = total // MICRO
    lines, _ = small
    out_weight, up_weight, down_weight = split_rows(rest)
    grad_two, grad_gain_two, grad_shift_two = layer_norm_back(resid_two, lines[6:7], grad_output)
    low_down = grad_two.astype(BF16)
    grad_act = dense(low_down, down_weight, NT)
    _, pull_gelu = jax.vjp(jax.nn.gelu, upward)
    low_up = pull_gelu(grad_act)[0].astype(BF16)
    grad_hidden = grad_two + dense(low_up, up_weight)
    grad_one, grad_gain_one, grad_shift_one = layer_norm_back(resid_one, lines[4:5], grad_hidden)
    low_branch = grad_one.astype(BF16)
    grad_comb = dense(low_branch, out_weight, NT).astype(BF16)
    vectors = (grad_gain_one, grad_shift_one, grad_gain_two, grad_shift_two)
    if later:
        names = [name for name in MATES if name not in LATE]
        values = (low_in, low_comb, low_up, low_act, low_branch, low_hidden, low_down, *vectors)
        return None, dict(zip(names, values)), (grad_comb.reshape(1, MICRO, piece, D), edges, lines, proj, grad_one, *kept)
    low_grads, grad_taps, swapped = attention_backward(count, grad_comb.reshape(1, MICRO, piece, D), edges, lines, kept, ident, carried)
    low_grads = low_grads.reshape(3, total, D)
    grad_in = grad_one + sum(dense(low_grads[part], proj[part], NT) for part in range(3))
    values = (low_in, low_comb, low_up, low_act, low_grads, low_branch, low_hidden, low_down, *vectors, grad_taps)
    return grad_in, dict(zip(MATES, values)), swapped


def plain_grads(mate):
    parts = [dense(mate["low_in"], mate["low_grads"][part], TN) for part in range(3)]
    parts = parts + [dense(mate[left], mate[right], TN) for left, right in (("low_comb", "low_branch"), ("low_up", "low_hidden"), ("low_act", "low_down"))]
    sums = [mate["low_grads"][0], mate["low_grads"][2], mate["low_branch"], mate["low_down"]]
    sums = [jnp.sum(one.astype(F32), axis=0) for one in sums]
    sums = sums + [jnp.sum(mate[name], axis=0) for name in MATES[8:12]]
    sums = sums + [jnp.sum(mate["low_up"].astype(F32), axis=0), mate["taps"][:, :, :TAPS].reshape(-1)]
    return jnp.concatenate(parts, axis=0).astype(BF16), jnp.concatenate(sums)


def moments(first, second, grad):
    return ADAM_ONE * first + (1.0 - ADAM_ONE) * grad, ADAM_TWO * second + (1.0 - ADAM_TWO) * grad * grad


def adam(weights, first, second, grad, rate, decay):
    correct_one = 1.0 - ADAM_ONE**STEP_COUNT
    correct_two = 1.0 - ADAM_TWO**STEP_COUNT
    new_first, new_second = moments(first, second, grad)
    step = new_first / correct_one / (jnp.sqrt(new_second / correct_two) + ADAM_EPSILON)
    return new_first, new_second, rate * (step + decay * weights)


def shards(
    hidden,
    bounds,
    cotangent,
    weights,
    small_params,
    first_big,
    second_big,
    first_small,
    second_small,
    outer_big,
    outer_small,
):
    count = lax.axis_size("dp")
    piece = hidden.shape[3]
    total = MICRO * piece
    low_weights = weights.astype(BF16)
    limits = bounds[0, :, 0, :]
    edges = jnp.pad(limits.astype(F32), ((0, 0), (0, LANES - limits.shape[1])))
    own_hidden, own_cotangent = hidden[0, :, 0], cotangent[0, :, 0]
    me = lax.axis_index("dp")
    start, last = me * piece, limits[:, -1].reshape(MICRO, 1, 1)
    if count == 16:
        (proj, rest), prepared, (own_hidden, own_cotangent) = gather(
            low_weights, ((0, 0, 1), (0, 1, PLANES)), own_hidden, own_cotangent, small_params, first_small[0], second_small[0]
        )
        half = count // MICRO
        start = (lax.broadcasted_iota(jnp.int32, (MICRO, 1, 1), 0) * half + lax.rem(me, half)) * piece
        last = jnp.where(me < half, limits[0, -1], limits[1, -1])
    else:
        prepared = arranged(small_params, first_small[0], second_small[0])
    positions = start + lax.broadcasted_iota(jnp.int32, (MICRO, piece, 1), 1)
    valid = positions < last
    activation = own_hidden.reshape(total, D).astype(F32)
    states = [None] * LAYERS
    smalls = [(prepared[level], prepared[LAYERS + level]) for level in range(LAYERS)]
    for level in range(LAYERS):
        if count == 16:
            spans = ((level + 1, 0, 1), (level + 1, 1, PLANES)) if level + 1 < LAYERS else ()
            activation, states[level], more = forward_layer(
                count, activation, proj, rest, smalls[level], edges, 1 + 4 * level, low_weights, spans
            )
            proj, rest = more or (None, None)
        else:
            rows = lax.all_gather(low_weights[level], "dp", axis=0, tiled=True)
            activation, states[level], _ = forward_layer(count, activation, rows[: 3 * D], rows[3 * D :], smalls[level], edges, 1)
    gradient = jnp.where(valid, own_cotangent.astype(F32), 0.0).reshape(total, D)
    mates = [None] * LAYERS
    for level in reversed(range(LAYERS)):
        carried = (activation.reshape(MICRO, piece, D),) if count == 16 and level == LAYERS - 1 else ()
        later = count == 16 and level == 0
        gradient, mates[level], swapped = backward_layer(count, gradient, smalls[level], edges, states[level], 2 + 4 * level, carried, later)
        activation = swapped[0] if carried else activation
    if count == 16:
        grad_big, mean_big, small_both, gradient = settle(
            mates, swapped, weights, first_big[0], second_big[0], *prepared[2 * LAYERS :]
        )
        new_smalls = finish(small_both, small_params, outer_small, first_small[0], second_small[0])
    else:
        rows, sums = zip(*[plain_grads(mate) for mate in mates])
        grad_big = jnp.stack([lax.psum_scatter(one, "dp", scatter_dimension=0, tiled=True).astype(F32) for one in rows])
        grad_small = lax.psum(jnp.stack(sums), "dp")
        reps = lax.axis_size("rep")
        delta_big = adam(weights, first_big[0], second_big[0], grad_big, LR_INNER, WEIGHT_DECAY)[2]
        delta_small = adam(small_params, first_small[0], second_small[0], grad_small, LR_SMALL, 0.0)[2]
        mean_big = lax.psum(delta_big.astype(BF16), "rep").astype(F32) / reps
        mean_small = lax.psum(delta_small.astype(BF16), "rep").astype(F32) / reps
        momentum = MOMENTUM * outer_small + mean_small
        new_smalls = (*moments(first_small[0], second_small[0], grad_small), momentum, small_params - LR_OUTER * (mean_small + MOMENTUM * momentum))
    new_first, new_second = moments(first_big[0], second_big[0], grad_big)
    new_first_small, new_second_small, outer_small_new, small_new = new_smalls
    outer_big_new = MOMENTUM * outer_big + mean_big
    weights_new = weights - LR_OUTER * (mean_big + MOMENTUM * outer_big_new)
    shape = (1, MICRO, 1, piece, D)
    return (
        activation.reshape(shape),
        gradient.reshape(shape),
        new_first[None],
        new_second[None],
        new_first_small[None],
        new_second_small[None],
        outer_big_new,
        outer_small_new,
        weights_new,
        small_new,
        weights_new.astype(BF16),
    )


def solution(mesh):
    placed = (
        P("rep", None, None, "dp", None),
        P("rep", None, None, None),
        P("rep", None, None, "dp", None),
        P(None, "dp", None),
        P(),
        P("rep", None, "dp", None),
        P("rep", None, "dp", None),
        P("rep", None, None),
        P("rep", None, None),
        P(None, "dp", None),
        P(),
    )
    return jax.shard_map(
        shards,
        mesh=mesh,
        in_specs=placed,
        out_specs=(
            P("rep", None, None, "dp", None),
            P("rep", None, None, "dp", None),
            P("rep", None, "dp", None),
            P("rep", None, "dp", None),
            P("rep", None, None),
            P("rep", None, None),
            P(None, "dp", None),
            P(),
            P(None, "dp", None),
            P(),
            P(None, "dp", None),
        ),
        check_vma=False,
    )
```
